32 devices in a mesh: batch: 4 (over z), seq: 8 (over y, x, core).
Axes of the slice: x: 2, y: 2, z: 4, core: 2. Of those that a mesh axis runs over, the one named last changes fastest.
Arguments:
- inputs: bfloat16 [4, 1024, 1024], P('batch', 'seq'), may hold values from -6 to 6
- lengths: int32 [4], P('batch'), may hold values from 256 to 1024, as said below
- adapter_index: int32 [4], P('batch'), may hold values from 0 to 7
- memory_picks: int32 [4, 1024, 4, 32], P('batch', 'seq'), may hold values from 0 to 65535, as said below
- input_weights: bfloat16 [5, 1024, 1024], replicated, may hold values from -0.1875 to 0.1875
- output_weights: bfloat16 [2, 1024, 1024], replicated, may hold values from -0.75 to 0.75
- adapter_down: bfloat16 [7, 8, 1024, 16], replicated, may hold values from -0.1875 to 0.1875
- adapter_up: bfloat16 [7, 8, 16, 1024], replicated, may hold values from -0.75 to 0.75
- attention_gain: bfloat16 [1024], replicated, may hold values from 0.099609375 to 1.8984375
- memory_gain: bfloat16 [1024], replicated, may hold values from 0.099609375 to 1.8984375
- half_keys: bfloat16 [2, 4, 256, 128], replicated, may hold values from -0.5 to 0.5
- memory_values: bfloat16 [65536, 1024], P(('batch', 'seq')), may hold values from -6 to 6
- cotangent: bfloat16 [4, 1024, 1024], P('batch', 'seq'), may hold values from -6 to 6
Outputs:
- output: bfloat16 [4, 1024, 1024], P('batch', 'seq')
- grad_input: bfloat16 [4, 1024, 1024], P('batch', 'seq')
- grad_down: float32 [7, 8, 1024, 16], replicated
- grad_up: float32 [7, 8, 16, 1024], replicated
The draws below stay inside these ranges and needn't reach their ends.
Inputs may be any that keep to these rules, and one draw needn't show every extreme that they name: The valid tokens of a sequence are its first lengths slots; some sequence fills all 1024 slots and some has exactly 256. `memory_picks`: the 32 picks of one token and memory head are distinct rows of one owner, owner k holding rows k * 2048 to (k + 1) * 2048 - 1 in the order of batch+seq. Among the 128 slots of one sequence on one device, at most 32 token-head pairs pick in the rows of any one owner, and in every draw some owner gets exactly 32 such pairs from every device.
All inputs are finite; a program needn't handle non-finite values.
Results may differ from the reference program's by a relative error of at most 0.022.
Values may be sent and summed in bfloat16 or wider, within the bound.
No kernel may reach another device: no remote copies, remote signals or barrier semaphores. Data moves between devices by JAX's collectives and lax.ppermute only.
A program may use at most 192 MiB of HBM per device.

```python
import jax
import jax.numpy as jnp
import numpy as np
from jax import lax

D = 1024
HEADS = 16
HEAD_DIM = 64
MHEADS = 4
KHALF = 128
NSUB = 256
PICKS = 32
RANK = 16
ADAPTERS = 8
TOK_DEV = 128
SLOTS = 1024
SEQS = 4
MEM_ROWS = 65536
OWNERS = 32
ROWS_DEV = 2048
CAP = 32


def draw_lengths(key, part):
    base = jax.random.randint(jax.random.fold_in(key, 1), (SEQS,), SLOTS // 4, SLOTS + 1)
    ordering = jax.random.permutation(jax.random.fold_in(key, 2), SEQS)
    base = base.at[ordering[0]].set(SLOTS)
    base = base.at[ordering[1]].set(SLOTS // 4)
    return base.astype(jnp.int32)


def draw_memory_picks(key, part):
    visits = TOK_DEV * MHEADS
    quarter = OWNERS // 4
    counts = np.array([CAP] * quarter + [3 * CAP // 4] * quarter + [CAP // 4] * quarter + [0] * (OWNERS - 3 * quarter))
    entries = jnp.asarray(np.repeat(np.arange(OWNERS), counts).astype(np.int32))
    blocks = SEQS * (SLOTS // TOK_DEV)
    hottest = jax.random.randint(jax.random.fold_in(key, 11), (), 0, OWNERS).astype(jnp.int32)
    spots = jnp.arange(OWNERS, dtype=jnp.int32)

    def one_block(block_key):
        shuffled = jax.random.permutation(jax.random.fold_in(block_key, 1), OWNERS).astype(jnp.int32)
        placed = jnp.where(shuffled == hottest, shuffled[0], jnp.where(spots == 0, hottest, shuffled))
        visit_owner = placed[entries]
        mixing = jax.random.permutation(jax.random.fold_in(block_key, 2), visits)
        visit_owner = visit_owner[mixing]
        base = jax.random.randint(jax.random.fold_in(block_key, 3), (visits,), 0, ROWS_DEV)
        stride = jax.random.randint(jax.random.fold_in(block_key, 4), (visits,), 0, ROWS_DEV // 2) * 2 + 1
        local_rows = (base[:, None] + stride[:, None] * jnp.arange(PICKS)[None, :]) % ROWS_DEV
        return visit_owner[:, None] * ROWS_DEV + local_rows
    block_keys = jax.random.split(jax.random.fold_in(key, 12), blocks)
    drawn = jax.vmap(one_block)(block_keys)
    return drawn.reshape(SEQS, SLOTS, MHEADS, PICKS).astype(jnp.int32)


def place_ends(values, rng, least, high):
    spot = [jax.random.randint(jax.random.fold_in(rng, axis), (), 0, length) for axis, length in enumerate(values.shape)]
    widest = values.shape.index(max(values.shape))
    beside = spot[:widest] + [(spot[widest] + 1) % values.shape[widest]] + spot[widest + 1:]
    return values.at[tuple(spot)].set(least).at[tuple(beside)].set(high)


def block_levels(stream_key, extent, pieces, least, largest):
    loudness = 1.0
    for axis_at, blocks in pieces:
        heights = jax.random.uniform(jax.random.fold_in(jax.random.fold_in(stream_key, 6), axis_at), (blocks,), jnp.float32, least / len(pieces), largest / len(pieces))
        loudness = loudness * jnp.repeat(jnp.exp(heights), extent[axis_at] // blocks).reshape((-1,) + (1,) * (len(extent) - 1 - axis_at))
    return loudness


def bell_draw(stream_key, dims, width, reach, cuts=(), kind=jnp.bfloat16):
    values = width * jax.random.normal(stream_key, dims, jnp.float32)
    if cuts:
        values = values * block_levels(stream_key, dims, cuts, -0.22, 0.18)
    return jnp.clip(values, -reach, reach).astype(kind)


def setup_inputs(seed: int = 0) -> dict:
    splits = jax.random.split(jax.random.key(seed), 14)
    return {
        "inputs": bell_draw(splits[0], (SEQS, SLOTS, D), 1.0, 6.0, ((0, 4), (1, 8))),
        "lengths": draw_lengths(jax.random.fold_in(splits[13], 71), 0),
        "adapter_index": place_ends(jax.random.randint(splits[2], (SEQS,), 0, ADAPTERS), jax.random.fold_in(splits[2], 1), 0, ADAPTERS - 1).astype(jnp.int32),
        "memory_picks": draw_memory_picks(jax.random.fold_in(splits[13], 71), 0),
        "input_weights": bell_draw(splits[4], (5, D, D), D ** -0.5, 0.1875),
        "output_weights": bell_draw(splits[5], (2, D, D), (D // 16) ** -0.5, 0.75),
        "adapter_down": bell_draw(splits[6], (7, ADAPTERS, D, RANK), D ** -0.5, 0.1875),
        "adapter_up": bell_draw(splits[7], (7, ADAPTERS, RANK, D), (4 * RANK) ** -0.5, 0.75),
        "attention_gain": jnp.clip(1.0 + 0.18 * jax.random.normal(splits[8], (D,), jnp.float32), 0.099609375, 1.8984375).astype(jnp.bfloat16),
        "memory_gain": jnp.clip(1.0 + 0.18 * jax.random.normal(splits[9], (D,), jnp.float32), 0.099609375, 1.8984375).astype(jnp.bfloat16),
        "half_keys": bell_draw(splits[10], (2, MHEADS, NSUB, KHALF), KHALF ** -0.5, 0.5),
        "memory_values": bell_draw(splits[11], (MEM_ROWS, D), 1.0, 6.0, ((0, 32),)),
        "cotangent": bell_draw(splits[12], (SEQS, SLOTS, D), 1.0, 6.0, ((0, 4), (1, 8))),
    }


EPS = 1e-06
NEG = -1e+30
HIGH = lax.Precision.HIGHEST

@jax.custom_vjp
def low(v):
    return lax.optimization_barrier(v.astype(jnp.bfloat16)).astype(jnp.float32)

@jax.custom_vjp
def low_back(v):
    return v

def low_keep(v):
    return (low(v), None)

def low_pass(kept, grad):
    return (grad,)

def back_keep(v):
    return (v, None)

def back_low(kept, grad):
    return (low(grad),)
low.defvjp(low_keep, low_pass)
low_back.defvjp(back_keep, back_low)

def product(left_side, right_side):
    return jnp.dot(left_side, right_side, precision=HIGH, preferred_element_type=jnp.float32)

def normalize(values, scales):
    return values * lax.rsqrt(lax.optimization_barrier(jnp.mean(values * values, axis=-1, keepdims=True)) + EPS) * scales

def project(inputs, weight, down_map, up_map):
    lowrank = low_back(low(product(inputs, down_map)))
    return product(inputs, weight) + product(lowrank, up_map)

def attend(queries, key_rows, value_rows, valid_length):
    rows_all = queries.shape[0]
    block_rows = min(512, rows_all)
    query_heads = queries.reshape(rows_all, HEADS, HEAD_DIM)
    key_heads = key_rows.reshape(rows_all, HEADS, HEAD_DIM)
    value_heads = value_rows.reshape(rows_all, HEADS, HEAD_DIM)
    key_place = jnp.arange(rows_all, dtype=jnp.int32)
    scaling = HEAD_DIM ** (-0.5)

    def one_block(offset):
        query_block = lax.dynamic_slice_in_dim(query_heads, offset, block_rows, 0)
        query_place = offset + jnp.arange(block_rows, dtype=jnp.int32)
        scores = low_back(jnp.einsum('qhc,khc->hqk', query_block, key_heads, precision=HIGH) * scaling)
        allowed = (key_place[None, :] <= query_place[:, None]) & (key_place[None, :] < valid_length)
        scores = jnp.where(allowed[None], scores, NEG)
        shifted = scores - lax.optimization_barrier(jnp.max(scores, axis=2, keepdims=True))
        exponent = jnp.exp(shifted)
        probability = low(exponent / lax.optimization_barrier(jnp.sum(exponent, axis=2, keepdims=True)))
        mixture = jnp.einsum('hqk,khc->qhc', probability, value_heads, precision=HIGH)
        mixture = jnp.where((query_place < valid_length)[:, None, None], mixture, 0.0)
        return mixture.reshape(block_rows, D)
    starts = jnp.arange(0, rows_all, block_rows, dtype=jnp.int32)
    return lax.map(jax.checkpoint(one_block), starts).reshape(rows_all, D)

def recall(memory_query, half_keys, memory_table, pick_rows):
    rows_all = memory_query.shape[0]
    query_halves = memory_query.reshape(rows_all, MHEADS, 2, KHALF)
    first_scores = low_back(jnp.einsum('thc,hjc->thj', query_halves[:, :, 0], half_keys[0], precision=HIGH))
    second_scores = low_back(jnp.einsum('thc,hjc->thj', query_halves[:, :, 1], half_keys[1], precision=HIGH))
    first_index = (pick_rows // NSUB).astype(jnp.int32)
    second_index = (pick_rows % NSUB).astype(jnp.int32)
    scores = jnp.take_along_axis(first_scores, first_index, axis=2) + jnp.take_along_axis(second_scores, second_index, axis=2)
    shifted = scores - lax.optimization_barrier(jnp.max(scores, axis=2, keepdims=True))
    exponent = jnp.exp(shifted)
    pick_weights = low(exponent / lax.optimization_barrier(jnp.sum(exponent, axis=2, keepdims=True)))
    block_rows = min(64, rows_all)

    def one_block(offset):
        weight_block = lax.dynamic_slice_in_dim(pick_weights, offset, block_rows, 0)
        index_block = lax.dynamic_slice_in_dim(pick_rows, offset, block_rows, 0)
        fetched = jnp.take(memory_table, index_block, axis=0)
        per_head = low(jnp.einsum('thk,thkd->thd', weight_block, fetched, precision=HIGH))
        return lax.optimization_barrier(jnp.sum(per_head, axis=1))
    offsets = jnp.arange(0, rows_all, block_rows, dtype=jnp.int32)
    return lax.map(jax.checkpoint(one_block), offsets).reshape(rows_all, D)

def layer(stream, valid_length, adapter, pick_rows, input_maps, output_maps, down_all, up_all, attention_gain, memory_gain, half_keys, memory_table):
    down_map = lax.dynamic_index_in_dim(down_all, adapter, 1, keepdims=False)
    up_map = lax.dynamic_index_in_dim(up_all, adapter, 1, keepdims=False)
    normed = low(normalize(stream, attention_gain))
    queries = low_back(low(project(normed, input_maps[0], down_map[0], up_map[0])))
    key_rows = low_back(low(project(normed, input_maps[1], down_map[1], up_map[1])))
    value_rows = low_back(low(project(normed, input_maps[2], down_map[2], up_map[2])))
    attended = low_back(low(attend(queries, key_rows, value_rows, valid_length)))
    branch = low_back(project(attended, output_maps[0], down_map[3], up_map[3]))
    middle = stream + branch
    normed_two = low(normalize(middle, memory_gain))
    memory_query = low_back(low(project(normed_two, input_maps[3], down_map[4], up_map[4])))
    gate_value = low_back(project(normed_two, input_maps[4], down_map[5], up_map[5]))
    memory = low_back(recall(memory_query, half_keys, memory_table, pick_rows))
    mixture = low_back(low(memory * (gate_value * jax.nn.sigmoid(gate_value))))
    result = project(mixture, output_maps[1], down_map[6], up_map[6])
    return middle + low_back(result)

def reference(inputs, lengths, adapter_index, memory_picks, input_weights, output_weights, adapter_down, adapter_up, attention_gain, memory_gain, half_keys, memory_values, cotangent):
    input_maps = input_weights.astype(jnp.float32)
    output_maps = output_weights.astype(jnp.float32)
    first_gain = attention_gain.astype(jnp.float32)
    second_gain = memory_gain.astype(jnp.float32)
    key_table = half_keys.astype(jnp.float32)
    memory_table = memory_values.astype(jnp.float32)

    def forward(stream_all, down_all, up_all):

        def per_sequence(running, sequence_items):
            stream, valid_length, adapter, pick_rows = sequence_items
            result = layer(stream, valid_length, adapter, pick_rows, input_maps, output_maps, down_all, up_all, first_gain, second_gain, key_table, memory_table)
            return (running, result)
        unused, outputs = lax.scan(per_sequence, jnp.zeros((), jnp.float32), (stream_all, lengths, adapter_index, memory_picks))
        return outputs
    outputs, pullback = jax.vjp(forward, inputs.astype(jnp.float32), adapter_down.astype(jnp.float32), adapter_up.astype(jnp.float32))
    grad_input, grad_down, grad_up = pullback(cotangent.astype(jnp.float32))
    return (outputs.astype(jnp.bfloat16), grad_input.astype(jnp.bfloat16), grad_down, grad_up)
```

```python
import functools

import jax
import jax.numpy as jnp
from jax import lax
from jax.experimental import pallas as pl
from jax.experimental.pallas import tpu as pltpu
from jax.sharding import PartitionSpec as P

HEAD_DIM = 64
MHEADS = 4
KHALF = 128
NSUB = 256
PICKS = 32
ADAPTERS = 8
RANK = 16
LANES = 128
EPS = 1e-06
NEG = -1e30
F32 = jnp.float32
BF16 = jnp.bfloat16
I32 = jnp.int32
ANY = pl.BlockSpec(memory_space=pl.ANY)
SMEM = pl.BlockSpec(memory_space=pltpu.SMEM)
VMEM = pl.BlockSpec(memory_space=pltpu.VMEM)
MIB = 1 << 20


def product(left, right):
    return lax.dot_general(left, right, (((1,), (0,)), ((), ())), preferred_element_type=F32)


def against(left, right):
    return lax.dot_general(left, right, (((1,), (1,)), ((), ())), preferred_element_type=F32)


def contract(left, right):
    return lax.dot_general(left, right, (((0,), (0,)), ((), ())), preferred_element_type=F32)


def iota(shape, axis):
    return lax.broadcasted_iota(I32, shape, axis)


def lane_pick(table, index):
    return jnp.take_along_axis(table, index, axis=1, mode="promise_in_bounds")


def shaped(shape, dtype):
    return jax.ShapeDtypeStruct(shape, dtype)


def call(kernel, name, outs, specs, scratch=(), vmem=32, flops=1 << 28, moved=1 << 22, aliases=None):
    many = isinstance(outs, (list, tuple))
    return pl.pallas_call(
        kernel,
        name=name,
        out_shape=outs,
        in_specs=specs,
        out_specs=[VMEM] * len(outs) if many else VMEM,
        scratch_shapes=list(scratch),
        input_output_aliases=aliases or {},
        compiler_params=pltpu.CompilerParams(vmem_limit_bytes=vmem * MIB),
        cost_estimate=pl.CostEstimate(flops=flops, bytes_accessed=moved, transcendentals=0),
    )


def fetch(pairs, sems):
    copies = [
        pltpu.make_async_copy(source, target, sems.at[place])
        for place, (source, target) in enumerate(pairs)
    ]
    for copy in copies:
        copy.start()
    return copies


def sema(count):
    return pltpu.SemaphoreType.DMA((count,))


def inverse_norm(values):
    return lax.rsqrt(jnp.mean(values * values, axis=1, keepdims=True) + EPS)


def norm_back(values, inverse, scales, incoming):
    weighted = incoming * scales
    inner = jnp.mean(weighted * values, axis=1, keepdims=True)
    return weighted * inverse - values * inverse * inverse * inverse * inner


def qkv_kernel(adapter, x_ref, gain_ref, w_any, dn_any, up_any, out_ref, norm_ref, rank_ref, w, dn, up, sems):
    groups, tokens, wide = out_ref.shape
    cols = wide // 3
    a = adapter[0]
    copies = fetch(
        [(dn_any.at[j, a], dn.at[pl.ds(RANK * j, RANK)]) for j in range(3)]
        + [(up_any.at[j, a], up.at[pl.ds(RANK * j, RANK)]) for j in range(3)]
        + [(w_any.at[j], w.at[j]) for j in range(3)],
        sems,
    )
    x = x_ref[...].astype(F32)
    normed = (x * inverse_norm(x) * gain_ref[...].astype(F32)).astype(BF16)
    norm_ref[...] = normed
    for copy in copies[:6]:
        copy.wait()
    ranks = against(normed, dn[...]).astype(BF16)
    rank_ref[...] = ranks
    place = iota((tokens, 3 * RANK), 1) // RANK
    for j in range(3):
        own = jnp.where(place == j, ranks.astype(F32), 0.0).astype(BF16)
        extra = product(own, up[...])
        copies[6 + j].wait()
        result = (product(normed, w[j]) + extra).astype(BF16)
        for s in range(groups):
            out_ref[s, :, j * cols : (j + 1) * cols] = result[:, s * cols : (s + 1) * cols]


def mix_back_kernel(adapter, cot_ref, w_any, dn_any, up_any, grad_ref, rank_ref, w, dn, up, sems):
    a = adapter[0]
    copies = fetch([(up_any.at[6, a], up), (dn_any.at[6, a], dn), (w_any.at[1], w)], sems)
    gy = cot_ref[...]
    copies[0].wait()
    ranks = against(gy, up[...]).astype(BF16)
    rank_ref[...] = ranks
    copies[1].wait()
    extra = product(ranks, dn[...])
    copies[2].wait()
    grad_ref[...] = (against(gy, w[...]) + extra).astype(BF16)


def route_kernel(rows_dev, owners, adapter, picks_ref, slot_ref, slot_col_ref, pick_ref, ids_ref):
    heads, picks, tokens = picks_ref.shape
    capacity = 2 * heads * tokens // owners
    groups = capacity // 8
    visits = heads * tokens
    owner = jnp.concatenate([picks_ref[h, 0:1, :] for h in range(heads)], axis=1) // rows_dev
    hot = jnp.where(iota((owners, visits), 0) == owner, 1.0, 0.0)
    before = jnp.where(iota((visits, visits), 0) < iota((visits, visits), 1), 1.0, 0.0).astype(BF16)
    counts = product(hot.astype(BF16), before)
    within = jnp.sum(hot * counts, axis=0, keepdims=True).astype(I32)
    slot = owner * capacity + within
    rows = [slot[:, h * tokens : (h + 1) * tokens] for h in range(heads)]
    stacked = jnp.concatenate(rows + [jnp.full((8 - heads, tokens), -1, I32)], axis=0)
    slot_ref[...] = stacked
    tall = jnp.concatenate([stacked, jnp.full((tokens - 8, tokens), -1, I32)], axis=0)
    slot_col_ref[...] = jnp.transpose(tall)
    packed = jnp.concatenate([picks_ref[h] for h in range(heads)], axis=0)
    by_token = jnp.transpose(packed)
    pick_ref[...] = by_token
    local = by_token % rows_dev
    lanes = iota((tokens, LANES), 1)
    total = jnp.zeros((owners * 8, LANES), F32)
    out_lane = iota((owners * 8, LANES), 1) // PICKS
    place = iota((owners * 8, tokens), 0)
    base = (place // 8) * capacity + place % 8
    for g in range(groups):
        high = jnp.zeros((owners * 8, LANES), F32)
        low = jnp.zeros((owners * 8, LANES), F32)
        for h in range(heads):
            chosen = jnp.where(base + g * 8 == rows[h], 1.0, 0.0).astype(BF16)
            own = jnp.where(lanes // PICKS == h, local, 0)
            own = tile_groups(own.astype(F32), heads).astype(I32)
            high = high + product(chosen, (own // 256).astype(F32).astype(BF16))
            low = low + product(chosen, (own % 256).astype(F32).astype(BF16))
        total = jnp.where(out_lane == g, high * 256.0 + low, total)
    ids_ref[...] = total.astype(I32) + adapter[0] * 65536


def tile_groups(values, count):
    total = values
    for turn in range(1, count):
        total = total + pltpu.roll(values, turn * PICKS, 1)
    return total


def prepare_kernel(groups, ids_ref, mask_ref, high_ref):
    senders = ids_ref.shape[0] // 8
    capacity = groups * 8

    def one(sender, carry):
        start = pl.multiple_of(sender * 8, 8)
        ids = ids_ref[pl.ds(start, 8), :] & 65535
        lane = iota((8, LANES), 1)
        high_total = jnp.zeros((8, LANES), I32)
        for g in range(groups):
            mask = jnp.zeros((8, LANES), I32)
            for r in range(PICKS):
                at = g * PICKS + r
                bit = (1 << r) if r < 31 else -(1 << 31)
                spread = jnp.broadcast_to(ids[:, at : at + 1], (8, LANES))
                mask = mask | jnp.where((spread & 127) == lane, bit, 0)
                high_total = high_total | jnp.where((spread >> 7) + g * PICKS == lane, bit, 0)
            mask_ref[pl.ds(pl.multiple_of(sender * capacity + g * 8, 8), 8), :] = mask
        high_ref[pl.ds(start, 8), :] = high_total
        return carry

    lax.fori_loop(0, senders, one, 0)


def recall_kernel(groups, mask_ref, high_ref, weight_ref, mem_any, out_any, mem, dense, staged, sems):
    items = mask_ref.shape[0]
    rows_dev = mem.shape[0]
    capacity = groups * 8
    chunks = rows_dev // LANES
    block = dense.shape[0]
    per_block = block // capacity
    copy = pltpu.make_async_copy(mem_any, mem, sems.at[0])
    copy.start()
    blocks = items // block
    for b in range(blocks):

        def one(local, carry):
            sender = b * per_block + local
            start = pl.multiple_of(sender * 8, 8)
            highs = high_ref[pl.ds(start, 8), :]
            weights = weight_ref[pl.ds(start, 8), :].astype(F32)
            for g in range(groups):
                mask = mask_ref[pl.ds(pl.multiple_of(sender * capacity + g * 8, 8), 8), :]
                for c in range(chunks):
                    at = g * PICKS + c
                    chosen = mask & jnp.broadcast_to(highs[:, at : at + 1], (8, LANES))
                    index = ((31 - lax.clz(chosen)) + g * PICKS) & 127
                    value = jnp.where(chosen != 0, lane_pick(weights, index), 0.0)
                    dense[pl.ds(pl.multiple_of(local * capacity + g * 8, 8), 8), c * LANES : (c + 1) * LANES] = value
            return carry

        lax.fori_loop(0, per_block, one, 0)
        if b == 0:
            copy.wait()
        if b >= 2:
            pltpu.make_async_copy(staged.at[b % 2], out_any.at[pl.ds((b - 2) * block, block)], sems.at[1 + b % 2]).wait()
        staged[b % 2] = product(dense[...].astype(BF16), mem[...]).astype(BF16)
        pltpu.make_async_copy(staged.at[b % 2], out_any.at[pl.ds(b * block, block)], sems.at[1 + b % 2]).start()
    for b in range(max(0, blocks - 2), blocks):
        pltpu.make_async_copy(staged.at[b % 2], out_any.at[pl.ds(b * block, block)], sems.at[1 + b % 2]).wait()


def recall_back_kernel(groups, ids_ref, grad_any, mem_any, out_ref, mem, grads, scores, sems):
    items = grad_any.shape[0]
    rows_dev = mem.shape[0]
    capacity = groups * 8
    chunks = rows_dev // LANES
    block = scores.shape[0]
    per_block = block // capacity
    blocks = items // block
    copies = fetch(
        [(mem_any, mem)] + [(grad_any.at[pl.ds(b * block, block)], grads.at[pl.ds(b * block, block)]) for b in range(blocks)],
        sems,
    )
    copies[0].wait()
    for b in range(blocks):
        copies[1 + b].wait()
        scores[...] = against(grads[b * block : (b + 1) * block, :], mem[...])

        def one(local, carry):
            start = pl.multiple_of((b * per_block + local) * 8, 8)
            ids = ids_ref[pl.ds(start, 8), :] & 65535
            low = ids & 127
            high = ids >> 7
            lane_group = iota((8, LANES), 1) // PICKS
            total = jnp.zeros((8, LANES), F32)
            for g in range(groups):
                key = jnp.where(lane_group == g, high, -1)
                for c in range(chunks):
                    part = scores[pl.ds(pl.multiple_of(local * capacity + g * 8, 8), 8), c * LANES : (c + 1) * LANES]
                    total = jnp.where(key == c, lane_pick(part, low), total)
            out_ref[pl.ds(start, 8), :] = total.astype(out_ref.dtype)
            return carry

        lax.fori_loop(0, per_block, one, 0)


def head_parts(values, h, spare):
    lane = iota(values.shape, 1)
    return jnp.where(lane // HEAD_DIM == h, values, jnp.where(lane == (1 - h) * HEAD_DIM, spare, 0.0)).astype(BF16)


def widen(values):
    if values.shape[1] == LANES:
        return values
    return jnp.concatenate([values, jnp.zeros((values.shape[0], LANES - values.shape[1]), values.dtype)], axis=1)


def attend_kernel(length, qkv_ref, o_ref, lse_ref):
    rows, wide = qkv_ref.shape
    cols = wide // 3
    heads = cols // HEAD_DIM
    size = min(256, rows)
    valid = length[0]
    bias = jnp.where(iota((rows, LANES), 0) < valid, 0.0, NEG)
    keys = widen(qkv_ref[:, cols : 2 * cols].astype(F32))
    key_parts = [head_parts(keys, h, bias) for h in range(heads)]
    values_t = jnp.transpose(widen(qkv_ref[:, 2 * cols :].astype(F32))).astype(BF16)
    for i in range(rows // size):
        first, last = i * size, (i + 1) * size
        queries = widen(qkv_ref[first:last, 0:cols].astype(F32)) * (HEAD_DIM**-0.5)
        mixed = jnp.zeros((LANES, size), F32)
        stats = []
        for h in range(heads):
            query = head_parts(queries, h, 1.0)
            near = against(key_parts[h][first:last], query)
            near = jnp.where(iota((size, size), 0) <= iota((size, size), 1), near, NEG)
            high = jnp.max(near, axis=0, keepdims=True)
            if i:
                far = against(key_parts[h][:first], query)
                high = jnp.maximum(high, jnp.max(far, axis=0, keepdims=True))
            near = jnp.exp(near - high)
            summed = jnp.sum(near, axis=0, keepdims=True)
            result = product(values_t[:, first:last], near.astype(BF16))
            if i:
                far = jnp.exp(far - high)
                summed = summed + jnp.sum(far, axis=0, keepdims=True)
                result = result + product(values_t[:, :first], far.astype(BF16))
            stats.append(high + jnp.log(summed))
            mixed = jnp.where(iota((LANES, size), 0) // HEAD_DIM == h, result / summed, mixed)
        mixed = jnp.where(first + iota((LANES, size), 1) < valid, mixed, 0.0)
        o_ref[first:last, :] = jnp.transpose(mixed)[:, :cols].astype(BF16)
        lse_ref[:, first:last] = jnp.concatenate(stats + [jnp.zeros((8 - heads, size), F32)], axis=0)


def attend_back_kernel(length, qkv_ref, go_ref, lse_ref, out_ref, dk, dv):
    rows, wide = qkv_ref.shape
    cols = wide // 3
    heads = cols // HEAD_DIM
    size = min(256, rows)
    valid = length[0]
    scaling = HEAD_DIM**-0.5
    bias = jnp.where(iota((rows, LANES), 0) < valid, 0.0, NEG)
    keys = widen(qkv_ref[:, cols : 2 * cols].astype(F32))
    keys_t = jnp.transpose(keys).astype(BF16)
    key_parts = [head_parts(keys, h, bias) for h in range(heads)]
    values = widen(qkv_ref[:, 2 * cols :])
    dk[...] = jnp.zeros_like(dk)
    dv[...] = jnp.zeros_like(dv)
    for i in range(rows // size):
        first, last = i * size, (i + 1) * size
        queries = widen(qkv_ref[first:last, 0:cols].astype(F32)) * scaling
        grads = widen(go_ref[first:last, :].astype(F32))
        dq = jnp.zeros((LANES, size), F32)
        for h in range(heads):
            query = head_parts(queries, h, 1.0)
            plain = head_parts(queries, h, 0.0)
            grad = head_parts(grads, h, 0.0)
            lse = lse_ref[h : h + 1, first:last]
            near = against(key_parts[h][first:last], query)
            near = jnp.where(iota((size, size), 0) <= iota((size, size), 1), near, NEG)
            near = jnp.exp(near - lse)
            near_gp = against(values[first:last], grad)
            delta = jnp.sum(near * near_gp, axis=0, keepdims=True)
            if i:
                far = jnp.exp(against(key_parts[h][:first], query) - lse)
                far_gp = against(values[:first], grad)
                delta = delta + jnp.sum(far * far_gp, axis=0, keepdims=True)
            near_gs = (near * (near_gp - delta)).astype(BF16)
            result = product(keys_t[:, first:last], near_gs)
            dk[first:last] += product(near_gs, plain)
            dv[first:last] += product(near.astype(BF16), grad)
            if i:
                far_gs = (far * (far_gp - delta)).astype(BF16)
                result = result + product(keys_t[:, :first], far_gs)
                dk[:first] += product(far_gs, plain)
                dv[:first] += product(far.astype(BF16), grad)
            dq = jnp.where(iota((LANES, size), 0) // HEAD_DIM == h, result, dq)
        out_ref[first:last, 0:cols] = (jnp.transpose(dq) * scaling)[:, :cols].astype(BF16)
    out_ref[:, cols : 2 * cols] = dk[:, :cols].astype(BF16)
    out_ref[:, 2 * cols :] = dv[:, :cols].astype(BF16)


def pick_chosen(tables, index):
    tokens = index.shape[0]
    low = index & 127
    key = (index >> 7) + (iota((tokens, LANES), 1) // PICKS) * (NSUB // LANES)
    total = jnp.zeros((tokens, LANES), F32)
    for h in range(MHEADS):
        for c in range(NSUB // LANES):
            found = lane_pick(tables[h][:, c * LANES : (c + 1) * LANES], low)
            total = jnp.where(key == h * (NSUB // LANES) + c, found, total)
    return total


def group_reduce(values, reducer, fill):
    group = iota(values.shape, 1) // PICKS
    total = jnp.zeros(values.shape, F32)
    for h in range(MHEADS):
        one = reducer(jnp.where(group == h, values, fill), axis=1, keepdims=True)
        total = jnp.where(group == h, one, total)
    return total


def middle_kernel(
    owners, adapter, o_ref, x_ref, gain_ref, picks_ref, slot_ref, keys_ref, w_in_any, w_out_any, dn_any, up_any,
    att_ref, rank_ref, mid_ref, norm_ref, weight_ref, send_ref, w, dn, up, sems,
):
    groups, tokens, cols = o_ref.shape
    a = adapter[0]
    copies = fetch(
        [(dn_any.at[3, a], dn.at[pl.ds(0, RANK)]), (dn_any.at[4, a], dn.at[pl.ds(RANK, RANK)]),
         (up_any.at[3, a], up.at[pl.ds(0, RANK)]), (up_any.at[4, a], up.at[pl.ds(RANK, RANK)]),
         (w_out_any.at[0], w.at[0]), (w_in_any.at[3], w.at[1])],
        sems,
    )
    attended = jnp.concatenate([o_ref[s] for s in range(groups)], axis=1)
    att_ref[...] = attended
    for copy in copies[:4]:
        copy.wait()
    rank_three = against(attended, dn[0:RANK, :]).astype(BF16)
    extra = product(rank_three, up[0:RANK, :])
    copies[4].wait()
    middle = x_ref[...].astype(F32) + (product(attended, w[0]) + extra)
    mid_ref[...] = middle
    normed = (middle * inverse_norm(middle) * gain_ref[...].astype(F32)).astype(BF16)
    norm_ref[...] = normed
    rank_four = against(normed, dn[RANK:, :]).astype(BF16)
    rank_ref[0] = rank_three
    rank_ref[1] = rank_four
    extra = product(rank_four, up[RANK:, :])
    copies[5].wait()
    query = (product(normed, w[1]) + extra).astype(BF16)
    first, second = [], []
    for h in range(MHEADS):
        base = 2 * h * KHALF
        first.append(against(query[:, base : base + KHALF], keys_ref[0, h]))
        second.append(against(query[:, base + KHALF : base + 2 * KHALF], keys_ref[1, h]))
    picks = picks_ref[...]
    scores = pick_chosen(first, picks // NSUB) + pick_chosen(second, picks % NSUB)
    exponent = jnp.exp(scores - group_reduce(scores, jnp.max, NEG))
    weights = exponent / group_reduce(exponent, jnp.sum, 0.0)
    weight_ref[...] = weights
    send_ref[...] = to_slots(weights, slot_ref, owners).astype(BF16)


def to_slots(weights, slot_ref, owners):
    tokens = weights.shape[0]
    capacity = 2 * MHEADS * tokens // owners
    lane_group = iota((tokens, LANES), 1) // PICKS
    tiled = [
        tile_groups(jnp.where(lane_group == h, weights, 0.0), MHEADS).astype(BF16) for h in range(MHEADS)
    ]
    place = iota((owners * 8, tokens), 0)
    base = (place // 8) * capacity + place % 8
    out_group = iota((owners * 8, LANES), 1) // PICKS
    total = jnp.zeros((owners * 8, LANES), F32)
    for g in range(capacity // 8):
        part = jnp.zeros((owners * 8, LANES), F32)
        for h in range(MHEADS):
            chosen = jnp.where(base + g * 8 == slot_ref[h : h + 1, :], 1.0, 0.0).astype(BF16)
            part = part + product(chosen, tiled[h])
        total = jnp.where(out_group == g, part, total)
    return total


def gate_kernel(
    owners, adapter, norm_ref, mix_ref, slot_ref, w_in_any, dn_any, up_any,
    rank_ref, gate_ref, grad_ref, w, dn, up, sems,
):
    tokens = norm_ref.shape[0]
    a = adapter[0]
    copies = fetch([(dn_any.at[5, a], dn), (up_any.at[5, a], up), (w_in_any.at[4], w)], sems)
    normed = norm_ref[...]
    copies[0].wait()
    ranks = against(normed, dn[...]).astype(BF16)
    rank_ref[...] = ranks
    copies[1].wait()
    extra = product(ranks, up[...])
    copies[2].wait()
    gate = product(normed, w[...]) + extra
    gate_ref[...] = gate
    memory_grad = (mix_ref[...].astype(F32) * (gate * jax.nn.sigmoid(gate))).astype(BF16)
    slots = grad_ref.shape[0]
    block = min(slots, 256)
    for b in range(slots // block):
        place = b * block + iota((block, tokens), 0)
        chosen = jnp.zeros((block, tokens), F32)
        for h in range(MHEADS):
            chosen = jnp.where(place == slot_ref[h : h + 1, :], 1.0, chosen)
        grad_ref[b * block : (b + 1) * block, :] = product(chosen.astype(BF16), memory_grad).astype(BF16)


def output_kernel(
    adapter, back_ref, slot_ref, gate_ref, mix_ref, mid_ref, w_in_any, w_out_any, dn_any, up_any,
    out_ref, mixed_ref, rank_ref, grank_ref, ggate_ref, part_ref, w, dn, up, sems,
):
    tokens = gate_ref.shape[0]
    slots = back_ref.shape[0]
    a = adapter[0]
    copies = fetch(
        [(dn_any.at[5, a], dn.at[0]), (up_any.at[5, a], up.at[0]), (dn_any.at[6, a], dn.at[1]),
         (up_any.at[6, a], up.at[1]), (w_in_any.at[4], w.at[0]), (w_out_any.at[1], w.at[1])],
        sems,
    )
    place = iota((tokens, slots), 1)
    chosen = jnp.zeros((tokens, slots), F32)
    for h in range(MHEADS):
        chosen = jnp.where(place == slot_ref[:, h : h + 1], 1.0, chosen)
    memory = product(chosen.astype(BF16), back_ref[...])
    gate = gate_ref[...]
    sigmoid = jax.nn.sigmoid(gate)
    mixed = (memory * (gate * sigmoid)).astype(BF16)
    mixed_ref[...] = mixed
    ggate = (mix_ref[...].astype(F32) * memory * sigmoid * (1.0 + gate * (1.0 - sigmoid))).astype(BF16)
    ggate_ref[...] = ggate
    for copy in copies[:4]:
        copy.wait()
    granks = against(ggate, up[0]).astype(BF16)
    grank_ref[...] = granks
    extra = product(granks, dn[0])
    copies[4].wait()
    part_ref[...] = against(ggate, w[0]) + extra
    ranks = against(mixed, dn[1]).astype(BF16)
    rank_ref[...] = ranks
    extra = product(ranks, up[1])
    copies[5].wait()
    out_ref[...] = (mid_ref[...] + (product(mixed, w[1]) + extra)).astype(BF16)


def query_kernel(
    owners, rows_dev, length, adapter, back_ref, slot_ref, picks_ref, weight_ref, part_ref, mid_ref, cot_ref, gain_ref,
    keys_ref, w_in_any, w_out_any, dn_any, up_any,
    go_ref, gquery_ref, grank_ref, gmid_ref, w, dn, up, sems,
):
    groups, tokens, cols = go_ref.shape
    a = adapter[0]
    copies = fetch(
        [(dn_any.at[3, a], dn.at[0]), (dn_any.at[4, a], dn.at[1]), (up_any.at[3, a], up.at[0]),
         (up_any.at[4, a], up.at[1]), (w_in_any.at[3], w.at[0]), (w_out_any.at[0], w.at[1])],
        sems,
    )
    capacity = 2 * MHEADS * tokens // owners
    slots = iota((tokens, owners * 8), 1)
    base = (slots // 8) * capacity + slots % 8
    lane_group = iota((tokens, LANES), 1) // PICKS
    back = back_ref[...]
    gw = jnp.zeros((tokens, LANES), F32)
    for h in range(MHEADS):
        part = jnp.zeros((tokens, LANES), F32)
        for g in range(capacity // 8):
            chosen = jnp.where(base + g * 8 == slot_ref[:, h : h + 1], 1.0, 0.0).astype(BF16)
            part = jnp.where(lane_group == g, product(chosen, back), part)
        gw = jnp.where(lane_group == h, tile_groups(part, MHEADS), gw)
    weights = weight_ref[...]
    gscore = weights * (gw - group_reduce(weights * gw, jnp.sum, 0.0))
    picks = picks_ref[...]
    first = picks // NSUB
    second = picks % NSUB
    lane = iota((tokens, LANES), 1)
    chunks = NSUB // LANES
    halves = []
    for h in range(MHEADS):
        sums = [[jnp.zeros((tokens, LANES), F32) for _ in range(chunks)] for _ in range(2)]
        for r in range(PICKS):
            at = h * PICKS + r
            value = jnp.broadcast_to(gscore[:, at : at + 1], (tokens, LANES))
            for half, index in enumerate((first, second)):
                spread = jnp.broadcast_to(index[:, at : at + 1], (tokens, LANES))
                for c in range(chunks):
                    sums[half][c] = sums[half][c] + jnp.where(spread == lane + c * LANES, value, 0.0)
        for half in range(2):
            both = jnp.concatenate(sums[half], axis=1).astype(BF16)
            halves.append(product(both, keys_ref[half, h]))
    gquery = jnp.concatenate(halves, axis=1).astype(BF16)
    gquery_ref[...] = gquery
    for copy in copies[:4]:
        copy.wait()
    granks = against(gquery, up[1]).astype(BF16)
    grank_ref[1] = granks
    extra = product(granks, dn[1])
    copies[4].wait()
    gnormed = against(gquery, w[0]) + extra + part_ref[...]
    middle = mid_ref[...]
    gmid = cot_ref[...].astype(F32) + norm_back(middle, inverse_norm(middle), gain_ref[...].astype(F32), gnormed)
    gmid_ref[...] = gmid
    low = gmid.astype(BF16)
    granks = against(low, up[0]).astype(BF16)
    grank_ref[0] = granks
    extra = product(granks, dn[0])
    copies[5].wait()
    go = against(low, w[1]) + extra
    row = lax.axis_index("seq") * tokens + iota((tokens, 1), 0)
    go = jnp.where(row < length[0], go, 0.0).astype(BF16)
    for s in range(groups):
        go_ref[s] = go[:, s * cols : (s + 1) * cols]


def place_columns(out_ref, row, values):
    groups, _, cols = out_ref.shape
    low = values.astype(BF16)
    for s in range(groups):
        out_ref[s, row : row + values.shape[0], :] = low[:, s * cols : (s + 1) * cols]


def factor_kernel(att_ref, norm_ref, mixed_ref, gmid_ref, gquery_ref, ggate_ref, cot_ref, r34, r5, r6, g34, g5, g6, out_ref):
    half = 4 * RANK
    sides = (
        (att_ref[...], gmid_ref[...].astype(BF16), r34[0], g34[0]),
        (norm_ref[...], gquery_ref[...], r34[1], g34[1]),
        (norm_ref[...], ggate_ref[...], r5[...], g5[...]),
        (mixed_ref[...], cot_ref[...], r6[...], g6[...]),
    )
    for j, (value, gy, rank, grank) in enumerate(sides):
        place_columns(out_ref, j * RANK, contract(grank, value))
        place_columns(out_ref, half + j * RANK, contract(rank, gy))


def entry_factor_kernel(adapter, grad_ref, norm_ref, ranks_ref, up_any, out_ref, gy_ref, grank_ref, up, sems):
    groups, tokens, wide = grad_ref.shape
    cols = wide // 3
    a = adapter[0]
    copies = fetch([(up_any.at[j, a], up.at[pl.ds(RANK * j, RANK)]) for j in range(3)], sems)
    gys = [
        jnp.concatenate([grad_ref[s, :, j * cols : (j + 1) * cols] for s in range(groups)], axis=1) for j in range(3)
    ]
    for copy in copies:
        copy.wait()
    place = iota((tokens, 3 * RANK), 1) // RANK
    granks = jnp.zeros((tokens, 3 * RANK), F32)
    ranks = ranks_ref[...]
    for j in range(3):
        gy_ref[j] = gys[j]
        granks = jnp.where(place == j, against(gys[j], up[...]), granks)
        up_grad = contract(ranks, gys[j])
        place_columns(out_ref, (3 + j) * RANK, up_grad[j * RANK : (j + 1) * RANK, :])
    granks = granks.astype(BF16)
    grank_ref[...] = granks
    place_columns(out_ref, 0, contract(granks, norm_ref[...]))


def entry_kernel(adapter, gy_ref, grank_ref, x_ref, gain_ref, gmid_ref, w_any, dn_any, out_ref, w, dn, sems):
    a = adapter[0]
    copies = fetch(
        [(dn_any.at[j, a], dn.at[pl.ds(RANK * j, RANK)]) for j in range(3)] + [(w_any.at[j], w.at[j]) for j in range(3)],
        sems,
    )
    x = x_ref[...].astype(F32)
    for copy in copies[:3]:
        copy.wait()
    total = product(grank_ref[...], dn[...])
    for j in range(3):
        copies[3 + j].wait()
        total = total + against(gy_ref[j], w[j])
    back = norm_back(x, inverse_norm(x), gain_ref[...].astype(F32), total)
    out_ref[...] = (gmid_ref[...] + back).astype(BF16)


def sum_kernel(parts_ref, out_ref):
    total = parts_ref[0].astype(F32)
    for s in range(1, parts_ref.shape[0]):
        total = total + parts_ref[s].astype(F32)
    total = total.astype(BF16)
    if len(out_ref.shape) == 2:
        out_ref[...] = total
    else:
        for k in range(out_ref.shape[0]):
            out_ref[k] = total


def spread_kernel(batches, ids_ref, early_ref, late_ref, down_any, up_any, stage, sems):
    seq = early_ref.shape[0] // batches
    cols = early_ref.shape[2]
    marks = [ids_ref[b * seq * 8 : b * seq * 8 + 1, 0:1] // 65536 for b in range(batches)]
    targets = (down_any, up_any)
    started = []
    count = 0
    for j in range(7):
        source, half, spot = (late_ref, 3, j) if j < 3 else (early_ref, 4, j - 3)
        for which in range(2):
            row = (which * half + spot) * RANK
            slot = count % 2
            if count >= 2:
                started[count - 2].wait()
            rows = [
                jnp.concatenate([source[b * seq + s, row : row + RANK, :] for s in range(seq)], axis=1).astype(F32)
                for b in range(batches)
            ]
            for k in range(ADAPTERS):
                total = jnp.zeros(rows[0].shape, F32)
                for b in range(batches):
                    total = total + jnp.where(marks[b] == k, rows[b], 0.0)
                stage[slot, k] = total
            copy = pltpu.make_async_copy(stage.at[slot], targets[which].at[j], sems.at[slot])
            copy.start()
            started.append(copy)
            count += 1
    started[-2].wait()
    started[-1].wait()


def exchange(values, axes):
    return lax.all_to_all(values, axes, split_axis=0, concat_axis=0, tiled=True)


def body(
    inputs, lengths, adapter_index, memory_picks, input_weights, output_weights, adapter_down, adapter_up,
    attention_gain, memory_gain, half_keys, memory_values, cotangent,
):
    both = ("batch", "seq")
    batches, seq = lax.axis_size("batch"), lax.axis_size("seq")
    owners = batches * seq
    tokens, width = inputs.shape[1], inputs.shape[2]
    rows = tokens * seq
    cols = width // seq
    rows_dev = memory_values.shape[0]
    capacity = 2 * tokens * MHEADS // owners
    groups = capacity // 8
    items = owners * capacity
    x, cot = inputs[0], cotangent[0]
    down = jnp.swapaxes(adapter_down, 2, 3)
    gain_one, gain_two = attention_gain.reshape(1, width), memory_gain.reshape(1, width)
    picks = jnp.transpose(memory_picks[0], (1, 2, 0))
    matrix = pltpu.VMEM((width, width), BF16)
    pair = pltpu.VMEM((2, width, width), BF16)
    triple = pltpu.VMEM((3, width, width), BF16)
    small = pltpu.VMEM((RANK, width), BF16)
    two_small = pltpu.VMEM((2, RANK, width), BF16)
    row_small = pltpu.VMEM((2 * RANK, width), BF16)
    three_small = pltpu.VMEM((3 * RANK, width), BF16)

    qkv, normed, ranks = call(
        qkv_kernel, "qkv",
        (shaped((seq, tokens, 3 * cols), BF16), shaped((tokens, width), BF16), shaped((tokens, 3 * RANK), BF16)),
        [SMEM, VMEM, VMEM, ANY, ANY, ANY], [triple, three_small, three_small, sema(9)],
    )(adapter_index, x, gain_one, input_weights, down, adapter_up)
    qkv_all = exchange(qkv, "seq").reshape(rows, 3 * cols)

    slot, slot_col, pick, ids_out = call(
        functools.partial(route_kernel, rows_dev, owners), "route",
        (shaped((8, tokens), I32), shaped((tokens, tokens), I32), shaped((tokens, LANES), I32), shaped((owners * 8, LANES), I32)),
        [SMEM, VMEM],
    )(adapter_index, picks)
    mix_grad, grank_six = call(
        mix_back_kernel, "mixback", (shaped((tokens, width), BF16), shaped((tokens, RANK), BF16)),
        [SMEM, VMEM, ANY, ANY, ANY], [matrix, small, small, sema(3)],
    )(adapter_index, cot, output_weights, down, adapter_up)

    attended, lse = call(
        attend_kernel, "attend", (shaped((rows, cols), BF16), shaped((8, rows), F32)), [SMEM, VMEM],
    )(lengths, qkv_all)
    o_all = exchange(attended.reshape(seq, tokens, cols), "seq")
    ids_out, qkv_all = lax.optimization_barrier((ids_out, qkv_all))
    ids = exchange(ids_out.reshape(owners, 8, LANES), both).reshape(owners * 8, LANES)
    ids, o_all = lax.optimization_barrier((ids, o_all))
    mask, high = call(
        functools.partial(prepare_kernel, groups), "prepare",
        (shaped((items, LANES), I32), shaped((owners * 8, LANES), I32)), [VMEM],
    )(ids)

    att, rank_pair, middle, normed_two, weights, weight_out = call(
        functools.partial(middle_kernel, owners), "middle",
        (shaped((tokens, width), BF16), shaped((2, tokens, RANK), BF16), shaped((tokens, width), F32),
         shaped((tokens, width), BF16), shaped((tokens, LANES), F32), shaped((owners * 8, LANES), BF16)),
        [SMEM, VMEM, VMEM, VMEM, VMEM, VMEM, VMEM, ANY, ANY, ANY, ANY], [pair, row_small, row_small, sema(6)],
    )(adapter_index, o_all, x, gain_two, pick, slot, half_keys, input_weights, output_weights, down, adapter_up)
    weight_in = exchange(weight_out.reshape(owners, 8, LANES), both).reshape(owners * 8, LANES)

    rank_five, gate, grad_out = call(
        functools.partial(gate_kernel, owners), "gate",
        (shaped((tokens, RANK), BF16), shaped((tokens, width), F32), shaped((items, width), BF16)),
        [SMEM, VMEM, VMEM, VMEM, ANY, ANY, ANY], [matrix, small, small, sema(3)],
    )(adapter_index, normed_two, mix_grad, slot, input_weights, down, adapter_up)
    weight_in, grad_out = lax.optimization_barrier((weight_in, grad_out))
    grad_in = exchange(grad_out.reshape(owners, capacity, width), both).reshape(items, width)

    block = min(items, 256)
    blocks = items // block
    sums = pl.pallas_call(
        functools.partial(recall_kernel, groups), name="recall", out_shape=shaped((items, width), BF16),
        in_specs=[VMEM, VMEM, VMEM, ANY], out_specs=ANY,
        scratch_shapes=[pltpu.VMEM((rows_dev, width), BF16), pltpu.VMEM((block, rows_dev), F32), pltpu.VMEM((2, block, width), BF16), sema(3)],
        compiler_params=pltpu.CompilerParams(vmem_limit_bytes=32 * MIB),
        cost_estimate=pl.CostEstimate(flops=1 << 32, bytes_accessed=8 << 20, transcendentals=0),
    )(mask, high, weight_in, memory_values)
    sums, grad_in = lax.optimization_barrier((sums, grad_in))
    back = exchange(sums.reshape(owners, capacity, width), both).reshape(items, width)

    found = call(
        functools.partial(recall_back_kernel, groups), "recallback", shaped((owners * 8, LANES), BF16),
        [VMEM, ANY, ANY],
        [pltpu.VMEM((rows_dev, width), BF16), pltpu.VMEM((items, width), BF16), pltpu.VMEM((block, rows_dev), F32), sema(1 + blocks)],
        flops=1 << 32,
    )(ids, grad_in, memory_values)
    found, back = lax.optimization_barrier((found, back))
    found_back = exchange(found.reshape(owners, 8, LANES), both).reshape(owners * 8, LANES)

    output, mixed, rank_six, grank_five, ggate, part = call(
        output_kernel, "output",
        (shaped((tokens, width), BF16), shaped((tokens, width), BF16), shaped((tokens, RANK), BF16),
         shaped((tokens, RANK), BF16), shaped((tokens, width), BF16), shaped((tokens, width), F32)),
        [SMEM, VMEM, VMEM, VMEM, VMEM, VMEM, ANY, ANY, ANY, ANY], [pair, two_small, two_small, sema(6)],
    )(adapter_index, back, slot_col, gate, mix_grad, middle, input_weights, output_weights, down, adapter_up)

    go, gquery, grank_pair, gmid = call(
        functools.partial(query_kernel, owners, rows_dev), "query",
        (shaped((seq, tokens, cols), BF16), shaped((tokens, width), BF16), shaped((2, tokens, RANK), BF16), shaped((tokens, width), F32)),
        [SMEM, SMEM, VMEM, VMEM, VMEM, VMEM, VMEM, VMEM, VMEM, VMEM, VMEM, ANY, ANY, ANY, ANY],
        [pair, two_small, two_small, sema(6)],
    )(lengths, adapter_index, found_back, slot_col, pick, weights, part, middle, cot, gain_two, half_keys,
      input_weights, output_weights, down, adapter_up)
    go_all = exchange(go, "seq").reshape(rows, cols)

    factors = call(
        factor_kernel, "factors", shaped((seq, 8 * RANK, cols), BF16), [VMEM] * 13,
    )(att, normed_two, mixed, gmid, gquery, ggate, cot, rank_pair, rank_five, rank_six, grank_pair, grank_five, grank_six)
    factors, go_all = lax.optimization_barrier((factors, go_all))
    early = call(sum_kernel, "sumearly", shaped((8 * RANK, cols), BF16), [VMEM])(exchange(factors, "seq"))
    early_all = lax.all_gather(early, both, axis=0, tiled=False)

    grads = call(
        attend_back_kernel, "attendback", shaped((rows, 3 * cols), BF16), [SMEM, VMEM, VMEM, VMEM],
        [pltpu.VMEM((rows, LANES), F32), pltpu.VMEM((rows, LANES), F32)], vmem=40,
    )(lengths, qkv_all, go_all, lse)
    grads_all = exchange(grads.reshape(seq, tokens, 3 * cols), "seq")

    late, gys, granks = call(
        entry_factor_kernel, "entryfactors",
        (shaped((seq, 6 * RANK, cols), BF16), shaped((3, tokens, width), BF16), shaped((tokens, 3 * RANK), BF16)),
        [SMEM, VMEM, VMEM, VMEM, ANY], [three_small, sema(3)],
    )(adapter_index, grads_all, normed, ranks, adapter_up)
    late_parts = exchange(late, "seq")
    late_sum = call(sum_kernel, "sumlate", shaped((owners, 6 * RANK, cols), BF16), [VMEM])(late_parts)
    late_all = exchange(late_sum, both)
    grad_input = call(
        entry_kernel, "entry", shaped((tokens, width), BF16), [SMEM, VMEM, VMEM, VMEM, VMEM, VMEM, ANY, ANY],
        [triple, three_small, sema(6)],
    )(adapter_index, gys, granks, x, gain_one, gmid, input_weights, down)
    full = shaped((7, ADAPTERS, RANK, width), F32)
    grad_down, grad_up = pl.pallas_call(
        functools.partial(spread_kernel, batches), name="spread", out_shape=(full, full),
        in_specs=[VMEM, VMEM, VMEM], out_specs=[ANY, ANY],
        scratch_shapes=[pltpu.VMEM((2, ADAPTERS, RANK, width), F32), sema(2)],
        compiler_params=pltpu.CompilerParams(vmem_limit_bytes=32 * MIB),
    )(ids, early_all, late_all)
    return (output[None], grad_input[None], jnp.swapaxes(grad_down, 2, 3), grad_up)


def solution(mesh):
    split = P("batch", "seq", None)
    return jax.shard_map(
        body,
        mesh=mesh,
        in_specs=(
            split, P("batch"), P("batch"), P("batch", "seq", None, None), P(), P(), P(), P(), P(), P(), P(),
            P(("batch", "seq"), None), split,
        ),
        out_specs=(split, split, P(), P()),
        check_vma=False,
    )
```

```python
import functools

import jax
import jax.numpy as jnp
from jax import lax
from jax.experimental import pallas as pl
from jax.experimental.pallas import tpu as pltpu
from jax.sharding import PartitionSpec as P

HEAD_DIM = 64
MHEADS = 4
KHALF = 128
NSUB = 256
PICKS = 32
ADAPTERS = 8
RANK = 16
LANES = 128
EPS = 1e-06
NEG = -1e30
F32 = jnp.float32
BF16 = jnp.bfloat16
I32 = jnp.int32
HBM = pl.BlockSpec(memory_space=pltpu.HBM)
SMEM = pl.BlockSpec(memory_space=pltpu.SMEM)
VMEM = pl.BlockSpec(memory_space=pltpu.VMEM)
MIB = 1 << 20


def product(left, right):
    return lax.dot_general(left, right, (((1,), (0,)), ((), ())), preferred_element_type=F32)


def against(left, right):
    return lax.dot_general(left, right, (((1,), (1,)), ((), ())), preferred_element_type=F32)


def contract(left, right):
    return lax.dot_general(left, right, (((0,), (0,)), ((), ())), preferred_element_type=F32)


def iota(shape, axis):
    return lax.broadcasted_iota(I32, shape, axis)


def lane_pick(table, index):
    return jnp.take_along_axis(table, index, axis=1, mode="promise_in_bounds")


def shaped(shape, dtype):
    return jax.ShapeDtypeStruct(shape, dtype)


def call(kernel, name, ins, outs, args, scratch=(), vmem=40, flops=1 << 28, moved=1 << 22, aliases=None):
    shapes = [(args[i].shape, args[i].dtype) for i, kind in enumerate(ins) if kind == "L"]
    stored = [(out.shape, out.dtype) for kind, out in outs if kind == "S"]
    count_in, count_out, count_user = len(ins), len(outs), len(scratch)

    def wrapped(*refs):
        given, results = list(refs[:count_in]), list(refs[count_in : count_in + count_out])
        rest = list(refs[count_in + count_out :])
        user, buffers = rest[:count_user], rest[count_user:]
        loads, stores = [], []
        for i, kind in enumerate(ins):
            if kind == "L":
                at = len(loads)
                loads.append(pltpu.make_async_copy(given[i], buffers[at], buffers[-1].at[at]))
                given[i] = buffers[at]
        for i, (kind, _) in enumerate(outs):
            if kind == "S":
                at = len(loads) + len(stores)
                stores.append(pltpu.make_async_copy(buffers[at], results[i], buffers[-1].at[at]))
                results[i] = buffers[at]
        for copy in loads:
            copy.start()

        def ready():
            for copy in loads:
                copy.wait()

        kernel(ready, *given, *results, *user)
        for copy in stores:
            copy.start()
        for copy in stores:
            copy.wait()

    spaces = {"V": VMEM, "L": HBM, "S": HBM, "H": HBM, "M": SMEM}
    autos = [pltpu.VMEM(*one) for one in shapes + stored]
    args = [
        pltpu.with_memory_space_constraint(one, pltpu.HBM) if kind in "LH" else one
        for kind, one in zip(ins, args, strict=True)
    ]
    return pl.pallas_call(
        wrapped,
        name=name,
        out_shape=[pltpu.HBM(out.shape, out.dtype) if kind in "SH" else out for kind, out in outs],
        in_specs=[spaces[kind] for kind in ins],
        out_specs=[spaces[kind] for kind, _ in outs],
        input_output_aliases=aliases or {},
        scratch_shapes=list(scratch) + autos + ([sema(len(autos))] if autos else []),
        compiler_params=pltpu.CompilerParams(vmem_limit_bytes=vmem * MIB),
        cost_estimate=pl.CostEstimate(flops=flops, bytes_accessed=moved, transcendentals=0),
    )(*args)


def fetch(pairs, sems):
    copies = [
        pltpu.make_async_copy(source, target, sems.at[place])
        for place, (source, target) in enumerate(pairs)
    ]
    for copy in copies:
        copy.start()
    return copies


def sema(count):
    return pltpu.SemaphoreType.DMA((count,))


def gain_row(ref):
    return ref[...].astype(F32)


def inverse_norm(values):
    return lax.rsqrt(jnp.mean(values * values, axis=1, keepdims=True) + EPS)


def norm_back(values, inverse, scales, incoming):
    weighted = incoming * scales
    inner = jnp.mean(weighted * values, axis=1, keepdims=True)
    return weighted * inverse - values * inverse * inverse * inverse * inner


def qkv_kernel(ready, adapter, x_ref, gain_ref, w_any, dn_any, up_any, out_ref, norm_ref, rank_ref, w, dn, up, sems):
    groups, tokens, wide = out_ref.shape
    cols = wide // 3
    a = adapter[0]
    copies = fetch(
        [(dn_any.at[j, a], dn.at[pl.ds(RANK * j, RANK)]) for j in range(3)]
        + [(up_any.at[j, a], up.at[pl.ds(RANK * j, RANK)]) for j in range(3)]
        + [(w_any.at[j], w.at[j]) for j in range(3)],
        sems,
    )
    ready()
    x = x_ref[...].astype(F32)
    normed = (x * inverse_norm(x) * gain_row(gain_ref)).astype(BF16)
    norm_ref[...] = normed
    for copy in copies[:6]:
        copy.wait()
    ranks = against(normed, dn[...]).astype(BF16)
    rank_ref[...] = ranks
    place = iota((tokens, 3 * RANK), 1) // RANK
    for j in range(3):
        own = jnp.where(place == j, ranks.astype(F32), 0.0).astype(BF16)
        extra = product(own, up[...])
        copies[6 + j].wait()
        result = (product(normed, w[j]) + extra).astype(BF16)
        for s in range(groups):
            out_ref[s, :, j * cols : (j + 1) * cols] = result[:, s * cols : (s + 1) * cols]


def mix_back_kernel(ready, adapter, cot_ref, w_any, dn_any, up_any, grad_ref, rank_ref, w, dn, up, sems):
    a = adapter[0]
    copies = fetch([(up_any.at[6, a], up), (dn_any.at[6, a], dn), (w_any.at[1], w)], sems)
    ready()
    gy = cot_ref[...]
    copies[0].wait()
    ranks = against(gy, up[...]).astype(BF16)
    rank_ref[...] = ranks
    copies[1].wait()
    extra = product(ranks, dn[...])
    copies[2].wait()
    grad_ref[...] = (against(gy, w[...]) + extra).astype(BF16)


def route_kernel(rows_dev, owners, ready, adapter, picks_ref, slot_ref, slot_col_ref, pick_ref, ids_ref):
    ready()
    heads, picks, tokens = picks_ref.shape
    capacity = 2 * heads * tokens // owners
    groups = capacity // 8
    visits = heads * tokens
    owner = jnp.concatenate([picks_ref[h, 0:1, :] for h in range(heads)], axis=1) // rows_dev
    hot = jnp.where(iota((owners, visits), 0) == owner, 1.0, 0.0)
    before = jnp.where(iota((visits, visits), 0) < iota((visits, visits), 1), 1.0, 0.0).astype(BF16)
    counts = product(hot.astype(BF16), before)
    within = jnp.sum(hot * counts, axis=0, keepdims=True).astype(I32)
    slot = owner * capacity + within
    rows = [slot[:, h * tokens : (h + 1) * tokens] for h in range(heads)]
    stacked = jnp.concatenate(rows + [jnp.full((8 - heads, tokens), -1, I32)], axis=0)
    slot_ref[...] = stacked
    tall = jnp.concatenate([stacked, jnp.full((tokens - 8, tokens), -1, I32)], axis=0)
    slot_col_ref[...] = jnp.transpose(tall)
    packed = jnp.concatenate([picks_ref[h] for h in range(heads)], axis=0)
    by_token = jnp.transpose(packed)
    pick_ref[...] = by_token
    local = by_token % rows_dev
    lanes = iota((tokens, LANES), 1)
    total = jnp.zeros((owners * 8, LANES), F32)
    out_lane = iota((owners * 8, LANES), 1) // PICKS
    place = iota((owners * 8, tokens), 0)
    base = (place // 8) * capacity + place % 8
    for g in range(groups):
        high = jnp.zeros((owners * 8, LANES), F32)
        low = jnp.zeros((owners * 8, LANES), F32)
        for h in range(heads):
            chosen = jnp.where(base + g * 8 == rows[h], 1.0, 0.0).astype(BF16)
            own = jnp.where(lanes // PICKS == h, local, 0)
            own = tile_groups(own.astype(F32), heads).astype(I32)
            high = high + product(chosen, (own // 256).astype(F32).astype(BF16))
            low = low + product(chosen, (own % 256).astype(F32).astype(BF16))
        total = jnp.where(out_lane == g, high * 256.0 + low, total)
    ids_ref[...] = total.astype(I32) + adapter[0] * 65536


def tile_groups(values, count):
    total = values
    for turn in range(1, count):
        total = total + pltpu.roll(values, turn * PICKS, 1)
    return total


def prepare_kernel(groups, rows_dev, ready, ids_ref, index_any, stage, sems):
    ready()
    places = ids_ref.shape[0]
    block = stage.shape[1]
    chunks = rows_dev // LANES
    high_rows = max(8, chunks)
    count = 0
    for k in range(places // LANES):
        by_pick = jnp.transpose(ids_ref[k * LANES : (k + 1) * LANES, :] & 65535)
        for g in range(groups):
            mask = jnp.zeros((LANES, LANES), I32)
            highs = jnp.zeros((high_rows, LANES), I32)
            for r in range(PICKS):
                bit = (1 << r) if r < 31 else -(1 << 31)
                row = by_pick[g * PICKS + r : g * PICKS + r + 1, :]
                mask = mask | jnp.where(row & 127 == iota((LANES, LANES), 0), bit, 0)
                highs = highs | jnp.where(row >> 7 == iota((high_rows, LANES), 0), bit, 0)
            slot = count % 2
            target = index_any.at[pl.ds(g * places + k * LANES, LANES)]
            copy = pltpu.make_async_copy(stage.at[slot], target, sems.at[slot])
            if count >= 2:
                copy.wait()
            for c in range(chunks):
                index = 31 - lax.clz(mask & highs[c : c + 1, :])
                stage[slot, :, c * LANES : (c + 1) * LANES] = jnp.transpose(index)
            copy.start()
            count += 1
    for slot in range(min(2, count)):
        pltpu.make_async_copy(stage.at[slot], index_any.at[pl.ds(0, LANES)], sems.at[slot]).wait()


def recall_kernel(groups, ready, weight_ref, index_any, mem_any, out_ref, mem, index, dense, sems):
    places = weight_ref.shape[0]
    rows_dev = mem.shape[0]
    chunks = rows_dev // LANES
    block = dense.shape[0]
    per_group = places // block
    blocks = groups * per_group
    seq = out_ref.shape[0]
    planes = block // (8 * seq)

    def load(b):
        return pltpu.make_async_copy(index_any.at[pl.ds(b * block, block)], index.at[b % 2], sems.at[1 + b % 2])

    load(0).start()
    if blocks > 1:
        load(1).start()
    copy = pltpu.make_async_copy(mem_any, mem, sems.at[0])
    copy.start()
    ready()
    for b in range(blocks):
        g, k = b // per_group, b % per_group
        load(b).wait()

        def one(step, carry):
            start = pl.multiple_of(step * 16, 16)
            weights = weight_ref[pl.ds(pl.multiple_of(k * block + start, 16), 16), :].astype(F32)
            for c in range(chunks):
                at = index[b % 2, pl.ds(start, 16), c * LANES : (c + 1) * LANES]
                value = lane_pick(weights, (at + g * PICKS) & 127)
                dense[pl.ds(start, 16), c * LANES : (c + 1) * LANES] = jnp.where(at >= 0, value, 0.0).astype(BF16)
            return carry

        lax.fori_loop(0, block // 16, one, 0)
        if b + 2 < blocks:
            load(b + 2).start()
        if b == 0:
            copy.wait()
        result = product(dense[...], mem[...]).astype(BF16)
        for i in range(planes):
            rows = result[i * seq * 8 : (i + 1) * seq * 8]
            out_ref[:, k * planes + i, g * 8 : (g + 1) * 8, :] = rows.reshape(seq, 8, rows.shape[1])


def recall_back_kernel(part, batches, groups, ready, ids_ref, *refs):
    before_ref = refs[0] if part else None
    grad_ref, mem_any, out_ref, mem, scores, sems = refs[part:]
    items, half = grad_ref.shape
    seq = items // (batches * groups * 8)
    rows_dev = mem.shape[0]
    capacity = groups * 8
    chunks = rows_dev // LANES
    block = scores.shape[0]
    per_block = block // capacity
    blocks = items // block
    copies = fetch([(mem_any.at[:, pl.ds(part * half, half)], mem)], sems)
    ready()
    copies[0].wait()
    for b in range(blocks):
        scores[...] = against(grad_ref[b * block : (b + 1) * block, :], mem[...])

        def one(local, carry):
            sender = b * per_block + local
            spot = lax.rem(sender, batches) * seq + sender // batches
            start = pl.multiple_of(spot * 8, 8)
            ids = ids_ref[pl.ds(start, 8), :] & 65535
            low = ids & 127
            high = ids >> 7
            lane_group = iota((8, LANES), 1) // PICKS
            total = jnp.zeros((8, LANES), F32)
            for g in range(groups):
                key = jnp.where(lane_group == g, high, -1)
                for c in range(chunks):
                    found = scores[pl.ds(pl.multiple_of(local * capacity + g * 8, 8), 8), c * LANES : (c + 1) * LANES]
                    total = jnp.where(key == c, lane_pick(found, low), total)
            if part:
                total = total + before_ref[pl.ds(start, 8), :]
            out_ref[pl.ds(start, 8), :] = total.astype(out_ref.dtype)
            return carry

        lax.fori_loop(0, per_block, one, 0)


def head_parts(values, h, spare):
    lane = iota(values.shape, 1)
    return jnp.where(lane // HEAD_DIM == h, values, jnp.where(lane == (1 - h) * HEAD_DIM, spare, 0.0)).astype(BF16)


def widen(values):
    if values.shape[1] == LANES:
        return values
    return jnp.concatenate([values, jnp.zeros((values.shape[0], LANES - values.shape[1]), values.dtype)], axis=1)


def attend_kernel(ready, length, qkv_ref, o_ref, lse_ref, saved_any, sems):
    ready()
    saving = pltpu.make_async_copy(qkv_ref, saved_any, sems.at[0])
    saving.start()
    rows, wide = qkv_ref.shape
    cols = wide // 3
    heads = cols // HEAD_DIM
    size = min(256, rows)
    valid = length[0]
    bias = jnp.where(iota((rows, LANES), 0) < valid, 0.0, NEG)
    keys = widen(qkv_ref[:, cols : 2 * cols].astype(F32))
    key_parts = [head_parts(keys, h, bias) for h in range(heads)]
    values_t = jnp.transpose(widen(qkv_ref[:, 2 * cols :].astype(F32))).astype(BF16)
    for i in range(rows // size):
        first, last = i * size, (i + 1) * size
        queries = widen(qkv_ref[first:last, 0:cols].astype(F32)) * (HEAD_DIM**-0.5)
        mixed = jnp.zeros((LANES, size), F32)
        stats = []
        for h in range(heads):
            query = head_parts(queries, h, 1.0)
            near = against(key_parts[h][first:last], query)
            near = jnp.where(iota((size, size), 0) <= iota((size, size), 1), near, NEG)
            high = jnp.max(near, axis=0, keepdims=True)
            if i:
                far = against(key_parts[h][:first], query)
                high = jnp.maximum(high, jnp.max(far, axis=0, keepdims=True))
            near = jnp.exp(near - high)
            summed = jnp.sum(near, axis=0, keepdims=True)
            result = product(values_t[:, first:last], near.astype(BF16))
            if i:
                far = jnp.exp(far - high)
                summed = summed + jnp.sum(far, axis=0, keepdims=True)
                result = result + product(values_t[:, :first], far.astype(BF16))
            stats.append(high + jnp.log(summed))
            mixed = jnp.where(iota((LANES, size), 0) // HEAD_DIM == h, result / summed, mixed)
        mixed = jnp.where(first + iota((LANES, size), 1) < valid, mixed, 0.0)
        o_ref[first:last, :] = jnp.transpose(mixed)[:, :cols].astype(BF16)
        lse_ref[:, first:last] = jnp.concatenate(stats + [jnp.zeros((8 - heads, size), F32)], axis=0)
    saving.wait()


def attend_back_kernel(ready, length, qkv_ref, go_ref, lse_ref, out_ref, dk, dv):
    ready()
    rows, wide = qkv_ref.shape
    cols = wide // 3
    heads = cols // HEAD_DIM
    size = min(256, rows)
    valid = length[0]
    scaling = HEAD_DIM**-0.5
    bias = jnp.where(iota((rows, LANES), 0) < valid, 0.0, NEG)
    keys = widen(qkv_ref[:, cols : 2 * cols].astype(F32))
    keys_t = jnp.transpose(keys).astype(BF16)
    key_parts = [head_parts(keys, h, bias) for h in range(heads)]
    values = widen(qkv_ref[:, 2 * cols :])
    dk[...] = jnp.zeros_like(dk)
    dv[...] = jnp.zeros_like(dv)
    for i in range(rows // size):
        first, last = i * size, (i + 1) * size
        queries = widen(qkv_ref[first:last, 0:cols].astype(F32)) * scaling
        grads = widen(go_ref[first:last, :].astype(F32))
        dq = jnp.zeros((LANES, size), F32)
        for h in range(heads):
            query = head_parts(queries, h, 1.0)
            plain = head_parts(queries, h, 0.0)
            grad = head_parts(grads, h, 0.0)
            lse = lse_ref[h : h + 1, first:last]
            near = against(key_parts[h][first:last], query)
            near = jnp.where(iota((size, size), 0) <= iota((size, size), 1), near, NEG)
            near = jnp.exp(near - lse)
            near_gp = against(values[first:last], grad)
            delta = jnp.sum(near * near_gp, axis=0, keepdims=True)
            if i:
                far = jnp.exp(against(key_parts[h][:first], query) - lse)
                far_gp = against(values[:first], grad)
                delta = delta + jnp.sum(far * far_gp, axis=0, keepdims=True)
            near_gs = (near * (near_gp - delta)).astype(BF16)
            result = product(keys_t[:, first:last], near_gs)
            dk[first:last] += product(near_gs, plain)
            dv[first:last] += product(near.astype(BF16), grad)
            if i:
                far_gs = (far * (far_gp - delta)).astype(BF16)
                result = result + product(keys_t[:, :first], far_gs)
                dk[:first] += product(far_gs, plain)
                dv[:first] += product(far.astype(BF16), grad)
            dq = jnp.where(iota((LANES, size), 0) // HEAD_DIM == h, result, dq)
        out_ref[first:last, 0:cols] = (jnp.transpose(dq) * scaling)[:, :cols].astype(BF16)
    out_ref[:, cols : 2 * cols] = dk[:, :cols].astype(BF16)
    out_ref[:, 2 * cols :] = dv[:, :cols].astype(BF16)


def pick_chosen(tables, index):
    tokens = index.shape[0]
    low = index & 127
    key = (index >> 7) + (iota((tokens, LANES), 1) // PICKS) * (NSUB // LANES)
    total = jnp.zeros((tokens, LANES), F32)
    for h in range(MHEADS):
        for c in range(NSUB // LANES):
            found = lane_pick(tables[h][:, c * LANES : (c + 1) * LANES], low)
            total = jnp.where(key == h * (NSUB // LANES) + c, found, total)
    return total


def group_reduce(values, reducer, fill):
    group = iota(values.shape, 1) // PICKS
    total = jnp.zeros(values.shape, F32)
    for h in range(MHEADS):
        one = reducer(jnp.where(group == h, values, fill), axis=1, keepdims=True)
        total = jnp.where(group == h, one, total)
    return total


def middle_kernel(
    ready, adapter, o_ref, x_ref, gain_ref, mix_ref, w_in_any, w_out_any, dn_any, up_any,
    left_ref, right_ref, att_ref, rank_ref, mid_ref, norm_ref, gate_ref, w, dn, up, sems,
):
    groups = o_ref.shape[0]
    a = adapter[0]
    copies = fetch(
        [(dn_any.at[3, a], dn.at[0]), (dn_any.at[5, a], dn.at[1]), (up_any.at[3, a], up.at[0]), (up_any.at[5, a], up.at[1]),
         (w_out_any.at[0], w.at[0]), (w_in_any.at[4], w.at[1])],
        sems,
    )
    ready()
    attended = jnp.concatenate([o_ref[s] for s in range(groups)], axis=1)
    att_ref[...] = attended
    for copy in copies[:4]:
        copy.wait()
    rank_three = against(attended, dn[0]).astype(BF16)
    extra = product(rank_three, up[0])
    copies[4].wait()
    middle = x_ref[...].astype(F32) + (product(attended, w[0]) + extra)
    mid_ref[...] = middle
    normed = (middle * inverse_norm(middle) * gain_row(gain_ref)).astype(BF16)
    norm_ref[...] = normed
    rank_five = against(normed, dn[1]).astype(BF16)
    rank_ref[0] = rank_three
    rank_ref[1] = rank_five
    extra = product(rank_five, up[1])
    copies[5].wait()
    gate = product(normed, w[1]) + extra
    gate_ref[...] = gate
    memory_grad = (mix_ref[...].astype(F32) * (gate * jax.nn.sigmoid(gate))).astype(BF16)
    half = left_ref.shape[1]
    left_ref[...] = memory_grad[:, :half]
    right_ref[...] = memory_grad[:, half:]


def scores_kernel(
    owners, ready, adapter, normed_ref, picks_ref, slot_ref, keys_ref, w_in_any, dn_any, up_any,
    send_ref, rank_ref, weight_ref, w, dn, up, sems,
):
    a = adapter[0]
    copies = fetch([(dn_any.at[4, a], dn), (up_any.at[4, a], up), (w_in_any.at[3], w)], sems)
    ready()
    normed = normed_ref[...]
    copies[0].wait()
    ranks = against(normed, dn[...]).astype(BF16)
    rank_ref[...] = ranks
    copies[1].wait()
    extra = product(ranks, up[...])
    copies[2].wait()
    query = (product(normed, w[...]) + extra).astype(BF16)
    first, second = [], []
    for h in range(MHEADS):
        base = 2 * h * KHALF
        first.append(against(query[:, base : base + KHALF], keys_ref[0, h]))
        second.append(against(query[:, base + KHALF : base + 2 * KHALF], keys_ref[1, h]))
    picks = picks_ref[...]
    scores = pick_chosen(first, picks // NSUB) + pick_chosen(second, picks % NSUB)
    exponent = jnp.exp(scores - group_reduce(scores, jnp.max, NEG))
    weights = exponent / group_reduce(exponent, jnp.sum, 0.0)
    weight_ref[...] = weights
    send_ref[...] = to_slots(weights, slot_ref, owners).astype(BF16)


def to_slots(weights, slot_ref, owners):
    tokens = weights.shape[0]
    capacity = 2 * MHEADS * tokens // owners
    lane_group = iota((tokens, LANES), 1) // PICKS
    tiled = [
        tile_groups(jnp.where(lane_group == h, weights, 0.0), MHEADS).astype(BF16) for h in range(MHEADS)
    ]
    place = iota((owners * 8, tokens), 0)
    base = (place // 8) * capacity + place % 8
    out_group = iota((owners * 8, LANES), 1) // PICKS
    total = jnp.zeros((owners * 8, LANES), F32)
    for g in range(capacity // 8):
        part = jnp.zeros((owners * 8, LANES), F32)
        for h in range(MHEADS):
            chosen = jnp.where(base + g * 8 == slot_ref[h : h + 1, :], 1.0, 0.0).astype(BF16)
            part = part + product(chosen, tiled[h])
        total = jnp.where(out_group == g, part, total)
    return total


def plane_hits(slot_ref, plane, seq, capacity):
    tokens = slot_ref.shape[1]
    place = plane * (seq * capacity) + iota((seq * capacity, tokens), 0)
    chosen = jnp.zeros((seq * capacity, tokens), F32)
    for h in range(MHEADS):
        chosen = jnp.where(place == slot_ref[h : h + 1, :], 1.0, chosen)
    return chosen.astype(BF16)


def scatter_kernel(ready, *refs):
    ready()
    out_ref = refs[-1]
    seq, batches, capacity, wide = out_ref.shape
    plane = lax.axis_index("batch")
    for k in range(batches):
        chosen = plane_hits(refs[k], plane, seq, capacity)
        rows = product(chosen, refs[batches + k][...]).astype(BF16)
        source = lax.rem(plane + (batches - k), batches)
        out_ref[:, pl.ds(source, 1)] = rows.reshape(seq, 1, capacity, wide)


def gather_kernel(ready, *refs):
    ready()
    batches = (len(refs) - 1) // 2
    back_ref = refs[batches]
    seq, _, capacity, wide = back_ref.shape
    plane = lax.axis_index("batch")
    for k in range(batches):
        chosen = plane_hits(refs[k], plane, seq, capacity)
        source = lax.rem(plane + (batches - k), batches)
        rows = back_ref[:, pl.ds(source, 1)].reshape(seq * capacity, wide)
        refs[batches + 1 + k][...] = contract(chosen, rows).astype(BF16)


def output_kernel(
    batches, ready, adapter, gate_ref, mix_ref, mid_ref, *refs
):
    w_in_any, w_out_any, dn_any, up_any, out_ref, mixed_ref, rank_ref, grank_ref, ggate_ref, part_ref, w, dn, up, sems = refs[batches:]
    a = adapter[0]
    copies = fetch(
        [(dn_any.at[5, a], dn.at[0]), (up_any.at[5, a], up.at[0]), (dn_any.at[6, a], dn.at[1]),
         (up_any.at[6, a], up.at[1]), (w_in_any.at[4], w.at[0]), (w_out_any.at[1], w.at[1])],
        sems,
    )
    ready()
    memory = refs[0][...].astype(F32)
    for k in range(1, batches):
        memory = memory + refs[k][...].astype(F32)
    gate = gate_ref[...]
    sigmoid = jax.nn.sigmoid(gate)
    mixed = (memory * (gate * sigmoid)).astype(BF16)
    mixed_ref[...] = mixed
    ggate = (mix_ref[...].astype(F32) * memory * sigmoid * (1.0 + gate * (1.0 - sigmoid))).astype(BF16)
    ggate_ref[...] = ggate
    for copy in copies[:4]:
        copy.wait()
    granks = against(ggate, up[0]).astype(BF16)
    grank_ref[...] = granks
    extra = product(granks, dn[0])
    copies[4].wait()
    part_ref[...] = against(ggate, w[0]) + extra
    ranks = against(mixed, dn[1]).astype(BF16)
    rank_ref[...] = ranks
    extra = product(ranks, up[1])
    copies[5].wait()
    out_ref[...] = (mid_ref[...] + (product(mixed, w[1]) + extra)).astype(BF16)


def query_kernel(
    owners, rows_dev, ready, length, adapter, back_ref, slot_ref, picks_ref, weight_ref, part_ref, mid_ref, cot_ref, gain_ref,
    keys_ref, w_in_any, w_out_any, dn_any, up_any,
    go_ref, gquery_ref, grank_ref, gmid_ref, w, dn, up, sems,
):
    groups, tokens, cols = go_ref.shape
    a = adapter[0]
    copies = fetch(
        [(dn_any.at[3, a], dn.at[0]), (dn_any.at[4, a], dn.at[1]), (up_any.at[3, a], up.at[0]),
         (up_any.at[4, a], up.at[1]), (w_in_any.at[3], w.at[0]), (w_out_any.at[0], w.at[1])],
        sems,
    )
    ready()
    capacity = 2 * MHEADS * tokens // owners
    slots = iota((tokens, owners * 8), 1)
    base = (slots // 8) * capacity + slots % 8
    lane_group = iota((tokens, LANES), 1) // PICKS
    back = back_ref[...]
    gw = jnp.zeros((tokens, LANES), F32)
    for h in range(MHEADS):
        part = jnp.zeros((tokens, LANES), F32)
        for g in range(capacity // 8):
            chosen = jnp.where(base + g * 8 == slot_ref[:, h : h + 1], 1.0, 0.0).astype(BF16)
            part = jnp.where(lane_group == g, product(chosen, back), part)
        gw = jnp.where(lane_group == h, tile_groups(part, MHEADS), gw)
    weights = weight_ref[...]
    gscore = jnp.transpose(weights * (gw - group_reduce(weights * gw, jnp.sum, 0.0)))
    span = rows_dev // NSUB
    halves = []
    for h in range(MHEADS):
        first = jnp.zeros((8, tokens), F32)
        second = jnp.zeros((NSUB, tokens), F32)
        origin = picks_ref[h, 0:1, :] // rows_dev
        for r in range(PICKS):
            at = h * PICKS + r
            pick = picks_ref[h, r : r + 1, :]
            value = gscore[at : at + 1, :]
            first = first + jnp.where((pick // NSUB) % span == iota((8, tokens), 0), value, 0.0)
            second = second + jnp.where(pick % NSUB == iota((NSUB, tokens), 0), value, 0.0)
        place = iota((NSUB, tokens), 0)
        wide = jnp.concatenate([first[:span]] * (NSUB // span), axis=0)
        wide = jnp.where(place // span == origin, wide, 0.0)
        halves.append(contract(wide.astype(BF16), keys_ref[0, h]))
        halves.append(contract(second.astype(BF16), keys_ref[1, h]))
    gquery = jnp.concatenate(halves, axis=1).astype(BF16)
    gquery_ref[...] = gquery
    for copy in copies[:4]:
        copy.wait()
    granks = against(gquery, up[1]).astype(BF16)
    grank_ref[1] = granks
    extra = product(granks, dn[1])
    copies[4].wait()
    gnormed = against(gquery, w[0]) + extra + part_ref[...]
    middle = mid_ref[...]
    gmid = cot_ref[...].astype(F32) + norm_back(middle, inverse_norm(middle), gain_row(gain_ref), gnormed)
    gmid_ref[...] = gmid
    low = gmid.astype(BF16)
    granks = against(low, up[0]).astype(BF16)
    grank_ref[0] = granks
    extra = product(granks, dn[0])
    copies[5].wait()
    go = against(low, w[1]) + extra
    row = lax.axis_index("seq") * tokens + iota((tokens, 1), 0)
    go = jnp.where(row < length[0], go, 0.0).astype(BF16)
    for s in range(groups):
        go_ref[s] = go[:, s * cols : (s + 1) * cols]


def place_columns(out_ref, row, values):
    groups, _, cols = out_ref.shape
    low = values.astype(BF16)
    for s in range(groups):
        out_ref[s, row : row + values.shape[0], :] = low[:, s * cols : (s + 1) * cols]


def factor_kernel(ready, att_ref, norm_ref, mixed_ref, gmid_ref, gquery_ref, ggate_ref, cot_ref, r35, r4, r6, g34, g5, g6, out_ref):
    ready()
    half = 4 * RANK
    sides = (
        (att_ref[...], gmid_ref[...].astype(BF16), r35[0], g34[0]),
        (norm_ref[...], gquery_ref[...], r4[...], g34[1]),
        (norm_ref[...], ggate_ref[...], r35[1], g5[...]),
        (mixed_ref[...], cot_ref[...], r6[...], g6[...]),
    )
    for j, (value, gy, rank, grank) in enumerate(sides):
        place_columns(out_ref, j * RANK, contract(grank, value))
        place_columns(out_ref, half + j * RANK, contract(rank, gy))


def entry_factor_kernel(ready, adapter, grad_ref, norm_ref, ranks_ref, up_any, out_ref, gy_ref, grank_ref, up, sems):
    groups, tokens, wide = grad_ref.shape
    cols = wide // 3
    a = adapter[0]
    copies = fetch([(up_any.at[j, a], up.at[pl.ds(RANK * j, RANK)]) for j in range(3)], sems)
    ready()
    gys = [
        jnp.concatenate([grad_ref[s, :, j * cols : (j + 1) * cols] for s in range(groups)], axis=1) for j in range(3)
    ]
    for copy in copies:
        copy.wait()
    place = iota((tokens, 3 * RANK), 1) // RANK
    granks = jnp.zeros((tokens, 3 * RANK), F32)
    ranks = ranks_ref[...]
    for j in range(3):
        gy_ref[j] = gys[j]
        granks = jnp.where(place == j, against(gys[j], up[...]), granks)
        up_grad = contract(ranks, gys[j])
        place_columns(out_ref, (3 + j) * RANK, up_grad[j * RANK : (j + 1) * RANK, :])
    granks = granks.astype(BF16)
    grank_ref[...] = granks
    place_columns(out_ref, 0, contract(granks, norm_ref[...]))


def entry_kernel(ready, adapter, gy_ref, grank_ref, x_ref, gain_ref, gmid_ref, w_any, dn_any, out_ref, w, dn, sems):
    a = adapter[0]
    copies = fetch(
        [(dn_any.at[j, a], dn.at[pl.ds(RANK * j, RANK)]) for j in range(3)] + [(w_any.at[j], w.at[j]) for j in range(3)],
        sems,
    )
    ready()
    x = x_ref[...].astype(F32)
    for copy in copies[:3]:
        copy.wait()
    total = product(grank_ref[...], dn[...])
    for j in range(3):
        copies[3 + j].wait()
        total = total + against(gy_ref[j], w[j])
    back = norm_back(x, inverse_norm(x), gain_row(gain_ref), total)
    out_ref[...] = (gmid_ref[...] + back).astype(BF16)


def sum_kernel(ready, parts_ref, out_ref):
    ready()
    total = parts_ref[0].astype(F32)
    for s in range(1, parts_ref.shape[0]):
        total = total + parts_ref[s].astype(F32)
    total = total.astype(BF16)
    if len(out_ref.shape) == 2:
        out_ref[...] = total
    else:
        for k in range(out_ref.shape[0]):
            out_ref[k] = total


def adapter_marks(ids_ref, batches):
    step = ids_ref.shape[0] // batches
    return [ids_ref[b * step : b * step + 1, 0:1] // 65536 for b in range(batches)]


def spread_block(rows, marks, target, stage, sem):
    for k in range(ADAPTERS):
        total = jnp.zeros(rows[0].shape, F32)
        for row, mark in zip(rows, marks, strict=True):
            total = total + jnp.where(mark == k, row, 0.0)
        stage[k] = total
    copy = pltpu.make_async_copy(stage, target, sem)
    copy.start()
    return copy


def spread_kernel(batches, ready, ids_ref, *refs):
    down_any, up_any, parts, stage, load_sems, sems = refs[-6:]
    seq = len(refs) - 6
    me, plane = lax.axis_index("seq"), lax.axis_index("batch")
    copies = fetch([(refs[m], parts.at[me ^ m]) for m in range(seq)], load_sems)
    ready()
    absolute = adapter_marks(ids_ref, batches)
    marks = []
    for k in range(batches):
        source = lax.rem(plane + (batches - k), batches)
        mark = absolute[0]
        for b in range(1, batches):
            mark = jnp.where(source == b, absolute[b], mark)
        marks.append(mark)
    for copy in copies:
        copy.wait()
    started = []
    for at in range(8):
        target = down_any.at[3 + at] if at < 4 else up_any.at[at - 1]
        if at >= 2:
            started[at - 2].wait()
        rows = [
            jnp.concatenate([parts[s, k, at * RANK : (at + 1) * RANK, :] for s in range(seq)], axis=1).astype(F32)
            for k in range(batches)
        ]
        started.append(spread_block(rows, marks, target, stage.at[at % 2], sems.at[at % 2]))
    started[-2].wait()
    started[-1].wait()


def last_spread_kernel(batches, ready, ids_ref, late_ref, down_in, up_in, down_any, up_any, stage, sems):
    seq = late_ref.shape[0] // batches
    ready()
    marks = adapter_marks(ids_ref, batches)
    started = []
    for at in range(6):
        rows = [
            jnp.concatenate([late_ref[b * seq + s, at * RANK : (at + 1) * RANK, :] for s in range(seq)], axis=1).astype(F32)
            for b in range(batches)
        ]
        target = down_any.at[at] if at < 3 else up_any.at[at - 3]
        started.append(spread_block(rows, marks, target, stage.at[at], sems.at[at]))
    for copy in started:
        copy.wait()


def along(values, axis, step, size):
    return lax.ppermute(values, axis, [(i, (i + step) % size) for i in range(size)])


def across(values, axis, mask, size):
    return lax.ppermute(values, axis, [(i, i ^ mask) for i in range(size)])


def exchange(values, axes):
    return lax.all_to_all(values, axes, split_axis=0, concat_axis=0, tiled=True)


def body(
    inputs, lengths, adapter_index, memory_picks, input_weights, output_weights, adapter_down, adapter_up,
    attention_gain, memory_gain, half_keys, memory_values, cotangent,
):
    both = ("batch", "seq")
    batches, seq = lax.axis_size("batch"), lax.axis_size("seq")
    owners = batches * seq
    tokens, width = inputs.shape[1], inputs.shape[2]
    rows, cols, half = tokens * seq, width // seq, width // 2
    rows_dev = memory_values.shape[0]
    capacity = 2 * tokens * MHEADS // owners
    groups = capacity // 8
    items = owners * capacity
    block = min(owners * 8, 256)
    x, cot = inputs[0], cotangent[0]
    down = jnp.swapaxes(adapter_down, 2, 3)
    gain_one, gain_two = attention_gain.reshape(1, width), memory_gain.reshape(1, width)
    picks = jnp.transpose(memory_picks[0], (1, 2, 0))
    matrix = pltpu.VMEM((width, width), BF16)
    pair = pltpu.VMEM((2, width, width), BF16)
    triple = pltpu.VMEM((3, width, width), BF16)
    small = pltpu.VMEM((RANK, width), BF16)
    two_small = pltpu.VMEM((2, RANK, width), BF16)
    three_small = pltpu.VMEM((3 * RANK, width), BF16)
    token_low, token_wide = shaped((tokens, width), BF16), shaped((tokens, width), F32)
    token_rank, token_lanes = shaped((tokens, RANK), BF16), shaped((tokens, LANES), F32)
    fixed = functools.partial

    qkv, normed, ranks = call(
        qkv_kernel, "qkv", "MLLHHH",
        [("V", shaped((seq, tokens, 3 * cols), BF16)), ("S", token_low), ("S", shaped((tokens, 3 * RANK), BF16))],
        (adapter_index, x, gain_one, input_weights, down, adapter_up), [triple, three_small, three_small, sema(9)],
    )
    qkv_all = exchange(qkv, "seq").reshape(rows, 3 * cols)

    slot, slot_col, pick, ids_out = call(
        fixed(route_kernel, rows_dev, owners), "route", "ML",
        [("V", shaped((8, tokens), I32)), ("S", shaped((tokens, tokens), I32)), ("S", shaped((tokens, LANES), I32)),
         ("V", shaped((owners * 8, LANES), I32))],
        (adapter_index, picks),
    )
    slots = [slot] + [along(slot, "batch", k, batches) for k in range(1, batches)]
    mix_grad, grank_six = call(
        mix_back_kernel, "mixback", "MLHHH", [("S", token_low), ("S", token_rank)],
        (adapter_index, cot, output_weights, down, adapter_up), [matrix, small, small, sema(3)],
    )

    attended, lse, qkv_saved = call(
        attend_kernel, "attend", "MV",
        [("V", shaped((rows, cols), BF16)), ("S", shaped((8, rows), F32)), ("H", shaped((rows, 3 * cols), BF16))],
        (lengths, qkv_all), [sema(1)],
    )
    o_all = exchange(attended.reshape(seq, tokens, cols), "seq")
    ids_out, o_all = lax.optimization_barrier((ids_out, o_all))
    ids = exchange(ids_out.reshape(owners, 8, LANES), both).reshape(owners * 8, LANES)

    left, right, att, rank_pair, middle, normed_two, gate = call(
        middle_kernel, "middle", "MVLLLHHHH",
        [("V", shaped((tokens, half), BF16)), ("V", shaped((tokens, half), BF16)), ("S", token_low),
         ("S", shaped((2, tokens, RANK), BF16)), ("S", token_wide), ("S", token_low), ("S", token_wide)],
        (adapter_index, o_all, x, gain_two, mix_grad, input_weights, output_weights, down, adapter_up),
        [pair, two_small, two_small, sema(6)],
    )
    lefts = [left] + [along(left, "batch", k, batches) for k in range(1, batches)]
    weight_out, rank_four, weights = call(
        fixed(scores_kernel, owners), "scores", "MLLLLHHH",
        [("V", shaped((owners * 8, LANES), BF16)), ("S", token_rank), ("S", token_lanes)],
        (adapter_index, normed_two, pick, slot, half_keys, input_weights, down, adapter_up), [matrix, small, small, sema(3)],
    )
    weight_out, ids = lax.optimization_barrier((weight_out, ids))
    weight_in = exchange(weight_out.reshape(owners, 8, LANES), both).reshape(owners * 8, LANES)
    (index,) = call(
        fixed(prepare_kernel, groups, rows_dev), "prepare", "L", [("H", shaped((items, rows_dev), I32))], (ids,),
        [pltpu.VMEM((2, LANES, rows_dev), I32), sema(2)],
    )
    right, lefts = lax.optimization_barrier((right, lefts))
    rights = [right] + [along(right, "batch", k, batches) for k in range(1, batches)]

    def scatter(parts, name):
        out = [("V", shaped((seq, batches, capacity, half), BF16))]
        return call(scatter_kernel, name, "L" * batches + "V" * batches, out, (*slots, *parts))[0]

    left_out = scatter(lefts, "scatterleft")
    left_out, weight_in = lax.optimization_barrier((left_out, weight_in))
    left_in = exchange(left_out, "seq").reshape(items, half)

    (sums,) = call(
        fixed(recall_kernel, groups), "recall", "VHH", [("V", shaped((seq, batches, capacity, width), BF16))],
        (weight_in, index, memory_values),
        [pltpu.VMEM((rows_dev, width), BF16), pltpu.VMEM((2, block, rows_dev), I32), pltpu.VMEM((block, rows_dev), BF16), sema(3)],
        flops=1 << 32,
    )
    sums, left_in = lax.optimization_barrier((sums, left_in))
    back = exchange(sums, "seq")

    def recall_back(part, name, grads, kind, dtype, *before):
        return call(
            fixed(recall_back_kernel, part, batches, groups), name, "L" + "L" * part + "VH",
            [(kind, shaped((owners * 8, LANES), dtype))], (ids, *before, grads, memory_values),
            [pltpu.VMEM((rows_dev, half), BF16), pltpu.VMEM((block, rows_dev), F32), sema(1)], flops=1 << 31,
        )[0]

    right_out = scatter(rights, "scatterright")
    right_out, back = lax.optimization_barrier((right_out, back))
    right_in = exchange(right_out, "seq").reshape(items, half)
    found_left = recall_back(0, "recallleft", left_in, "S", F32)
    pieces = call(
        gather_kernel, "gather", "L" * batches + "V", [("V", token_low) for _ in range(batches)], (*slots, back),
    )
    pieces = [pieces[0]] + [along(pieces[k], "batch", batches - k, batches) for k in range(1, batches)]
    found = recall_back(1, "recallright", right_in, "V", BF16, found_left)
    found_back = exchange(found.reshape(owners, 8, LANES), both).reshape(owners * 8, LANES)

    output, mixed, rank_six, grank_five, ggate, part = call(
        fixed(output_kernel, batches), "output", "MLLL" + "V" * batches + "HHHH",
        [("S", token_low), ("S", token_low), ("S", token_rank), ("S", token_rank), ("S", token_low), ("S", token_wide)],
        (adapter_index, gate, mix_grad, middle, *pieces, input_weights, output_weights, down, adapter_up),
        [pair, two_small, two_small, sema(6)],
    )

    go, gquery, grank_pair, gmid = call(
        fixed(query_kernel, owners, rows_dev), "query", "MMVLLLLLLLLHHHH",
        [("V", shaped((seq, tokens, cols), BF16)), ("S", token_low), ("S", shaped((2, tokens, RANK), BF16)), ("S", token_wide)],
        (lengths, adapter_index, found_back, slot_col, picks, weights, part, middle, cot, gain_two, half_keys,
         input_weights, output_weights, down, adapter_up),
        [pair, two_small, two_small, sema(6)],
    )
    go_all = exchange(go, "seq").reshape(rows, cols)
    (factors,) = call(
        factor_kernel, "factors", "L" * 13, [("V", shaped((seq, 8 * RANK, cols), BF16))],
        (att, normed_two, mixed, gmid, gquery, ggate, cot, rank_pair, rank_four, rank_six, grank_pair, grank_five, grank_six),
    )
    factors, go_all = lax.optimization_barrier((factors, go_all))
    early_parts = exchange(factors, "seq")

    (grads,) = call(
        attend_back_kernel, "attendback", "MLVL", [("V", shaped((rows, 3 * cols), BF16))], (lengths, qkv_saved, go_all, lse),
        [pltpu.VMEM((rows, LANES), F32), pltpu.VMEM((rows, LANES), F32)],
    )
    grads, early_parts = lax.optimization_barrier((grads, early_parts))
    grads_all = exchange(grads.reshape(seq, tokens, 3 * cols), "seq")
    (some,) = call(sum_kernel, "sumearly", "V", [("V", shaped((8 * RANK, cols), BF16))], (early_parts,))
    some = jnp.stack([some] + [along(some, "batch", k, batches) for k in range(1, batches)])
    late, gys, granks = call(
        entry_factor_kernel, "entryfactors", "MVLLH",
        [("V", shaped((seq, 6 * RANK, cols), BF16)), ("S", shaped((3, tokens, width), BF16)), ("S", shaped((tokens, 3 * RANK), BF16))],
        (adapter_index, grads_all, normed, ranks, adapter_up), [three_small, sema(3)],
    )
    late, some = lax.optimization_barrier((late, some))
    some = [some] + [across(some, "seq", m, seq) for m in range(1, seq)]
    late_parts = exchange(late, "seq")
    (late_sum,) = call(sum_kernel, "sumlate", "V", [("V", shaped((owners, 6 * RANK, cols), BF16))], (late_parts,))
    late_all = exchange(late_sum, both)
    (grad_input,) = call(
        entry_kernel, "entry", "MLLLLLHH", [("S", token_low)],
        (adapter_index, gys, granks, x, gain_one, gmid, input_weights, down), [triple, three_small, sema(6)],
    )
    full = shaped((7, ADAPTERS, RANK, width), F32)
    grad_down, grad_up = call(
        fixed(spread_kernel, batches), "spread", "L" + "H" * seq, [("H", full), ("H", full)], (ids, *some),
        [pltpu.VMEM((seq, batches, 8 * RANK, cols), BF16), pltpu.VMEM((2, ADAPTERS, RANK, width), F32), sema(seq), sema(2)],
    )
    grad_down, grad_up = call(
        fixed(last_spread_kernel, batches), "lastspread", "LVHH", [("H", full), ("H", full)],
        (ids, late_all, grad_down, grad_up), [pltpu.VMEM((6, ADAPTERS, RANK, width), F32), sema(6)], aliases={2: 0, 3: 1},
    )
    return (output[None], grad_input[None], jnp.swapaxes(grad_down, 2, 3), grad_up)


def solution(mesh):
    split = P("batch", "seq", None)
    return jax.shard_map(
        body,
        mesh=mesh,
        in_specs=(
            split, P("batch"), P("batch"), P("batch", "seq", None, None), P(), P(), P(), P(), P(), P(), P(),
            P(("batch", "seq"), None), split,
        ),
        out_specs=(split, split, P(), P()),
        check_vma=False,
    )
```

```python
import functools

import jax
import jax.numpy as jnp
from jax import lax
from jax.experimental import pallas as pl
from jax.experimental.pallas import tpu as pltpu
from jax.sharding import PartitionSpec as P

HEAD_DIM = 64
MHEADS = 4
KHALF = 128
NSUB = 256
PICKS = 32
ADAPTERS = 8
RANK = 16
LANES = 128
EPS = 1e-06
NEG = -1e30
F32 = jnp.float32
BF16 = jnp.bfloat16
I32 = jnp.int32
HBM = pl.BlockSpec(memory_space=pltpu.HBM)
SMEM = pl.BlockSpec(memory_space=pltpu.SMEM)
VMEM = pl.BlockSpec(memory_space=pltpu.VMEM)
MIB = 1 << 20


def product(left, right):
    return lax.dot_general(left, right, (((1,), (0,)), ((), ())), preferred_element_type=F32)


def against(left, right):
    return lax.dot_general(left, right, (((1,), (1,)), ((), ())), preferred_element_type=F32)


def contract(left, right):
    return lax.dot_general(left, right, (((0,), (0,)), ((), ())), preferred_element_type=F32)


def iota(shape, axis):
    return lax.broadcasted_iota(I32, shape, axis)


def lane_pick(table, index):
    return jnp.take_along_axis(table, index, axis=1, mode="promise_in_bounds")


def shaped(shape, dtype):
    return jax.ShapeDtypeStruct(shape, dtype)


class Stage:
    def __init__(self, loads, stores):
        self.loads, self.stores = loads, stores
        self.waited, self.begun = set(), set()
        for _, copy in loads:
            copy.start()

    def __call__(self, *refs):
        for at, (ref, copy) in enumerate(self.loads):
            if at not in self.waited and (not refs or any(ref is one for one in refs)):
                self.waited.add(at)
                copy.wait()

    def send(self, *refs):
        for at, (ref, copy) in enumerate(self.stores):
            if at not in self.begun and (not refs or any(ref is one for one in refs)):
                self.begun.add(at)
                copy.start()

    def finish(self):
        self()
        self.send()
        for _, copy in self.stores:
            copy.wait()


def call(kernel, name, ins, outs, args, scratch=(), vmem=40, flops=1 << 28, moved=1 << 22, aliases=None):
    shapes = [(args[i].shape, args[i].dtype) for i, kind in enumerate(ins) if kind == "L"]
    stored = [(out.shape, out.dtype) for kind, out in outs if kind == "S"]
    count_in, count_out, count_user = len(ins), len(outs), len(scratch)

    def wrapped(*refs):
        given, results = list(refs[:count_in]), list(refs[count_in : count_in + count_out])
        rest = list(refs[count_in + count_out :])
        user, buffers = rest[:count_user], rest[count_user:]
        loads, stores = [], []
        for i, kind in enumerate(ins):
            if kind == "L":
                at = len(loads)
                loads.append((buffers[at], pltpu.make_async_copy(given[i], buffers[at], buffers[-1].at[at])))
                given[i] = buffers[at]
        for i, (kind, _) in enumerate(outs):
            if kind == "S":
                at = len(loads) + len(stores)
                stores.append((buffers[at], pltpu.make_async_copy(buffers[at], results[i], buffers[-1].at[at])))
                results[i] = buffers[at]
        stage = Stage(loads, stores)
        kernel(stage, *given, *results, *user)
        stage.finish()

    spaces = {"V": VMEM, "L": HBM, "S": HBM, "H": HBM, "M": SMEM}
    autos = [pltpu.VMEM(*one) for one in shapes + stored]
    args = [
        pltpu.with_memory_space_constraint(one, pltpu.HBM) if kind in "LH" else one
        for kind, one in zip(ins, args, strict=True)
    ]
    return pl.pallas_call(
        wrapped,
        name=name,
        out_shape=[pltpu.HBM(out.shape, out.dtype) if kind in "SH" else out for kind, out in outs],
        in_specs=[spaces[kind] for kind in ins],
        out_specs=[spaces[kind] for kind, _ in outs],
        input_output_aliases=aliases or {},
        scratch_shapes=list(scratch) + autos + ([sema(len(autos))] if autos else []),
        compiler_params=pltpu.CompilerParams(vmem_limit_bytes=vmem * MIB),
        cost_estimate=pl.CostEstimate(flops=flops, bytes_accessed=moved, transcendentals=0),
    )(*args)


def fetch(pairs, sems):
    copies = [
        pltpu.make_async_copy(source, target, sems.at[place])
        for place, (source, target) in enumerate(pairs)
    ]
    for copy in copies:
        copy.start()
    return copies


def sema(count):
    return pltpu.SemaphoreType.DMA((count,))


def gain_row(ref):
    return ref[...].astype(F32).reshape(1, ref.shape[0])


def inverse_norm(values):
    return lax.rsqrt(jnp.mean(values * values, axis=1, keepdims=True) + EPS)


def norm_back(values, inverse, scales, incoming):
    weighted = incoming * scales
    inner = jnp.mean(weighted * values, axis=1, keepdims=True)
    return weighted * inverse - values * inverse * inverse * inverse * inner


def qkv_kernel(ready, adapter, x_ref, gain_ref, w_any, dn_any, up_any, out_ref, norm_ref, rank_ref, w, dn, up, sems):
    groups, tokens, wide = out_ref.shape
    cols = wide // 3
    a = adapter[0]
    copies = fetch(
        [(dn_any.at[j, a], dn.at[pl.ds(RANK * j, RANK)]) for j in range(3)]
        + [(up_any.at[j, a], up.at[pl.ds(RANK * j, RANK)]) for j in range(3)]
        + [(w_any.at[j], w.at[j]) for j in range(3)],
        sems,
    )
    ready()
    x = x_ref[...].astype(F32)
    normed = (x * inverse_norm(x) * gain_row(gain_ref)).astype(BF16)
    norm_ref[...] = normed
    ready.send(norm_ref)
    for copy in copies[:6]:
        copy.wait()
    ranks = against(normed, dn[...]).astype(BF16)
    rank_ref[...] = ranks
    ready.send(rank_ref)
    place = iota((tokens, 3 * RANK), 1) // RANK
    for j in range(3):
        own = jnp.where(place == j, ranks.astype(F32), 0.0).astype(BF16)
        extra = product(own, up[...])
        copies[6 + j].wait()
        result = (product(normed, w[j]) + extra).astype(BF16)
        for s in range(groups):
            out_ref[s, :, j * cols : (j + 1) * cols] = result[:, s * cols : (s + 1) * cols]


def mix_back_kernel(ready, adapter, cot_ref, w_any, dn_any, up_any, grad_ref, rank_ref, w, dn, up, sems):
    a = adapter[0]
    copies = fetch([(up_any.at[6, a], up), (dn_any.at[6, a], dn), (w_any.at[1], w)], sems)
    ready()
    gy = cot_ref[...]
    copies[0].wait()
    ranks = against(gy, up[...]).astype(BF16)
    rank_ref[...] = ranks
    copies[1].wait()
    extra = product(ranks, dn[...])
    copies[2].wait()
    grad_ref[...] = (against(gy, w[...]) + extra).astype(BF16)


def route_kernel(rows_dev, owners, ready, adapter, picks_ref, slot_ref, slot_col_ref, pick_ref, ids_ref):
    ready()
    heads, picks, tokens = picks_ref.shape
    capacity = 2 * heads * tokens // owners
    groups = capacity // 8
    visits = heads * tokens
    owner = jnp.concatenate([picks_ref[h, 0:1, :] for h in range(heads)], axis=1) // rows_dev
    hot = jnp.where(iota((owners, visits), 0) == owner, 1.0, 0.0)
    before = jnp.where(iota((visits, visits), 0) < iota((visits, visits), 1), 1.0, 0.0).astype(BF16)
    counts = product(hot.astype(BF16), before)
    within = jnp.sum(hot * counts, axis=0, keepdims=True).astype(I32)
    slot = owner * capacity + within
    rows = [slot[:, h * tokens : (h + 1) * tokens] for h in range(heads)]
    stacked = jnp.concatenate(rows + [jnp.full((8 - heads, tokens), -1, I32)], axis=0)
    slot_ref[...] = stacked
    tall = jnp.concatenate([stacked, jnp.full((tokens - 8, tokens), -1, I32)], axis=0)
    slot_col_ref[...] = jnp.transpose(tall)
    packed = jnp.concatenate([picks_ref[h] for h in range(heads)], axis=0)
    by_token = jnp.transpose(packed)
    pick_ref[...] = by_token
    local = by_token % rows_dev
    lanes = iota((tokens, LANES), 1)
    total = jnp.zeros((owners * 8, LANES), F32)
    out_lane = iota((owners * 8, LANES), 1) // PICKS
    place = iota((owners * 8, tokens), 0)
    base = (place // 8) * capacity + place % 8
    for g in range(groups):
        high = jnp.zeros((owners * 8, LANES), F32)
        low = jnp.zeros((owners * 8, LANES), F32)
        for h in range(heads):
            chosen = jnp.where(base + g * 8 == rows[h], 1.0, 0.0).astype(BF16)
            own = jnp.where(lanes // PICKS == h, local, 0)
            own = tile_groups(own.astype(F32), heads).astype(I32)
            high = high + product(chosen, (own // 256).astype(F32).astype(BF16))
            low = low + product(chosen, (own % 256).astype(F32).astype(BF16))
        total = jnp.where(out_lane == g, high * 256.0 + low, total)
    ids_ref[...] = total.astype(I32) + adapter[0] * 65536


def tile_groups(values, count):
    total = values
    for turn in range(1, count):
        total = total + pltpu.roll(values, turn * PICKS, 1)
    return total


def prepare_kernel(groups, rows_dev, ready, ids_ref, index_any, stage, turned, sems):
    ready()
    places = ids_ref.shape[0]
    chunks = rows_dev // LANES
    high_rows = max(8, chunks)
    steps = groups * (places // LANES)
    for k in range(places // LANES):
        turned[k] = jnp.transpose(ids_ref[k * LANES : (k + 1) * LANES, :] & 65535)

    def put(step, slot):
        target = index_any.at[pl.ds(pl.multiple_of(step * LANES, LANES), LANES)]
        return pltpu.make_async_copy(stage.at[slot], target, sems.at[slot])

    def one(step, carry):
        k, g = lax.rem(step, places // LANES), step // (places // LANES)
        slot = lax.rem(step, 2)
        mask = jnp.zeros((LANES, LANES), I32)
        highs = jnp.zeros((high_rows, LANES), I32)
        for r in range(PICKS):
            bit = (1 << r) if r < 31 else -(1 << 31)
            row = turned[k, pl.ds(g * PICKS + r, 1), :]
            mask = mask | jnp.where(row & 127 == iota((LANES, LANES), 0), bit, 0)
            highs = highs | jnp.where(row >> 7 == iota((high_rows, LANES), 0), bit, 0)

        @pl.when(step >= 2)
        def _():
            put(step - 2, slot).wait()

        for c in range(chunks):
            index = 31 - lax.clz(mask & highs[c : c + 1, :])
            stage[slot, :, c * LANES : (c + 1) * LANES] = jnp.transpose(index).astype(jnp.int16)
        put(step, slot).start()
        return carry

    lax.fori_loop(0, steps, one, 0)
    for step in range(max(0, steps - 2), steps):
        put(step, step % 2).wait()


def recall_kernel(groups, ready, weight_ref, index_any, mem_any, out_ref, mem, index, dense, sems):
    places = weight_ref.shape[0]
    rows_dev = mem.shape[0]
    chunks = rows_dev // LANES
    block = dense.shape[1]
    per_group = places // block
    blocks = groups * per_group
    seq = out_ref.shape[0]
    planes = block // (8 * seq)

    def load(b, slot):
        source = index_any.at[pl.ds(pl.multiple_of(b * block, block), block)]
        return pltpu.make_async_copy(source, index.at[slot], sems.at[1 + slot])

    load(0, 0).start()
    copy = pltpu.make_async_copy(mem_any, mem, sems.at[0])
    copy.start()

    def gather(b, side):
        g, k = b // per_group, lax.rem(b, per_group)
        load(b, side).wait()

        @pl.when(b + 1 < blocks)
        def _():
            load(b + 1, 1 - side).start()

        for start in range(0, block, 16):
            weights = weight_ref[pl.ds(pl.multiple_of(k * block + start, 16), 16), :].astype(F32)
            for c in range(chunks):
                at = index[side, start : start + 16, c * LANES : (c + 1) * LANES].astype(I32)
                value = lane_pick(weights, (at + g * PICKS) & 127)
                dense[side, start : start + 16, c * LANES : (c + 1) * LANES] = jnp.where(at >= 0, value, 0.0).astype(BF16)

    def multiply(b, side):
        g, k = b // per_group, lax.rem(b, per_group)
        result = product(dense[side], mem[...]).astype(BF16)
        for i in range(planes):
            rows = result[i * seq * 8 : (i + 1) * seq * 8]
            out_ref[:, k * planes + i, pl.ds(pl.multiple_of(g * 8, 8), 8), :] = rows.reshape(seq, 8, rows.shape[1])

    gather(0, 0)
    copy.wait()

    def whole(i, carry):
        gather(2 * i + 1, 1)
        multiply(2 * i, 0)

        @pl.when(2 * i + 2 < blocks)
        def _():
            gather(2 * i + 2, 0)
            multiply(2 * i + 1, 1)

        @pl.when(2 * i + 2 >= blocks)
        def _():
            multiply(2 * i + 1, 1)

        return carry

    lax.fori_loop(0, blocks // 2, whole, 0)


def recall_back_kernel(part, batches, groups, ready, ids_ref, *refs):
    before_ref = refs[0] if part else None
    grad_ref, mem_any, out_ref, mem, scores, sems = refs[part:]
    items, half = grad_ref.shape
    seq = items // (batches * groups * 8)
    rows_dev = mem.shape[0]
    capacity = groups * 8
    chunks = rows_dev // LANES
    block = scores.shape[0]
    per_block = block // capacity
    blocks = items // block
    copies = fetch([(mem_any.at[:, pl.ds(part * half, half)], mem)], sems)
    ready()
    copies[0].wait()

    def whole(b, outer):
        scores[...] = against(grad_ref[pl.ds(pl.multiple_of(b * block, block), block), :], mem[...])

        lane_group = iota((8, LANES), 1) // PICKS
        for local in range(per_block):
            sender = b * per_block + local
            spot = lax.rem(sender, batches) * seq + sender // batches
            start = pl.multiple_of(spot * 8, 8)
            ids = ids_ref[pl.ds(start, 8), :] & 65535
            low = ids & 127
            high = ids >> 7
            total = before_ref[pl.ds(start, 8), :] if part else jnp.zeros((8, LANES), F32)
            for g in range(groups):
                key = jnp.where(lane_group == g, high, -1)
                here = jnp.zeros((8, LANES), F32)
                row = local * capacity + g * 8
                for c in range(chunks):
                    found = scores[row : row + 8, c * LANES : (c + 1) * LANES]
                    here = jnp.where(key == c, lane_pick(found, low), here)
                total = total + here
            out_ref[pl.ds(start, 8), :] = total.astype(out_ref.dtype)
        return outer

    lax.fori_loop(0, blocks, whole, 0)


def head_parts(values, h, spare):
    lane = iota(values.shape, 1)
    return jnp.where(lane // HEAD_DIM == h, values, jnp.where(lane == (1 - h) * HEAD_DIM, spare, 0.0)).astype(BF16)


def widen(values):
    if values.shape[1] == LANES:
        return values
    return jnp.concatenate([values, jnp.zeros((values.shape[0], LANES - values.shape[1]), values.dtype)], axis=1)


def attend_kernel(ready, length, qkv_ref, o_ref, lse_ref, saved_any, sems):
    ready()
    saving = pltpu.make_async_copy(qkv_ref, saved_any, sems.at[0])
    saving.start()
    rows, wide = qkv_ref.shape
    cols = wide // 3
    heads = cols // HEAD_DIM
    size = min(256, rows)
    valid = length[0]
    bias = jnp.where(iota((rows, LANES), 0) < valid, 0.0, NEG)
    keys = widen(qkv_ref[:, cols : 2 * cols].astype(F32))
    key_parts = [head_parts(keys, h, bias) for h in range(heads)]
    values_t = jnp.transpose(widen(qkv_ref[:, 2 * cols :].astype(F32))).astype(BF16)
    for i in range(rows // size):
        first, last = i * size, (i + 1) * size
        queries = widen(qkv_ref[first:last, 0:cols].astype(F32)) * (HEAD_DIM**-0.5)
        mixed = jnp.zeros((LANES, size), F32)
        stats = []
        for h in range(heads):
            query = head_parts(queries, h, 1.0)
            near = against(key_parts[h][first:last], query)
            near = jnp.where(iota((size, size), 0) <= iota((size, size), 1), near, NEG)
            high = jnp.max(near, axis=0, keepdims=True)
            if i:
                far = against(key_parts[h][:first], query)
                high = jnp.maximum(high, jnp.max(far, axis=0, keepdims=True))
            near = jnp.exp(near - high)
            summed = jnp.sum(near, axis=0, keepdims=True)
            result = product(values_t[:, first:last], near.astype(BF16))
            if i:
                far = jnp.exp(far - high)
                summed = summed + jnp.sum(far, axis=0, keepdims=True)
                result = result + product(values_t[:, :first], far.astype(BF16))
            stats.append(high + jnp.log(summed))
            mixed = jnp.where(iota((LANES, size), 0) // HEAD_DIM == h, result / summed, mixed)
        mixed = jnp.where(first + iota((LANES, size), 1) < valid, mixed, 0.0)
        o_ref[first:last, :] = jnp.transpose(mixed)[:, :cols].astype(BF16)
        lse_ref[:, first:last] = jnp.concatenate(stats + [jnp.zeros((8 - heads, size), F32)], axis=0)
    saving.wait()


def attend_back_kernel(ready, length, qkv_ref, go_ref, lse_ref, out_ref, dk, dv):
    ready()
    rows, wide = qkv_ref.shape
    cols = wide // 3
    heads = cols // HEAD_DIM
    size = min(256, rows)
    valid = length[0]
    scaling = HEAD_DIM**-0.5
    bias = jnp.where(iota((rows, LANES), 0) < valid, 0.0, NEG)
    keys = widen(qkv_ref[:, cols : 2 * cols].astype(F32))
    keys_t = jnp.transpose(keys).astype(BF16)
    key_parts = [head_parts(keys, h, bias) for h in range(heads)]
    values = widen(qkv_ref[:, 2 * cols :])
    dk[...] = jnp.zeros_like(dk)
    dv[...] = jnp.zeros_like(dv)
    for i in range(rows // size):
        first, last = i * size, (i + 1) * size
        queries = widen(qkv_ref[first:last, 0:cols].astype(F32)) * scaling
        grads = widen(go_ref[first:last, :].astype(F32))
        dq = jnp.zeros((LANES, size), F32)
        for h in range(heads):
            query = head_parts(queries, h, 1.0)
            plain = head_parts(queries, h, 0.0)
            grad = head_parts(grads, h, 0.0)
            lse = lse_ref[h : h + 1, first:last]
            near = against(key_parts[h][first:last], query)
            near = jnp.where(iota((size, size), 0) <= iota((size, size), 1), near, NEG)
            near = jnp.exp(near - lse)
            near_gp = against(values[first:last], grad)
            delta = jnp.sum(near * near_gp, axis=0, keepdims=True)
            if i:
                far = jnp.exp(against(key_parts[h][:first], query) - lse)
                far_gp = against(values[:first], grad)
                delta = delta + jnp.sum(far * far_gp, axis=0, keepdims=True)
            near_gs = (near * (near_gp - delta)).astype(BF16)
            result = product(keys_t[:, first:last], near_gs)
            dk[first:last] += product(near_gs, plain)
            dv[first:last] += product(near.astype(BF16), grad)
            if i:
                far_gs = (far * (far_gp - delta)).astype(BF16)
                result = result + product(keys_t[:, :first], far_gs)
                dk[:first] += product(far_gs, plain)
                dv[:first] += product(far.astype(BF16), grad)
            dq = jnp.where(iota((LANES, size), 0) // HEAD_DIM == h, result, dq)
        out_ref[first:last, 0:cols] = (jnp.transpose(dq) * scaling)[:, :cols].astype(BF16)
    out_ref[:, cols : 2 * cols] = dk[:, :cols].astype(BF16)
    out_ref[:, 2 * cols :] = dv[:, :cols].astype(BF16)


def pick_chosen(tables, index):
    tokens = index.shape[0]
    low = index & 127
    key = (index >> 7) + (iota((tokens, LANES), 1) // PICKS) * (NSUB // LANES)
    total = jnp.zeros((tokens, LANES), F32)
    for h in range(MHEADS):
        for c in range(NSUB // LANES):
            found = lane_pick(tables[h][:, c * LANES : (c + 1) * LANES], low)
            total = jnp.where(key == h * (NSUB // LANES) + c, found, total)
    return total


def group_reduce(values, reducer, fill):
    group = iota(values.shape, 1) // PICKS
    total = jnp.zeros(values.shape, F32)
    for h in range(MHEADS):
        one = reducer(jnp.where(group == h, values, fill), axis=1, keepdims=True)
        total = jnp.where(group == h, one, total)
    return total


def middle_kernel(
    ready, adapter, o_ref, x_ref, gain_ref, mix_ref, w_in_any, w_out_any, dn_any, up_any,
    left_ref, right_ref, same_ref, att_ref, rank_ref, mid_ref, norm_ref, gate_ref, w, dn, up, sems,
):
    groups = o_ref.shape[0]
    a = adapter[0]
    copies = fetch(
        [(dn_any.at[3, a], dn.at[0]), (dn_any.at[5, a], dn.at[1]), (up_any.at[3, a], up.at[0]), (up_any.at[5, a], up.at[1]),
         (w_out_any.at[0], w.at[0]), (w_in_any.at[4], w.at[1])],
        sems,
    )
    attended = jnp.concatenate([o_ref[s] for s in range(groups)], axis=1)
    att_ref[...] = attended
    ready.send(att_ref)
    for copy in copies[:4]:
        copy.wait()
    rank_three = against(attended, dn[0]).astype(BF16)
    extra = product(rank_three, up[0])
    copies[4].wait()
    ready(x_ref, gain_ref)
    middle = x_ref[...].astype(F32) + (product(attended, w[0]) + extra)
    mid_ref[...] = middle
    normed = (middle * inverse_norm(middle) * gain_row(gain_ref)).astype(BF16)
    norm_ref[...] = normed
    same_ref[...] = normed
    ready.send(mid_ref, norm_ref)
    rank_five = against(normed, dn[1]).astype(BF16)
    rank_ref[0] = rank_three
    rank_ref[1] = rank_five
    extra = product(rank_five, up[1])
    copies[5].wait()
    gate = product(normed, w[1]) + extra
    gate_ref[...] = gate
    ready.send(rank_ref, gate_ref)
    ready(mix_ref)
    memory_grad = (mix_ref[...].astype(F32) * (gate * jax.nn.sigmoid(gate))).astype(BF16)
    half = left_ref.shape[1]
    left_ref[...] = memory_grad[:, :half]
    right_ref[...] = memory_grad[:, half:]


def scores_kernel(
    owners, ready, adapter, normed_ref, picks_ref, slot_ref, keys_ref, w_in_any, dn_any, up_any,
    send_ref, rank_ref, weight_ref, w, dn, up, sems,
):
    a = adapter[0]
    copies = fetch([(dn_any.at[4, a], dn), (up_any.at[4, a], up), (w_in_any.at[3], w)], sems)
    normed = normed_ref[...]
    copies[0].wait()
    ranks = against(normed, dn[...]).astype(BF16)
    rank_ref[...] = ranks
    copies[1].wait()
    extra = product(ranks, up[...])
    copies[2].wait()
    query = (product(normed, w[...]) + extra).astype(BF16)
    ready()
    ready.send(rank_ref)
    first, second = [], []
    for h in range(MHEADS):
        base = 2 * h * KHALF
        first.append(against(query[:, base : base + KHALF], keys_ref[0, h]))
        second.append(against(query[:, base + KHALF : base + 2 * KHALF], keys_ref[1, h]))
    picks = picks_ref[...]
    scores = pick_chosen(first, picks // NSUB) + pick_chosen(second, picks % NSUB)
    exponent = jnp.exp(scores - group_reduce(scores, jnp.max, NEG))
    weights = exponent / group_reduce(exponent, jnp.sum, 0.0)
    weight_ref[...] = weights
    ready.send(weight_ref)
    send_ref[...] = to_slots(weights, slot_ref, owners).astype(BF16)


def to_slots(weights, slot_ref, owners):
    tokens = weights.shape[0]
    capacity = 2 * MHEADS * tokens // owners
    lane_group = iota((tokens, LANES), 1) // PICKS
    tiled = [
        tile_groups(jnp.where(lane_group == h, weights, 0.0), MHEADS).astype(BF16) for h in range(MHEADS)
    ]
    place = iota((owners * 8, tokens), 0)
    base = (place // 8) * capacity + place % 8
    out_group = iota((owners * 8, LANES), 1) // PICKS
    total = jnp.zeros((owners * 8, LANES), F32)
    for g in range(capacity // 8):
        part = jnp.zeros((owners * 8, LANES), F32)
        for h in range(MHEADS):
            chosen = jnp.where(base + g * 8 == slot_ref[h : h + 1, :], 1.0, 0.0).astype(BF16)
            part = part + product(chosen, tiled[h])
        total = jnp.where(out_group == g, part, total)
    return total


def plane_hits(slot_ref, plane, seq, capacity):
    tokens = slot_ref.shape[1]
    place = plane * (seq * capacity) + iota((seq * capacity, tokens), 0)
    chosen = jnp.zeros((seq * capacity, tokens), F32)
    for h in range(MHEADS):
        chosen = jnp.where(place == slot_ref[h : h + 1, :], 1.0, chosen)
    return chosen.astype(BF16)


def scatter_kernel(ready, *refs):
    ready()
    out_ref = refs[-1]
    seq, batches, capacity, wide = out_ref.shape
    plane = lax.axis_index("batch")
    for k in range(batches):
        chosen = plane_hits(refs[k], plane, seq, capacity)
        rows = product(chosen, refs[batches + k][...]).astype(BF16)
        source = lax.rem(plane + (batches - k), batches)
        out_ref[:, pl.ds(source, 1)] = rows.reshape(seq, 1, capacity, wide)


def gather_kernel(ready, *refs):
    ready()
    batches = (len(refs) - 1) // 2
    back_ref = refs[batches]
    seq, _, capacity, wide = back_ref.shape
    plane = lax.axis_index("batch")
    for k in range(batches):
        chosen = plane_hits(refs[k], plane, seq, capacity)
        source = lax.rem(plane + (batches - k), batches)
        rows = back_ref[:, pl.ds(source, 1)].reshape(seq * capacity, wide)
        refs[batches + 1 + k][...] = contract(chosen, rows).astype(BF16)


def memory_kernel(batches, ready, adapter, gate_ref, mix_ref, *refs):
    w_in_any, dn_any, up_any, mixed_ref, grank_ref, ggate_ref, part_ref, w, dn, up, sems = refs[batches:]
    a = adapter[0]
    copies = fetch([(dn_any.at[5, a], dn), (up_any.at[5, a], up), (w_in_any.at[4], w)], sems)
    ready()
    memory = refs[0][...].astype(F32)
    for k in range(1, batches):
        memory = memory + refs[k][...].astype(F32)
    gate = gate_ref[...]
    sigmoid = jax.nn.sigmoid(gate)
    mixed_ref[...] = (memory * (gate * sigmoid)).astype(BF16)
    ggate = (mix_ref[...].astype(F32) * memory * sigmoid * (1.0 + gate * (1.0 - sigmoid))).astype(BF16)
    ggate_ref[...] = ggate
    for copy in copies[:2]:
        copy.wait()
    granks = against(ggate, up[...]).astype(BF16)
    grank_ref[...] = granks
    extra = product(granks, dn[...])
    copies[2].wait()
    ready.send(mixed_ref, ggate_ref, grank_ref)
    part_ref[...] = against(ggate, w[...]) + extra


def output_kernel(ready, adapter, mixed_ref, mid_ref, w_out_any, dn_any, up_any, out_ref, rank_ref, w, dn, up, sems):
    a = adapter[0]
    copies = fetch([(dn_any.at[6, a], dn), (up_any.at[6, a], up), (w_out_any.at[1], w)], sems)
    ready()
    mixed = mixed_ref[...]
    for copy in copies[:2]:
        copy.wait()
    ranks = against(mixed, dn[...]).astype(BF16)
    rank_ref[...] = ranks
    extra = product(ranks, up[...])
    copies[2].wait()
    out_ref[...] = (mid_ref[...] + (product(mixed, w[...]) + extra)).astype(BF16)


def query_kernel(
    owners, rows_dev, ready, length, adapter, back_ref, slot_ref, picks_ref, weight_ref, part_ref, mid_ref, cot_ref, gain_ref,
    keys_ref, w_in_any, w_out_any, dn_any, up_any,
    go_ref, gquery_ref, grank_ref, gmid_ref, w, dn, up, turned, sems,
):
    groups, tokens, cols = go_ref.shape
    a = adapter[0]
    copies = fetch(
        [(dn_any.at[3, a], dn.at[0]), (dn_any.at[4, a], dn.at[1]), (up_any.at[3, a], up.at[0]),
         (up_any.at[4, a], up.at[1]), (w_in_any.at[3], w.at[0]), (w_out_any.at[0], w.at[1])],
        sems,
    )
    ready(slot_ref, weight_ref)
    capacity = 2 * MHEADS * tokens // owners
    slots = iota((tokens, owners * 8), 1)
    base = (slots // 8) * capacity + slots % 8
    lane_group = iota((tokens, LANES), 1) // PICKS
    back = back_ref[...]
    gw = jnp.zeros((tokens, LANES), F32)
    for h in range(MHEADS):
        part = jnp.zeros((tokens, LANES), F32)
        for g in range(capacity // 8):
            chosen = jnp.where(base + g * 8 == slot_ref[:, h : h + 1], 1.0, 0.0).astype(BF16)
            part = jnp.where(lane_group == g, product(chosen, back), part)
        gw = jnp.where(lane_group == h, tile_groups(part, MHEADS), gw)
    weights = weight_ref[...]
    gscore = jnp.transpose(weights * (gw - group_reduce(weights * gw, jnp.sum, 0.0)))
    turned[...] = gscore
    ready(picks_ref, keys_ref)
    span = rows_dev // NSUB
    halves = []
    for h in range(MHEADS):

        def one(r, sums):
            pick = picks_ref[h, pl.ds(r, 1), :]
            value = turned[pl.ds(h * PICKS + r, 1), :]
            low = jnp.where((pick // NSUB) % span == iota((8, tokens), 0), value, 0.0)
            return sums[0] + low, sums[1] + jnp.where(pick % NSUB == iota((NSUB, tokens), 0), value, 0.0)

        start = (jnp.zeros((8, tokens), F32), jnp.zeros((NSUB, tokens), F32))
        first, second = lax.fori_loop(0, PICKS, one, start, unroll=8)
        origin = picks_ref[h, 0:1, :] // rows_dev
        place = iota((NSUB, tokens), 0)
        wide = jnp.concatenate([first[:span]] * (NSUB // span), axis=0)
        wide = jnp.where(place // span == origin, wide, 0.0)
        halves.append(contract(wide.astype(BF16), keys_ref[0, h]))
        halves.append(contract(second.astype(BF16), keys_ref[1, h]))
    gquery = jnp.concatenate(halves, axis=1).astype(BF16)
    gquery_ref[...] = gquery
    ready.send(gquery_ref)
    ready()
    for copy in copies[:4]:
        copy.wait()
    granks = against(gquery, up[1]).astype(BF16)
    grank_ref[1] = granks
    extra = product(granks, dn[1])
    copies[4].wait()
    gnormed = against(gquery, w[0]) + extra + part_ref[...]
    middle = mid_ref[...]
    gmid = cot_ref[...].astype(F32) + norm_back(middle, inverse_norm(middle), gain_row(gain_ref), gnormed)
    gmid_ref[...] = gmid
    ready.send(gmid_ref)
    low = gmid.astype(BF16)
    granks = against(low, up[0]).astype(BF16)
    grank_ref[0] = granks
    ready.send(grank_ref)
    extra = product(granks, dn[0])
    copies[5].wait()
    go = against(low, w[1]) + extra
    row = lax.axis_index("seq") * tokens + iota((tokens, 1), 0)
    go = jnp.where(row < length[0], go, 0.0).astype(BF16)
    for s in range(groups):
        go_ref[s] = go[:, s * cols : (s + 1) * cols]


def place_columns(out_ref, row, values):
    groups, _, cols = out_ref.shape
    low = values.astype(BF16)
    for s in range(groups):
        out_ref[s, row : row + values.shape[0], :] = low[:, s * cols : (s + 1) * cols]


def factor_kernel(ready, att_ref, norm_ref, mixed_ref, gmid_ref, gquery_ref, ggate_ref, cot_ref, r35, r4, r6, g34, g5, g6, out_ref):
    ready()
    half = 4 * RANK
    sides = (
        (att_ref[...], gmid_ref[...].astype(BF16), r35[0], g34[0]),
        (norm_ref[...], gquery_ref[...], r4[...], g34[1]),
        (norm_ref[...], ggate_ref[...], r35[1], g5[...]),
        (mixed_ref[...], cot_ref[...], r6[...], g6[...]),
    )
    for j, (value, gy, rank, grank) in enumerate(sides):
        place_columns(out_ref, j * RANK, contract(grank, value))
        place_columns(out_ref, half + j * RANK, contract(rank, gy))


def entry_factor_kernel(ready, adapter, grad_ref, norm_ref, ranks_ref, up_any, out_ref, gy_ref, grank_ref, up, sems):
    groups, tokens, wide = grad_ref.shape
    cols = wide // 3
    a = adapter[0]
    copies = fetch([(up_any.at[j, a], up.at[pl.ds(RANK * j, RANK)]) for j in range(3)], sems)
    gys = [
        jnp.concatenate([grad_ref[s, :, j * cols : (j + 1) * cols] for s in range(groups)], axis=1) for j in range(3)
    ]
    for j in range(3):
        gy_ref[j] = gys[j]
    ready.send(gy_ref)
    for copy in copies:
        copy.wait()
    ready()
    place = iota((tokens, 3 * RANK), 1) // RANK
    granks = jnp.zeros((tokens, 3 * RANK), F32)
    ranks = ranks_ref[...]
    for j in range(3):
        granks = jnp.where(place == j, against(gys[j], up[...]), granks)
        up_grad = contract(ranks, gys[j])
        place_columns(out_ref, (3 + j) * RANK, up_grad[j * RANK : (j + 1) * RANK, :])
    granks = granks.astype(BF16)
    grank_ref[...] = granks
    ready.send(grank_ref)
    place_columns(out_ref, 0, contract(granks, norm_ref[...]))


def entry_kernel(ready, adapter, gy_ref, grank_ref, x_ref, gain_ref, gmid_ref, w_any, dn_any, out_ref, w, dn, sems):
    a = adapter[0]
    copies = fetch(
        [(dn_any.at[j, a], dn.at[pl.ds(RANK * j, RANK)]) for j in range(3)] + [(w_any.at[j], w.at[j]) for j in range(3)],
        sems,
    )
    ready()
    x = x_ref[...].astype(F32)
    for copy in copies[:3]:
        copy.wait()
    total = product(grank_ref[...], dn[...])
    for j in range(3):
        copies[3 + j].wait()
        total = total + against(gy_ref[j], w[j])
    back = norm_back(x, inverse_norm(x), gain_row(gain_ref), total)
    out_ref[...] = (gmid_ref[...] + back).astype(BF16)


def sum_kernel(ready, parts_ref, out_ref):
    ready()
    total = parts_ref[0].astype(F32)
    for s in range(1, parts_ref.shape[0]):
        total = total + parts_ref[s].astype(F32)
    out_ref[...] = total.astype(BF16)


def stack_kernel(ready, *refs):
    for k in range(refs[-1].shape[0]):
        refs[-1][k] = refs[k][...]


def relative_marks(ids_ref, batches):
    plane = lax.axis_index("batch")
    absolute = adapter_marks(ids_ref, batches)
    marks = []
    for k in range(batches):
        source = lax.rem(plane + (batches - k), batches)
        mark = absolute[0]
        for b in range(1, batches):
            mark = jnp.where(source == b, absolute[b], mark)
        marks.append(mark)
    return marks


def adapter_marks(ids_ref, batches):
    step = ids_ref.shape[0] // batches
    return [ids_ref[b * step : b * step + 1, 0:1] // 65536 for b in range(batches)]


def spread_block(rows, marks, target, stage, sem):
    for k in range(ADAPTERS):
        total = jnp.zeros(rows[0].shape, F32)
        for row, mark in zip(rows, marks, strict=True):
            total = total + jnp.where(mark == k, row, 0.0)
        stage[k] = total
    copy = pltpu.make_async_copy(stage, target, sem)
    copy.start()
    return copy


def spread_kernel(batches, ready, ids_ref, *refs):
    down_any, up_any, parts, stage, load_sems, sems = refs[-6:]
    seq = parts.shape[0]
    me = lax.axis_index("seq")
    copies = fetch([(refs[m % 2].at[m // 2], parts.at[me ^ m]) for m in range(seq)], load_sems)
    ready()
    marks = relative_marks(ids_ref, batches)
    for copy in copies:
        copy.wait()
    started = []
    for at in range(8):
        target = down_any.at[3 + at] if at < 4 else up_any.at[at - 1]
        if at >= 2:
            started[at - 2].wait()
        rows = [
            jnp.concatenate([parts[s, k, at * RANK : (at + 1) * RANK, :] for s in range(seq)], axis=1).astype(F32)
            for k in range(batches)
        ]
        started.append(spread_block(rows, marks, target, stage.at[at % 2], sems.at[at % 2]))
    started[-2].wait()
    started[-1].wait()


def last_spread_kernel(batches, ready, ids_ref, down_in, up_in, *refs):
    down_any, up_any, parts, stage, load_sems, sems = refs[-6:]
    seq = parts.shape[0]
    me = lax.axis_index("seq")
    copies = fetch([(refs[m % 2].at[m // 2], parts.at[me ^ m]) for m in range(seq)], load_sems)
    ready()
    marks = relative_marks(ids_ref, batches)
    for copy in copies:
        copy.wait()
    started = []
    for at in range(6):
        rows = [
            jnp.concatenate([parts[s, k, at * RANK : (at + 1) * RANK, :] for s in range(seq)], axis=1).astype(F32)
            for k in range(batches)
        ]
        target = down_any.at[at] if at < 3 else up_any.at[at - 3]
        started.append(spread_block(rows, marks, target, stage.at[at], sems.at[at]))
    for copy in started:
        copy.wait()


def along(values, axis, step, size):
    return lax.ppermute(values, axis, [(i, (i + step) % size) for i in range(size)])


def across(values, axis, mask, size):
    return lax.ppermute(values, axis, [(i, i ^ mask) for i in range(size)])


def to_pairs(values, axis, size):
    return [values] + [across(values, axis, m, size) for m in range(2, size, 2)]


def stacked(values, name):
    shape = shaped((len(values), *values[0].shape), values[0].dtype)
    return call(stack_kernel, name, "V" * len(values), [("V", shape)], values)[0]


def exchange(values, axes):
    return lax.all_to_all(values, axes, split_axis=0, concat_axis=0, tiled=True)


def body(
    inputs, lengths, adapter_index, memory_picks, input_weights, output_weights, adapter_down, adapter_up,
    attention_gain, memory_gain, half_keys, memory_values, cotangent,
):
    both = ("batch", "seq")
    batches, seq = lax.axis_size("batch"), lax.axis_size("seq")
    owners = batches * seq
    tokens, width = inputs.shape[1], inputs.shape[2]
    rows, cols, half = tokens * seq, width // seq, width // 2
    rows_dev = memory_values.shape[0]
    capacity = 2 * tokens * MHEADS // owners
    groups = capacity // 8
    items = owners * capacity
    block = min(owners * 8, 256)
    x, cot = inputs[0], cotangent[0]
    down = jnp.swapaxes(adapter_down, 2, 3)
    gain_one, gain_two = attention_gain, memory_gain
    picks = jnp.transpose(memory_picks[0], (1, 2, 0))
    matrix = pltpu.VMEM((width, width), BF16)
    pair = pltpu.VMEM((2, width, width), BF16)
    triple = pltpu.VMEM((3, width, width), BF16)
    small = pltpu.VMEM((RANK, width), BF16)
    two_small = pltpu.VMEM((2, RANK, width), BF16)
    three_small = pltpu.VMEM((3 * RANK, width), BF16)
    token_low, token_wide = shaped((tokens, width), BF16), shaped((tokens, width), F32)
    token_rank, token_lanes = shaped((tokens, RANK), BF16), shaped((tokens, LANES), F32)
    fixed = functools.partial

    qkv, normed, ranks = call(
        qkv_kernel, "qkv", "MLLHHH",
        [("V", shaped((seq, tokens, 3 * cols), BF16)), ("S", token_low), ("S", shaped((tokens, 3 * RANK), BF16))],
        (adapter_index, x, gain_one, input_weights, down, adapter_up), [triple, three_small, three_small, sema(9)],
    )
    qkv_all = exchange(qkv, "seq").reshape(rows, 3 * cols)

    slot, slot_col, pick, ids_out = call(
        fixed(route_kernel, rows_dev, owners), "route", "ML",
        [("V", shaped((8, tokens), I32)), ("S", shaped((tokens, tokens), I32)), ("S", shaped((tokens, LANES), I32)),
         ("V", shaped((owners * 8, LANES), I32))],
        (adapter_index, picks),
    )
    slots = [slot] + [along(slot, "batch", k, batches) for k in range(1, batches)]
    mix_grad, grank_six = call(
        mix_back_kernel, "mixback", "MLHHH", [("S", token_low), ("S", token_rank)],
        (adapter_index, cot, output_weights, down, adapter_up), [matrix, small, small, sema(3)],
    )

    qkv_all, mix_grad, ids_out, slots = lax.optimization_barrier((qkv_all, mix_grad, ids_out, slots))
    attended, lse, qkv_saved = call(
        attend_kernel, "attend", "MV",
        [("V", shaped((rows, cols), BF16)), ("S", shaped((8, rows), F32)), ("H", shaped((rows, 3 * cols), BF16))],
        (lengths, qkv_all), [sema(1)],
    )
    ids = exchange(ids_out.reshape(owners, 8, LANES), both).reshape(owners * 8, LANES)
    attended, ids = lax.optimization_barrier((attended, ids))
    o_all = exchange(attended.reshape(seq, tokens, cols), "seq")
    (index,) = call(
        fixed(prepare_kernel, groups, rows_dev), "prepare", "L", [("H", shaped((items, rows_dev), jnp.int16))], (ids,),
        [pltpu.VMEM((2, LANES, rows_dev), jnp.int16), pltpu.VMEM((owners * 8 // LANES, LANES, LANES), I32), sema(2)],
    )
    o_all, index = lax.optimization_barrier((o_all, index))
    left, right, same_two, att, rank_pair, middle, normed_two, gate = call(
        middle_kernel, "middle", "MVLLLHHHH",
        [("V", shaped((tokens, half), BF16)), ("V", shaped((tokens, half), BF16)), ("V", token_low), ("S", token_low),
         ("S", shaped((2, tokens, RANK), BF16)), ("S", token_wide), ("S", token_low), ("S", token_wide)],
        (adapter_index, o_all, x, gain_two, mix_grad, input_weights, output_weights, down, adapter_up),
        [pair, two_small, two_small, sema(6)],
    )
    lefts = [left] + [along(left, "batch", k, batches) for k in range(1, batches)]
    weight_out, rank_four, weights = call(
        fixed(scores_kernel, owners), "scores", "MVLLLHHH",
        [("V", shaped((owners * 8, LANES), BF16)), ("S", token_rank), ("S", token_lanes)],
        (adapter_index, same_two, pick, slot, half_keys, input_weights, down, adapter_up), [matrix, small, small, sema(3)],
    )
    weight_in = exchange(weight_out.reshape(owners, 8, LANES), both).reshape(owners * 8, LANES)
    right, lefts = lax.optimization_barrier((right, lefts))
    rights = [right] + [along(right, "batch", k, batches) for k in range(1, batches)]

    def scatter(parts, name):
        out = [("V", shaped((seq, batches, capacity, half), BF16))]
        return call(scatter_kernel, name, "L" * batches + "V" * batches, out, (*slots, *parts))[0]

    left_out = scatter(lefts, "scatterleft")
    left_out, weight_in = lax.optimization_barrier((left_out, weight_in))
    left_in = exchange(left_out, "seq").reshape(items, half)

    (sums,) = call(
        fixed(recall_kernel, groups), "recall", "VHH", [("V", shaped((seq, batches, capacity, width), BF16))],
        (weight_in, index, memory_values),
        [pltpu.VMEM((rows_dev, width), BF16), pltpu.VMEM((2, block, rows_dev), jnp.int16), pltpu.VMEM((2, block, rows_dev), BF16), sema(3)],
        flops=1 << 32,
    )
    sums, left_in = lax.optimization_barrier((sums, left_in))
    back = exchange(sums, "seq")

    def recall_back(part, name, grads, kind, dtype, *before):
        return call(
            fixed(recall_back_kernel, part, batches, groups), name, "L" + "L" * part + "VH",
            [(kind, shaped((owners * 8, LANES), dtype))], (ids, *before, grads, memory_values),
            [pltpu.VMEM((rows_dev, half), BF16), pltpu.VMEM((block, rows_dev), F32), sema(1)], flops=1 << 31,
        )[0]

    right_out = scatter(rights, "scatterright")
    found_left = recall_back(0, "recallleft", left_in, "S", F32)
    right_out, back, found_left = lax.optimization_barrier((right_out, back, found_left))
    right_in = exchange(right_out, "seq").reshape(items, half)
    pieces = call(
        gather_kernel, "gather", "L" * batches + "V", [("V", token_low) for _ in range(batches)], (*slots, back),
    )
    pieces = [pieces[0]] + [along(pieces[k], "batch", batches - k, batches) for k in range(1, batches)]
    found = recall_back(1, "recallright", right_in, "V", BF16, found_left)
    found_back = exchange(found.reshape(owners, 8, LANES), both).reshape(owners * 8, LANES)

    mixed, grank_five, ggate, part = call(
        fixed(memory_kernel, batches), "memory", "MLL" + "V" * batches + "HHH",
        [("S", token_low), ("S", token_rank), ("S", token_low), ("S", token_wide)],
        (adapter_index, gate, mix_grad, *pieces, input_weights, down, adapter_up), [matrix, small, small, sema(3)],
    )

    go, gquery, grank_pair, gmid = call(
        fixed(query_kernel, owners, rows_dev), "query", "MMVLLLLLLLLHHHH",
        [("V", shaped((seq, tokens, cols), BF16)), ("S", token_low), ("S", shaped((2, tokens, RANK), BF16)), ("S", token_wide)],
        (lengths, adapter_index, found_back, slot_col, picks, weights, part, middle, cot, gain_two, half_keys,
         input_weights, output_weights, down, adapter_up),
        [pair, two_small, two_small, pltpu.VMEM((LANES, tokens), F32), sema(6)],
    )
    go_all = exchange(go, "seq").reshape(rows, cols)
    mixed, go = lax.optimization_barrier((mixed, go))
    output, rank_six = call(
        output_kernel, "output", "MLLHHH", [("S", token_low), ("S", token_rank)],
        (adapter_index, mixed, middle, output_weights, down, adapter_up), [matrix, small, small, sema(3)],
    )
    (factors,) = call(
        factor_kernel, "factors", "L" * 13, [("V", shaped((seq, 8 * RANK, cols), BF16))],
        (att, normed_two, mixed, gmid, gquery, ggate, cot, rank_pair, rank_four, rank_six, grank_pair, grank_five, grank_six),
    )
    factors, go_all = lax.optimization_barrier((factors, go_all))
    early_parts = exchange(factors, "seq")

    (grads,) = call(
        attend_back_kernel, "attendback", "MLVL", [("V", shaped((rows, 3 * cols), BF16))], (lengths, qkv_saved, go_all, lse),
        [pltpu.VMEM((rows, LANES), F32), pltpu.VMEM((rows, LANES), F32)],
    )
    grads, early_parts = lax.optimization_barrier((grads, early_parts))
    grads_all = exchange(grads.reshape(seq, tokens, 3 * cols), "seq")
    (some,) = call(sum_kernel, "sumearly", "V", [("V", shaped((8 * RANK, cols), BF16))], (early_parts,))
    some = [some] + [along(some, "batch", k, batches) for k in range(1, batches)]
    some = stacked(some, "stackearly")
    late, gys, granks = call(
        entry_factor_kernel, "entryfactors", "MVLLH",
        [("V", shaped((seq, 6 * RANK, cols), BF16)), ("S", shaped((3, tokens, width), BF16)), ("S", shaped((tokens, 3 * RANK), BF16))],
        (adapter_index, grads_all, normed, ranks, adapter_up), [three_small, sema(3)],
    )
    late, some = lax.optimization_barrier((late, some))
    late_parts = exchange(late, "seq")
    some = to_pairs(some, "seq", seq)
    (grad_input,) = call(
        entry_kernel, "entry", "MLLLLLHH", [("S", token_low)],
        (adapter_index, gys, granks, x, gain_one, gmid, input_weights, down), [triple, three_small, sema(6)],
    )
    late_parts, some, grad_input = lax.optimization_barrier((late_parts, some, grad_input))
    (late_sum,) = call(sum_kernel, "sumlate", "V", [("V", shaped((6 * RANK, cols), BF16))], (late_parts,))
    late_sums = [late_sum] + [along(late_sum, "batch", k, batches) for k in range(1, batches)]
    some = stacked(some, "pairsearly")
    late_sums, some = lax.optimization_barrier((late_sums, some))
    late_all = to_pairs(stacked(late_sums, "stacklate"), "seq", seq)
    some = (some, across(some, "seq", 1, seq))
    full = shaped((7, ADAPTERS, RANK, width), F32)
    grad_down, grad_up = call(
        fixed(spread_kernel, batches), "spread", "LVV", [("H", full), ("H", full)], (ids, *some),
        [pltpu.VMEM((seq, batches, 8 * RANK, cols), BF16), pltpu.VMEM((2, ADAPTERS, RANK, width), F32), sema(seq), sema(2)],
    )
    late_all, grad_down, grad_up = lax.optimization_barrier((late_all, grad_down, grad_up))
    late_all = stacked(late_all, "pairslate")
    late_all = (late_all, across(late_all, "seq", 1, seq))
    grad_down, grad_up = call(
        fixed(last_spread_kernel, batches), "lastspread", "LHHVV", [("H", full), ("H", full)],
        (ids, grad_down, grad_up, *late_all),
        [pltpu.VMEM((seq, batches, 6 * RANK, cols), BF16), pltpu.VMEM((6, ADAPTERS, RANK, width), F32), sema(seq), sema(6)],
        aliases={1: 0, 2: 1},
    )
    return (output[None], grad_input[None], jnp.swapaxes(grad_down, 2, 3), grad_up)


def solution(mesh):
    split = P("batch", "seq", None)
    return jax.shard_map(
        body,
        mesh=mesh,
        in_specs=(
            split, P("batch"), P("batch"), P("batch", "seq", None, None), P(), P(), P(), P(), P(), P(), P(),
            P(("batch", "seq"), None), split,
        ),
        out_specs=(split, split, P(), P()),
        check_vma=False,
    )
```

```python
import functools

import jax
import jax.numpy as jnp
from jax import lax
from jax.experimental import pallas as pl
from jax.experimental.pallas import tpu as pltpu
from jax.sharding import PartitionSpec as P

HEAD_DIM = 64
MHEADS = 4
KHALF = 128
NSUB = 256
PICKS = 32
ADAPTERS = 8
RANK = 16
LANES = 128
ADAPTER_STEP = 4096
EPS = 1e-06
NEG = -1e30
F32 = jnp.float32
BF16 = jnp.bfloat16
I32 = jnp.int32
HBM = pl.BlockSpec(memory_space=pltpu.HBM)
SMEM = pl.BlockSpec(memory_space=pltpu.SMEM)
VMEM = pl.BlockSpec(memory_space=pltpu.VMEM)
MIB = 1 << 20


def product(left, right):
    return lax.dot_general(left, right, (((1,), (0,)), ((), ())), preferred_element_type=F32)


def against(left, right):
    return lax.dot_general(left, right, (((1,), (1,)), ((), ())), preferred_element_type=F32)


def contract(left, right):
    return lax.dot_general(left, right, (((0,), (0,)), ((), ())), preferred_element_type=F32)


def iota(shape, axis):
    return lax.broadcasted_iota(I32, shape, axis)


def lane_pick(table, index):
    return jnp.take_along_axis(table, index, axis=1, mode="promise_in_bounds")


def shaped(shape, dtype):
    return jax.ShapeDtypeStruct(shape, dtype)


class Stage:
    def __init__(self, loads, stores):
        self.loads, self.stores = loads, stores
        self.waited, self.begun = set(), set()
        for _, copy in loads:
            copy.start()

    def __call__(self, *refs):
        for at, (ref, copy) in enumerate(self.loads):
            if at not in self.waited and (not refs or any(ref is one for one in refs)):
                self.waited.add(at)
                copy.wait()

    def send(self, *refs):
        for at, (ref, copy) in enumerate(self.stores):
            if at not in self.begun and (not refs or any(ref is one for one in refs)):
                self.begun.add(at)
                copy.start()

    def finish(self):
        self()
        self.send()
        for _, copy in self.stores:
            copy.wait()


def call(kernel, name, ins, outs, args, scratch=(), vmem=40, flops=1 << 28, moved=1 << 22, aliases=None):
    shapes = [(args[i].shape, args[i].dtype) for i, kind in enumerate(ins) if kind == "L"]
    stored = [(out.shape, out.dtype) for kind, out in outs if kind == "S"]
    count_in, count_out, count_user = len(ins), len(outs), len(scratch)

    def wrapped(*refs):
        given, results = list(refs[:count_in]), list(refs[count_in : count_in + count_out])
        rest = list(refs[count_in + count_out :])
        user, buffers = rest[:count_user], rest[count_user:]
        loads, stores = [], []
        for i, kind in enumerate(ins):
            if kind == "L":
                at = len(loads)
                loads.append((buffers[at], pltpu.make_async_copy(given[i], buffers[at], buffers[-1].at[at])))
                given[i] = buffers[at]
        for i, (kind, _) in enumerate(outs):
            if kind == "S":
                at = len(loads) + len(stores)
                stores.append((buffers[at], pltpu.make_async_copy(buffers[at], results[i], buffers[-1].at[at])))
                results[i] = buffers[at]
        stage = Stage(loads, stores)
        kernel(stage, *given, *results, *user)
        stage.finish()

    spaces = {"V": VMEM, "L": HBM, "S": HBM, "H": HBM, "M": SMEM}
    autos = [pltpu.VMEM(*one) for one in shapes + stored]
    args = [
        pltpu.with_memory_space_constraint(one, pltpu.HBM) if kind in "LH" else one
        for kind, one in zip(ins, args, strict=True)
    ]
    return pl.pallas_call(
        wrapped,
        name=name,
        out_shape=[pltpu.HBM(out.shape, out.dtype) if kind in "SH" else out for kind, out in outs],
        in_specs=[spaces[kind] for kind in ins],
        out_specs=[spaces[kind] for kind, _ in outs],
        input_output_aliases=aliases or {},
        scratch_shapes=list(scratch) + autos + ([sema(len(autos))] if autos else []),
        compiler_params=pltpu.CompilerParams(vmem_limit_bytes=vmem * MIB),
        cost_estimate=pl.CostEstimate(flops=flops, bytes_accessed=moved, transcendentals=0),
    )(*args)


def fetch(pairs, sems):
    copies = [
        pltpu.make_async_copy(source, target, sems.at[place])
        for place, (source, target) in enumerate(pairs)
    ]
    for copy in copies:
        copy.start()
    return copies


def sema(count):
    return pltpu.SemaphoreType.DMA((count,))


def gain_row(ref):
    return ref[...].astype(F32).reshape(1, ref.shape[0])


def inverse_norm(values):
    return lax.rsqrt(jnp.mean(values * values, axis=1, keepdims=True) + EPS)


def norm_back(values, inverse, scales, incoming):
    weighted = incoming * scales
    inner = jnp.mean(weighted * values, axis=1, keepdims=True)
    return weighted * inverse - values * inverse * inverse * inverse * inner


def qkv_kernel(ready, adapter, x_ref, gain_ref, w_any, dn_any, up_any, out_ref, norm_ref, rank_ref, w, dn, up, sems):
    groups, tokens, wide = out_ref.shape
    cols = wide // 3
    a = adapter[0]
    copies = fetch(
        [(dn_any.at[j, a], dn.at[pl.ds(RANK * j, RANK)]) for j in range(3)]
        + [(up_any.at[j, a], up.at[pl.ds(RANK * j, RANK)]) for j in range(3)]
        + [(w_any.at[j], w.at[j]) for j in range(3)],
        sems,
    )
    ready()
    x = x_ref[...].astype(F32)
    normed = (x * inverse_norm(x) * gain_row(gain_ref)).astype(BF16)
    norm_ref[...] = normed
    ready.send(norm_ref)
    for copy in copies[:6]:
        copy.wait()
    ranks = against(normed, dn[...]).astype(BF16)
    rank_ref[...] = ranks
    ready.send(rank_ref)
    place = iota((tokens, 3 * RANK), 1) // RANK
    for j in range(3):
        own = jnp.where(place == j, ranks.astype(F32), 0.0).astype(BF16)
        extra = product(own, up[...])
        copies[6 + j].wait()
        result = (product(normed, w[j]) + extra).astype(BF16)
        for s in range(groups):
            out_ref[s, :, j * cols : (j + 1) * cols] = result[:, s * cols : (s + 1) * cols]


def mix_back_kernel(ready, adapter, cot_ref, w_any, dn_any, up_any, grad_ref, rank_ref, w, dn, up, sems):
    a = adapter[0]
    copies = fetch([(up_any.at[6, a], up), (dn_any.at[6, a], dn), (w_any.at[1], w)], sems)
    ready()
    gy = cot_ref[...]
    copies[0].wait()
    ranks = against(gy, up[...]).astype(BF16)
    rank_ref[...] = ranks
    copies[1].wait()
    extra = product(ranks, dn[...])
    copies[2].wait()
    grad_ref[...] = (against(gy, w[...]) + extra).astype(BF16)


def route_kernel(rows_dev, owners, ready, adapter, picks_ref, slot_ref, slot_col_ref, pick_ref, *ids_refs):
    ready()
    heads, picks, tokens = picks_ref.shape
    capacity = 2 * heads * tokens // owners
    groups = capacity // 8
    visits = heads * tokens
    owner = jnp.concatenate([picks_ref[h, 0:1, :] for h in range(heads)], axis=1) // rows_dev
    hot = jnp.where(iota((owners, visits), 0) == owner, 1.0, 0.0)
    before = jnp.where(iota((visits, visits), 0) < iota((visits, visits), 1), 1.0, 0.0).astype(BF16)
    counts = product(hot.astype(BF16), before)
    within = jnp.sum(hot * counts, axis=0, keepdims=True).astype(I32)
    slot = owner * capacity + within
    rows = [slot[:, h * tokens : (h + 1) * tokens] for h in range(heads)]
    stacked = jnp.concatenate(rows + [jnp.full((8 - heads, tokens), -1, I32)], axis=0)
    slot_ref[...] = stacked
    tall = jnp.concatenate([stacked, jnp.full((tokens - 8, tokens), -1, I32)], axis=0)
    slot_col_ref[...] = jnp.transpose(tall)
    packed = jnp.concatenate([picks_ref[h] for h in range(heads)], axis=0)
    by_token = jnp.transpose(packed)
    pick_ref[...] = by_token
    local = by_token % rows_dev
    lanes = iota((tokens, LANES), 1)
    total = jnp.zeros((owners * 8, LANES), F32)
    out_lane = iota((owners * 8, LANES), 1) // PICKS
    place = iota((owners * 8, tokens), 0)
    base = (place // 8) * capacity + place % 8
    for g in range(groups):
        high = jnp.zeros((owners * 8, LANES), F32)
        low = jnp.zeros((owners * 8, LANES), F32)
        for h in range(heads):
            chosen = jnp.where(base + g * 8 == rows[h], 1.0, 0.0).astype(BF16)
            own = jnp.where(lanes // PICKS == h, local, 0)
            own = tile_groups(own.astype(F32), heads).astype(I32)
            high = high + product(chosen, (own // 256).astype(F32).astype(BF16))
            low = low + product(chosen, (own % 256).astype(F32).astype(BF16))
        total = jnp.where(out_lane == g, high * 256.0 + low, total)
    batches = len(ids_refs) - 1
    part = owners * 8 // batches
    ids_refs[-1][...] = total.astype(I32) + adapter[0] * ADAPTER_STEP
    for k in range(batches):
        target = lax.rem(lax.axis_index("batch") + k, batches)
        ids_refs[k][...] = ids_refs[-1][pl.ds(pl.multiple_of(target * part, part), part), :]


def tile_groups(values, count):
    total = values
    for turn in range(1, count):
        total = total + pltpu.roll(values, turn * PICKS, 1)
    return total


def prepare_kernel(groups, rows_dev, batches, ready, sent_ref, ids_ref, index_any, stage, turned, sems):
    ready()
    seq, _, cols = sent_ref.shape
    lanes = groups * PICKS
    chunks = 2 * lanes // cols
    for k in range(batches):
        source = lax.rem(lax.axis_index("batch") + (batches - k), batches)
        for s in range(seq):
            both = [
                sent_ref[s, (chunk * batches + k) * 8 : (chunk * batches + k + 1) * 8, :].astype(F32)
                for chunk in range(chunks)
            ]
            both = jnp.concatenate(both, axis=1).astype(I32)
            ids = widen(both[:, :lanes] * 256 + both[:, lanes:])
            ids_ref[pl.ds(pl.multiple_of((source * seq + s) * 8, 8), 8), :] = ids
    ready.send(ids_ref)
    places = ids_ref.shape[0]
    chunks = rows_dev // LANES
    high_rows = max(8, chunks)
    steps = groups * (places // LANES)
    for k in range(places // LANES):
        turned[k] = jnp.transpose(ids_ref[k * LANES : (k + 1) * LANES, :] & (ADAPTER_STEP - 1))

    def put(step, slot):
        target = index_any.at[pl.ds(pl.multiple_of(step * LANES, LANES), LANES)]
        return pltpu.make_async_copy(stage.at[slot], target, sems.at[slot])

    def one(step, carry):
        k, g = lax.rem(step, places // LANES), step // (places // LANES)
        slot = lax.rem(step, 2)
        mask = jnp.zeros((LANES, LANES), I32)
        highs = jnp.zeros((high_rows, LANES), I32)
        for r in range(PICKS):
            bit = (1 << r) if r < 31 else -(1 << 31)
            row = turned[k, pl.ds(g * PICKS + r, 1), :]
            mask = mask | jnp.where(row & 127 == iota((LANES, LANES), 0), bit, 0)
            highs = highs | jnp.where(row >> 7 == iota((high_rows, LANES), 0), bit, 0)

        @pl.when(step >= 2)
        def _():
            put(step - 2, slot).wait()

        for c in range(chunks):
            index = 31 - lax.clz(mask & highs[c : c + 1, :])
            stage[slot, :, c * LANES : (c + 1) * LANES] = jnp.transpose(index).astype(jnp.int16)
        put(step, slot).start()
        return carry

    lax.fori_loop(0, steps, one, 0)
    for step in range(max(0, steps - 2), steps):
        put(step, step % 2).wait()


def recall_kernel(groups, ready, weight_ref, index_any, mem_any, out_ref, mem, index, dense, sems):
    places = weight_ref.shape[0]
    rows_dev = mem.shape[0]
    chunks = rows_dev // LANES
    block = dense.shape[1]
    per_group = places // block
    blocks = groups * per_group
    seq = out_ref.shape[0]
    planes = block // (8 * seq)

    def load(b, slot):
        source = index_any.at[pl.ds(pl.multiple_of(b * block, block), block)]
        return pltpu.make_async_copy(source, index.at[slot], sems.at[1 + slot])

    load(0, 0).start()
    copy = pltpu.make_async_copy(mem_any, mem, sems.at[0])
    copy.start()

    def gather(b, side):
        g, k = b // per_group, lax.rem(b, per_group)
        load(b, side).wait()

        @pl.when(b + 1 < blocks)
        def _():
            load(b + 1, 1 - side).start()

        for start in range(0, block, 16):
            weights = weight_ref[pl.ds(pl.multiple_of(k * block + start, 16), 16), :].astype(F32)
            for c in range(chunks):
                at = index[side, start : start + 16, c * LANES : (c + 1) * LANES].astype(I32)
                value = lane_pick(weights, (at + g * PICKS) & 127)
                dense[side, start : start + 16, c * LANES : (c + 1) * LANES] = jnp.where(at >= 0, value, 0.0).astype(BF16)

    def multiply(b, side):
        g, k = b // per_group, lax.rem(b, per_group)
        result = product(dense[side], mem[...]).astype(BF16)
        for i in range(planes):
            rows = result[i * seq * 8 : (i + 1) * seq * 8]
            out_ref[:, k * planes + i, pl.ds(pl.multiple_of(g * 8, 8), 8), :] = rows.reshape(seq, 8, rows.shape[1])

    gather(0, 0)
    copy.wait()

    def whole(i, carry):
        gather(2 * i + 1, 1)
        multiply(2 * i, 0)

        @pl.when(2 * i + 2 < blocks)
        def _():
            gather(2 * i + 2, 0)
            multiply(2 * i + 1, 1)

        @pl.when(2 * i + 2 >= blocks)
        def _():
            multiply(2 * i + 1, 1)

        return carry

    lax.fori_loop(0, blocks // 2, whole, 0)


def recall_back_kernel(part, batches, groups, ready, ids_ref, *refs):
    before_ref = refs[0] if part else None
    grad_ref, mem_any, out_ref, mem, scores, sems = refs[part:]
    items, half = grad_ref.shape
    seq = items // (batches * groups * 8)
    rows_dev = mem.shape[0]
    capacity = groups * 8
    chunks = rows_dev // LANES
    block = scores.shape[0]
    per_block = block // capacity
    blocks = items // block
    copies = fetch([(mem_any.at[:, pl.ds(part * half, half)], mem)], sems)
    ready()
    copies[0].wait()

    def whole(b, outer):
        scores[...] = against(grad_ref[pl.ds(pl.multiple_of(b * block, block), block), :], mem[...])

        lane_group = iota((8, LANES), 1) // PICKS
        for local in range(per_block):
            sender = b * per_block + local
            spot = lax.rem(sender, batches) * seq + sender // batches
            start = pl.multiple_of(spot * 8, 8)
            ids = ids_ref[pl.ds(start, 8), :] & (ADAPTER_STEP - 1)
            low = ids & 127
            high = ids >> 7
            total = before_ref[pl.ds(start, 8), :] if part else jnp.zeros((8, LANES), F32)
            for g in range(groups):
                key = jnp.where(lane_group == g, high, -1)
                here = jnp.zeros((8, LANES), F32)
                row = local * capacity + g * 8
                for c in range(chunks):
                    found = scores[row : row + 8, c * LANES : (c + 1) * LANES]
                    here = jnp.where(key == c, lane_pick(found, low), here)
                total = total + here
            out_ref[pl.ds(start, 8), :] = total.astype(out_ref.dtype)
        return outer

    lax.fori_loop(0, blocks, whole, 0)


def head_parts(values, h, spare):
    lane = iota(values.shape, 1)
    return jnp.where(lane // HEAD_DIM == h, values, jnp.where(lane == (1 - h) * HEAD_DIM, spare, 0.0)).astype(BF16)


def widen(values):
    if values.shape[1] == LANES:
        return values
    return jnp.concatenate([values, jnp.zeros((values.shape[0], LANES - values.shape[1]), values.dtype)], axis=1)


def attend_kernel(groups, batches, ready, length, qkv_ref, *refs):
    o_ref, lse_ref, saved_any, sems = refs[batches:]
    ready()
    saving = pltpu.make_async_copy(qkv_ref, saved_any, sems.at[0])
    saving.start()
    rows, wide = qkv_ref.shape
    cols = wide // 3
    seq = o_ref.shape[0]
    lanes = groups * PICKS
    for s in range(seq):
        ids = jnp.concatenate([refs[k][s * 8 : (s + 1) * 8, :lanes] for k in range(batches)], axis=0)
        both = jnp.concatenate([ids // 256, ids % 256], axis=1).astype(F32).astype(BF16)
        for chunk in range(2 * lanes // cols):
            start = rows // seq + chunk * batches * 8
            o_ref[s, start : start + batches * 8, :] = both[:, chunk * cols : (chunk + 1) * cols]
    heads = cols // HEAD_DIM
    size = min(256, rows)
    valid = length[0]
    bias = jnp.where(iota((rows, LANES), 0) < valid, 0.0, NEG)
    keys = widen(qkv_ref[:, cols : 2 * cols].astype(F32))
    key_parts = [head_parts(keys, h, bias) for h in range(heads)]
    values_t = jnp.transpose(widen(qkv_ref[:, 2 * cols :].astype(F32))).astype(BF16)
    for i in range(rows // size):
        first, last = i * size, (i + 1) * size
        queries = widen(qkv_ref[first:last, 0:cols].astype(F32)) * (HEAD_DIM**-0.5)
        mixed = jnp.zeros((LANES, size), F32)
        stats = []
        for h in range(heads):
            query = head_parts(queries, h, 1.0)
            near = against(key_parts[h][first:last], query)
            near = jnp.where(iota((size, size), 0) <= iota((size, size), 1), near, NEG)
            high = jnp.max(near, axis=0, keepdims=True)
            if i:
                far = against(key_parts[h][:first], query)
                high = jnp.maximum(high, jnp.max(far, axis=0, keepdims=True))
            near = jnp.exp(near - high)
            summed = jnp.sum(near, axis=0, keepdims=True)
            result = product(values_t[:, first:last], near.astype(BF16))
            if i:
                far = jnp.exp(far - high)
                summed = summed + jnp.sum(far, axis=0, keepdims=True)
                result = result + product(values_t[:, :first], far.astype(BF16))
            stats.append(high + jnp.log(summed))
            mixed = jnp.where(iota((LANES, size), 0) // HEAD_DIM == h, result / summed, mixed)
        mixed = jnp.where(first + iota((LANES, size), 1) < valid, mixed, 0.0)
        low = jnp.transpose(mixed)[:, :cols].astype(BF16)
        tokens = rows // seq
        for part in range(max(1, size // tokens)):
            o_ref[first // tokens + part, 0:tokens, :] = low[part * tokens : (part + 1) * tokens]
        lse_ref[:, first:last] = jnp.concatenate(stats + [jnp.zeros((8 - heads, size), F32)], axis=0)
    saving.wait()


def attend_back_kernel(ready, length, qkv_ref, go_ref, lse_ref, out_ref, dk, dv):
    ready()
    rows, wide = qkv_ref.shape
    cols = wide // 3
    heads = cols // HEAD_DIM
    size = min(256, rows)
    valid = length[0]
    scaling = HEAD_DIM**-0.5
    bias = jnp.where(iota((rows, LANES), 0) < valid, 0.0, NEG)
    keys = widen(qkv_ref[:, cols : 2 * cols].astype(F32))
    keys_t = jnp.transpose(keys).astype(BF16)
    key_parts = [head_parts(keys, h, bias) for h in range(heads)]
    values = widen(qkv_ref[:, 2 * cols :])
    dk[...] = jnp.zeros_like(dk)
    dv[...] = jnp.zeros_like(dv)
    for i in range(rows // size):
        first, last = i * size, (i + 1) * size
        queries = widen(qkv_ref[first:last, 0:cols].astype(F32)) * scaling
        grads = widen(go_ref[first:last, :].astype(F32))
        dq = jnp.zeros((LANES, size), F32)
        for h in range(heads):
            query = head_parts(queries, h, 1.0)
            plain = head_parts(queries, h, 0.0)
            grad = head_parts(grads, h, 0.0)
            lse = lse_ref[h : h + 1, first:last]
            near = against(key_parts[h][first:last], query)
            near = jnp.where(iota((size, size), 0) <= iota((size, size), 1), near, NEG)
            near = jnp.exp(near - lse)
            near_gp = against(values[first:last], grad)
            delta = jnp.sum(near * near_gp, axis=0, keepdims=True)
            if i:
                far = jnp.exp(against(key_parts[h][:first], query) - lse)
                far_gp = against(values[:first], grad)
                delta = delta + jnp.sum(far * far_gp, axis=0, keepdims=True)
            near_gs = (near * (near_gp - delta)).astype(BF16)
            result = product(keys_t[:, first:last], near_gs)
            dk[first:last] += product(near_gs, plain)
            dv[first:last] += product(near.astype(BF16), grad)
            if i:
                far_gs = (far * (far_gp - delta)).astype(BF16)
                result = result + product(keys_t[:, :first], far_gs)
                dk[:first] += product(far_gs, plain)
                dv[:first] += product(far.astype(BF16), grad)
            dq = jnp.where(iota((LANES, size), 0) // HEAD_DIM == h, result, dq)
        out_ref[first:last, 0:cols] = (jnp.transpose(dq) * scaling)[:, :cols].astype(BF16)
    out_ref[:, cols : 2 * cols] = dk[:, :cols].astype(BF16)
    out_ref[:, 2 * cols :] = dv[:, :cols].astype(BF16)


def pick_chosen(tables, index):
    tokens = index.shape[0]
    low = index & 127
    key = (index >> 7) + (iota((tokens, LANES), 1) // PICKS) * (NSUB // LANES)
    total = jnp.zeros((tokens, LANES), F32)
    for h in range(MHEADS):
        for c in range(NSUB // LANES):
            found = lane_pick(tables[h][:, c * LANES : (c + 1) * LANES], low)
            total = jnp.where(key == h * (NSUB // LANES) + c, found, total)
    return total


def group_reduce(values, reducer, fill):
    group = iota(values.shape, 1) // PICKS
    total = jnp.zeros(values.shape, F32)
    for h in range(MHEADS):
        one = reducer(jnp.where(group == h, values, fill), axis=1, keepdims=True)
        total = jnp.where(group == h, one, total)
    return total


def middle_kernel(
    ready, adapter, o_ref, x_ref, gain_ref, mix_ref, w_in_any, w_out_any, dn_any, up_any,
    left_ref, right_ref, same_ref, sent_ref, att_ref, rank_ref, mid_ref, norm_ref, gate_ref, w, dn, up, sems,
):
    groups = o_ref.shape[0]
    a = adapter[0]
    copies = fetch(
        [(dn_any.at[3, a], dn.at[0]), (dn_any.at[5, a], dn.at[1]), (up_any.at[3, a], up.at[0]), (up_any.at[5, a], up.at[1]),
         (w_out_any.at[0], w.at[0]), (w_in_any.at[4], w.at[1])],
        sems,
    )
    tokens = att_ref.shape[0]
    attended = jnp.concatenate([o_ref[s, 0:tokens, :] for s in range(groups)], axis=1)
    sent_ref[...] = o_ref[:, tokens:, :]
    ready.send(sent_ref)
    att_ref[...] = attended
    ready.send(att_ref)
    for copy in copies[:4]:
        copy.wait()
    rank_three = against(attended, dn[0]).astype(BF16)
    extra = product(rank_three, up[0])
    copies[4].wait()
    ready(x_ref, gain_ref)
    middle = x_ref[...].astype(F32) + (product(attended, w[0]) + extra)
    mid_ref[...] = middle
    normed = (middle * inverse_norm(middle) * gain_row(gain_ref)).astype(BF16)
    norm_ref[...] = normed
    same_ref[...] = normed
    ready.send(mid_ref, norm_ref)
    rank_five = against(normed, dn[1]).astype(BF16)
    rank_ref[0] = rank_three
    rank_ref[1] = rank_five
    extra = product(rank_five, up[1])
    copies[5].wait()
    gate = product(normed, w[1]) + extra
    gate_ref[...] = gate
    ready.send(rank_ref, gate_ref)
    ready(mix_ref)
    memory_grad = (mix_ref[...].astype(F32) * (gate * jax.nn.sigmoid(gate))).astype(BF16)
    half = left_ref.shape[1]
    left_ref[...] = memory_grad[:, :half]
    right_ref[...] = memory_grad[:, half:]


def scores_kernel(
    owners, ready, adapter, normed_ref, picks_ref, slot_ref, keys_ref, w_in_any, dn_any, up_any,
    send_ref, rank_ref, weight_ref, w, dn, up, sems,
):
    a = adapter[0]
    copies = fetch([(dn_any.at[4, a], dn), (up_any.at[4, a], up), (w_in_any.at[3], w)], sems)
    normed = normed_ref[...]
    copies[0].wait()
    ranks = against(normed, dn[...]).astype(BF16)
    rank_ref[...] = ranks
    copies[1].wait()
    extra = product(ranks, up[...])
    copies[2].wait()
    query = (product(normed, w[...]) + extra).astype(BF16)
    ready()
    ready.send(rank_ref)
    first, second = [], []
    for h in range(MHEADS):
        base = 2 * h * KHALF
        first.append(against(query[:, base : base + KHALF], keys_ref[0, h]))
        second.append(against(query[:, base + KHALF : base + 2 * KHALF], keys_ref[1, h]))
    picks = picks_ref[...]
    scores = pick_chosen(first, picks // NSUB) + pick_chosen(second, picks % NSUB)
    exponent = jnp.exp(scores - group_reduce(scores, jnp.max, NEG))
    weights = exponent / group_reduce(exponent, jnp.sum, 0.0)
    weight_ref[...] = weights
    ready.send(weight_ref)
    send_ref[...] = to_slots(weights, slot_ref, owners).astype(BF16)


def to_slots(weights, slot_ref, owners):
    tokens = weights.shape[0]
    capacity = 2 * MHEADS * tokens // owners
    lane_group = iota((tokens, LANES), 1) // PICKS
    tiled = [
        tile_groups(jnp.where(lane_group == h, weights, 0.0), MHEADS).astype(BF16) for h in range(MHEADS)
    ]
    place = iota((owners * 8, tokens), 0)
    base = (place // 8) * capacity + place % 8
    out_group = iota((owners * 8, LANES), 1) // PICKS
    total = jnp.zeros((owners * 8, LANES), F32)
    for g in range(capacity // 8):
        part = jnp.zeros((owners * 8, LANES), F32)
        for h in range(MHEADS):
            chosen = jnp.where(base + g * 8 == slot_ref[h : h + 1, :], 1.0, 0.0).astype(BF16)
            part = part + product(chosen, tiled[h])
        total = jnp.where(out_group == g, part, total)
    return total


def plane_hits(slot_ref, plane, seq, capacity):
    tokens = slot_ref.shape[1]
    place = plane * (seq * capacity) + iota((seq * capacity, tokens), 0)
    chosen = jnp.zeros((seq * capacity, tokens), F32)
    for h in range(MHEADS):
        chosen = jnp.where(place == slot_ref[h : h + 1, :], 1.0, chosen)
    return chosen.astype(BF16)


def scatter_kernel(ready, *refs):
    ready()
    out_ref = refs[-1]
    seq, batches, capacity, wide = out_ref.shape
    plane = lax.axis_index("batch")
    for k in range(batches):
        chosen = plane_hits(refs[k], plane, seq, capacity)
        rows = product(chosen, refs[batches + k][...]).astype(BF16)
        source = lax.rem(plane + (batches - k), batches)
        out_ref[:, pl.ds(source, 1)] = rows.reshape(seq, 1, capacity, wide)


def gather_kernel(ready, *refs):
    ready()
    batches = (len(refs) - 1) // 2
    back_ref = refs[batches]
    seq, _, capacity, wide = back_ref.shape
    plane = lax.axis_index("batch")
    for k in range(batches):
        chosen = plane_hits(refs[k], plane, seq, capacity)
        source = lax.rem(plane + (batches - k), batches)
        rows = back_ref[:, pl.ds(source, 1)].reshape(seq * capacity, wide)
        refs[batches + 1 + k][...] = contract(chosen, rows).astype(BF16)


def memory_kernel(batches, ready, adapter, gate_ref, mix_ref, *refs):
    w_in_any, dn_any, up_any, mixed_ref, grank_ref, ggate_ref, part_ref, w, dn, up, sems = refs[batches:]
    a = adapter[0]
    copies = fetch([(dn_any.at[5, a], dn), (up_any.at[5, a], up), (w_in_any.at[4], w)], sems)
    ready()
    memory = refs[0][...].astype(F32)
    for k in range(1, batches):
        memory = memory + refs[k][...].astype(F32)
    gate = gate_ref[...]
    sigmoid = jax.nn.sigmoid(gate)
    mixed_ref[...] = (memory * (gate * sigmoid)).astype(BF16)
    ggate = (mix_ref[...].astype(F32) * memory * sigmoid * (1.0 + gate * (1.0 - sigmoid))).astype(BF16)
    ggate_ref[...] = ggate
    for copy in copies[:2]:
        copy.wait()
    granks = against(ggate, up[...]).astype(BF16)
    grank_ref[...] = granks
    extra = product(granks, dn[...])
    copies[2].wait()
    ready.send(mixed_ref, ggate_ref, grank_ref)
    part_ref[...] = against(ggate, w[...]) + extra


def output_kernel(ready, adapter, mixed_ref, mid_ref, w_out_any, dn_any, up_any, out_ref, rank_ref, w, dn, up, sems):
    a = adapter[0]
    copies = fetch([(dn_any.at[6, a], dn), (up_any.at[6, a], up), (w_out_any.at[1], w)], sems)
    ready()
    mixed = mixed_ref[...]
    for copy in copies[:2]:
        copy.wait()
    ranks = against(mixed, dn[...]).astype(BF16)
    rank_ref[...] = ranks
    extra = product(ranks, up[...])
    copies[2].wait()
    out_ref[...] = (mid_ref[...] + (product(mixed, w[...]) + extra)).astype(BF16)


def query_kernel(
    owners, rows_dev, ready, length, adapter, back_ref, slot_ref, picks_ref, weight_ref, part_ref, mid_ref, cot_ref, gain_ref,
    keys_ref, w_in_any, w_out_any, dn_any, up_any,
    go_ref, gquery_ref, grank_ref, gmid_ref, w, dn, up, turned, sems,
):
    groups, tokens, cols = go_ref.shape
    a = adapter[0]
    copies = fetch(
        [(dn_any.at[3, a], dn.at[0]), (dn_any.at[4, a], dn.at[1]), (up_any.at[3, a], up.at[0]),
         (up_any.at[4, a], up.at[1]), (w_in_any.at[3], w.at[0]), (w_out_any.at[0], w.at[1])],
        sems,
    )
    ready(slot_ref, weight_ref)
    capacity = 2 * MHEADS * tokens // owners
    slots = iota((tokens, owners * 8), 1)
    base = (slots // 8) * capacity + slots % 8
    lane_group = iota((tokens, LANES), 1) // PICKS
    back = back_ref[...]
    gw = jnp.zeros((tokens, LANES), F32)
    for h in range(MHEADS):
        part = jnp.zeros((tokens, LANES), F32)
        for g in range(capacity // 8):
            chosen = jnp.where(base + g * 8 == slot_ref[:, h : h + 1], 1.0, 0.0).astype(BF16)
            part = jnp.where(lane_group == g, product(chosen, back), part)
        gw = jnp.where(lane_group == h, tile_groups(part, MHEADS), gw)
    weights = weight_ref[...]
    gscore = jnp.transpose(weights * (gw - group_reduce(weights * gw, jnp.sum, 0.0)))
    turned[...] = gscore
    ready(picks_ref, keys_ref)
    span = rows_dev // NSUB
    halves = []
    for h in range(MHEADS):

        def one(r, sums):
            pick = picks_ref[h, pl.ds(r, 1), :]
            value = turned[pl.ds(h * PICKS + r, 1), :]
            low = jnp.where((pick // NSUB) % span == iota((8, tokens), 0), value, 0.0)
            hit = (pick % NSUB).astype(jnp.int16) == lax.broadcasted_iota(jnp.int16, (NSUB, tokens), 0)
            return sums[0] + low, sums[1] + jnp.where(hit, value.astype(BF16), jnp.zeros((), BF16))

        start = (jnp.zeros((8, tokens), F32), jnp.zeros((NSUB, tokens), BF16))
        first, second = lax.fori_loop(0, PICKS, one, start, unroll=8)
        origin = picks_ref[h, 0:1, :] // rows_dev
        place = iota((NSUB, tokens), 0)
        wide = jnp.concatenate([first[:span]] * (NSUB // span), axis=0)
        wide = jnp.where(place // span == origin, wide, 0.0)
        halves.append(contract(wide.astype(BF16), keys_ref[0, h]))
        halves.append(contract(second, keys_ref[1, h]))
    gquery = jnp.concatenate(halves, axis=1).astype(BF16)
    gquery_ref[...] = gquery
    ready.send(gquery_ref)
    ready()
    for copy in copies[:4]:
        copy.wait()
    granks = against(gquery, up[1]).astype(BF16)
    grank_ref[1] = granks
    extra = product(granks, dn[1])
    copies[4].wait()
    gnormed = against(gquery, w[0]) + extra + part_ref[...]
    middle = mid_ref[...]
    gmid = cot_ref[...].astype(F32) + norm_back(middle, inverse_norm(middle), gain_row(gain_ref), gnormed)
    gmid_ref[...] = gmid
    ready.send(gmid_ref)
    low = gmid.astype(BF16)
    granks = against(low, up[0]).astype(BF16)
    grank_ref[0] = granks
    ready.send(grank_ref)
    extra = product(granks, dn[0])
    copies[5].wait()
    go = against(low, w[1]) + extra
    row = lax.axis_index("seq") * tokens + iota((tokens, 1), 0)
    go = jnp.where(row < length[0], go, 0.0).astype(BF16)
    for s in range(groups):
        go_ref[s] = go[:, s * cols : (s + 1) * cols]


def place_columns(out_ref, row, values):
    groups, _, cols = out_ref.shape
    low = values.astype(BF16)
    for s in range(groups):
        out_ref[s, row : row + values.shape[0], :] = low[:, s * cols : (s + 1) * cols]


def factor_kernel(ready, att_ref, norm_ref, mixed_ref, gmid_ref, gquery_ref, ggate_ref, cot_ref, r35, r4, r6, g34, g5, g6, out_ref):
    ready()
    half = 4 * RANK
    sides = (
        (att_ref[...], gmid_ref[...].astype(BF16), r35[0], g34[0]),
        (norm_ref[...], gquery_ref[...], r4[...], g34[1]),
        (norm_ref[...], ggate_ref[...], r35[1], g5[...]),
        (mixed_ref[...], cot_ref[...], r6[...], g6[...]),
    )
    for j, (value, gy, rank, grank) in enumerate(sides):
        place_columns(out_ref, j * RANK, contract(grank, value))
        place_columns(out_ref, half + j * RANK, contract(rank, gy))


def entry_factor_kernel(ready, adapter, grad_ref, norm_ref, ranks_ref, up_any, out_ref, gy_ref, grank_ref, up, sems):
    groups, tokens, wide = grad_ref.shape
    cols = wide // 3
    a = adapter[0]
    copies = fetch([(up_any.at[j, a], up.at[pl.ds(RANK * j, RANK)]) for j in range(3)], sems)
    gys = [
        jnp.concatenate([grad_ref[s, :, j * cols : (j + 1) * cols] for s in range(groups)], axis=1) for j in range(3)
    ]
    for j in range(3):
        gy_ref[j] = gys[j]
    ready.send(gy_ref)
    for copy in copies:
        copy.wait()
    ready()
    place = iota((tokens, 3 * RANK), 1) // RANK
    granks = jnp.zeros((tokens, 3 * RANK), F32)
    ranks = ranks_ref[...]
    for j in range(3):
        granks = jnp.where(place == j, against(gys[j], up[...]), granks)
        up_grad = contract(ranks, gys[j])
        place_columns(out_ref, (3 + j) * RANK, up_grad[j * RANK : (j + 1) * RANK, :])
    granks = granks.astype(BF16)
    grank_ref[...] = granks
    ready.send(grank_ref)
    place_columns(out_ref, 0, contract(granks, norm_ref[...]))


def entry_kernel(ready, adapter, gy_ref, grank_ref, x_ref, gain_ref, gmid_ref, w_any, dn_any, out_ref, w, dn, sems):
    a = adapter[0]
    copies = fetch(
        [(dn_any.at[j, a], dn.at[pl.ds(RANK * j, RANK)]) for j in range(3)] + [(w_any.at[j], w.at[j]) for j in range(3)],
        sems,
    )
    ready()
    x = x_ref[...].astype(F32)
    for copy in copies[:3]:
        copy.wait()
    total = product(grank_ref[...], dn[...])
    for j in range(3):
        copies[3 + j].wait()
        total = total + against(gy_ref[j], w[j])
    back = norm_back(x, inverse_norm(x), gain_row(gain_ref), total)
    out_ref[...] = (gmid_ref[...] + back).astype(BF16)


def sum_kernel(ready, parts_ref, out_ref):
    ready()
    total = parts_ref[0].astype(F32)
    for s in range(1, parts_ref.shape[0]):
        total = total + parts_ref[s].astype(F32)
    out_ref[...] = total.astype(BF16)


def stack_kernel(ready, *refs):
    for k in range(refs[-1].shape[0]):
        refs[-1][k] = refs[k][...]


def relative_marks(ids_ref, batches):
    plane = lax.axis_index("batch")
    absolute = adapter_marks(ids_ref, batches)
    marks = []
    for k in range(batches):
        source = lax.rem(plane + (batches - k), batches)
        mark = absolute[0]
        for b in range(1, batches):
            mark = jnp.where(source == b, absolute[b], mark)
        marks.append(mark)
    return marks


def adapter_marks(ids_ref, batches):
    step = ids_ref.shape[0] // batches
    return [ids_ref[b * step : b * step + 1, 0:1] // ADAPTER_STEP for b in range(batches)]


def spread_block(rows, marks, target, stage, sem):
    for k in range(ADAPTERS):
        total = jnp.zeros(rows[0].shape, F32)
        for row, mark in zip(rows, marks, strict=True):
            total = total + jnp.where(mark == k, row, 0.0)
        stage[k] = total
    copy = pltpu.make_async_copy(stage, target, sem)
    copy.start()
    return copy


def spread_kernel(batches, ready, ids_ref, *refs):
    down_any, up_any, parts, stage, load_sems, sems = refs[-6:]
    seq = parts.shape[0]
    me = lax.axis_index("seq")
    copies = fetch([(refs[m % 2].at[m // 2], parts.at[me ^ m]) for m in range(seq)], load_sems)
    ready()
    marks = relative_marks(ids_ref, batches)
    for copy in copies:
        copy.wait()
    started = []
    for at in range(8):
        target = down_any.at[3 + at] if at < 4 else up_any.at[at - 1]
        if at >= 2:
            started[at - 2].wait()
        rows = [
            jnp.concatenate([parts[s, k, at * RANK : (at + 1) * RANK, :] for s in range(seq)], axis=1).astype(F32)
            for k in range(batches)
        ]
        started.append(spread_block(rows, marks, target, stage.at[at % 2], sems.at[at % 2]))
    started[-2].wait()
    started[-1].wait()


def last_spread_kernel(batches, ready, ids_ref, down_in, up_in, *refs):
    down_any, up_any, parts, stage, load_sems, sems = refs[-6:]
    seq = parts.shape[0]
    me = lax.axis_index("seq")
    copies = fetch([(refs[m % 2].at[m // 2], parts.at[me ^ m]) for m in range(seq)], load_sems)
    ready()
    marks = relative_marks(ids_ref, batches)
    for copy in copies:
        copy.wait()
    started = []
    for at in range(6):
        rows = [
            jnp.concatenate([parts[s, k, at * RANK : (at + 1) * RANK, :] for s in range(seq)], axis=1).astype(F32)
            for k in range(batches)
        ]
        target = down_any.at[at] if at < 3 else up_any.at[at - 3]
        started.append(spread_block(rows, marks, target, stage.at[at], sems.at[at]))
    for copy in started:
        copy.wait()


def along(values, axis, step, size):
    return lax.ppermute(values, axis, [(i, (i + step) % size) for i in range(size)])


def across(values, axis, mask, size):
    return lax.ppermute(values, axis, [(i, i ^ mask) for i in range(size)])


def to_pairs(values, axis, size):
    return [values] + [across(values, axis, m, size) for m in range(2, size, 2)]


def stacked(values, name):
    shape = shaped((len(values), *values[0].shape), values[0].dtype)
    return call(stack_kernel, name, "V" * len(values), [("V", shape)], values)[0]


def exchange(values, axes):
    return lax.all_to_all(values, axes, split_axis=0, concat_axis=0, tiled=True)


def body(
    inputs, lengths, adapter_index, memory_picks, input_weights, output_weights, adapter_down, adapter_up,
    attention_gain, memory_gain, half_keys, memory_values, cotangent,
):
    both = ("batch", "seq")
    batches, seq = lax.axis_size("batch"), lax.axis_size("seq")
    owners = batches * seq
    tokens, width = inputs.shape[1], inputs.shape[2]
    rows, cols, half = tokens * seq, width // seq, width // 2
    rows_dev = memory_values.shape[0]
    capacity = 2 * tokens * MHEADS // owners
    groups = capacity // 8
    items = owners * capacity
    block = min(owners * 8, 256)
    carried = 2 * groups * PICKS // cols * batches * 8
    x, cot = inputs[0], cotangent[0]
    down = jnp.swapaxes(adapter_down, 2, 3)
    gain_one, gain_two = attention_gain, memory_gain
    picks = jnp.transpose(memory_picks[0], (1, 2, 0))
    matrix = pltpu.VMEM((width, width), BF16)
    pair = pltpu.VMEM((2, width, width), BF16)
    triple = pltpu.VMEM((3, width, width), BF16)
    small = pltpu.VMEM((RANK, width), BF16)
    two_small = pltpu.VMEM((2, RANK, width), BF16)
    three_small = pltpu.VMEM((3 * RANK, width), BF16)
    token_low, token_wide = shaped((tokens, width), BF16), shaped((tokens, width), F32)
    token_rank, token_lanes = shaped((tokens, RANK), BF16), shaped((tokens, LANES), F32)
    fixed = functools.partial

    qkv, normed, ranks = call(
        qkv_kernel, "qkv", "MLLHHH",
        [("V", shaped((seq, tokens, 3 * cols), BF16)), ("S", token_low), ("S", shaped((tokens, 3 * RANK), BF16))],
        (adapter_index, x, gain_one, input_weights, down, adapter_up), [triple, three_small, three_small, sema(9)],
    )
    qkv_all = exchange(qkv, "seq").reshape(rows, 3 * cols)

    slot, slot_col, pick, *ids_out = call(
        fixed(route_kernel, rows_dev, owners), "route", "ML",
        [("V", shaped((8, tokens), I32)), ("S", shaped((tokens, tokens), I32)), ("S", shaped((tokens, LANES), I32)),
         *[("V", shaped((seq * 8, LANES), I32)) for _ in range(batches)]],
        (adapter_index, picks), [pltpu.VMEM((owners * 8, LANES), I32)],
    )
    ids_out = [ids_out[0]] + [along(ids_out[k], "batch", k, batches) for k in range(1, batches)]
    qkv_all, ids_out = lax.optimization_barrier((qkv_all, ids_out))
    attended, lse, qkv_saved = call(
        fixed(attend_kernel, groups, batches), "attend", "MV" + "V" * batches,
        [("V", shaped((seq, tokens + carried, cols), BF16)), ("S", shaped((8, rows), F32)), ("H", shaped((rows, 3 * cols), BF16))],
        (lengths, qkv_all, *ids_out), [sema(1)],
    )
    o_all = exchange(attended, "seq")
    slot, late_cot, attended = lax.optimization_barrier((slot, cot, attended))
    slots = [slot] + [along(slot, "batch", k, batches) for k in range(1, batches)]
    mix_grad, grank_six = call(
        mix_back_kernel, "mixback", "MLHHH", [("S", token_low), ("S", token_rank)],
        (adapter_index, late_cot, output_weights, down, adapter_up), [matrix, small, small, sema(3)],
    )

    o_all, mix_grad, slots = lax.optimization_barrier((o_all, mix_grad, slots))
    left, right, same_two, sent, att, rank_pair, middle, normed_two, gate = call(
        middle_kernel, "middle", "MVLLLHHHH",
        [("V", shaped((tokens, half), BF16)), ("V", shaped((tokens, half), BF16)), ("V", token_low),
         ("S", shaped((seq, carried, cols), BF16)), ("S", token_low),
         ("S", shaped((2, tokens, RANK), BF16)), ("S", token_wide), ("S", token_low), ("S", token_wide)],
        (adapter_index, o_all, x, gain_two, mix_grad, input_weights, output_weights, down, adapter_up),
        [pair, two_small, two_small, sema(6)],
    )
    lefts = [left] + [along(left, "batch", k, batches) for k in range(1, batches)]
    weight_out, rank_four, weights = call(
        fixed(scores_kernel, owners), "scores", "MVLLLHHH",
        [("V", shaped((owners * 8, LANES), BF16)), ("S", token_rank), ("S", token_lanes)],
        (adapter_index, same_two, pick, slot, half_keys, input_weights, down, adapter_up), [matrix, small, small, sema(3)],
    )
    weight_in = exchange(weight_out.reshape(owners, 8, LANES), both).reshape(owners * 8, LANES)
    right, lefts = lax.optimization_barrier((right, lefts))
    rights = [right] + [along(right, "batch", k, batches) for k in range(1, batches)]

    def scatter(parts, name):
        out = [("V", shaped((seq, batches, capacity, half), BF16))]
        return call(scatter_kernel, name, "L" * batches + "V" * batches, out, (*slots, *parts))[0]

    left_out = scatter(lefts, "scatterleft")
    sent, left_out = lax.optimization_barrier((sent, left_out))
    ids, index = call(
        fixed(prepare_kernel, groups, rows_dev, batches), "prepare", "L",
        [("S", shaped((owners * 8, LANES), I32)), ("H", shaped((items, rows_dev), jnp.int16))], (sent,),
        [pltpu.VMEM((2, LANES, rows_dev), jnp.int16), pltpu.VMEM((owners * 8 // LANES, LANES, LANES), I32), sema(2)],
    )
    left_out, weight_in = lax.optimization_barrier((left_out, weight_in))
    left_in = exchange(left_out, "seq").reshape(items, half)

    (sums,) = call(
        fixed(recall_kernel, groups), "recall", "VHH", [("V", shaped((seq, batches, capacity, width), BF16))],
        (weight_in, index, memory_values),
        [pltpu.VMEM((rows_dev, width), BF16), pltpu.VMEM((2, block, rows_dev), jnp.int16), pltpu.VMEM((2, block, rows_dev), BF16), sema(3)],
        flops=1 << 32,
    )
    sums, left_in = lax.optimization_barrier((sums, left_in))
    back = exchange(sums, "seq")

    def recall_back(part, name, grads, kind, dtype, *before):
        return call(
            fixed(recall_back_kernel, part, batches, groups), name, "L" + "L" * part + "VH",
            [(kind, shaped((owners * 8, LANES), dtype))], (ids, *before, grads, memory_values),
            [pltpu.VMEM((rows_dev, half), BF16), pltpu.VMEM((block, rows_dev), F32), sema(1)], flops=1 << 31,
        )[0]

    right_out = scatter(rights, "scatterright")
    found_left = recall_back(0, "recallleft", left_in, "S", F32)
    right_out, back, found_left = lax.optimization_barrier((right_out, back, found_left))
    right_in = exchange(right_out, "seq").reshape(items, half)
    pieces = call(
        gather_kernel, "gather", "L" * batches + "V", [("V", token_low) for _ in range(batches)], (*slots, back),
    )
    pieces = [pieces[0]] + [along(pieces[k], "batch", batches - k, batches) for k in range(1, batches)]
    found = recall_back(1, "recallright", right_in, "V", BF16, found_left)
    found_back = exchange(found.reshape(owners, 8, LANES), both).reshape(owners * 8, LANES)

    mixed, grank_five, ggate, part = call(
        fixed(memory_kernel, batches), "memory", "MLL" + "V" * batches + "HHH",
        [("S", token_low), ("S", token_rank), ("S", token_low), ("S", token_wide)],
        (adapter_index, gate, mix_grad, *pieces, input_weights, down, adapter_up), [matrix, small, small, sema(3)],
    )

    go, gquery, grank_pair, gmid = call(
        fixed(query_kernel, owners, rows_dev), "query", "MMVLLLLLLLLHHHH",
        [("V", shaped((seq, tokens, cols), BF16)), ("S", token_low), ("S", shaped((2, tokens, RANK), BF16)), ("S", token_wide)],
        (lengths, adapter_index, found_back, slot_col, picks, weights, part, middle, cot, gain_two, half_keys,
         input_weights, output_weights, down, adapter_up),
        [pair, two_small, two_small, pltpu.VMEM((LANES, tokens), F32), sema(6)],
    )
    go_all = exchange(go, "seq").reshape(rows, cols)
    mixed, go = lax.optimization_barrier((mixed, go))
    output, rank_six = call(
        output_kernel, "output", "MLLHHH", [("S", token_low), ("S", token_rank)],
        (adapter_index, mixed, middle, output_weights, down, adapter_up), [matrix, small, small, sema(3)],
    )
    (factors,) = call(
        factor_kernel, "factors", "L" * 13, [("V", shaped((seq, 8 * RANK, cols), BF16))],
        (att, normed_two, mixed, gmid, gquery, ggate, cot, rank_pair, rank_four, rank_six, grank_pair, grank_five, grank_six),
    )
    factors, go_all = lax.optimization_barrier((factors, go_all))
    early_parts = exchange(factors, "seq")

    (grads,) = call(
        attend_back_kernel, "attendback", "MLVL", [("V", shaped((rows, 3 * cols), BF16))], (lengths, qkv_saved, go_all, lse),
        [pltpu.VMEM((rows, LANES), F32), pltpu.VMEM((rows, LANES), F32)],
    )
    grads, early_parts = lax.optimization_barrier((grads, early_parts))
    grads_all = exchange(grads.reshape(seq, tokens, 3 * cols), "seq")
    (some,) = call(sum_kernel, "sumearly", "V", [("V", shaped((8 * RANK, cols), BF16))], (early_parts,))
    some = [some] + [along(some, "batch", k, batches) for k in range(1, batches)]
    some = stacked(some, "stackearly")
    late, gys, granks = call(
        entry_factor_kernel, "entryfactors", "MVLLH",
        [("V", shaped((seq, 6 * RANK, cols), BF16)), ("S", shaped((3, tokens, width), BF16)), ("S", shaped((tokens, 3 * RANK), BF16))],
        (adapter_index, grads_all, normed, ranks, adapter_up), [three_small, sema(3)],
    )
    late, some = lax.optimization_barrier((late, some))
    late_parts = exchange(late, "seq")
    some = to_pairs(some, "seq", seq)
    (grad_input,) = call(
        entry_kernel, "entry", "MLLLLLHH", [("S", token_low)],
        (adapter_index, gys, granks, x, gain_one, gmid, input_weights, down), [triple, three_small, sema(6)],
    )
    late_parts, some, grad_input = lax.optimization_barrier((late_parts, some, grad_input))
    (late_sum,) = call(sum_kernel, "sumlate", "V", [("V", shaped((6 * RANK, cols), BF16))], (late_parts,))
    late_sums = [late_sum] + [along(late_sum, "batch", k, batches) for k in range(1, batches)]
    some = stacked(some, "pairsearly")
    late_sums, some = lax.optimization_barrier((late_sums, some))
    late_all = to_pairs(stacked(late_sums, "stacklate"), "seq", seq)
    some = (some, across(some, "seq", 1, seq))
    full = shaped((7, ADAPTERS, RANK, width), F32)
    grad_down, grad_up = call(
        fixed(spread_kernel, batches), "spread", "LVV", [("H", full), ("H", full)], (ids, *some),
        [pltpu.VMEM((seq, batches, 8 * RANK, cols), BF16), pltpu.VMEM((2, ADAPTERS, RANK, width), F32), sema(seq), sema(2)],
    )
    late_all, grad_down, grad_up = lax.optimization_barrier((late_all, grad_down, grad_up))
    late_all = stacked(late_all, "pairslate")
    late_all = (late_all, across(late_all, "seq", 1, seq))
    grad_down, grad_up = call(
        fixed(last_spread_kernel, batches), "lastspread", "LHHVV", [("H", full), ("H", full)],
        (ids, grad_down, grad_up, *late_all),
        [pltpu.VMEM((seq, batches, 6 * RANK, cols), BF16), pltpu.VMEM((6, ADAPTERS, RANK, width), F32), sema(seq), sema(6)],
        aliases={1: 0, 2: 1},
    )
    return (output[None], grad_input[None], jnp.swapaxes(grad_down, 2, 3), grad_up)


def solution(mesh):
    split = P("batch", "seq", None)
    return jax.shard_map(
        body,
        mesh=mesh,
        in_specs=(
            split, P("batch"), P("batch"), P("batch", "seq", None, None), P(), P(), P(), P(), P(), P(), P(),
            P(("batch", "seq"), None), split,
        ),
        out_specs=(split, split, P(), P()),
        check_vma=False,
    )
```

```python
import functools

import jax
import jax.numpy as jnp
from jax import lax
from jax.experimental import pallas as pl
from jax.experimental.pallas import tpu as pltpu
from jax.sharding import PartitionSpec as P

HEAD_DIM = 64
MHEADS = 4
KHALF = 128
NSUB = 256
PICKS = 32
ADAPTERS = 8
RANK = 16
LANES = 128
ADAPTER_STEP = 4096
RECALL_ROWS = 128
EPS = 1e-06
NEG = -1e30
F32 = jnp.float32
BF16 = jnp.bfloat16
I32 = jnp.int32
HBM = pl.BlockSpec(memory_space=pltpu.HBM)
SMEM = pl.BlockSpec(memory_space=pltpu.SMEM)
VMEM = pl.BlockSpec(memory_space=pltpu.VMEM)
MIB = 1 << 20


def product(left, right):
    return lax.dot_general(left, right, (((1,), (0,)), ((), ())), preferred_element_type=F32)


def against(left, right):
    return lax.dot_general(left, right, (((1,), (1,)), ((), ())), preferred_element_type=F32)


def contract(left, right):
    return lax.dot_general(left, right, (((0,), (0,)), ((), ())), preferred_element_type=F32)


def iota(shape, axis):
    return lax.broadcasted_iota(I32, shape, axis)


def lane_pick(table, index):
    return jnp.take_along_axis(table, index, axis=1, mode="promise_in_bounds")


def shaped(shape, dtype):
    return jax.ShapeDtypeStruct(shape, dtype)


class Stage:
    def __init__(self, loads, stores):
        self.loads, self.stores = loads, stores
        self.waited, self.begun = set(), set()
        for _, copy in loads:
            copy.start()

    def __call__(self, *refs):
        for at, (ref, copy) in enumerate(self.loads):
            if at not in self.waited and (not refs or any(ref is one for one in refs)):
                self.waited.add(at)
                copy.wait()

    def send(self, *refs):
        for at, (ref, copy) in enumerate(self.stores):
            if at not in self.begun and (not refs or any(ref is one for one in refs)):
                self.begun.add(at)
                copy.start()

    def finish(self):
        self()
        self.send()
        for _, copy in self.stores:
            copy.wait()


def call(kernel, name, ins, outs, args, scratch=(), vmem=40, flops=1 << 28, moved=1 << 22, aliases=None):
    shapes = [(args[i].shape, args[i].dtype) for i, kind in enumerate(ins) if kind == "L"]
    stored = [(out.shape, out.dtype) for kind, out in outs if kind == "S"]
    count_in, count_out, count_user = len(ins), len(outs), len(scratch)

    def wrapped(*refs):
        given, results = list(refs[:count_in]), list(refs[count_in : count_in + count_out])
        rest = list(refs[count_in + count_out :])
        user, buffers = rest[:count_user], rest[count_user:]
        loads, stores = [], []
        for i, kind in enumerate(ins):
            if kind == "L":
                at = len(loads)
                loads.append((buffers[at], pltpu.make_async_copy(given[i], buffers[at], buffers[-1].at[at])))
                given[i] = buffers[at]
        for i, (kind, _) in enumerate(outs):
            if kind == "S":
                at = len(loads) + len(stores)
                stores.append((buffers[at], pltpu.make_async_copy(buffers[at], results[i], buffers[-1].at[at])))
                results[i] = buffers[at]
        stage = Stage(loads, stores)
        kernel(stage, *given, *results, *user)
        stage.finish()

    spaces = {"V": VMEM, "L": HBM, "S": HBM, "H": HBM, "M": SMEM}
    autos = [pltpu.VMEM(*one) for one in shapes + stored]
    args = [
        pltpu.with_memory_space_constraint(one, pltpu.HBM) if kind in "LH" else one
        for kind, one in zip(ins, args, strict=True)
    ]
    return pl.pallas_call(
        wrapped,
        name=name,
        out_shape=[pltpu.HBM(out.shape, out.dtype) if kind in "SH" else out for kind, out in outs],
        in_specs=[spaces[kind] for kind in ins],
        out_specs=[spaces[kind] for kind, _ in outs],
        input_output_aliases=aliases or {},
        scratch_shapes=list(scratch) + autos + ([sema(len(autos))] if autos else []),
        compiler_params=pltpu.CompilerParams(vmem_limit_bytes=vmem * MIB),
        cost_estimate=pl.CostEstimate(flops=flops, bytes_accessed=moved, transcendentals=0),
    )(*args)


def fetch(pairs, sems):
    copies = [
        pltpu.make_async_copy(source, target, sems.at[place])
        for place, (source, target) in enumerate(pairs)
    ]
    for copy in copies:
        copy.start()
    return copies


def sema(count):
    return pltpu.SemaphoreType.DMA((count,))


def gain_row(ref):
    return ref[...].astype(F32).reshape(1, ref.shape[0])


def inverse_norm(values):
    return lax.rsqrt(jnp.mean(values * values, axis=1, keepdims=True) + EPS)


def norm_back(values, inverse, scales, incoming):
    weighted = incoming * scales
    inner = jnp.mean(weighted * values, axis=1, keepdims=True)
    return weighted * inverse - values * inverse * inverse * inverse * inner


def qkv_kernel(ready, adapter, x_ref, gain_ref, w_any, dn_any, up_any, out_ref, norm_ref, rank_ref, w, dn, up, sems):
    groups, tokens, wide = out_ref.shape
    cols = wide // 3
    a = adapter[0]
    copies = fetch(
        [(dn_any.at[j, a], dn.at[pl.ds(RANK * j, RANK)]) for j in range(3)]
        + [(up_any.at[j, a], up.at[pl.ds(RANK * j, RANK)]) for j in range(3)]
        + [(w_any.at[j], w.at[j]) for j in range(3)],
        sems,
    )
    ready()
    x = x_ref[...].astype(F32)
    normed = (x * inverse_norm(x) * gain_row(gain_ref)).astype(BF16)
    norm_ref[...] = normed
    ready.send(norm_ref)
    for copy in copies[:6]:
        copy.wait()
    ranks = against(normed, dn[...]).astype(BF16)
    rank_ref[...] = ranks
    ready.send(rank_ref)
    place = iota((tokens, 3 * RANK), 1) // RANK
    for j in range(3):
        own = jnp.where(place == j, ranks.astype(F32), 0.0).astype(BF16)
        extra = product(own, up[...])
        copies[6 + j].wait()
        result = (product(normed, w[j]) + extra).astype(BF16)
        for s in range(groups):
            out_ref[s, :, j * cols : (j + 1) * cols] = result[:, s * cols : (s + 1) * cols]


def mix_back_kernel(ready, adapter, cot_ref, w_any, dn_any, up_any, grad_ref, rank_ref, w, dn, up, sems):
    a = adapter[0]
    copies = fetch([(up_any.at[6, a], up), (dn_any.at[6, a], dn), (w_any.at[1], w)], sems)
    ready()
    gy = cot_ref[...]
    copies[0].wait()
    ranks = against(gy, up[...]).astype(BF16)
    rank_ref[...] = ranks
    copies[1].wait()
    extra = product(ranks, dn[...])
    copies[2].wait()
    grad_ref[...] = (against(gy, w[...]) + extra).astype(BF16)


def route_kernel(rows_dev, owners, ready, adapter, picks_ref, slot_ref, slot_col_ref, pick_ref, *ids_refs):
    ready()
    heads, picks, tokens = picks_ref.shape
    capacity = 2 * heads * tokens // owners
    groups = capacity // 8
    visits = heads * tokens
    owner = jnp.concatenate([picks_ref[h, 0:1, :] for h in range(heads)], axis=1) // rows_dev
    hot = jnp.where(iota((owners, visits), 0) == owner, 1.0, 0.0)
    before = jnp.where(iota((visits, visits), 0) < iota((visits, visits), 1), 1.0, 0.0).astype(BF16)
    counts = product(hot.astype(BF16), before)
    within = jnp.sum(hot * counts, axis=0, keepdims=True).astype(I32)
    slot = owner * capacity + within
    rows = [slot[:, h * tokens : (h + 1) * tokens] for h in range(heads)]
    stacked = jnp.concatenate(rows + [jnp.full((8 - heads, tokens), -1, I32)], axis=0)
    slot_ref[...] = stacked
    tall = jnp.concatenate([stacked, jnp.full((tokens - 8, tokens), -1, I32)], axis=0)
    slot_col_ref[...] = jnp.transpose(tall)
    packed = jnp.concatenate([picks_ref[h] for h in range(heads)], axis=0)
    by_token = jnp.transpose(packed)
    pick_ref[...] = by_token
    local = by_token % rows_dev
    lanes = iota((tokens, LANES), 1)
    total = jnp.zeros((owners * 8, LANES), F32)
    out_lane = iota((owners * 8, LANES), 1) // PICKS
    place = iota((owners * 8, tokens), 0)
    base = (place // 8) * capacity + place % 8
    for g in range(groups):
        high = jnp.zeros((owners * 8, LANES), F32)
        low = jnp.zeros((owners * 8, LANES), F32)
        for h in range(heads):
            chosen = jnp.where(base + g * 8 == rows[h], 1.0, 0.0).astype(BF16)
            own = jnp.where(lanes // PICKS == h, local, 0)
            own = tile_groups(own.astype(F32), heads).astype(I32)
            high = high + product(chosen, (own // 256).astype(F32).astype(BF16))
            low = low + product(chosen, (own % 256).astype(F32).astype(BF16))
        total = jnp.where(out_lane == g, high * 256.0 + low, total)
    batches = len(ids_refs) - 1
    part = owners * 8 // batches
    ids_refs[-1][...] = total.astype(I32) + adapter[0] * ADAPTER_STEP
    for k in range(batches):
        target = lax.rem(lax.axis_index("batch") + k, batches)
        ids_refs[k][...] = ids_refs[-1][pl.ds(pl.multiple_of(target * part, part), part), :]


def tile_groups(values, count):
    total = values
    for turn in range(1, count):
        total = total + pltpu.roll(values, turn * PICKS, 1)
    return total


def prepare_kernel(groups, rows_dev, batches, ready, sent_ref, ids_ref, index_any, stage, turned, sems):
    ready()
    seq, _, cols = sent_ref.shape
    lanes = groups * PICKS
    chunks = 2 * lanes // cols
    for k in range(batches):
        source = lax.rem(lax.axis_index("batch") + (batches - k), batches)
        for s in range(seq):
            both = [
                sent_ref[s, (chunk * batches + k) * 8 : (chunk * batches + k + 1) * 8, :].astype(F32)
                for chunk in range(chunks)
            ]
            both = jnp.concatenate(both, axis=1).astype(I32)
            ids = widen(both[:, :lanes] * 256 + both[:, lanes:])
            ids_ref[pl.ds(pl.multiple_of((source * seq + s) * 8, 8), 8), :] = ids
    ready.send(ids_ref)
    places = ids_ref.shape[0]
    chunks = rows_dev // LANES
    high_rows = max(8, chunks)
    steps = groups * (places // LANES)
    for k in range(places // LANES):
        turned[k] = jnp.transpose(ids_ref[k * LANES : (k + 1) * LANES, :] & (ADAPTER_STEP - 1))

    def put(step, slot):
        target = index_any.at[pl.ds(pl.multiple_of(step * LANES, LANES), LANES)]
        return pltpu.make_async_copy(stage.at[slot], target, sems.at[slot])

    def one(step, carry):
        k, g = lax.rem(step, places // LANES), step // (places // LANES)
        slot = lax.rem(step, 2)
        mask = jnp.zeros((LANES, LANES), I32)
        highs = jnp.zeros((high_rows, LANES), I32)
        for r in range(PICKS):
            bit = (1 << r) if r < 31 else -(1 << 31)
            row = turned[k, pl.ds(g * PICKS + r, 1), :]
            mask = mask | jnp.where(row & 127 == iota((LANES, LANES), 0), bit, 0)
            highs = highs | jnp.where(row >> 7 == iota((high_rows, LANES), 0), bit, 0)

        @pl.when(step >= 2)
        def _():
            put(step - 2, slot).wait()

        for c in range(chunks):
            index = 31 - lax.clz(mask & highs[c : c + 1, :])
            stage[slot, :, c * LANES : (c + 1) * LANES] = jnp.transpose(index).astype(jnp.int16)
        put(step, slot).start()
        return carry

    lax.fori_loop(0, steps, one, 0)
    for step in range(max(0, steps - 2), steps):
        put(step, step % 2).wait()


def recall_kernel(groups, ready, weight_ref, index_any, mem_any, out_any, mem, index, dense, staged, sems):
    places = weight_ref.shape[0]
    rows_dev = mem.shape[0]
    chunks = rows_dev // LANES
    block = dense.shape[1]
    per_group = places // block
    blocks = groups * per_group
    seq = out_any.shape[0]
    planes = block // (8 * seq)

    def load(b, slot):
        source = index_any.at[pl.ds(pl.multiple_of(b * block, block), block)]
        return pltpu.make_async_copy(source, index.at[slot], sems.at[1 + slot])

    load(0, 0).start()
    copy = pltpu.make_async_copy(mem_any, mem, sems.at[0])
    copy.start()

    def gather(b, side):
        load(b, side).wait()

        @pl.when(b + 1 < blocks)
        def _():
            load(b + 1, 1 - side).start()

        pick(b, side)

    def pick(b, side):
        g, k = b // per_group, lax.rem(b, per_group)
        for start in range(0, block, 16):
            weights = weight_ref[pl.ds(pl.multiple_of(k * block + start, 16), 16), :].astype(F32)
            for c in range(chunks):
                at = index[side, start : start + 16, c * LANES : (c + 1) * LANES].astype(I32)
                value = lane_pick(weights, (at + g * PICKS) & 127)
                dense[side, start : start + 16, c * LANES : (c + 1) * LANES] = jnp.where(at >= 0, value, 0.0).astype(BF16)

    def save(b, side):
        g, k = b // per_group, lax.rem(b, per_group)
        return [
            pltpu.make_async_copy(
                staged.at[side, pl.ds(i * seq, seq)],
                out_any.at[:, k * planes + i, pl.ds(pl.multiple_of(g * 8, 8), 8), :],
                sems.at[3 + side * planes + i],
            )
            for i in range(planes)
        ]

    def multiply(b, side):
        result = product(dense[side], mem[...]).astype(BF16)

        @pl.when(b >= 2)
        def _():
            for one in save(b - 2, side):
                one.wait()

        staged[side] = result.reshape(block // 8, 8, result.shape[1])
        for one in save(b, side):
            one.start()

    gather(0, 0)
    copy.wait()

    def whole(i, carry):
        gather(2 * i + 1, 1)
        multiply(2 * i, 0)

        @pl.when(2 * i + 2 < blocks)
        def _():
            load(2 * i + 2, 0).wait()
            load(2 * i + 3, 1).start()

        pick(jnp.minimum(2 * i + 2, blocks - 1), 0)
        multiply(2 * i + 1, 1)
        return carry

    lax.fori_loop(0, blocks // 2, whole, 0)
    for b in range(blocks - 2, blocks):
        for one in save(b, b % 2):
            one.wait()


def recall_back_kernel(part, batches, groups, ready, ids_ref, *refs):
    before_ref = refs[0] if part else None
    grad_ref, mem_any, out_ref, mem, scores, sems = refs[part:]
    items, half = grad_ref.shape
    seq = items // (batches * groups * 8)
    rows_dev = mem.shape[0]
    capacity = groups * 8
    chunks = rows_dev // LANES
    block = scores.shape[0]
    per_block = block // capacity
    blocks = items // block
    copies = fetch([(mem_any.at[:, pl.ds(part * half, half)], mem)], sems)
    ready()
    copies[0].wait()

    def whole(b, outer):
        scores[...] = against(grad_ref[pl.ds(pl.multiple_of(b * block, block), block), :], mem[...])

        lane_group = iota((8, LANES), 1) // PICKS
        for local in range(per_block):
            sender = b * per_block + local
            spot = lax.rem(sender, batches) * seq + sender // batches
            start = pl.multiple_of(spot * 8, 8)
            ids = ids_ref[pl.ds(start, 8), :] & (ADAPTER_STEP - 1)
            low = ids & 127
            high = ids >> 7
            total = before_ref[pl.ds(start, 8), :] if part else jnp.zeros((8, LANES), F32)
            for g in range(groups):
                key = jnp.where(lane_group == g, high, -1)
                here = jnp.zeros((8, LANES), F32)
                row = local * capacity + g * 8
                for c in range(chunks):
                    found = scores[row : row + 8, c * LANES : (c + 1) * LANES]
                    here = jnp.where(key == c, lane_pick(found, low), here)
                total = total + here
            out_ref[pl.ds(start, 8), :] = total.astype(out_ref.dtype)
        return outer

    lax.fori_loop(0, blocks, whole, 0)


def head_parts(values, h, spare):
    lane = iota(values.shape, 1)
    return jnp.where(lane // HEAD_DIM == h, values, jnp.where(lane == (1 - h) * HEAD_DIM, spare, 0.0)).astype(BF16)


def widen(values):
    if values.shape[1] == LANES:
        return values
    return jnp.concatenate([values, jnp.zeros((values.shape[0], LANES - values.shape[1]), values.dtype)], axis=1)


def attend_kernel(groups, batches, ready, length, qkv_ref, *refs):
    o_ref, lse_ref, saved_any, parts, values_t, mixed, sems = refs[batches:]
    ready()
    saving = pltpu.make_async_copy(qkv_ref, saved_any, sems.at[0])
    saving.start()
    rows, wide = qkv_ref.shape
    cols = wide // 3
    seq = o_ref.shape[0]
    lanes = groups * PICKS
    for s in range(seq):
        ids = jnp.concatenate([refs[k][s * 8 : (s + 1) * 8, :lanes] for k in range(batches)], axis=0)
        both = jnp.concatenate([ids // 256, ids % 256], axis=1).astype(F32).astype(BF16)
        for chunk in range(2 * lanes // cols):
            start = rows // seq + chunk * batches * 8
            o_ref[s, start : start + batches * 8, :] = both[:, chunk * cols : (chunk + 1) * cols]
    heads = cols // HEAD_DIM
    size = min(256, rows)
    valid = length[0]
    bias = jnp.where(iota((rows, LANES), 0) < valid, 0.0, NEG)
    keys = widen(qkv_ref[:, cols : 2 * cols].astype(F32))
    values_t[...] = jnp.transpose(widen(qkv_ref[:, 2 * cols :].astype(F32))).astype(BF16)
    lse_ref[...] = jnp.zeros_like(lse_ref)

    def one(h, carry):
        parts[...] = head_parts(keys, h, bias)
        for i in range(rows // size):
            first, last = i * size, (i + 1) * size
            queries = widen(qkv_ref[first:last, 0:cols].astype(F32)) * (HEAD_DIM**-0.5)
            query = head_parts(queries, h, 1.0)
            near = against(parts[first:last], query)
            near = jnp.where(iota((size, size), 0) <= iota((size, size), 1), near, NEG)
            high = jnp.max(near, axis=0, keepdims=True)
            if i:
                far = against(parts[:first], query)
                high = jnp.maximum(high, jnp.max(far, axis=0, keepdims=True))
            near = jnp.exp(near - high)
            summed = jnp.sum(near, axis=0, keepdims=True)
            result = product(values_t[:, first:last], near.astype(BF16))
            if i:
                far = jnp.exp(far - high)
                summed = summed + jnp.sum(far, axis=0, keepdims=True)
                result = result + product(values_t[:, :first], far.astype(BF16))
            lse_ref[pl.ds(h, 1), first:last] = high + jnp.log(summed)
            own = iota((LANES, size), 0) // HEAD_DIM == h
            mixed[:, first:last] = jnp.where(own, result / summed, mixed[:, first:last])
        return carry

    mixed[...] = jnp.zeros_like(mixed)
    lax.fori_loop(0, heads, one, 0)
    ready.send(lse_ref)
    tokens = rows // seq
    for s in range(seq):
        first = s * tokens
        kept = jnp.where(first + iota((LANES, tokens), 1) < valid, mixed[:, first : first + tokens], 0.0)
        o_ref[s, 0:tokens, :] = jnp.transpose(kept)[:, :cols].astype(BF16)
    saving.wait()


def attend_back_kernel(ready, length, qkv_ref, go_ref, lse_ref, out_ref, dk, dv, dq, parts, keys_t, values):
    ready()
    rows, wide = qkv_ref.shape
    cols = wide // 3
    heads = cols // HEAD_DIM
    size = min(256, rows)
    valid = length[0]
    scaling = HEAD_DIM**-0.5
    bias = jnp.where(iota((rows, LANES), 0) < valid, 0.0, NEG)
    keys = widen(qkv_ref[:, cols : 2 * cols].astype(F32))
    keys_t[...] = jnp.transpose(keys).astype(BF16)
    values[...] = widen(qkv_ref[:, 2 * cols :])
    dk[...] = jnp.zeros_like(dk)
    dv[...] = jnp.zeros_like(dv)
    dq[...] = jnp.zeros_like(dq)

    def one(h, carry):
        parts[...] = head_parts(keys, h, bias)
        for i in range(rows // size):
            first, last = i * size, (i + 1) * size
            queries = widen(qkv_ref[first:last, 0:cols].astype(F32)) * scaling
            grads = widen(go_ref[first:last, :].astype(F32))
            query = head_parts(queries, h, 1.0)
            plain = head_parts(queries, h, 0.0)
            grad = head_parts(grads, h, 0.0)
            lse = lse_ref[pl.ds(h, 1), first:last]
            near = against(parts[first:last], query)
            near = jnp.where(iota((size, size), 0) <= iota((size, size), 1), near, NEG)
            near = jnp.exp(near - lse)
            near_gp = against(values[first:last], grad)
            delta = jnp.sum(near * near_gp, axis=0, keepdims=True)
            if i:
                far = jnp.exp(against(parts[:first], query) - lse)
                far_gp = against(values[:first], grad)
                delta = delta + jnp.sum(far * far_gp, axis=0, keepdims=True)
            near_gs = (near * (near_gp - delta)).astype(BF16)
            result = product(keys_t[:, first:last], near_gs)
            dk[first:last] += product(near_gs, plain)
            dv[first:last] += product(near.astype(BF16), grad)
            if i:
                far_gs = (far * (far_gp - delta)).astype(BF16)
                result = result + product(keys_t[:, :first], far_gs)
                dk[:first] += product(far_gs, plain)
                dv[:first] += product(far.astype(BF16), grad)
            own = iota((LANES, size), 0) // HEAD_DIM == h
            dq[:, first:last] = jnp.where(own, result, dq[:, first:last])
        return carry

    lax.fori_loop(0, heads, one, 0)
    out_ref[:, 0:cols] = (jnp.transpose(dq[...]) * scaling)[:, :cols].astype(BF16)
    out_ref[:, cols : 2 * cols] = dk[:, :cols].astype(BF16)
    out_ref[:, 2 * cols :] = dv[:, :cols].astype(BF16)


def pick_chosen(tables, index):
    tokens = index.shape[0]
    low = index & 127
    key = (index >> 7) + (iota((tokens, LANES), 1) // PICKS) * (NSUB // LANES)
    total = jnp.zeros((tokens, LANES), F32)
    for h in range(MHEADS):
        for c in range(NSUB // LANES):
            found = lane_pick(tables[h][:, c * LANES : (c + 1) * LANES], low)
            total = jnp.where(key == h * (NSUB // LANES) + c, found, total)
    return total


def group_reduce(values, reducer, fill):
    group = iota(values.shape, 1) // PICKS
    total = jnp.zeros(values.shape, F32)
    for h in range(MHEADS):
        one = reducer(jnp.where(group == h, values, fill), axis=1, keepdims=True)
        total = jnp.where(group == h, one, total)
    return total


def middle_kernel(
    ready, adapter, o_ref, x_ref, gain_ref, mix_ref, w_in_any, w_out_any, dn_any, up_any,
    left_ref, right_ref, same_ref, sent_ref, att_ref, rank_ref, mid_ref, norm_ref, gate_ref, w, dn, up, sems,
):
    groups = o_ref.shape[0]
    a = adapter[0]
    copies = fetch(
        [(dn_any.at[3, a], dn.at[0]), (dn_any.at[5, a], dn.at[1]), (up_any.at[3, a], up.at[0]), (up_any.at[5, a], up.at[1]),
         (w_out_any.at[0], w.at[0]), (w_in_any.at[4], w.at[1])],
        sems,
    )
    tokens = att_ref.shape[0]
    attended = jnp.concatenate([o_ref[s, 0:tokens, :] for s in range(groups)], axis=1)
    sent_ref[...] = o_ref[:, tokens:, :]
    ready.send(sent_ref)
    att_ref[...] = attended
    ready.send(att_ref)
    for copy in copies[:4]:
        copy.wait()
    rank_three = against(attended, dn[0]).astype(BF16)
    extra = product(rank_three, up[0])
    copies[4].wait()
    ready(x_ref, gain_ref)
    middle = x_ref[...].astype(F32) + (product(attended, w[0]) + extra)
    mid_ref[...] = middle
    normed = (middle * inverse_norm(middle) * gain_row(gain_ref)).astype(BF16)
    norm_ref[...] = normed
    same_ref[...] = normed
    ready.send(mid_ref, norm_ref)
    rank_five = against(normed, dn[1]).astype(BF16)
    rank_ref[0] = rank_three
    rank_ref[1] = rank_five
    extra = product(rank_five, up[1])
    copies[5].wait()
    gate = product(normed, w[1]) + extra
    gate_ref[...] = gate
    ready.send(rank_ref, gate_ref)
    ready(mix_ref)
    memory_grad = (mix_ref[...].astype(F32) * (gate * jax.nn.sigmoid(gate))).astype(BF16)
    half = left_ref.shape[1]
    left_ref[...] = memory_grad[:, :half]
    right_ref[...] = memory_grad[:, half:]


def scores_kernel(
    owners, ready, adapter, normed_ref, picks_ref, slot_ref, keys_ref, w_in_any, dn_any, up_any,
    send_ref, rank_ref, weight_ref, w, dn, up, sems,
):
    a = adapter[0]
    copies = fetch([(dn_any.at[4, a], dn), (up_any.at[4, a], up), (w_in_any.at[3], w)], sems)
    normed = normed_ref[...]
    copies[0].wait()
    ranks = against(normed, dn[...]).astype(BF16)
    rank_ref[...] = ranks
    copies[1].wait()
    extra = product(ranks, up[...])
    copies[2].wait()
    query = (product(normed, w[...]) + extra).astype(BF16)
    ready()
    ready.send(rank_ref)
    first, second = [], []
    for h in range(MHEADS):
        base = 2 * h * KHALF
        first.append(against(query[:, base : base + KHALF], keys_ref[0, h]))
        second.append(against(query[:, base + KHALF : base + 2 * KHALF], keys_ref[1, h]))
    picks = picks_ref[...]
    scores = pick_chosen(first, picks // NSUB) + pick_chosen(second, picks % NSUB)
    exponent = jnp.exp(scores - group_reduce(scores, jnp.max, NEG))
    weights = exponent / group_reduce(exponent, jnp.sum, 0.0)
    weight_ref[...] = weights
    ready.send(weight_ref)
    send_ref[...] = to_slots(weights, slot_ref, owners).astype(BF16)


def to_slots(weights, slot_ref, owners):
    tokens = weights.shape[0]
    capacity = 2 * MHEADS * tokens // owners
    lane_group = iota((tokens, LANES), 1) // PICKS
    tiled = [
        tile_groups(jnp.where(lane_group == h, weights, 0.0), MHEADS).astype(BF16) for h in range(MHEADS)
    ]
    place = iota((owners * 8, tokens), 0)
    base = (place // 8) * capacity + place % 8
    out_group = iota((owners * 8, LANES), 1) // PICKS
    total = jnp.zeros((owners * 8, LANES), F32)
    for g in range(capacity // 8):
        part = jnp.zeros((owners * 8, LANES), F32)
        for h in range(MHEADS):
            chosen = jnp.where(base + g * 8 == slot_ref[h : h + 1, :], 1.0, 0.0).astype(BF16)
            part = part + product(chosen, tiled[h])
        total = jnp.where(out_group == g, part, total)
    return total


def plane_hits(slot_ref, plane, seq, capacity):
    tokens = slot_ref.shape[1]
    place = plane * (seq * capacity) + iota((seq * capacity, tokens), 0)
    chosen = jnp.zeros((seq * capacity, tokens), F32)
    for h in range(MHEADS):
        chosen = jnp.where(place == slot_ref[h : h + 1, :], 1.0, chosen)
    return chosen.astype(BF16)


def scatter_kernel(ready, *refs):
    ready()
    out_ref = refs[-1]
    seq, batches, capacity, wide = out_ref.shape
    plane = lax.axis_index("batch")
    for k in range(batches):
        chosen = plane_hits(refs[k], plane, seq, capacity)
        rows = product(chosen, refs[batches + k][...]).astype(BF16)
        source = lax.rem(plane + (batches - k), batches)
        out_ref[:, pl.ds(source, 1)] = rows.reshape(seq, 1, capacity, wide)


def gather_kernel(ready, *refs):
    ready()
    batches = (len(refs) - 1) // 2
    back_ref = refs[batches]
    seq, _, capacity, wide = back_ref.shape
    plane = lax.axis_index("batch")
    for k in range(batches):
        chosen = plane_hits(refs[k], plane, seq, capacity)
        source = lax.rem(plane + (batches - k), batches)
        rows = back_ref[:, pl.ds(source, 1)].reshape(seq * capacity, wide)
        refs[batches + 1 + k][...] = contract(chosen, rows).astype(BF16)


def memory_kernel(batches, ready, adapter, gate_ref, mix_ref, *refs):
    w_in_any, dn_any, up_any, mixed_ref, grank_ref, ggate_ref, part_ref, w, dn, up, sems = refs[batches:]
    a = adapter[0]
    copies = fetch([(dn_any.at[5, a], dn), (up_any.at[5, a], up), (w_in_any.at[4], w)], sems)
    ready()
    memory = refs[0][...].astype(F32)
    for k in range(1, batches):
        memory = memory + refs[k][...].astype(F32)
    gate = gate_ref[...]
    sigmoid = jax.nn.sigmoid(gate)
    mixed_ref[...] = (memory * (gate * sigmoid)).astype(BF16)
    ggate = (mix_ref[...].astype(F32) * memory * sigmoid * (1.0 + gate * (1.0 - sigmoid))).astype(BF16)
    ggate_ref[...] = ggate
    for copy in copies[:2]:
        copy.wait()
    granks = against(ggate, up[...]).astype(BF16)
    grank_ref[...] = granks
    extra = product(granks, dn[...])
    copies[2].wait()
    ready.send(mixed_ref, ggate_ref, grank_ref)
    part_ref[...] = against(ggate, w[...]) + extra


def output_kernel(ready, adapter, mixed_ref, mid_ref, w_out_any, dn_any, up_any, out_ref, rank_ref, w, dn, up, sems):
    a = adapter[0]
    copies = fetch([(dn_any.at[6, a], dn), (up_any.at[6, a], up), (w_out_any.at[1], w)], sems)
    ready()
    mixed = mixed_ref[...]
    for copy in copies[:2]:
        copy.wait()
    ranks = against(mixed, dn[...]).astype(BF16)
    rank_ref[...] = ranks
    extra = product(ranks, up[...])
    copies[2].wait()
    out_ref[...] = (mid_ref[...] + (product(mixed, w[...]) + extra)).astype(BF16)


def query_kernel(
    owners, rows_dev, ready, length, adapter, back_ref, slot_ref, picks_ref, weight_ref, part_ref, mid_ref, cot_ref, gain_ref,
    keys_ref, w_in_any, w_out_any, dn_any, up_any,
    go_ref, gquery_ref, grank_ref, gmid_ref, w, dn, up, turned, sems,
):
    groups, tokens, cols = go_ref.shape
    a = adapter[0]
    copies = fetch(
        [(dn_any.at[3, a], dn.at[0]), (dn_any.at[4, a], dn.at[1]), (up_any.at[3, a], up.at[0]),
         (up_any.at[4, a], up.at[1]), (w_in_any.at[3], w.at[0]), (w_out_any.at[0], w.at[1])],
        sems,
    )
    ready(slot_ref, weight_ref)
    capacity = 2 * MHEADS * tokens // owners
    slots = iota((tokens, owners * 8), 1)
    base = (slots // 8) * capacity + slots % 8
    lane_group = iota((tokens, LANES), 1) // PICKS
    back = back_ref[...]
    gw = jnp.zeros((tokens, LANES), F32)
    for h in range(MHEADS):
        part = jnp.zeros((tokens, LANES), F32)
        for g in range(capacity // 8):
            chosen = jnp.where(base + g * 8 == slot_ref[:, h : h + 1], 1.0, 0.0).astype(BF16)
            part = jnp.where(lane_group == g, product(chosen, back), part)
        gw = jnp.where(lane_group == h, tile_groups(part, MHEADS), gw)
    weights = weight_ref[...]
    gscore = jnp.transpose(weights * (gw - group_reduce(weights * gw, jnp.sum, 0.0)))
    turned[...] = gscore
    ready(picks_ref, keys_ref)
    span = rows_dev // NSUB
    halves = []
    for h in range(MHEADS):

        def one(r, sums):
            pick = picks_ref[h, pl.ds(r, 1), :]
            value = turned[pl.ds(h * PICKS + r, 1), :]
            low = jnp.where((pick // NSUB) % span == iota((8, tokens), 0), value, 0.0)
            hit = (pick % NSUB).astype(jnp.int16) == lax.broadcasted_iota(jnp.int16, (NSUB, tokens), 0)
            return sums[0] + low, sums[1] + jnp.where(hit, value.astype(BF16), jnp.zeros((), BF16))

        start = (jnp.zeros((8, tokens), F32), jnp.zeros((NSUB, tokens), BF16))
        first, second = lax.fori_loop(0, PICKS, one, start, unroll=8)
        origin = picks_ref[h, 0:1, :] // rows_dev
        place = iota((NSUB, tokens), 0)
        wide = jnp.concatenate([first[:span]] * (NSUB // span), axis=0)
        wide = jnp.where(place // span == origin, wide, 0.0)
        halves.append(contract(wide.astype(BF16), keys_ref[0, h]))
        halves.append(contract(second, keys_ref[1, h]))
    gquery = jnp.concatenate(halves, axis=1).astype(BF16)
    gquery_ref[...] = gquery
    ready.send(gquery_ref)
    ready()
    for copy in copies[:4]:
        copy.wait()
    granks = against(gquery, up[1]).astype(BF16)
    grank_ref[1] = granks
    extra = product(granks, dn[1])
    copies[4].wait()
    gnormed = against(gquery, w[0]) + extra + part_ref[...]
    middle = mid_ref[...]
    gmid = cot_ref[...].astype(F32) + norm_back(middle, inverse_norm(middle), gain_row(gain_ref), gnormed)
    gmid_ref[...] = gmid
    ready.send(gmid_ref)
    low = gmid.astype(BF16)
    granks = against(low, up[0]).astype(BF16)
    grank_ref[0] = granks
    ready.send(grank_ref)
    extra = product(granks, dn[0])
    copies[5].wait()
    go = against(low, w[1]) + extra
    row = lax.axis_index("seq") * tokens + iota((tokens, 1), 0)
    go = jnp.where(row < length[0], go, 0.0).astype(BF16)
    for s in range(groups):
        go_ref[s] = go[:, s * cols : (s + 1) * cols]


def place_columns(out_ref, row, values):
    groups, _, cols = out_ref.shape
    low = values.astype(BF16)
    for s in range(groups):
        out_ref[s, row : row + values.shape[0], :] = low[:, s * cols : (s + 1) * cols]


def factor_kernel(ready, att_ref, norm_ref, mixed_ref, gmid_ref, gquery_ref, ggate_ref, cot_ref, r35, r4, r6, g34, g5, g6, out_ref):
    ready()
    half = 4 * RANK
    sides = (
        (att_ref[...], gmid_ref[...].astype(BF16), r35[0], g34[0]),
        (norm_ref[...], gquery_ref[...], r4[...], g34[1]),
        (norm_ref[...], ggate_ref[...], r35[1], g5[...]),
        (mixed_ref[...], cot_ref[...], r6[...], g6[...]),
    )
    for j, (value, gy, rank, grank) in enumerate(sides):
        place_columns(out_ref, j * RANK, contract(grank, value))
        place_columns(out_ref, half + j * RANK, contract(rank, gy))


def entry_factor_kernel(ready, adapter, grad_ref, norm_ref, ranks_ref, up_any, out_ref, gy_ref, grank_ref, up, sems):
    groups, tokens, wide = grad_ref.shape
    cols = wide // 3
    a = adapter[0]
    copies = fetch([(up_any.at[j, a], up.at[pl.ds(RANK * j, RANK)]) for j in range(3)], sems)
    gys = [
        jnp.concatenate([grad_ref[s, :, j * cols : (j + 1) * cols] for s in range(groups)], axis=1) for j in range(3)
    ]
    for j in range(3):
        gy_ref[j] = gys[j]
    ready.send(gy_ref)
    for copy in copies:
        copy.wait()
    ready()
    place = iota((tokens, 3 * RANK), 1) // RANK
    granks = jnp.zeros((tokens, 3 * RANK), F32)
    ranks = ranks_ref[...]
    for j in range(3):
        granks = jnp.where(place == j, against(gys[j], up[...]), granks)
        up_grad = contract(ranks, gys[j])
        place_columns(out_ref, (3 + j) * RANK, up_grad[j * RANK : (j + 1) * RANK, :])
    granks = granks.astype(BF16)
    grank_ref[...] = granks
    ready.send(grank_ref)
    place_columns(out_ref, 0, contract(granks, norm_ref[...]))


def entry_kernel(ready, adapter, gy_ref, grank_ref, x_ref, gain_ref, gmid_ref, w_any, dn_any, out_ref, w, dn, sems):
    a = adapter[0]
    copies = fetch(
        [(dn_any.at[j, a], dn.at[pl.ds(RANK * j, RANK)]) for j in range(3)] + [(w_any.at[j], w.at[j]) for j in range(3)],
        sems,
    )
    ready()
    x = x_ref[...].astype(F32)
    for copy in copies[:3]:
        copy.wait()
    total = product(grank_ref[...], dn[...])
    for j in range(3):
        copies[3 + j].wait()
        total = total + against(gy_ref[j], w[j])
    back = norm_back(x, inverse_norm(x), gain_row(gain_ref), total)
    out_ref[...] = (gmid_ref[...] + back).astype(BF16)


def sum_kernel(ready, parts_ref, out_ref):
    ready()
    total = parts_ref[0].astype(F32)
    for s in range(1, parts_ref.shape[0]):
        total = total + parts_ref[s].astype(F32)
    out_ref[...] = total.astype(BF16)


def stack_kernel(ready, *refs):
    for k in range(refs[-1].shape[0]):
        refs[-1][k] = refs[k][...]


def relative_marks(ids_ref, batches):
    plane = lax.axis_index("batch")
    absolute = adapter_marks(ids_ref, batches)
    marks = []
    for k in range(batches):
        source = lax.rem(plane + (batches - k), batches)
        mark = absolute[0]
        for b in range(1, batches):
            mark = jnp.where(source == b, absolute[b], mark)
        marks.append(mark)
    return marks


def adapter_marks(ids_ref, batches):
    step = ids_ref.shape[0] // batches
    return [ids_ref[b * step : b * step + 1, 0:1] // ADAPTER_STEP for b in range(batches)]


def spread_rows(parts, marks, runs, stage, sems):
    seq, batches = parts.shape[:2]
    for target, origin, base, count in runs:

        def put(i, target=target, origin=origin, base=base):
            return pltpu.make_async_copy(stage.at[base + i], target.at[origin + i], sems.at[base + i])

        def one(i, carry, put=put, base=base):
            start = pl.multiple_of((base + i) * RANK, RANK)
            rows = [
                jnp.concatenate([parts[s, k, pl.ds(start, RANK), :] for s in range(seq)], axis=1).astype(F32)
                for k in range(batches)
            ]
            for k in range(ADAPTERS):
                total = jnp.zeros(rows[0].shape, F32)
                for row, mark in zip(rows, marks, strict=True):
                    total = total + jnp.where(mark == k, row, 0.0)
                stage[base + i, k] = total
            put(i).start()
            return carry

        lax.fori_loop(0, count, one, 0)
    for target, origin, base, count in runs:
        for i in range(count):
            pltpu.make_async_copy(stage.at[base + i], target.at[origin + i], sems.at[base + i]).wait()


def spread_kernel(batches, ready, ids_ref, *refs):
    down_any, up_any, parts, stage, load_sems, sems = refs[-6:]
    seq = parts.shape[0]
    me = lax.axis_index("seq")
    copies = fetch([(refs[m % 2].at[m // 2], parts.at[me ^ m]) for m in range(seq)], load_sems)
    ready()
    marks = relative_marks(ids_ref, batches)
    for copy in copies:
        copy.wait()
    spread_rows(parts, marks, ((down_any, 3, 0, 4), (up_any, 3, 4, 4)), stage, sems)


def last_spread_kernel(batches, ready, ids_ref, down_in, up_in, *refs):
    down_any, up_any, parts, stage, load_sems, sems = refs[-6:]
    seq = parts.shape[0]
    me = lax.axis_index("seq")
    copies = fetch([(refs[m % 2].at[m // 2], parts.at[me ^ m]) for m in range(seq)], load_sems)
    ready()
    marks = relative_marks(ids_ref, batches)
    for copy in copies:
        copy.wait()
    spread_rows(parts, marks, ((down_any, 0, 0, 3), (up_any, 0, 3, 3)), stage, sems)


def along(values, axis, step, size):
    return lax.ppermute(values, axis, [(i, (i + step) % size) for i in range(size)])


def across(values, axis, mask, size):
    return lax.ppermute(values, axis, [(i, i ^ mask) for i in range(size)])


def to_pairs(values, axis, size):
    return [values] + [across(values, axis, m, size) for m in range(2, size, 2)]


def stacked(values, name):
    shape = shaped((len(values), *values[0].shape), values[0].dtype)
    return call(stack_kernel, name, "V" * len(values), [("V", shape)], values)[0]


def exchange(values, axes):
    return lax.all_to_all(values, axes, split_axis=0, concat_axis=0, tiled=True)


def body(
    inputs, lengths, adapter_index, memory_picks, input_weights, output_weights, adapter_down, adapter_up,
    attention_gain, memory_gain, half_keys, memory_values, cotangent,
):
    both = ("batch", "seq")
    batches, seq = lax.axis_size("batch"), lax.axis_size("seq")
    owners = batches * seq
    tokens, width = inputs.shape[1], inputs.shape[2]
    rows, cols, half = tokens * seq, width // seq, width // 2
    rows_dev = memory_values.shape[0]
    capacity = 2 * tokens * MHEADS // owners
    groups = capacity // 8
    items = owners * capacity
    block = min(owners * 8, 256)
    small_block = RECALL_ROWS
    carried = 2 * groups * PICKS // cols * batches * 8
    x, cot = inputs[0], cotangent[0]
    down = jnp.swapaxes(adapter_down, 2, 3)
    gain_one, gain_two = attention_gain, memory_gain
    picks = jnp.transpose(memory_picks[0], (1, 2, 0))
    matrix = pltpu.VMEM((width, width), BF16)
    pair = pltpu.VMEM((2, width, width), BF16)
    triple = pltpu.VMEM((3, width, width), BF16)
    small = pltpu.VMEM((RANK, width), BF16)
    two_small = pltpu.VMEM((2, RANK, width), BF16)
    three_small = pltpu.VMEM((3 * RANK, width), BF16)
    token_low, token_wide = shaped((tokens, width), BF16), shaped((tokens, width), F32)
    token_rank, token_lanes = shaped((tokens, RANK), BF16), shaped((tokens, LANES), F32)
    fixed = functools.partial

    qkv, normed, ranks = call(
        qkv_kernel, "qkv", "MLLHHH",
        [("V", shaped((seq, tokens, 3 * cols), BF16)), ("S", token_low), ("S", shaped((tokens, 3 * RANK), BF16))],
        (adapter_index, x, gain_one, input_weights, down, adapter_up), [triple, three_small, three_small, sema(9)],
    )
    qkv_all = exchange(qkv, "seq").reshape(rows, 3 * cols)

    slot, slot_col, pick, *ids_out = call(
        fixed(route_kernel, rows_dev, owners), "route", "ML",
        [("V", shaped((8, tokens), I32)), ("S", shaped((tokens, tokens), I32)), ("S", shaped((tokens, LANES), I32)),
         *[("V", shaped((seq * 8, LANES), I32)) for _ in range(batches)]],
        (adapter_index, picks), [pltpu.VMEM((owners * 8, LANES), I32)],
    )
    ids_out = [ids_out[0]] + [along(ids_out[k], "batch", k, batches) for k in range(1, batches)]
    qkv_all, ids_out = lax.optimization_barrier((qkv_all, ids_out))
    attended, lse, qkv_saved = call(
        fixed(attend_kernel, groups, batches), "attend", "MV" + "V" * batches,
        [("V", shaped((seq, tokens + carried, cols), BF16)), ("S", shaped((8, rows), F32)), ("H", shaped((rows, 3 * cols), BF16))],
        (lengths, qkv_all, *ids_out),
        [pltpu.VMEM((rows, LANES), BF16), pltpu.VMEM((LANES, rows), BF16), pltpu.VMEM((LANES, rows), F32), sema(1)],
    )
    o_all = exchange(attended, "seq")
    slot, late_cot, attended = lax.optimization_barrier((slot, cot, attended))
    slots = [slot] + [along(slot, "batch", k, batches) for k in range(1, batches)]
    mix_grad, grank_six = call(
        mix_back_kernel, "mixback", "MLHHH", [("S", token_low), ("S", token_rank)],
        (adapter_index, late_cot, output_weights, down, adapter_up), [matrix, small, small, sema(3)],
    )

    o_all, mix_grad, slots = lax.optimization_barrier((o_all, mix_grad, slots))
    left, right, same_two, sent, att, rank_pair, middle, normed_two, gate = call(
        middle_kernel, "middle", "MVLLLHHHH",
        [("V", shaped((tokens, half), BF16)), ("V", shaped((tokens, half), BF16)), ("V", token_low),
         ("S", shaped((seq, carried, cols), BF16)), ("S", token_low),
         ("S", shaped((2, tokens, RANK), BF16)), ("S", token_wide), ("S", token_low), ("S", token_wide)],
        (adapter_index, o_all, x, gain_two, mix_grad, input_weights, output_weights, down, adapter_up),
        [pair, two_small, two_small, sema(6)],
    )
    lefts = [left] + [along(left, "batch", k, batches) for k in range(1, batches)]
    weight_out, rank_four, weights = call(
        fixed(scores_kernel, owners), "scores", "MVLLLHHH",
        [("V", shaped((owners * 8, LANES), BF16)), ("S", token_rank), ("S", token_lanes)],
        (adapter_index, same_two, pick, slot, half_keys, input_weights, down, adapter_up), [matrix, small, small, sema(3)],
    )
    weight_in = exchange(weight_out.reshape(owners, 8, LANES), both).reshape(owners * 8, LANES)
    right, lefts = lax.optimization_barrier((right, lefts))
    rights = [right] + [along(right, "batch", k, batches) for k in range(1, batches)]

    def scatter(parts, name):
        out = [("V", shaped((seq, batches, capacity, half), BF16))]
        return call(scatter_kernel, name, "L" * batches + "V" * batches, out, (*slots, *parts))[0]

    left_out = scatter(lefts, "scatterleft")
    sent, left_out = lax.optimization_barrier((sent, left_out))
    ids, index = call(
        fixed(prepare_kernel, groups, rows_dev, batches), "prepare", "L",
        [("S", shaped((owners * 8, LANES), I32)), ("H", shaped((items, rows_dev), jnp.int16))], (sent,),
        [pltpu.VMEM((2, LANES, rows_dev), jnp.int16), pltpu.VMEM((owners * 8 // LANES, LANES, LANES), I32), sema(2)],
    )
    left_out, weight_in = lax.optimization_barrier((left_out, weight_in))
    left_in = exchange(left_out, "seq").reshape(items, half)

    (sums,) = call(
        fixed(recall_kernel, groups), "recall", "VHH", [("H", shaped((seq, batches, capacity, width), BF16))],
        (weight_in, index, memory_values),
        [pltpu.VMEM((rows_dev, width), BF16), pltpu.VMEM((2, small_block, rows_dev), jnp.int16), pltpu.VMEM((2, small_block, rows_dev), BF16),
         pltpu.VMEM((2, small_block // 8, 8, width), BF16), sema(3 + 2 * (small_block // (8 * seq)))],
        flops=1 << 32,
    )
    sums, left_in = lax.optimization_barrier((sums, left_in))
    back = exchange(sums, "seq")

    def recall_back(part, name, grads, kind, dtype, *before):
        return call(
            fixed(recall_back_kernel, part, batches, groups), name, "L" + "L" * part + "VH",
            [(kind, shaped((owners * 8, LANES), dtype))], (ids, *before, grads, memory_values),
            [pltpu.VMEM((rows_dev, half), BF16), pltpu.VMEM((block, rows_dev), F32), sema(1)], flops=1 << 31,
        )[0]

    right_out = scatter(rights, "scatterright")
    found_left = recall_back(0, "recallleft", left_in, "S", F32)
    right_out, back, found_left = lax.optimization_barrier((right_out, back, found_left))
    right_in = exchange(right_out, "seq").reshape(items, half)
    pieces = call(
        gather_kernel, "gather", "L" * batches + "V", [("V", token_low) for _ in range(batches)], (*slots, back),
    )
    pieces = [pieces[0]] + [along(pieces[k], "batch", batches - k, batches) for k in range(1, batches)]
    found = recall_back(1, "recallright", right_in, "V", BF16, found_left)
    found_back = exchange(found.reshape(owners, 8, LANES), both).reshape(owners * 8, LANES)

    mixed, grank_five, ggate, part = call(
        fixed(memory_kernel, batches), "memory", "MLL" + "V" * batches + "HHH",
        [("S", token_low), ("S", token_rank), ("S", token_low), ("S", token_wide)],
        (adapter_index, gate, mix_grad, *pieces, input_weights, down, adapter_up), [matrix, small, small, sema(3)],
    )

    go, gquery, grank_pair, gmid = call(
        fixed(query_kernel, owners, rows_dev), "query", "MMVLLLLLLLLHHHH",
        [("V", shaped((seq, tokens, cols), BF16)), ("S", token_low), ("S", shaped((2, tokens, RANK), BF16)), ("S", token_wide)],
        (lengths, adapter_index, found_back, slot_col, picks, weights, part, middle, cot, gain_two, half_keys,
         input_weights, output_weights, down, adapter_up),
        [pair, two_small, two_small, pltpu.VMEM((LANES, tokens), F32), sema(6)],
    )
    go_all = exchange(go, "seq").reshape(rows, cols)
    mixed, go = lax.optimization_barrier((mixed, go))
    output, rank_six = call(
        output_kernel, "output", "MLLHHH", [("S", token_low), ("S", token_rank)],
        (adapter_index, mixed, middle, output_weights, down, adapter_up), [matrix, small, small, sema(3)],
    )
    (factors,) = call(
        factor_kernel, "factors", "L" * 13, [("V", shaped((seq, 8 * RANK, cols), BF16))],
        (att, normed_two, mixed, gmid, gquery, ggate, cot, rank_pair, rank_four, rank_six, grank_pair, grank_five, grank_six),
    )
    factors, go_all = lax.optimization_barrier((factors, go_all))
    early_parts = exchange(factors, "seq")

    (grads,) = call(
        attend_back_kernel, "attendback", "MLVL", [("V", shaped((rows, 3 * cols), BF16))], (lengths, qkv_saved, go_all, lse),
        [pltpu.VMEM((rows, LANES), F32), pltpu.VMEM((rows, LANES), F32), pltpu.VMEM((LANES, rows), F32),
         pltpu.VMEM((rows, LANES), BF16), pltpu.VMEM((LANES, rows), BF16), pltpu.VMEM((rows, LANES), BF16)],
    )
    grads, early_parts = lax.optimization_barrier((grads, early_parts))
    grads_all = exchange(grads.reshape(seq, tokens, 3 * cols), "seq")
    (some,) = call(sum_kernel, "sumearly", "V", [("V", shaped((8 * RANK, cols), BF16))], (early_parts,))
    some = [some] + [along(some, "batch", k, batches) for k in range(1, batches)]
    some = stacked(some, "stackearly")
    late, gys, granks = call(
        entry_factor_kernel, "entryfactors", "MVLLH",
        [("V", shaped((seq, 6 * RANK, cols), BF16)), ("S", shaped((3, tokens, width), BF16)), ("S", shaped((tokens, 3 * RANK), BF16))],
        (adapter_index, grads_all, normed, ranks, adapter_up), [three_small, sema(3)],
    )
    late, some = lax.optimization_barrier((late, some))
    late_parts = exchange(late, "seq")
    some = to_pairs(some, "seq", seq)
    (grad_input,) = call(
        entry_kernel, "entry", "MLLLLLHH", [("S", token_low)],
        (adapter_index, gys, granks, x, gain_one, gmid, input_weights, down), [triple, three_small, sema(6)],
    )
    late_parts, some, grad_input = lax.optimization_barrier((late_parts, some, grad_input))
    (late_sum,) = call(sum_kernel, "sumlate", "V", [("V", shaped((6 * RANK, cols), BF16))], (late_parts,))
    late_sums = [late_sum] + [along(late_sum, "batch", k, batches) for k in range(1, batches)]
    some = stacked(some, "pairsearly")
    late_sums, some = lax.optimization_barrier((late_sums, some))
    late_all = to_pairs(stacked(late_sums, "stacklate"), "seq", seq)
    some = (some, across(some, "seq", 1, seq))
    full = shaped((7, ADAPTERS, RANK, width), F32)
    grad_down, grad_up = call(
        fixed(spread_kernel, batches), "spread", "LVV", [("H", full), ("H", full)], (ids, *some),
        [pltpu.VMEM((seq, batches, 8 * RANK, cols), BF16), pltpu.VMEM((8, ADAPTERS, RANK, width), F32), sema(seq), sema(8)],
    )
    late_all, grad_down, grad_up = lax.optimization_barrier((late_all, grad_down, grad_up))
    late_all = stacked(late_all, "pairslate")
    late_all = (late_all, across(late_all, "seq", 1, seq))
    grad_down, grad_up = call(
        fixed(last_spread_kernel, batches), "lastspread", "LHHVV", [("H", full), ("H", full)],
        (ids, grad_down, grad_up, *late_all),
        [pltpu.VMEM((seq, batches, 6 * RANK, cols), BF16), pltpu.VMEM((6, ADAPTERS, RANK, width), F32), sema(seq), sema(6)],
        aliases={1: 0, 2: 1},
    )
    return (output[None], grad_input[None], jnp.swapaxes(grad_down, 2, 3), grad_up)


def solution(mesh):
    split = P("batch", "seq", None)
    return jax.shard_map(
        body,
        mesh=mesh,
        in_specs=(
            split, P("batch"), P("batch"), P("batch", "seq", None, None), P(), P(), P(), P(), P(), P(), P(),
            P(("batch", "seq"), None), split,
        ),
        out_specs=(split, split, P(), P()),
        check_vma=False,
    )
```

```python
import functools

import jax
import jax.numpy as jnp
from jax import lax
from jax.experimental import pallas as pl
from jax.experimental.pallas import tpu as pltpu
from jax.sharding import PartitionSpec as P

HEAD_DIM = 64
MHEADS = 4
KHALF = 128
NSUB = 256
PICKS = 32
ADAPTERS = 8
RANK = 16
LANES = 128
ADAPTER_STEP = 4096
RECALL_ROWS = 128
EPS = 1e-06
NEG = -1e30
F32 = jnp.float32
BF16 = jnp.bfloat16
I32 = jnp.int32
HBM = pl.BlockSpec(memory_space=pltpu.HBM)
SMEM = pl.BlockSpec(memory_space=pltpu.SMEM)
VMEM = pl.BlockSpec(memory_space=pltpu.VMEM)
MIB = 1 << 20


def product(left, right):
    return lax.dot_general(left, right, (((1,), (0,)), ((), ())), preferred_element_type=F32)


def against(left, right):
    return lax.dot_general(left, right, (((1,), (1,)), ((), ())), preferred_element_type=F32)


def contract(left, right):
    return lax.dot_general(left, right, (((0,), (0,)), ((), ())), preferred_element_type=F32)


def iota(shape, axis):
    return lax.broadcasted_iota(I32, shape, axis)


def lane_pick(table, index):
    return jnp.take_along_axis(table, index, axis=1, mode="promise_in_bounds")


def shaped(shape, dtype):
    return jax.ShapeDtypeStruct(shape, dtype)


class Stage:
    def __init__(self, loads, stores):
        self.loads, self.stores = loads, stores
        self.waited, self.begun = set(), set()
        for _, copy in loads:
            copy.start()

    def __call__(self, *refs):
        for at, (ref, copy) in enumerate(self.loads):
            if at not in self.waited and (not refs or any(ref is one for one in refs)):
                self.waited.add(at)
                copy.wait()

    def send(self, *refs):
        for at, (ref, copy) in enumerate(self.stores):
            if at not in self.begun and (not refs or any(ref is one for one in refs)):
                self.begun.add(at)
                copy.start()

    def finish(self):
        self()
        self.send()
        for _, copy in self.stores:
            copy.wait()


def call(kernel, name, ins, outs, args, scratch=(), vmem=40, flops=1 << 12, moved=1 << 12, aliases=None):
    shapes = [(args[i].shape, args[i].dtype) for i, kind in enumerate(ins) if kind == "L"]
    stored = [(out.shape, out.dtype) for kind, out in outs if kind == "S"]
    count_in, count_out, count_user = len(ins), len(outs), len(scratch)

    def wrapped(*refs):
        given, results = list(refs[:count_in]), list(refs[count_in : count_in + count_out])
        rest = list(refs[count_in + count_out :])
        user, buffers = rest[:count_user], rest[count_user:]
        loads, stores = [], []
        for i, kind in enumerate(ins):
            if kind == "L":
                at = len(loads)
                loads.append((buffers[at], pltpu.make_async_copy(given[i], buffers[at], buffers[-1].at[at])))
                given[i] = buffers[at]
        for i, (kind, _) in enumerate(outs):
            if kind == "S":
                at = len(loads) + len(stores)
                stores.append((buffers[at], pltpu.make_async_copy(buffers[at], results[i], buffers[-1].at[at])))
                results[i] = buffers[at]
        stage = Stage(loads, stores)
        kernel(stage, *given, *results, *user)
        stage.finish()

    spaces = {"V": VMEM, "L": HBM, "S": HBM, "H": HBM, "M": SMEM}
    autos = [pltpu.VMEM(*one) for one in shapes + stored]
    args = [
        pltpu.with_memory_space_constraint(one, pltpu.HBM) if kind in "LH" else one
        for kind, one in zip(ins, args, strict=True)
    ]
    return pl.pallas_call(
        wrapped,
        name=name,
        out_shape=[pltpu.HBM(out.shape, out.dtype) if kind in "SH" else out for kind, out in outs],
        in_specs=[spaces[kind] for kind in ins],
        out_specs=[spaces[kind] for kind, _ in outs],
        input_output_aliases=aliases or {},
        scratch_shapes=list(scratch) + autos + ([sema(len(autos))] if autos else []),
        compiler_params=pltpu.CompilerParams(vmem_limit_bytes=vmem * MIB),
        cost_estimate=pl.CostEstimate(flops=flops, bytes_accessed=moved, transcendentals=0),
    )(*args)


def fetch(pairs, sems):
    copies = [
        pltpu.make_async_copy(source, target, sems.at[place])
        for place, (source, target) in enumerate(pairs)
    ]
    for copy in copies:
        copy.start()
    return copies


def sema(count):
    return pltpu.SemaphoreType.DMA((count,))


def gain_row(ref):
    return ref[...].astype(F32).reshape(1, ref.shape[0])


def inverse_norm(values):
    return lax.rsqrt(jnp.mean(values * values, axis=1, keepdims=True) + EPS)


def norm_back(values, inverse, scales, incoming):
    weighted = incoming * scales
    inner = jnp.mean(weighted * values, axis=1, keepdims=True)
    return weighted * inverse - values * inverse * inverse * inverse * inner


def qkv_kernel(ready, adapter, x_ref, gain_ref, w_any, dn_any, up_any, out_ref, norm_ref, w, dn, up, sems):
    groups, tokens, wide = out_ref.shape
    cols = wide // 3
    a = adapter[0]
    copies = fetch(
        [(dn_any.at[j, a], dn.at[pl.ds(RANK * j, RANK)]) for j in range(3)]
        + [(up_any.at[j, a], up.at[pl.ds(RANK * j, RANK)]) for j in range(3)]
        + [(w_any.at[j], w.at[j]) for j in range(3)],
        sems,
    )
    ready()
    x = x_ref[...].astype(F32)
    normed = (x * inverse_norm(x) * gain_row(gain_ref)).astype(BF16)
    width = normed.shape[1]
    norm_ref[:, :width] = normed
    for copy in copies[:6]:
        copy.wait()
    ranks = against(normed, dn[...])
    norm_ref[:, width:] = widen(ranks).astype(BF16)
    ready.send(norm_ref)
    place = iota((tokens, 3 * RANK), 1) // RANK
    for j in range(3):
        own = jnp.where(place == j, ranks, 0.0).astype(BF16)
        extra = product(own, up[...])
        copies[6 + j].wait()
        result = (product(normed, w[j]) + extra).astype(BF16)
        for s in range(groups):
            out_ref[s, :, j * cols : (j + 1) * cols] = result[:, s * cols : (s + 1) * cols]


def mix_back_kernel(ready, adapter, cot_ref, w_any, dn_any, up_any, grad_ref, rank_ref, w, dn, up, sems):
    a = adapter[0]
    copies = fetch([(up_any.at[6, a], up), (dn_any.at[6, a], dn), (w_any.at[1], w)], sems)
    ready()
    gy = cot_ref[...]
    copies[0].wait()
    ranks = against(gy, up[...]).astype(BF16)
    rank_ref[...] = ranks
    copies[1].wait()
    extra = product(ranks, dn[...])
    copies[2].wait()
    grad_ref[...] = (against(gy, w[...]) + extra).astype(BF16)


def route_kernel(rows_dev, owners, ready, adapter, picks_ref, slot_ref, slot_col_ref, pick_ref, *ids_refs):
    ready()
    heads, picks, tokens = picks_ref.shape
    capacity = 2 * heads * tokens // owners
    groups = capacity // 8
    visits = heads * tokens
    owner = jnp.concatenate([picks_ref[h, 0:1, :] for h in range(heads)], axis=1) // rows_dev
    hot = jnp.where(iota((owners, visits), 0) == owner, 1.0, 0.0)
    before = jnp.where(iota((visits, visits), 0) < iota((visits, visits), 1), 1.0, 0.0).astype(BF16)
    counts = product(hot.astype(BF16), before)
    within = jnp.sum(hot * counts, axis=0, keepdims=True).astype(I32)
    slot = owner * capacity + within
    rows = [slot[:, h * tokens : (h + 1) * tokens] for h in range(heads)]
    stacked = jnp.concatenate(rows + [jnp.full((8 - heads, tokens), -1, I32)], axis=0)
    slot_ref[...] = stacked
    tall = jnp.concatenate([stacked, jnp.full((tokens - 8, tokens), -1, I32)], axis=0)
    slot_col_ref[...] = jnp.transpose(tall)
    packed = jnp.concatenate([picks_ref[h] for h in range(heads)], axis=0)
    by_token = jnp.transpose(packed)
    pick_ref[...] = by_token
    local = by_token % rows_dev
    lanes = iota((tokens, LANES), 1)
    total = jnp.zeros((owners * 8, LANES), F32)
    out_lane = iota((owners * 8, LANES), 1) // PICKS
    place = iota((owners * 8, tokens), 0)
    base = (place // 8) * capacity + place % 8
    for g in range(groups):
        high = jnp.zeros((owners * 8, LANES), F32)
        low = jnp.zeros((owners * 8, LANES), F32)
        for h in range(heads):
            chosen = jnp.where(base + g * 8 == rows[h], 1.0, 0.0).astype(BF16)
            own = jnp.where(lanes // PICKS == h, local, 0)
            own = tile_groups(own.astype(F32), heads).astype(I32)
            high = high + product(chosen, (own // 256).astype(F32).astype(BF16))
            low = low + product(chosen, (own % 256).astype(F32).astype(BF16))
        total = jnp.where(out_lane == g, high * 256.0 + low, total)
    batches = len(ids_refs) - 1
    part = owners * 8 // batches
    ids_refs[-1][...] = total.astype(I32) + adapter[0] * ADAPTER_STEP
    for k in range(batches):
        target = lax.rem(lax.axis_index("batch") + k, batches)
        ids_refs[k][0:part, :] = ids_refs[-1][pl.ds(pl.multiple_of(target * part, part), part), :]
        ids_refs[k][part:, :] = stacked


def tile_groups(values, count):
    total = values
    for turn in range(1, count):
        total = total + pltpu.roll(values, turn * PICKS, 1)
    return total


def prepare_kernel(groups, rows_dev, batches, ready, sent_ref, ids_ref, index_any, stage, turned, sems):
    ready()
    seq, _, cols = sent_ref.shape
    lanes = groups * PICKS
    chunks = 2 * lanes // cols
    for k in range(batches):
        source = lax.rem(lax.axis_index("batch") + (batches - k), batches)
        for s in range(seq):
            both = [
                sent_ref[s, (chunk * batches + k) * 8 : (chunk * batches + k + 1) * 8, :].astype(F32)
                for chunk in range(chunks)
            ]
            both = jnp.concatenate(both, axis=1).astype(I32)
            ids = widen(both[:, :lanes] * 256 + both[:, lanes:])
            ids_ref[pl.ds(pl.multiple_of((source * seq + s) * 8, 8), 8), :] = ids
    ready.send(ids_ref)
    places = ids_ref.shape[0]
    chunks = rows_dev // LANES
    high_rows = max(8, chunks)
    steps = groups * (places // LANES)
    for k in range(places // LANES):
        turned[k] = jnp.transpose(ids_ref[k * LANES : (k + 1) * LANES, :] & (ADAPTER_STEP - 1))

    def put(step, slot):
        target = index_any.at[pl.ds(pl.multiple_of(step * LANES, LANES), LANES)]
        return pltpu.make_async_copy(stage.at[slot], target, sems.at[slot])

    def one(step, carry):
        k, g = lax.rem(step, places // LANES), step // (places // LANES)
        slot = lax.rem(step, 2)
        mask = jnp.zeros((LANES, LANES), I32)
        highs = jnp.zeros((high_rows, LANES), I32)
        for r in range(PICKS):
            bit = (1 << r) if r < 31 else -(1 << 31)
            row = turned[k, pl.ds(g * PICKS + r, 1), :]
            mask = mask | jnp.where(row & 127 == iota((LANES, LANES), 0), bit, 0)
            highs = highs | jnp.where(row >> 7 == iota((high_rows, LANES), 0), bit, 0)

        @pl.when(step >= 2)
        def _():
            put(step - 2, slot).wait()

        for c in range(chunks):
            index = 31 - lax.clz(mask & highs[c : c + 1, :])
            stage[slot, :, c * LANES : (c + 1) * LANES] = jnp.transpose(index).astype(jnp.int16)
        put(step, slot).start()
        return carry

    lax.fori_loop(0, steps, one, 0)
    for step in range(max(0, steps - 2), steps):
        put(step, step % 2).wait()


def recall_kernel(groups, ready, weight_ref, index_any, mem_any, out_any, mem, index, dense, staged, sems):
    places = weight_ref.shape[0]
    rows_dev = mem.shape[0]
    chunks = rows_dev // LANES
    block = dense.shape[1]
    per_group = places // block
    blocks = groups * per_group
    seq = out_any.shape[0]
    planes = block // (8 * seq)

    def load(b, slot):
        source = index_any.at[pl.ds(pl.multiple_of(b * block, block), block)]
        return pltpu.make_async_copy(source, index.at[slot], sems.at[1 + slot])

    load(0, 0).start()
    copy = pltpu.make_async_copy(mem_any, mem, sems.at[0])
    copy.start()

    def gather(b, side):
        load(b, side).wait()

        @pl.when(b + 1 < blocks)
        def _():
            load(b + 1, 1 - side).start()

        pick(b, side)

    def pick(b, side):
        g, k = b // per_group, lax.rem(b, per_group)
        for start in range(0, block, 16):
            weights = weight_ref[pl.ds(pl.multiple_of(k * block + start, 16), 16), :].astype(F32)
            for c in range(chunks):
                at = index[side, start : start + 16, c * LANES : (c + 1) * LANES].astype(I32)
                value = lane_pick(weights, (at + g * PICKS) & 127)
                dense[side, start : start + 16, c * LANES : (c + 1) * LANES] = jnp.where(at >= 0, value, 0.0).astype(BF16)

    def save(b, side):
        g, k = b // per_group, lax.rem(b, per_group)
        return [
            pltpu.make_async_copy(
                staged.at[side, pl.ds(i * seq, seq)],
                out_any.at[:, k * planes + i, pl.ds(pl.multiple_of(g * 8, 8), 8), :],
                sems.at[3 + side * planes + i],
            )
            for i in range(planes)
        ]

    def multiply(b, side):
        result = product(dense[side], mem[...]).astype(BF16)

        @pl.when(b >= 2)
        def _():
            for one in save(b - 2, side):
                one.wait()

        staged[side] = result.reshape(block // 8, 8, result.shape[1])
        for one in save(b, side):
            one.start()

    gather(0, 0)
    copy.wait()

    def whole(i, carry):
        gather(2 * i + 1, 1)
        multiply(2 * i, 0)

        @pl.when(2 * i + 2 < blocks)
        def _():
            load(2 * i + 2, 0).wait()
            load(2 * i + 3, 1).start()

        pick(jnp.minimum(2 * i + 2, blocks - 1), 0)
        multiply(2 * i + 1, 1)
        return carry

    lax.fori_loop(0, blocks // 2, whole, 0)
    for b in range(blocks - 2, blocks):
        for one in save(b, b % 2):
            one.wait()


def recall_back_kernel(part, batches, groups, ready, ids_ref, *refs):
    before_ref = refs[0] if part else None
    grad_ref, mem_any, out_ref, mem, scores, sems = refs[part:]
    items, half = grad_ref.shape
    seq = items // (batches * groups * 8)
    rows_dev = mem.shape[0]
    capacity = groups * 8
    chunks = rows_dev // LANES
    block = scores.shape[0]
    per_block = block // capacity
    blocks = items // block
    copies = fetch([(mem_any.at[:, pl.ds(part * half, half)], mem)], sems)
    ready()
    copies[0].wait()

    def whole(b, outer):
        scores[...] = against(grad_ref[pl.ds(pl.multiple_of(b * block, block), block), :], mem[...])

        lane_group = iota((8, LANES), 1) // PICKS
        for local in range(per_block):
            sender = b * per_block + local
            spot = lax.rem(sender, batches) * seq + sender // batches
            start = pl.multiple_of(spot * 8, 8)
            ids = ids_ref[pl.ds(start, 8), :] & (ADAPTER_STEP - 1)
            low = ids & 127
            high = ids >> 7
            total = before_ref[pl.ds(start, 8), :] if part else jnp.zeros((8, LANES), F32)
            for g in range(groups):
                key = jnp.where(lane_group == g, high, -1)
                here = jnp.zeros((8, LANES), F32)
                row = local * capacity + g * 8
                for c in range(chunks):
                    found = scores[row : row + 8, c * LANES : (c + 1) * LANES]
                    here = jnp.where(key == c, lane_pick(found, low), here)
                total = total + here
            out_ref[pl.ds(start, 8), :] = total.astype(out_ref.dtype)
        return outer

    lax.fori_loop(0, blocks, whole, 0)


def head_parts(values, h, spare):
    lane = iota(values.shape, 1)
    return jnp.where(lane // HEAD_DIM == h, values, jnp.where(lane == (1 - h) * HEAD_DIM, spare, 0.0)).astype(BF16)


def widen(values):
    if values.shape[1] == LANES:
        return values
    return jnp.concatenate([values, jnp.zeros((values.shape[0], LANES - values.shape[1]), values.dtype)], axis=1)


def attend_kernel(groups, batches, ready, length, qkv_ref, *refs):
    o_ref, lse_ref, slots_ref, saved_any, parts, values_t, mixed, sems = refs[batches:]
    ready()
    saving = pltpu.make_async_copy(qkv_ref, saved_any, sems.at[0])
    saving.start()
    rows, wide = qkv_ref.shape
    cols = wide // 3
    seq = o_ref.shape[0]
    lanes = groups * PICKS
    for k in range(batches):
        slots_ref[k] = refs[k][seq * 8 :, :]
    ready.send(slots_ref)
    for s in range(seq):
        ids = jnp.concatenate([refs[k][s * 8 : (s + 1) * 8, :lanes] for k in range(batches)], axis=0)
        both = jnp.concatenate([ids // 256, ids % 256], axis=1).astype(F32).astype(BF16)
        for chunk in range(2 * lanes // cols):
            start = rows // seq + chunk * batches * 8
            o_ref[s, start : start + batches * 8, :] = both[:, chunk * cols : (chunk + 1) * cols]
    heads = cols // HEAD_DIM
    size = min(256, rows)
    valid = length[0]
    bias = jnp.where(iota((rows, LANES), 0) < valid, 0.0, NEG)
    keys = widen(qkv_ref[:, cols : 2 * cols].astype(F32))
    values_t[...] = jnp.transpose(widen(qkv_ref[:, 2 * cols :].astype(F32))).astype(BF16)
    lse_ref[...] = jnp.zeros_like(lse_ref)

    def one(h, carry):
        parts[...] = head_parts(keys, h, bias)
        for i in range(rows // size):
            first, last = i * size, (i + 1) * size
            queries = widen(qkv_ref[first:last, 0:cols].astype(F32)) * (HEAD_DIM**-0.5)
            query = head_parts(queries, h, 1.0)
            near = against(parts[first:last], query)
            near = jnp.where(iota((size, size), 0) <= iota((size, size), 1), near, NEG)
            high = jnp.max(near, axis=0, keepdims=True)
            if i:
                far = against(parts[:first], query)
                high = jnp.maximum(high, jnp.max(far, axis=0, keepdims=True))
            near = jnp.exp(near - high)
            summed = jnp.sum(near, axis=0, keepdims=True)
            result = product(values_t[:, first:last], near.astype(BF16))
            if i:
                far = jnp.exp(far - high)
                summed = summed + jnp.sum(far, axis=0, keepdims=True)
                result = result + product(values_t[:, :first], far.astype(BF16))
            lse_ref[pl.ds(h, 1), first:last] = high + jnp.log(summed)
            own = iota((LANES, size), 0) // HEAD_DIM == h
            mixed[:, first:last] = jnp.where(own, result / summed, mixed[:, first:last])
        return carry

    mixed[...] = jnp.zeros_like(mixed)
    lax.fori_loop(0, heads, one, 0)
    ready.send(lse_ref)
    tokens = rows // seq
    for s in range(seq):
        first = s * tokens
        kept = jnp.where(first + iota((LANES, tokens), 1) < valid, mixed[:, first : first + tokens], 0.0)
        o_ref[s, 0:tokens, :] = jnp.transpose(kept)[:, :cols].astype(BF16)
    saving.wait()


def attend_back_kernel(
    ready, length, adapter, qkv_ref, go_ref, lse_ref, even_ref, odd_ref, up_any,
    out_ref, upgrad_ref, dk, dv, dq, parts, keys_t, values, grads_all, norms, up, sems,
):
    a = adapter[0]
    seq = out_ref.shape[0]
    me = lax.axis_index("seq")
    tokens = even_ref.shape[1]
    copies = fetch(
        [(up_any.at[j, a], up.at[pl.ds(RANK * j, RANK)]) for j in range(3)]
        + [
            ((even_ref, odd_ref)[m % 2].at[m // 2], norms.at[pl.ds(pl.multiple_of((me ^ m) * tokens, tokens), tokens)])
            for m in range(seq)
        ],
        sems,
    )
    ready()
    rows, wide = qkv_ref.shape
    cols = wide // 3
    heads = cols // HEAD_DIM
    size = min(256, rows)
    valid = length[0]
    scaling = HEAD_DIM**-0.5
    bias = jnp.where(iota((rows, LANES), 0) < valid, 0.0, NEG)
    keys = widen(qkv_ref[:, cols : 2 * cols].astype(F32))
    keys_t[...] = jnp.transpose(keys).astype(BF16)
    values[...] = widen(qkv_ref[:, 2 * cols :])
    dk[...] = jnp.zeros_like(dk)
    dv[...] = jnp.zeros_like(dv)
    dq[...] = jnp.zeros_like(dq)

    def one(h, carry):
        parts[...] = head_parts(keys, h, bias)
        for i in range(rows // size):
            first, last = i * size, (i + 1) * size
            queries = widen(qkv_ref[first:last, 0:cols].astype(F32)) * scaling
            grads = widen(go_ref[first:last, :].astype(F32))
            query = head_parts(queries, h, 1.0)
            plain = head_parts(queries, h, 0.0)
            grad = head_parts(grads, h, 0.0)
            lse = lse_ref[pl.ds(h, 1), first:last]
            near = against(parts[first:last], query)
            near = jnp.where(iota((size, size), 0) <= iota((size, size), 1), near, NEG)
            near = jnp.exp(near - lse)
            near_gp = against(values[first:last], grad)
            delta = jnp.sum(near * near_gp, axis=0, keepdims=True)
            if i:
                far = jnp.exp(against(parts[:first], query) - lse)
                far_gp = against(values[:first], grad)
                delta = delta + jnp.sum(far * far_gp, axis=0, keepdims=True)
            near_gs = (near * (near_gp - delta)).astype(BF16)
            result = product(keys_t[:, first:last], near_gs)
            dk[first:last] += product(near_gs, plain)
            dv[first:last] += product(near.astype(BF16), grad)
            if i:
                far_gs = (far * (far_gp - delta)).astype(BF16)
                result = result + product(keys_t[:, :first], far_gs)
                dk[:first] += product(far_gs, plain)
                dv[:first] += product(far.astype(BF16), grad)
            own = iota((LANES, size), 0) // HEAD_DIM == h
            dq[:, first:last] = jnp.where(own, result, dq[:, first:last])
        return carry

    lax.fori_loop(0, heads, one, 0)
    grads_all[:, 0:cols] = (jnp.transpose(dq[...]) * scaling)[:, :cols].astype(BF16)
    grads_all[:, cols : 2 * cols] = dk[:, :cols].astype(BF16)
    grads_all[:, 2 * cols :] = dv[:, :cols].astype(BF16)
    for s in range(seq):
        out_ref[s, 0:tokens, :] = grads_all[s * tokens : (s + 1) * tokens, :]
    for copy in copies:
        copy.wait()
    own = jnp.zeros((3 * RANK, cols), F32)
    for s in range(seq):
        own = jnp.where(me == s, up[:, s * cols : (s + 1) * cols].astype(F32), own)
    own = own.astype(BF16)
    place = iota((rows, 3 * RANK), 1) // RANK
    granks = jnp.zeros((rows, 3 * RANK), F32)
    for j in range(3):
        granks = jnp.where(place == j, against(grads_all[:, j * cols : (j + 1) * cols], own), granks)
    width = norms.shape[1] - LANES
    down = contract(granks.astype(BF16), norms[:, :width]).astype(BF16)
    both = contract(norms[:, width:], grads_all[...]).astype(BF16)
    for j in range(3):
        row = j * RANK
        upgrad_ref[row : row + RANK, :] = both[row : row + RANK, j * cols : (j + 1) * cols]
        for s in range(seq):
            out_ref[s, tokens:, j * cols : (j + 1) * cols] = down[row : row + RANK, s * cols : (s + 1) * cols]


def pick_chosen(tables, index):
    tokens = index.shape[0]
    low = index & 127
    key = (index >> 7) + (iota((tokens, LANES), 1) // PICKS) * (NSUB // LANES)
    total = jnp.zeros((tokens, LANES), F32)
    for h in range(MHEADS):
        for c in range(NSUB // LANES):
            found = lane_pick(tables[h][:, c * LANES : (c + 1) * LANES], low)
            total = jnp.where(key == h * (NSUB // LANES) + c, found, total)
    return total


def group_reduce(values, reducer, fill):
    group = iota(values.shape, 1) // PICKS
    total = jnp.zeros(values.shape, F32)
    for h in range(MHEADS):
        one = reducer(jnp.where(group == h, values, fill), axis=1, keepdims=True)
        total = jnp.where(group == h, one, total)
    return total


def middle_kernel(
    ready, adapter, o_ref, x_ref, gain_ref, mix_ref, w_in_any, w_out_any, dn_any, up_any,
    left_ref, right_ref, same_ref, sent_ref, att_ref, rank_ref, mid_ref, norm_ref, gate_ref, w, dn, up, sems,
):
    groups = o_ref.shape[0]
    a = adapter[0]
    copies = fetch(
        [(dn_any.at[3, a], dn.at[0]), (dn_any.at[5, a], dn.at[1]), (up_any.at[3, a], up.at[0]), (up_any.at[5, a], up.at[1]),
         (w_out_any.at[0], w.at[0]), (w_in_any.at[4], w.at[1])],
        sems,
    )
    tokens = att_ref.shape[0]
    attended = jnp.concatenate([o_ref[s, 0:tokens, :] for s in range(groups)], axis=1)
    sent_ref[...] = o_ref[:, tokens:, :]
    ready.send(sent_ref)
    att_ref[...] = attended
    ready.send(att_ref)
    for copy in copies[:4]:
        copy.wait()
    rank_three = against(attended, dn[0]).astype(BF16)
    extra = product(rank_three, up[0])
    copies[4].wait()
    ready(x_ref, gain_ref)
    middle = x_ref[...].astype(F32) + (product(attended, w[0]) + extra)
    mid_ref[...] = middle
    normed = (middle * inverse_norm(middle) * gain_row(gain_ref)).astype(BF16)
    norm_ref[...] = normed
    same_ref[...] = normed
    ready.send(mid_ref, norm_ref)
    rank_five = against(normed, dn[1]).astype(BF16)
    rank_ref[0] = rank_three
    rank_ref[1] = rank_five
    extra = product(rank_five, up[1])
    copies[5].wait()
    gate = product(normed, w[1]) + extra
    gate_ref[...] = gate
    ready.send(rank_ref, gate_ref)
    ready(mix_ref)
    memory_grad = (mix_ref[...].astype(F32) * (gate * jax.nn.sigmoid(gate))).astype(BF16)
    half = left_ref.shape[1]
    left_ref[...] = memory_grad[:, :half]
    right_ref[...] = memory_grad[:, half:]


def scores_kernel(
    owners, ready, adapter, normed_ref, picks_ref, slot_ref, keys_ref, w_in_any, dn_any, up_any,
    send_ref, rank_ref, weight_ref, w, dn, up, sems,
):
    a = adapter[0]
    copies = fetch([(dn_any.at[4, a], dn), (up_any.at[4, a], up), (w_in_any.at[3], w)], sems)
    normed = normed_ref[...]
    copies[0].wait()
    ranks = against(normed, dn[...]).astype(BF16)
    rank_ref[...] = ranks
    copies[1].wait()
    extra = product(ranks, up[...])
    copies[2].wait()
    query = (product(normed, w[...]) + extra).astype(BF16)
    ready()
    ready.send(rank_ref)
    first, second = [], []
    for h in range(MHEADS):
        base = 2 * h * KHALF
        first.append(against(query[:, base : base + KHALF], keys_ref[0, h]))
        second.append(against(query[:, base + KHALF : base + 2 * KHALF], keys_ref[1, h]))
    picks = picks_ref[...]
    scores = pick_chosen(first, picks // NSUB) + pick_chosen(second, picks % NSUB)
    exponent = jnp.exp(scores - group_reduce(scores, jnp.max, NEG))
    weights = exponent / group_reduce(exponent, jnp.sum, 0.0)
    weight_ref[...] = weights
    ready.send(weight_ref)
    send_ref[...] = to_slots(weights, slot_ref, owners).astype(BF16)


def to_slots(weights, slot_ref, owners):
    tokens = weights.shape[0]
    capacity = 2 * MHEADS * tokens // owners
    lane_group = iota((tokens, LANES), 1) // PICKS
    tiled = [
        tile_groups(jnp.where(lane_group == h, weights, 0.0), MHEADS).astype(BF16) for h in range(MHEADS)
    ]
    place = iota((owners * 8, tokens), 0)
    base = (place // 8) * capacity + place % 8
    out_group = iota((owners * 8, LANES), 1) // PICKS
    total = jnp.zeros((owners * 8, LANES), F32)
    for g in range(capacity // 8):
        part = jnp.zeros((owners * 8, LANES), F32)
        for h in range(MHEADS):
            chosen = jnp.where(base + g * 8 == slot_ref[h : h + 1, :], 1.0, 0.0).astype(BF16)
            part = part + product(chosen, tiled[h])
        total = jnp.where(out_group == g, part, total)
    return total


def plane_hits(slots_ref, k, plane, seq, capacity):
    tokens = slots_ref.shape[2]
    place = plane * (seq * capacity) + iota((seq * capacity, tokens), 0)
    chosen = jnp.zeros((seq * capacity, tokens), F32)
    for h in range(MHEADS):
        chosen = jnp.where(place == slots_ref[k, h : h + 1, :], 1.0, chosen)
    return chosen.astype(BF16)


def scatter_kernel(ready, slots_ref, *refs):
    ready()
    out_ref = refs[-1]
    seq, batches, capacity, wide = out_ref.shape
    plane = lax.axis_index("batch")
    for k in range(batches):
        chosen = plane_hits(slots_ref, k, plane, seq, capacity)
        rows = product(chosen, refs[k][...]).astype(BF16)
        source = lax.rem(plane + (batches - k), batches)
        out_ref[:, pl.ds(source, 1)] = rows.reshape(seq, 1, capacity, wide)


def gather_kernel(ready, slots_ref, back_ref, *refs):
    ready()
    seq, batches, capacity, wide = back_ref.shape
    plane = lax.axis_index("batch")
    for k in range(batches):
        chosen = plane_hits(slots_ref, k, plane, seq, capacity)
        source = lax.rem(plane + (batches - k), batches)
        rows = back_ref[:, pl.ds(source, 1)].reshape(seq * capacity, wide)
        refs[k][...] = contract(chosen, rows).astype(BF16)


def memory_kernel(batches, ready, adapter, gate_ref, mix_ref, *refs):
    w_in_any, dn_any, up_any, mixed_ref, grank_ref, ggate_ref, part_ref, w, dn, up, sems = refs[batches:]
    a = adapter[0]
    copies = fetch([(dn_any.at[5, a], dn), (up_any.at[5, a], up), (w_in_any.at[4], w)], sems)
    ready()
    memory = refs[0][...].astype(F32)
    for k in range(1, batches):
        memory = memory + refs[k][...].astype(F32)
    gate = gate_ref[...]
    sigmoid = jax.nn.sigmoid(gate)
    mixed_ref[...] = (memory * (gate * sigmoid)).astype(BF16)
    ggate = (mix_ref[...].astype(F32) * memory * sigmoid * (1.0 + gate * (1.0 - sigmoid))).astype(BF16)
    ggate_ref[...] = ggate
    for copy in copies[:2]:
        copy.wait()
    granks = against(ggate, up[...]).astype(BF16)
    grank_ref[...] = granks
    extra = product(granks, dn[...])
    copies[2].wait()
    ready.send(mixed_ref, ggate_ref, grank_ref)
    part_ref[...] = against(ggate, w[...]) + extra


def output_kernel(ready, adapter, mixed_ref, mid_ref, w_out_any, dn_any, up_any, out_ref, rank_ref, w, dn, up, sems):
    a = adapter[0]
    copies = fetch([(dn_any.at[6, a], dn), (up_any.at[6, a], up), (w_out_any.at[1], w)], sems)
    ready()
    mixed = mixed_ref[...]
    for copy in copies[:2]:
        copy.wait()
    ranks = against(mixed, dn[...]).astype(BF16)
    rank_ref[...] = ranks
    extra = product(ranks, up[...])
    copies[2].wait()
    out_ref[...] = (mid_ref[...] + (product(mixed, w[...]) + extra)).astype(BF16)


def query_kernel(
    owners, rows_dev, ready, length, adapter, back_ref, slot_ref, picks_ref, weight_ref, part_ref, mid_ref, cot_ref, gain_ref,
    keys_ref, w_in_any, w_out_any, dn_any, up_any,
    go_ref, gquery_ref, grank_ref, gmid_ref, w, dn, up, turned, sems,
):
    groups, tokens, cols = go_ref.shape
    a = adapter[0]
    copies = fetch(
        [(dn_any.at[3, a], dn.at[0]), (dn_any.at[4, a], dn.at[1]), (up_any.at[3, a], up.at[0]),
         (up_any.at[4, a], up.at[1]), (w_in_any.at[3], w.at[0]), (w_out_any.at[0], w.at[1])],
        sems,
    )
    ready(slot_ref, weight_ref)
    capacity = 2 * MHEADS * tokens // owners
    slots = iota((tokens, owners * 8), 1)
    base = (slots // 8) * capacity + slots % 8
    lane_group = iota((tokens, LANES), 1) // PICKS
    back = back_ref[...]
    gw = jnp.zeros((tokens, LANES), F32)
    for h in range(MHEADS):
        part = jnp.zeros((tokens, LANES), F32)
        for g in range(capacity // 8):
            chosen = jnp.where(base + g * 8 == slot_ref[:, h : h + 1], 1.0, 0.0).astype(BF16)
            part = jnp.where(lane_group == g, product(chosen, back), part)
        gw = jnp.where(lane_group == h, tile_groups(part, MHEADS), gw)
    weights = weight_ref[...]
    gscore = jnp.transpose(weights * (gw - group_reduce(weights * gw, jnp.sum, 0.0)))
    turned[...] = gscore
    ready(picks_ref, keys_ref)
    span = rows_dev // NSUB
    halves = []
    for h in range(MHEADS):

        def one(r, sums):
            pick = picks_ref[h, pl.ds(r, 1), :]
            value = turned[pl.ds(h * PICKS + r, 1), :]
            low = jnp.where((pick // NSUB) % span == iota((8, tokens), 0), value, 0.0)
            hit = (pick % NSUB).astype(jnp.int16) == lax.broadcasted_iota(jnp.int16, (NSUB, tokens), 0)
            return sums[0] + low, sums[1] + jnp.where(hit, value.astype(BF16), jnp.zeros((), BF16))

        start = (jnp.zeros((8, tokens), F32), jnp.zeros((NSUB, tokens), BF16))
        first, second = lax.fori_loop(0, PICKS, one, start, unroll=8)
        origin = picks_ref[h, 0:1, :] // rows_dev
        place = iota((NSUB, tokens), 0)
        wide = jnp.concatenate([first[:span]] * (NSUB // span), axis=0)
        wide = jnp.where(place // span == origin, wide, 0.0)
        halves.append(contract(wide.astype(BF16), keys_ref[0, h]))
        halves.append(contract(second, keys_ref[1, h]))
    gquery = jnp.concatenate(halves, axis=1).astype(BF16)
    gquery_ref[...] = gquery
    ready.send(gquery_ref)
    ready()
    for copy in copies[:4]:
        copy.wait()
    granks = against(gquery, up[1]).astype(BF16)
    grank_ref[1] = granks
    extra = product(granks, dn[1])
    copies[4].wait()
    gnormed = against(gquery, w[0]) + extra + part_ref[...]
    middle = mid_ref[...]
    gmid = cot_ref[...].astype(F32) + norm_back(middle, inverse_norm(middle), gain_row(gain_ref), gnormed)
    gmid_ref[...] = gmid
    ready.send(gmid_ref)
    low = gmid.astype(BF16)
    granks = against(low, up[0]).astype(BF16)
    grank_ref[0] = granks
    ready.send(grank_ref)
    extra = product(granks, dn[0])
    copies[5].wait()
    go = against(low, w[1]) + extra
    row = lax.axis_index("seq") * tokens + iota((tokens, 1), 0)
    go = jnp.where(row < length[0], go, 0.0).astype(BF16)
    for s in range(groups):
        go_ref[s] = go[:, s * cols : (s + 1) * cols]


def place_columns(out_ref, row, values):
    groups, _, cols = out_ref.shape
    low = values.astype(BF16)
    for s in range(groups):
        out_ref[s, row : row + values.shape[0], :] = low[:, s * cols : (s + 1) * cols]


def factor_kernel(ready, att_ref, norm_ref, mixed_ref, gmid_ref, gquery_ref, ggate_ref, cot_ref, r35, r4, r6, g34, g5, g6, out_ref):
    ready()
    half = 4 * RANK
    sides = (
        (att_ref[...], gmid_ref[...].astype(BF16), r35[0], g34[0]),
        (norm_ref[...], gquery_ref[...], r4[...], g34[1]),
        (norm_ref[...], ggate_ref[...], r35[1], g5[...]),
        (mixed_ref[...], cot_ref[...], r6[...], g6[...]),
    )
    for j, (value, gy, rank, grank) in enumerate(sides):
        place_columns(out_ref, j * RANK, contract(grank, value))
        place_columns(out_ref, half + j * RANK, contract(rank, gy))


def late_kernel(ready, grads_ref, upgrad_ref, out_ref):
    seq, _, wide = grads_ref.shape
    cols = wide // 3
    tokens = grads_ref.shape[1] - RANK
    total = grads_ref[0, tokens:, :].astype(F32)
    for s in range(1, seq):
        total = total + grads_ref[s, tokens:, :].astype(F32)
    total = total.astype(BF16)
    for j in range(3):
        out_ref[j * RANK : (j + 1) * RANK, :] = total[:, j * cols : (j + 1) * cols]
    ready()
    out_ref[3 * RANK :, :] = upgrad_ref[...]


def entry_kernel(ready, adapter, grads_ref, x_ref, gain_ref, gmid_ref, w_any, dn_any, up_any, out_ref, w, dn, up, sems):
    a = adapter[0]
    seq, _, wide = grads_ref.shape
    cols = wide // 3
    tokens = out_ref.shape[0]
    copies = fetch(
        [(up_any.at[j, a], up.at[pl.ds(RANK * j, RANK)]) for j in range(3)]
        + [(dn_any.at[j, a], dn.at[pl.ds(RANK * j, RANK)]) for j in range(3)]
        + [(w_any.at[j], w.at[j]) for j in range(3)],
        sems,
    )
    gys = [
        jnp.concatenate([grads_ref[s, 0:tokens, j * cols : (j + 1) * cols] for s in range(seq)], axis=1) for j in range(3)
    ]
    for copy in copies[:6]:
        copy.wait()
    place = iota((tokens, 3 * RANK), 1) // RANK
    granks = jnp.zeros((tokens, 3 * RANK), F32)
    for j in range(3):
        granks = jnp.where(place == j, against(gys[j], up[...]), granks)
    total = product(granks.astype(BF16), dn[...])
    for j in range(3):
        copies[6 + j].wait()
        total = total + against(gys[j], w[j])
    ready()
    x = x_ref[...].astype(F32)
    back = norm_back(x, inverse_norm(x), gain_row(gain_ref), total)
    out_ref[...] = (gmid_ref[...] + back).astype(BF16)


def sum_kernel(ready, parts_ref, out_ref):
    ready()
    total = parts_ref[0].astype(F32)
    for s in range(1, parts_ref.shape[0]):
        total = total + parts_ref[s].astype(F32)
    out_ref[...] = total.astype(BF16)


def stack_kernel(ready, *refs):
    for k in range(refs[-1].shape[0]):
        refs[-1][k] = refs[k][...]


def relative_marks(ids_ref, batches):
    plane = lax.axis_index("batch")
    absolute = adapter_marks(ids_ref, batches)
    marks = []
    for k in range(batches):
        source = lax.rem(plane + (batches - k), batches)
        mark = absolute[0]
        for b in range(1, batches):
            mark = jnp.where(source == b, absolute[b], mark)
        marks.append(mark)
    return marks


def adapter_marks(ids_ref, batches):
    step = ids_ref.shape[0] // batches
    return [ids_ref[b * step : b * step + 1, 0:1] // ADAPTER_STEP for b in range(batches)]


def spread_rows(parts, marks, runs, stage, sems):
    seq, batches = parts.shape[:2]
    for target, origin, base, count in runs:

        def put(i, target=target, origin=origin, base=base):
            return pltpu.make_async_copy(stage.at[base + i], target.at[origin + i], sems.at[base + i])

        def one(i, carry, put=put, base=base):
            start = pl.multiple_of((base + i) * RANK, RANK)
            rows = [
                jnp.concatenate([parts[s, k, pl.ds(start, RANK), :] for s in range(seq)], axis=1).astype(F32)
                for k in range(batches)
            ]
            for k in range(ADAPTERS):
                total = jnp.zeros(rows[0].shape, F32)
                for row, mark in zip(rows, marks, strict=True):
                    total = total + jnp.where(mark == k, row, 0.0)
                stage[base + i, k] = total
            put(i).start()
            return carry

        lax.fori_loop(0, count, one, 0)
    for target, origin, base, count in runs:
        for i in range(count):
            pltpu.make_async_copy(stage.at[base + i], target.at[origin + i], sems.at[base + i]).wait()


def spread_kernel(batches, ready, ids_ref, *refs):
    down_any, up_any, parts, stage, load_sems, sems = refs[-6:]
    seq = parts.shape[0]
    me = lax.axis_index("seq")
    copies = fetch([(refs[m % 2].at[m // 2], parts.at[me ^ m]) for m in range(seq)], load_sems)
    ready()
    marks = relative_marks(ids_ref, batches)
    for copy in copies:
        copy.wait()
    spread_rows(parts, marks, ((down_any, 3, 0, 4), (up_any, 3, 4, 4)), stage, sems)


def last_spread_kernel(batches, ready, ids_ref, down_in, up_in, *refs):
    down_any, up_any, parts, stage, load_sems, sems = refs[-6:]
    seq = parts.shape[0]
    me = lax.axis_index("seq")
    copies = fetch([(refs[m % 2].at[m // 2], parts.at[me ^ m]) for m in range(seq)], load_sems)
    ready()
    marks = relative_marks(ids_ref, batches)
    for copy in copies:
        copy.wait()
    spread_rows(parts, marks, ((down_any, 0, 0, 3), (up_any, 0, 3, 3)), stage, sems)


def along(values, axis, step, size):
    return lax.ppermute(values, axis, [(i, (i + step) % size) for i in range(size)])


def across(values, axis, mask, size):
    return lax.ppermute(values, axis, [(i, i ^ mask) for i in range(size)])


def to_pairs(values, axis, size):
    return [values] + [across(values, axis, m, size) for m in range(2, size, 2)]


def stacked(values, name, kind="V"):
    shape = shaped((len(values), *values[0].shape), values[0].dtype)
    return call(stack_kernel, name, "V" * len(values), [(kind, shape)], values)[0]


def exchange(values, axes):
    return lax.all_to_all(values, axes, split_axis=0, concat_axis=0, tiled=True)


def body(
    inputs, lengths, adapter_index, memory_picks, input_weights, output_weights, adapter_down, adapter_up,
    attention_gain, memory_gain, half_keys, memory_values, cotangent,
):
    both = ("batch", "seq")
    batches, seq = lax.axis_size("batch"), lax.axis_size("seq")
    owners = batches * seq
    tokens, width = inputs.shape[1], inputs.shape[2]
    rows, cols, half = tokens * seq, width // seq, width // 2
    rows_dev = memory_values.shape[0]
    capacity = 2 * tokens * MHEADS // owners
    groups = capacity // 8
    items = owners * capacity
    block = min(owners * 8, 256)
    small_block = RECALL_ROWS
    carried = 2 * groups * PICKS // cols * batches * 8
    x, cot = inputs[0], cotangent[0]
    down = jnp.swapaxes(adapter_down, 2, 3)
    gain_one, gain_two = attention_gain, memory_gain
    picks = jnp.transpose(memory_picks[0], (1, 2, 0))
    matrix = pltpu.VMEM((width, width), BF16)
    pair = pltpu.VMEM((2, width, width), BF16)
    triple = pltpu.VMEM((3, width, width), BF16)
    small = pltpu.VMEM((RANK, width), BF16)
    two_small = pltpu.VMEM((2, RANK, width), BF16)
    three_small = pltpu.VMEM((3 * RANK, width), BF16)
    token_low, token_wide = shaped((tokens, width), BF16), shaped((tokens, width), F32)
    token_rank, token_lanes = shaped((tokens, RANK), BF16), shaped((tokens, LANES), F32)
    fixed = functools.partial

    qkv, normed = call(
        qkv_kernel, "qkv", "MLLHHH",
        [("V", shaped((seq, tokens, 3 * cols), BF16)), ("S", shaped((tokens, width + LANES), BF16))],
        (adapter_index, x, gain_one, input_weights, down, adapter_up), [triple, three_small, three_small, sema(9)],
    )
    qkv_all = exchange(qkv, "seq").reshape(rows, 3 * cols)

    slot, slot_col, pick, *ids_out = call(
        fixed(route_kernel, rows_dev, owners), "route", "ML",
        [("S", shaped((8, tokens), I32)), ("S", shaped((tokens, tokens), I32)), ("S", shaped((tokens, LANES), I32)),
         *[("V", shaped((seq * 8 + 8, LANES), I32)) for _ in range(batches)]],
        (adapter_index, picks), [pltpu.VMEM((owners * 8, LANES), I32)],
    )
    ids_out = [ids_out[0]] + [along(ids_out[k], "batch", k, batches) for k in range(1, batches)]
    mix_grad, grank_six = call(
        mix_back_kernel, "mixback", "MLHHH", [("S", token_low), ("S", token_rank)],
        (adapter_index, cot, output_weights, down, adapter_up), [matrix, small, small, sema(3)],
    )

    qkv_all, ids_out, mix_grad = lax.optimization_barrier((qkv_all, ids_out, mix_grad))
    attended, lse, slots, qkv_saved = call(
        fixed(attend_kernel, groups, batches), "attend", "MV" + "V" * batches,
        [("V", shaped((seq, tokens + carried, cols), BF16)), ("S", shaped((8, rows), F32)),
         ("S", shaped((batches, 8, LANES), I32)), ("H", shaped((rows, 3 * cols), BF16))],
        (lengths, qkv_all, *ids_out),
        [pltpu.VMEM((rows, LANES), BF16), pltpu.VMEM((LANES, rows), BF16), pltpu.VMEM((LANES, rows), F32), sema(1)],
    )
    o_all = exchange(attended, "seq")
    normed, attended = lax.optimization_barrier((normed, attended))
    normed_all = to_pairs(normed, "seq", seq)

    left, right, same_two, sent, att, rank_pair, middle, normed_two, gate = call(
        middle_kernel, "middle", "MVLLLHHHH",
        [("V", shaped((tokens, half), BF16)), ("V", shaped((tokens, half), BF16)), ("V", token_low),
         ("S", shaped((seq, carried, cols), BF16)), ("S", token_low),
         ("S", shaped((2, tokens, RANK), BF16)), ("S", token_wide), ("S", token_low), ("S", token_wide)],
        (adapter_index, o_all, x, gain_two, mix_grad, input_weights, output_weights, down, adapter_up),
        [pair, two_small, two_small, sema(6)],
    )
    lefts = [left] + [along(left, "batch", k, batches) for k in range(1, batches)]
    weight_out, rank_four, weights = call(
        fixed(scores_kernel, owners), "scores", "MVLLLHHH",
        [("V", shaped((owners * 8, LANES), BF16)), ("S", token_rank), ("S", token_lanes)],
        (adapter_index, same_two, pick, slot, half_keys, input_weights, down, adapter_up), [matrix, small, small, sema(3)],
    )
    weight_out, normed_all = lax.optimization_barrier((weight_out, normed_all))
    weight_in = exchange(weight_out.reshape(owners, 8, LANES), both).reshape(owners * 8, LANES)
    right, lefts = lax.optimization_barrier((right, lefts))
    rights = [right] + [along(right, "batch", k, batches) for k in range(1, batches)]

    def scatter(parts, name):
        out = [("V", shaped((seq, batches, capacity, half), BF16))]
        return call(scatter_kernel, name, "L" + "V" * batches, out, (slots, *parts))[0]

    left_out = scatter(lefts, "scatterleft")
    normed_all, left_out = lax.optimization_barrier((normed_all, left_out))
    normed_all = stacked(normed_all, "pairsnorm", "S")
    sent, left_out = lax.optimization_barrier((sent, left_out))
    ids, index = call(
        fixed(prepare_kernel, groups, rows_dev, batches), "prepare", "L",
        [("S", shaped((owners * 8, LANES), I32)), ("H", shaped((items, rows_dev), jnp.int16))], (sent,),
        [pltpu.VMEM((2, LANES, rows_dev), jnp.int16), pltpu.VMEM((owners * 8 // LANES, LANES, LANES), I32), sema(2)],
    )
    left_out, weight_in, normed_all = lax.optimization_barrier((left_out, weight_in, normed_all))
    normed_all = (normed_all, across(normed_all, "seq", 1, seq))
    left_in = exchange(left_out, "seq").reshape(items, half)

    (sums,) = call(
        fixed(recall_kernel, groups), "recall", "VHH", [("H", shaped((seq, batches, capacity, width), BF16))],
        (weight_in, index, memory_values),
        [pltpu.VMEM((rows_dev, width), BF16), pltpu.VMEM((2, small_block, rows_dev), jnp.int16), pltpu.VMEM((2, small_block, rows_dev), BF16),
         pltpu.VMEM((2, small_block // 8, 8, width), BF16), sema(3 + 2 * (small_block // (8 * seq)))],
        flops=1 << 12,
    )
    sums, left_in = lax.optimization_barrier((sums, left_in))
    back = exchange(sums, "seq")

    def recall_back(part, name, grads, kind, dtype, *before):
        return call(
            fixed(recall_back_kernel, part, batches, groups), name, "L" + "L" * part + "VH",
            [(kind, shaped((owners * 8, LANES), dtype))], (ids, *before, grads, memory_values),
            [pltpu.VMEM((rows_dev, half), BF16), pltpu.VMEM((block, rows_dev), F32), sema(1)],
        )[0]

    rights, normed_all = lax.optimization_barrier((rights, normed_all))
    right_out = scatter(rights, "scatterright")
    found_left = recall_back(0, "recallleft", left_in, "S", F32)
    right_out, back, found_left = lax.optimization_barrier((right_out, back, found_left))
    right_in = exchange(right_out, "seq").reshape(items, half)
    pieces = call(
        gather_kernel, "gather", "LV", [("V", token_low) for _ in range(batches)], (slots, back),
    )
    pieces = [pieces[0]] + [along(pieces[k], "batch", batches - k, batches) for k in range(1, batches)]
    found = recall_back(1, "recallright", right_in, "V", BF16, found_left)
    found_back = exchange(found.reshape(owners, 8, LANES), both).reshape(owners * 8, LANES)

    mixed, grank_five, ggate, part = call(
        fixed(memory_kernel, batches), "memory", "MLL" + "V" * batches + "HHH",
        [("S", token_low), ("S", token_rank), ("S", token_low), ("S", token_wide)],
        (adapter_index, gate, mix_grad, *pieces, input_weights, down, adapter_up), [matrix, small, small, sema(3)],
    )

    go, gquery, grank_pair, gmid = call(
        fixed(query_kernel, owners, rows_dev), "query", "MMVLLLLLLLLHHHH",
        [("V", shaped((seq, tokens, cols), BF16)), ("S", token_low), ("S", shaped((2, tokens, RANK), BF16)), ("S", token_wide)],
        (lengths, adapter_index, found_back, slot_col, picks, weights, part, middle, cot, gain_two, half_keys,
         input_weights, output_weights, down, adapter_up),
        [pair, two_small, two_small, pltpu.VMEM((LANES, tokens), F32), sema(6)],
    )
    go_all = exchange(go, "seq").reshape(rows, cols)
    mixed, go = lax.optimization_barrier((mixed, go))
    output, rank_six = call(
        output_kernel, "output", "MLLHHH", [("S", token_low), ("S", token_rank)],
        (adapter_index, mixed, middle, output_weights, down, adapter_up), [matrix, small, small, sema(3)],
    )
    (factors,) = call(
        factor_kernel, "factors", "L" * 13, [("V", shaped((seq, 8 * RANK, cols), BF16))],
        (att, normed_two, mixed, gmid, gquery, ggate, cot, rank_pair, rank_four, rank_six, grank_pair, grank_five, grank_six),
    )
    factors, go_all = lax.optimization_barrier((factors, go_all))
    early_parts = exchange(factors, "seq")

    grads, up_grads = call(
        attend_back_kernel, "attendback", "MMLVLHHH",
        [("V", shaped((seq, tokens + RANK, 3 * cols), BF16)), ("S", shaped((3 * RANK, cols), BF16))],
        (lengths, adapter_index, qkv_saved, go_all, lse, *normed_all, adapter_up),
        [pltpu.VMEM((rows, LANES), F32), pltpu.VMEM((rows, LANES), F32), pltpu.VMEM((LANES, rows), F32),
         pltpu.VMEM((rows, LANES), BF16), pltpu.VMEM((LANES, rows), BF16), pltpu.VMEM((rows, LANES), BF16),
         pltpu.VMEM((rows, 3 * cols), BF16), pltpu.VMEM((rows, width + LANES), BF16), three_small, sema(3 + seq)],
    )
    grads, early_parts = lax.optimization_barrier((grads, early_parts))
    grads_all = exchange(grads, "seq")
    (some,) = call(sum_kernel, "sumearly", "V", [("V", shaped((8 * RANK, cols), BF16))], (early_parts,))
    some = [some] + [along(some, "batch", k, batches) for k in range(1, batches)]
    some = stacked(some, "stackearly")
    some = to_pairs(some, "seq", seq)
    (late_sum,) = call(late_kernel, "late", "VL", [("V", shaped((6 * RANK, cols), BF16))], (grads_all, up_grads))
    (grad_input,) = call(
        entry_kernel, "entry", "MVLLLHHH", [("S", token_low)],
        (adapter_index, grads_all, x, gain_one, gmid, input_weights, down, adapter_up),
        [triple, three_small, three_small, sema(9)],
    )
    late_sums = [late_sum] + [along(late_sum, "batch", k, batches) for k in range(1, batches)]
    some = stacked(some, "pairsearly")
    late_sums, some, grad_input = lax.optimization_barrier((late_sums, some, grad_input))
    late_all = to_pairs(stacked(late_sums, "stacklate"), "seq", seq)
    some = (some, across(some, "seq", 1, seq))
    full = shaped((7, ADAPTERS, RANK, width), F32)
    grad_down, grad_up = call(
        fixed(spread_kernel, batches), "spread", "LVV", [("H", full), ("H", full)], (ids, *some),
        [pltpu.VMEM((seq, batches, 8 * RANK, cols), BF16), pltpu.VMEM((8, ADAPTERS, RANK, width), F32), sema(seq), sema(8)],
    )
    late_all, grad_down, grad_up = lax.optimization_barrier((late_all, grad_down, grad_up))
    late_all = stacked(late_all, "pairslate")
    late_all = (late_all, across(late_all, "seq", 1, seq))
    grad_down, grad_up = call(
        fixed(last_spread_kernel, batches), "lastspread", "LHHVV", [("H", full), ("H", full)],
        (ids, grad_down, grad_up, *late_all),
        [pltpu.VMEM((seq, batches, 6 * RANK, cols), BF16), pltpu.VMEM((6, ADAPTERS, RANK, width), F32), sema(seq), sema(6)],
        aliases={1: 0, 2: 1},
    )
    return (output[None], grad_input[None], jnp.swapaxes(grad_down, 2, 3), grad_up)


def solution(mesh):
    split = P("batch", "seq", None)
    return jax.shard_map(
        body,
        mesh=mesh,
        in_specs=(
            split, P("batch"), P("batch"), P("batch", "seq", None, None), P(), P(), P(), P(), P(), P(), P(),
            P(("batch", "seq"), None), split,
        ),
        out_specs=(split, split, P(), P()),
        check_vma=False,
    )
```

```python
import functools

import jax
import jax.numpy as jnp
from jax import lax
from jax.experimental import pallas as pl
from jax.experimental.pallas import tpu as pltpu
from jax.sharding import PartitionSpec as P

HEAD_DIM = 64
MHEADS = 4
KHALF = 128
NSUB = 256
PICKS = 32
ADAPTERS = 8
RANK = 16
LANES = 128
ADAPTER_STEP = 4096
QUERY_UNROLL = 8
RECALL_ROWS = 256
EPS = 1e-06
NEG = -1e30
F32 = jnp.float32
BF16 = jnp.bfloat16
I32 = jnp.int32
HBM = pl.BlockSpec(memory_space=pltpu.HBM)
SMEM = pl.BlockSpec(memory_space=pltpu.SMEM)
VMEM = pl.BlockSpec(memory_space=pltpu.VMEM)
MIB = 1 << 20


def product(left, right):
    return lax.dot_general(left, right, (((1,), (0,)), ((), ())), preferred_element_type=F32)


def against(left, right):
    return lax.dot_general(left, right, (((1,), (1,)), ((), ())), preferred_element_type=F32)


def contract(left, right):
    return lax.dot_general(left, right, (((0,), (0,)), ((), ())), preferred_element_type=F32)


def iota(shape, axis):
    return lax.broadcasted_iota(I32, shape, axis)


def short_pick(table, index):
    numbers = lax.GatherDimensionNumbers(
        offset_dims=(), collapsed_slice_dims=(1,), start_index_map=(1,), operand_batching_dims=(0,), start_indices_batching_dims=(0,)
    )
    return lax.gather(table, index[:, :, None], numbers, (1, 1), mode=lax.GatherScatterMode.PROMISE_IN_BOUNDS)


def lane_pick(table, index):
    return jnp.take_along_axis(table, index, axis=1, mode="promise_in_bounds")


def shaped(shape, dtype):
    return jax.ShapeDtypeStruct(shape, dtype)


class Stage:
    def __init__(self, loads, stores):
        self.loads, self.stores = loads, stores
        self.waited, self.begun = set(), set()
        for _, copy in loads:
            copy.start()

    def __call__(self, *refs):
        for at, (ref, copy) in enumerate(self.loads):
            if at not in self.waited and (not refs or any(ref is one for one in refs)):
                self.waited.add(at)
                copy.wait()

    def send(self, *refs):
        for at, (ref, copy) in enumerate(self.stores):
            if at not in self.begun and (not refs or any(ref is one for one in refs)):
                self.begun.add(at)
                copy.start()

    def finish(self):
        self()
        self.send()
        for _, copy in self.stores:
            copy.wait()


def call(kernel, name, ins, outs, args, scratch=(), vmem=40, flops=1 << 12, moved=1 << 12, aliases=None):
    shapes = [(args[i].shape, args[i].dtype) for i, kind in enumerate(ins) if kind == "L"]
    stored = [(out.shape, out.dtype) for kind, out in outs if kind == "S"]
    count_in, count_out, count_user = len(ins), len(outs), len(scratch)

    def wrapped(*refs):
        given, results = list(refs[:count_in]), list(refs[count_in : count_in + count_out])
        rest = list(refs[count_in + count_out :])
        user, buffers = rest[:count_user], rest[count_user:]
        loads, stores = [], []
        for i, kind in enumerate(ins):
            if kind == "L":
                at = len(loads)
                loads.append((buffers[at], pltpu.make_async_copy(given[i], buffers[at], buffers[-1].at[at])))
                given[i] = buffers[at]
        for i, (kind, _) in enumerate(outs):
            if kind == "S":
                at = len(loads) + len(stores)
                stores.append((buffers[at], pltpu.make_async_copy(buffers[at], results[i], buffers[-1].at[at])))
                results[i] = buffers[at]
        stage = Stage(loads, stores)
        kernel(stage, *given, *results, *user)
        stage.finish()

    spaces = {"V": VMEM, "L": HBM, "S": HBM, "H": HBM, "M": SMEM}
    autos = [pltpu.VMEM(*one) for one in shapes + stored]
    args = [
        pltpu.with_memory_space_constraint(one, pltpu.HBM) if kind in "LH" else one
        for kind, one in zip(ins, args, strict=True)
    ]
    return pl.pallas_call(
        wrapped,
        name=name,
        out_shape=[pltpu.HBM(out.shape, out.dtype) if kind in "SH" else out for kind, out in outs],
        in_specs=[spaces[kind] for kind in ins],
        out_specs=[spaces[kind] for kind, _ in outs],
        input_output_aliases=aliases or {},
        scratch_shapes=list(scratch) + autos + ([sema(len(autos))] if autos else []),
        compiler_params=pltpu.CompilerParams(vmem_limit_bytes=vmem * MIB),
        cost_estimate=pl.CostEstimate(flops=flops, bytes_accessed=moved, transcendentals=0),
    )(*args)


def fetch(pairs, sems):
    copies = [
        pltpu.make_async_copy(source, target, sems.at[place])
        for place, (source, target) in enumerate(pairs)
    ]
    for copy in copies:
        copy.start()
    return copies


def sema(count):
    return pltpu.SemaphoreType.DMA((count,))


def gain_row(ref):
    return ref[...].astype(F32).reshape(1, ref.shape[0])


def inverse_norm(values):
    return lax.rsqrt(jnp.mean(values * values, axis=1, keepdims=True) + EPS)


def norm_back(values, inverse, scales, incoming):
    weighted = incoming * scales
    inner = jnp.mean(weighted * values, axis=1, keepdims=True)
    return weighted * inverse - values * inverse * inverse * inverse * inner


def qkv_kernel(ready, adapter, x_ref, gain_ref, w_any, dn_any, up_any, out_ref, norm_ref, w, dn, up, sems):
    groups, tokens, wide = out_ref.shape
    cols = wide // 3
    a = adapter[0]
    copies = fetch(
        [(dn_any.at[j, a], dn.at[pl.ds(RANK * j, RANK)]) for j in range(3)]
        + [(up_any.at[j, a], up.at[pl.ds(RANK * j, RANK)]) for j in range(3)]
        + [(w_any.at[j], w.at[j]) for j in range(3)],
        sems,
    )
    ready()
    x = x_ref[...].astype(F32)
    normed = (x * inverse_norm(x) * gain_row(gain_ref)).astype(BF16)
    width = normed.shape[1]
    norm_ref[:, :width] = normed
    for copy in copies[:6]:
        copy.wait()
    ranks = against(normed, dn[...])
    norm_ref[:, width:] = widen(ranks).astype(BF16)
    ready.send(norm_ref)
    place = iota((tokens, 3 * RANK), 1) // RANK
    for j in range(3):
        own = jnp.where(place == j, ranks, 0.0).astype(BF16)
        extra = product(own, up[...])
        copies[6 + j].wait()
        result = (product(normed, w[j]) + extra).astype(BF16)
        for s in range(groups):
            out_ref[s, :, j * cols : (j + 1) * cols] = result[:, s * cols : (s + 1) * cols]


def mix_back_kernel(ready, adapter, cot_ref, w_any, dn_any, up_any, grad_ref, rank_ref, w, dn, up, sems):
    a = adapter[0]
    copies = fetch([(up_any.at[6, a], up), (dn_any.at[6, a], dn), (w_any.at[1], w)], sems)
    ready()
    gy = cot_ref[...]
    copies[0].wait()
    ranks = against(gy, up[...]).astype(BF16)
    rank_ref[...] = ranks
    copies[1].wait()
    extra = product(ranks, dn[...])
    copies[2].wait()
    grad_ref[...] = (against(gy, w[...]) + extra).astype(BF16)


def route_kernel(rows_dev, owners, ready, adapter, picks_ref, slot_ref, slot_col_ref, pick_ref, *ids_refs):
    ready()
    heads, picks, tokens = picks_ref.shape
    capacity = 2 * heads * tokens // owners
    groups = capacity // 8
    visits = heads * tokens
    owner = jnp.concatenate([picks_ref[h, 0:1, :] for h in range(heads)], axis=1) // rows_dev
    hot = jnp.where(iota((owners, visits), 0) == owner, 1.0, 0.0)
    before = jnp.where(iota((visits, visits), 0) < iota((visits, visits), 1), 1.0, 0.0).astype(BF16)
    counts = product(hot.astype(BF16), before)
    within = jnp.sum(hot * counts, axis=0, keepdims=True).astype(I32)
    slot = owner * capacity + within
    rows = [slot[:, h * tokens : (h + 1) * tokens] for h in range(heads)]
    stacked = jnp.concatenate(rows + [jnp.full((8 - heads, tokens), -1, I32)], axis=0)
    slot_ref[...] = stacked
    tall = jnp.concatenate([stacked, jnp.full((tokens - 8, tokens), -1, I32)], axis=0)
    slot_col_ref[...] = jnp.transpose(tall)
    packed = jnp.concatenate([picks_ref[h] for h in range(heads)], axis=0)
    by_token = jnp.transpose(packed)
    pick_ref[...] = by_token
    local = by_token % rows_dev
    lanes = iota((tokens, LANES), 1)
    total = jnp.zeros((owners * 8, LANES), F32)
    out_lane = iota((owners * 8, LANES), 1) // PICKS
    place = iota((owners * 8, tokens), 0)
    base = (place // 8) * capacity + place % 8
    for g in range(groups):
        high = jnp.zeros((owners * 8, LANES), F32)
        low = jnp.zeros((owners * 8, LANES), F32)
        for h in range(heads):
            chosen = jnp.where(base + g * 8 == rows[h], 1.0, 0.0).astype(BF16)
            own = jnp.where(lanes // PICKS == h, local, 0)
            own = tile_groups(own.astype(F32), heads).astype(I32)
            high = high + product(chosen, (own // 256).astype(F32).astype(BF16))
            low = low + product(chosen, (own % 256).astype(F32).astype(BF16))
        total = jnp.where(out_lane == g, high * 256.0 + low, total)
    batches = len(ids_refs) - 1
    part = owners * 8 // batches
    ids_refs[-1][...] = total.astype(I32) + adapter[0] * ADAPTER_STEP
    for k in range(batches):
        target = lax.rem(lax.axis_index("batch") + k, batches)
        ids_refs[k][0:part, :] = ids_refs[-1][pl.ds(pl.multiple_of(target * part, part), part), :]
        ids_refs[k][part:, :] = stacked


def tile_groups(values, count):
    total = values
    for turn in range(1, count):
        total = total + pltpu.roll(values, turn * PICKS, 1)
    return total


def prepare_kernel(groups, rows_dev, batches, ready, sent_ref, ids_ref, index_any, stage, turned, sems):
    ready()
    seq, _, cols = sent_ref.shape
    lanes = groups * PICKS
    chunks = 2 * lanes // cols
    for k in range(batches):
        source = lax.rem(lax.axis_index("batch") + (batches - k), batches)
        for s in range(seq):
            both = [
                sent_ref[s, (chunk * batches + k) * 8 : (chunk * batches + k + 1) * 8, :].astype(F32)
                for chunk in range(chunks)
            ]
            both = jnp.concatenate(both, axis=1).astype(I32)
            ids = widen(both[:, :lanes] * 256 + both[:, lanes:])
            ids_ref[pl.ds(pl.multiple_of((source * seq + s) * 8, 8), 8), :] = ids
    ready.send(ids_ref)
    places = ids_ref.shape[0]
    chunks = rows_dev // LANES
    high_rows = max(8, chunks)
    steps = groups * (places // LANES)
    for k in range(places // LANES):
        turned[k] = jnp.transpose(ids_ref[k * LANES : (k + 1) * LANES, :] & (ADAPTER_STEP - 1))

    def put(step, slot):
        target = index_any.at[pl.ds(pl.multiple_of(step * LANES, LANES), LANES)]
        return pltpu.make_async_copy(stage.at[slot], target, sems.at[slot])

    def one(step, carry):
        k, g = lax.rem(step, places // LANES), step // (places // LANES)
        slot = lax.rem(step, 2)
        mask = jnp.zeros((LANES, LANES), I32)
        highs = jnp.zeros((high_rows, LANES), I32)
        for r in range(PICKS):
            bit = (1 << r) if r < 31 else -(1 << 31)
            row = turned[k, pl.ds(g * PICKS + r, 1), :]
            mask = mask | jnp.where(row & 127 == iota((LANES, LANES), 0), bit, 0)
            highs = highs | jnp.where(row >> 7 == iota((high_rows, LANES), 0), bit, 0)

        @pl.when(step >= 2)
        def _():
            put(step - 2, slot).wait()

        for c in range(chunks):
            index = 31 - lax.clz(mask & highs[c : c + 1, :])
            stage[slot, :, c * LANES : (c + 1) * LANES] = jnp.transpose(index.astype(jnp.int16))
        put(step, slot).start()
        return carry

    lax.fori_loop(0, steps, one, 0)
    for step in range(max(0, steps - 2), steps):
        put(step, step % 2).wait()


def recall_kernel(groups, ready, weight_ref, index_any, mem_any, out_any, mem, index, dense, staged, sems):
    places = weight_ref.shape[0]
    rows_dev = mem.shape[0]
    chunks = rows_dev // LANES
    block = dense.shape[1]
    per_group = places // block
    blocks = groups * per_group
    seq = out_any.shape[0]
    planes = block // (8 * seq)

    def load(b, slot):
        source = index_any.at[pl.ds(pl.multiple_of(b * block, block), block)]
        return pltpu.make_async_copy(source, index.at[slot], sems.at[1 + slot])

    load(0, 0).start()
    copy = pltpu.make_async_copy(mem_any, mem, sems.at[0])
    copy.start()

    def gather(b, side):
        load(b, side).wait()

        @pl.when(b + 1 < blocks)
        def _():
            load(b + 1, 1 - side).start()

        pick(b, side)

    def pick(b, side):
        g, k = b // per_group, lax.rem(b, per_group)
        for start in range(0, block, 16):
            weights = weight_ref[pl.ds(pl.multiple_of(k * block + start, 16), 16), :]
            shift = jnp.full((16, LANES), g * PICKS, I32).astype(jnp.int16)
            for c in range(chunks):
                at = index[side, start : start + 16, c * LANES : (c + 1) * LANES]
                value = short_pick(weights, (at + shift) & jnp.int16(127))
                dense[side, start : start + 16, c * LANES : (c + 1) * LANES] = jnp.where(at >= 0, value, jnp.zeros((), BF16))

    def save(b, side):
        g, k = b // per_group, lax.rem(b, per_group)
        return [
            pltpu.make_async_copy(
                staged.at[side, pl.ds(i * seq, seq)],
                out_any.at[:, k * planes + i, pl.ds(pl.multiple_of(g * 8, 8), 8), :],
                sems.at[3 + side * planes + i],
            )
            for i in range(planes)
        ]

    def multiply(b, side):
        result = product(dense[side], mem[...]).astype(BF16)

        @pl.when(b >= 2)
        def _():
            for one in save(b - 2, side):
                one.wait()

        staged[side] = result.reshape(block // 8, 8, result.shape[1])
        for one in save(b, side):
            one.start()

    gather(0, 0)
    copy.wait()

    def whole(i, carry):
        gather(2 * i + 1, 1)
        multiply(2 * i, 0)

        @pl.when(2 * i + 2 < blocks)
        def _():
            load(2 * i + 2, 0).wait()
            load(2 * i + 3, 1).start()

        pick(jnp.minimum(2 * i + 2, blocks - 1), 0)
        multiply(2 * i + 1, 1)
        return carry

    lax.fori_loop(0, blocks // 2, whole, 0)
    for b in range(blocks - 2, blocks):
        for one in save(b, b % 2):
            one.wait()


def recall_back_kernel(part, batches, groups, ready, ids_ref, *refs):
    before_ref = refs[0] if part else None
    grad_ref, mem_any, out_ref, mem, scores, sems = refs[part:]
    items, half = grad_ref.shape
    seq = items // (batches * groups * 8)
    rows_dev = mem.shape[0]
    capacity = groups * 8
    chunks = rows_dev // LANES
    block = scores.shape[0]
    per_block = block // capacity
    blocks = items // block
    copies = fetch([(mem_any.at[:, pl.ds(part * half, half)], mem)], sems)
    ready()
    copies[0].wait()

    def whole(b, outer):
        scores[...] = against(grad_ref[pl.ds(pl.multiple_of(b * block, block), block), :], mem[...])

        lane_group = iota((8, LANES), 1) // PICKS
        for local in range(per_block):
            sender = b * per_block + local
            spot = lax.rem(sender, batches) * seq + sender // batches
            start = pl.multiple_of(spot * 8, 8)
            ids = ids_ref[pl.ds(start, 8), :] & (ADAPTER_STEP - 1)
            low = ids & 127
            high = ids >> 7
            total = before_ref[pl.ds(start, 8), :] if part else jnp.zeros((8, LANES), F32)
            for g in range(groups):
                key = jnp.where(lane_group == g, high, -1)
                here = jnp.zeros((8, LANES), F32)
                row = local * capacity + g * 8
                for c in range(chunks):
                    found = scores[row : row + 8, c * LANES : (c + 1) * LANES]
                    here = jnp.where(key == c, lane_pick(found, low), here)
                total = total + here
            out_ref[pl.ds(start, 8), :] = total.astype(out_ref.dtype)
        return outer

    lax.fori_loop(0, blocks, whole, 0)


def head_parts(values, h, spare):
    lane = iota(values.shape, 1)
    return jnp.where(lane // HEAD_DIM == h, values, jnp.where(lane == (1 - h) * HEAD_DIM, spare, 0.0)).astype(BF16)


def widen(values):
    if values.shape[1] == LANES:
        return values
    return jnp.concatenate([values, jnp.zeros((values.shape[0], LANES - values.shape[1]), values.dtype)], axis=1)


def attend_kernel(groups, batches, ready, length, qkv_ref, *refs):
    o_ref, lse_ref, slots_ref, saved_any, parts, values_t, mixed, sems = refs[batches:]
    ready()
    saving = pltpu.make_async_copy(qkv_ref, saved_any, sems.at[0])
    saving.start()
    rows, wide = qkv_ref.shape
    cols = wide // 3
    seq = o_ref.shape[0]
    lanes = groups * PICKS
    for k in range(batches):
        slots_ref[k] = refs[k][seq * 8 :, :]
    ready.send(slots_ref)
    for s in range(seq):
        ids = jnp.concatenate([refs[k][s * 8 : (s + 1) * 8, :lanes] for k in range(batches)], axis=0)
        both = jnp.concatenate([ids // 256, ids % 256], axis=1).astype(F32).astype(BF16)
        for chunk in range(2 * lanes // cols):
            start = rows // seq + chunk * batches * 8
            o_ref[s, start : start + batches * 8, :] = both[:, chunk * cols : (chunk + 1) * cols]
    heads = cols // HEAD_DIM
    size = min(256, rows)
    valid = length[0]
    bias = jnp.where(iota((rows, LANES), 0) < valid, 0.0, NEG)
    keys = widen(qkv_ref[:, cols : 2 * cols].astype(F32))
    values_t[...] = jnp.transpose(widen(qkv_ref[:, 2 * cols :].astype(F32))).astype(BF16)
    lse_ref[...] = jnp.zeros_like(lse_ref)

    def one(h, carry):
        parts[...] = head_parts(keys, h, bias)
        for i in range(rows // size):
            first, last = i * size, (i + 1) * size
            queries = widen(qkv_ref[first:last, 0:cols].astype(F32)) * (HEAD_DIM**-0.5)
            query = head_parts(queries, h, 1.0)
            near = against(parts[first:last], query)
            near = jnp.where(iota((size, size), 0) <= iota((size, size), 1), near, NEG)
            high = jnp.max(near, axis=0, keepdims=True)
            if i:
                far = against(parts[:first], query)
                high = jnp.maximum(high, jnp.max(far, axis=0, keepdims=True))
            near = jnp.exp(near - high)
            summed = jnp.sum(near, axis=0, keepdims=True)
            result = product(values_t[:, first:last], near.astype(BF16))
            if i:
                far = jnp.exp(far - high)
                summed = summed + jnp.sum(far, axis=0, keepdims=True)
                result = result + product(values_t[:, :first], far.astype(BF16))
            lse_ref[pl.ds(h, 1), first:last] = high + jnp.log(summed)
            own = iota((LANES, size), 0) // HEAD_DIM == h
            mixed[:, first:last] = jnp.where(own, result / summed, mixed[:, first:last])
        return carry

    mixed[...] = jnp.zeros_like(mixed)
    lax.fori_loop(0, heads, one, 0)
    ready.send(lse_ref)
    tokens = rows // seq
    for s in range(seq):
        first = s * tokens
        kept = jnp.where(first + iota((LANES, tokens), 1) < valid, mixed[:, first : first + tokens], 0.0)
        o_ref[s, 0:tokens, :] = jnp.transpose(kept)[:, :cols].astype(BF16)
    saving.wait()


def attend_back_kernel(
    ready, length, adapter, qkv_ref, go_ref, lse_ref, even_ref, odd_ref, up_any,
    out_ref, upgrad_ref, dk, dv, dq, parts, keys_t, values, grads_all, norms, up, sems,
):
    a = adapter[0]
    seq = out_ref.shape[0]
    me = lax.axis_index("seq")
    tokens = even_ref.shape[1]
    copies = fetch(
        [(up_any.at[j, a], up.at[pl.ds(RANK * j, RANK)]) for j in range(3)]
        + [
            ((even_ref, odd_ref)[m % 2].at[m // 2], norms.at[pl.ds(pl.multiple_of((me ^ m) * tokens, tokens), tokens)])
            for m in range(seq)
        ],
        sems,
    )
    ready()
    rows, wide = qkv_ref.shape
    cols = wide // 3
    heads = cols // HEAD_DIM
    size = min(256, rows)
    valid = length[0]
    scaling = HEAD_DIM**-0.5
    bias = jnp.where(iota((rows, LANES), 0) < valid, 0.0, NEG)
    keys = widen(qkv_ref[:, cols : 2 * cols].astype(F32))
    keys_t[...] = jnp.transpose(keys).astype(BF16)
    values[...] = widen(qkv_ref[:, 2 * cols :])
    dk[...] = jnp.zeros_like(dk)
    dv[...] = jnp.zeros_like(dv)
    dq[...] = jnp.zeros_like(dq)

    def one(h, carry):
        parts[...] = head_parts(keys, h, bias)
        for i in range(rows // size):
            first, last = i * size, (i + 1) * size
            queries = widen(qkv_ref[first:last, 0:cols].astype(F32)) * scaling
            grads = widen(go_ref[first:last, :].astype(F32))
            query = head_parts(queries, h, 1.0)
            plain = head_parts(queries, h, 0.0)
            grad = head_parts(grads, h, 0.0)
            lse = lse_ref[pl.ds(h, 1), first:last]
            near = against(parts[first:last], query)
            near = jnp.where(iota((size, size), 0) <= iota((size, size), 1), near, NEG)
            near = jnp.exp(near - lse)
            near_gp = against(values[first:last], grad)
            delta = jnp.sum(near * near_gp, axis=0, keepdims=True)
            if i:
                far = jnp.exp(against(parts[:first], query) - lse)
                far_gp = against(values[:first], grad)
                delta = delta + jnp.sum(far * far_gp, axis=0, keepdims=True)
            near_gs = (near * (near_gp - delta)).astype(BF16)
            result = product(keys_t[:, first:last], near_gs)
            dk[first:last] += product(near_gs, plain)
            dv[first:last] += product(near.astype(BF16), grad)
            if i:
                far_gs = (far * (far_gp - delta)).astype(BF16)
                result = result + product(keys_t[:, :first], far_gs)
                dk[:first] += product(far_gs, plain)
                dv[:first] += product(far.astype(BF16), grad)
            own = iota((LANES, size), 0) // HEAD_DIM == h
            dq[:, first:last] = jnp.where(own, result, dq[:, first:last])
        return carry

    lax.fori_loop(0, heads, one, 0)
    grads_all[:, 0:cols] = (jnp.transpose(dq[...]) * scaling)[:, :cols].astype(BF16)
    grads_all[:, cols : 2 * cols] = dk[:, :cols].astype(BF16)
    grads_all[:, 2 * cols :] = dv[:, :cols].astype(BF16)
    for s in range(seq):
        out_ref[s, 0:tokens, :] = grads_all[s * tokens : (s + 1) * tokens, :]
    for copy in copies:
        copy.wait()
    own = jnp.zeros((3 * RANK, cols), F32)
    for s in range(seq):
        own = jnp.where(me == s, up[:, s * cols : (s + 1) * cols].astype(F32), own)
    own = own.astype(BF16)
    place = iota((rows, 3 * RANK), 1) // RANK
    granks = jnp.zeros((rows, 3 * RANK), F32)
    for j in range(3):
        granks = jnp.where(place == j, against(grads_all[:, j * cols : (j + 1) * cols], own), granks)
    width = norms.shape[1] - LANES
    down = contract(granks.astype(BF16), norms[:, :width]).astype(BF16)
    both = contract(norms[:, width:], grads_all[...]).astype(BF16)
    for j in range(3):
        row = j * RANK
        upgrad_ref[row : row + RANK, :] = both[row : row + RANK, j * cols : (j + 1) * cols]
        for s in range(seq):
            out_ref[s, tokens:, j * cols : (j + 1) * cols] = down[row : row + RANK, s * cols : (s + 1) * cols]


def pick_chosen(tables, index):
    tokens = index.shape[0]
    low = index & 127
    key = (index >> 7) + (iota((tokens, LANES), 1) // PICKS) * (NSUB // LANES)
    total = jnp.zeros((tokens, LANES), F32)
    for h in range(MHEADS):
        for c in range(NSUB // LANES):
            found = lane_pick(tables[h][:, c * LANES : (c + 1) * LANES], low)
            total = jnp.where(key == h * (NSUB // LANES) + c, found, total)
    return total


def group_reduce(values, reducer, fill):
    group = iota(values.shape, 1) // PICKS
    total = jnp.zeros(values.shape, F32)
    for h in range(MHEADS):
        one = reducer(jnp.where(group == h, values, fill), axis=1, keepdims=True)
        total = jnp.where(group == h, one, total)
    return total


def middle_kernel(
    ready, adapter, o_ref, x_ref, gain_ref, mix_ref, w_in_any, w_out_any, dn_any, up_any,
    left_ref, right_ref, same_ref, ahead_ref, sent_ref, att_ref, rank_ref, mid_ref, norm_ref, gate_ref, w, dn, up, sems,
):
    groups = o_ref.shape[0]
    a = adapter[0]
    copies = fetch(
        [(dn_any.at[3, a], dn.at[0]), (dn_any.at[5, a], dn.at[1]), (up_any.at[3, a], up.at[0]), (up_any.at[5, a], up.at[1]),
         (w_out_any.at[0], w.at[0]), (w_in_any.at[4], w.at[1]), (w_in_any.at[3], ahead_ref)],
        sems,
    )
    tokens = att_ref.shape[0]
    attended = jnp.concatenate([o_ref[s, 0:tokens, :] for s in range(groups)], axis=1)
    sent_ref[...] = o_ref[:, tokens:, :]
    ready.send(sent_ref)
    att_ref[...] = attended
    ready.send(att_ref)
    for copy in copies[:4]:
        copy.wait()
    rank_three = against(attended, dn[0]).astype(BF16)
    extra = product(rank_three, up[0])
    copies[4].wait()
    ready(x_ref, gain_ref)
    middle = x_ref[...].astype(F32) + (product(attended, w[0]) + extra)
    mid_ref[...] = middle
    normed = (middle * inverse_norm(middle) * gain_row(gain_ref)).astype(BF16)
    norm_ref[...] = normed
    same_ref[...] = normed
    ready.send(mid_ref, norm_ref)
    rank_five = against(normed, dn[1]).astype(BF16)
    rank_ref[0] = rank_three
    rank_ref[1] = rank_five
    extra = product(rank_five, up[1])
    copies[5].wait()
    gate = product(normed, w[1]) + extra
    gate_ref[...] = gate
    ready.send(rank_ref, gate_ref)
    ready(mix_ref)
    memory_grad = (mix_ref[...].astype(F32) * (gate * jax.nn.sigmoid(gate))).astype(BF16)
    half = left_ref.shape[1]
    left_ref[...] = memory_grad[:, :half]
    right_ref[...] = memory_grad[:, half:]
    copies[6].wait()


def scores_kernel(
    owners, ready, adapter, normed_ref, w_ref, picks_ref, slot_ref, keys_ref, dn_any, up_any,
    send_ref, rank_ref, weight_ref, dn, up, sems,
):
    a = adapter[0]
    copies = fetch([(dn_any.at[4, a], dn), (up_any.at[4, a], up)], sems)
    normed = normed_ref[...]
    copies[0].wait()
    ranks = against(normed, dn[...]).astype(BF16)
    rank_ref[...] = ranks
    copies[1].wait()
    extra = product(ranks, up[...])
    query = (product(normed, w_ref[...]) + extra).astype(BF16)
    ready()
    ready.send(rank_ref)
    first, second = [], []
    for h in range(MHEADS):
        base = 2 * h * KHALF
        first.append(against(query[:, base : base + KHALF], keys_ref[0, h]))
        second.append(against(query[:, base + KHALF : base + 2 * KHALF], keys_ref[1, h]))
    picks = picks_ref[...]
    scores = pick_chosen(first, picks // NSUB) + pick_chosen(second, picks % NSUB)
    exponent = jnp.exp(scores - group_reduce(scores, jnp.max, NEG))
    weights = exponent / group_reduce(exponent, jnp.sum, 0.0)
    weight_ref[...] = weights
    ready.send(weight_ref)
    send_ref[...] = to_slots(weights, slot_ref, owners).astype(BF16)


def to_slots(weights, slot_ref, owners):
    tokens = weights.shape[0]
    capacity = 2 * MHEADS * tokens // owners
    lane_group = iota((tokens, LANES), 1) // PICKS
    tiled = [
        tile_groups(jnp.where(lane_group == h, weights, 0.0), MHEADS).astype(BF16) for h in range(MHEADS)
    ]
    place = iota((owners * 8, tokens), 0)
    base = (place // 8) * capacity + place % 8
    out_group = iota((owners * 8, LANES), 1) // PICKS
    total = jnp.zeros((owners * 8, LANES), F32)
    for g in range(capacity // 8):
        part = jnp.zeros((owners * 8, LANES), F32)
        for h in range(MHEADS):
            chosen = jnp.where(base + g * 8 == slot_ref[h : h + 1, :], 1.0, 0.0).astype(BF16)
            part = part + product(chosen, tiled[h])
        total = jnp.where(out_group == g, part, total)
    return total


def plane_hits(slots_ref, k, plane, seq, capacity):
    tokens = slots_ref.shape[2]
    place = plane * (seq * capacity) + iota((seq * capacity, tokens), 0)
    chosen = jnp.zeros((seq * capacity, tokens), F32)
    for h in range(MHEADS):
        chosen = jnp.where(place == slots_ref[k, h : h + 1, :], 1.0, chosen)
    return chosen.astype(BF16)


def scatter_kernel(ready, slots_ref, *refs):
    ready()
    out_ref = refs[-1]
    seq, batches, capacity, wide = out_ref.shape
    plane = lax.axis_index("batch")
    for k in range(batches):
        chosen = plane_hits(slots_ref, k, plane, seq, capacity)
        rows = product(chosen, refs[k][...]).astype(BF16)
        source = lax.rem(plane + (batches - k), batches)
        out_ref[:, pl.ds(source, 1)] = rows.reshape(seq, 1, capacity, wide)


def gather_kernel(ready, slots_ref, back_ref, *refs):
    ready()
    seq, batches, capacity, wide = back_ref.shape
    plane = lax.axis_index("batch")
    for k in range(batches):
        chosen = plane_hits(slots_ref, k, plane, seq, capacity)
        source = lax.rem(plane + (batches - k), batches)
        rows = back_ref[:, pl.ds(source, 1)].reshape(seq * capacity, wide)
        refs[k][...] = contract(chosen, rows).astype(BF16)


def memory_kernel(batches, ready, adapter, gate_ref, mix_ref, *refs):
    w_in_any, dn_any, up_any, mixed_ref, grank_ref, ggate_ref, part_ref, w, dn, up, sems = refs[batches:]
    a = adapter[0]
    copies = fetch([(dn_any.at[5, a], dn), (up_any.at[5, a], up), (w_in_any.at[4], w)], sems)
    ready()
    memory = refs[0][...].astype(F32)
    for k in range(1, batches):
        memory = memory + refs[k][...].astype(F32)
    gate = gate_ref[...]
    sigmoid = jax.nn.sigmoid(gate)
    mixed_ref[...] = (memory * (gate * sigmoid)).astype(BF16)
    ggate = (mix_ref[...].astype(F32) * memory * sigmoid * (1.0 + gate * (1.0 - sigmoid))).astype(BF16)
    ggate_ref[...] = ggate
    for copy in copies[:2]:
        copy.wait()
    granks = against(ggate, up[...]).astype(BF16)
    grank_ref[...] = granks
    extra = product(granks, dn[...])
    copies[2].wait()
    ready.send(mixed_ref, ggate_ref, grank_ref)
    part_ref[...] = against(ggate, w[...]) + extra


def output_kernel(ready, adapter, mixed_ref, mid_ref, w_out_any, dn_any, up_any, out_ref, rank_ref, w, dn, up, sems):
    a = adapter[0]
    copies = fetch([(dn_any.at[6, a], dn), (up_any.at[6, a], up), (w_out_any.at[1], w)], sems)
    ready()
    mixed = mixed_ref[...]
    for copy in copies[:2]:
        copy.wait()
    ranks = against(mixed, dn[...]).astype(BF16)
    rank_ref[...] = ranks
    extra = product(ranks, up[...])
    copies[2].wait()
    out_ref[...] = (mid_ref[...] + (product(mixed, w[...]) + extra)).astype(BF16)


def query_kernel(
    owners, rows_dev, ready, length, adapter, back_ref, slot_ref, picks_ref, weight_ref, part_ref, mid_ref, cot_ref, gain_ref,
    keys_ref, w_in_any, w_out_any, dn_any, up_any,
    go_ref, gquery_ref, grank_ref, gmid_ref, w, dn, up, turned, sems,
):
    groups, tokens, cols = go_ref.shape
    a = adapter[0]
    copies = fetch(
        [(dn_any.at[3, a], dn.at[0]), (dn_any.at[4, a], dn.at[1]), (up_any.at[3, a], up.at[0]),
         (up_any.at[4, a], up.at[1]), (w_in_any.at[3], w.at[0]), (w_out_any.at[0], w.at[1])],
        sems,
    )
    ready(slot_ref, weight_ref)
    capacity = 2 * MHEADS * tokens // owners
    slots = iota((tokens, owners * 8), 1)
    base = (slots // 8) * capacity + slots % 8
    lane_group = iota((tokens, LANES), 1) // PICKS
    back = back_ref[...]
    gw = jnp.zeros((tokens, LANES), F32)
    for h in range(MHEADS):
        part = jnp.zeros((tokens, LANES), F32)
        for g in range(capacity // 8):
            chosen = jnp.where(base + g * 8 == slot_ref[:, h : h + 1], 1.0, 0.0).astype(BF16)
            part = jnp.where(lane_group == g, product(chosen, back), part)
        gw = jnp.where(lane_group == h, tile_groups(part, MHEADS), gw)
    weights = weight_ref[...]
    gscore = jnp.transpose(weights * (gw - group_reduce(weights * gw, jnp.sum, 0.0)))
    turned[...] = gscore
    ready(picks_ref, keys_ref)
    span = rows_dev // NSUB

    def head(h, carry):
        def one(r, sums):
            pick = picks_ref[h, pl.ds(r, 1), :]
            value = turned[pl.ds(h * PICKS + r, 1), :]
            low = jnp.where((pick // NSUB) % span == iota((8, tokens), 0), value, 0.0)
            hit = (pick % NSUB).astype(jnp.int16) == lax.broadcasted_iota(jnp.int16, (NSUB, tokens), 0)
            return sums[0] + low, sums[1] + jnp.where(hit, value.astype(BF16), jnp.zeros((), BF16))

        start = (jnp.zeros((8, tokens), F32), jnp.zeros((NSUB, tokens), BF16))
        first, second = lax.fori_loop(0, PICKS, one, start, unroll=QUERY_UNROLL)
        origin = picks_ref[h, 0:1, :] // rows_dev
        place = iota((NSUB, tokens), 0)
        wide = jnp.concatenate([first[:span]] * (NSUB // span), axis=0)
        wide = jnp.where(place // span == origin, wide, 0.0)
        at = pl.multiple_of(h * 2 * KHALF, 2 * KHALF)
        gquery_ref[:, pl.ds(at, KHALF)] = contract(wide.astype(BF16), keys_ref[0, h]).astype(BF16)
        gquery_ref[:, pl.ds(at + KHALF, KHALF)] = contract(second, keys_ref[1, h]).astype(BF16)
        return carry

    lax.fori_loop(0, MHEADS, head, 0)
    gquery = gquery_ref[...]
    ready.send(gquery_ref)
    ready()
    for copy in copies[:4]:
        copy.wait()
    granks = against(gquery, up[1]).astype(BF16)
    grank_ref[1] = granks
    extra = product(granks, dn[1])
    copies[4].wait()
    gnormed = against(gquery, w[0]) + extra + part_ref[...]
    middle = mid_ref[...]
    gmid = cot_ref[...].astype(F32) + norm_back(middle, inverse_norm(middle), gain_row(gain_ref), gnormed)
    gmid_ref[...] = gmid
    ready.send(gmid_ref)
    low = gmid.astype(BF16)
    granks = against(low, up[0]).astype(BF16)
    grank_ref[0] = granks
    ready.send(grank_ref)
    extra = product(granks, dn[0])
    copies[5].wait()
    go = against(low, w[1]) + extra
    row = lax.axis_index("seq") * tokens + iota((tokens, 1), 0)
    go = jnp.where(row < length[0], go, 0.0).astype(BF16)
    for s in range(groups):
        go_ref[s] = go[:, s * cols : (s + 1) * cols]


def place_columns(out_ref, row, values):
    groups, _, cols = out_ref.shape
    low = values.astype(BF16)
    for s in range(groups):
        out_ref[s, row : row + values.shape[0], :] = low[:, s * cols : (s + 1) * cols]


def factor_kernel(ready, att_ref, norm_ref, mixed_ref, gmid_ref, gquery_ref, ggate_ref, cot_ref, r35, r4, r6, g34, g5, g6, out_ref):
    ready()
    half = 4 * RANK
    sides = (
        (att_ref[...], gmid_ref[...].astype(BF16), r35[0], g34[0]),
        (norm_ref[...], gquery_ref[...], r4[...], g34[1]),
        (norm_ref[...], ggate_ref[...], r35[1], g5[...]),
        (mixed_ref[...], cot_ref[...], r6[...], g6[...]),
    )
    for j, (value, gy, rank, grank) in enumerate(sides):
        place_columns(out_ref, j * RANK, contract(grank, value))
        place_columns(out_ref, half + j * RANK, contract(rank, gy))


def late_kernel(ready, grads_ref, upgrad_ref, out_ref):
    seq, _, wide = grads_ref.shape
    cols = wide // 3
    tokens = grads_ref.shape[1] - RANK
    total = grads_ref[0, tokens:, :].astype(F32)
    for s in range(1, seq):
        total = total + grads_ref[s, tokens:, :].astype(F32)
    total = total.astype(BF16)
    for j in range(3):
        out_ref[j * RANK : (j + 1) * RANK, :] = total[:, j * cols : (j + 1) * cols]
    ready()
    out_ref[3 * RANK :, :] = upgrad_ref[...]


def entry_kernel(ready, adapter, grads_ref, x_ref, gain_ref, gmid_ref, w_any, dn_any, up_any, out_ref, w, gy, total, dn, up, sems):
    a = adapter[0]
    seq, _, wide = grads_ref.shape
    cols = wide // 3
    tokens = out_ref.shape[0]
    copies = fetch(
        [(up_any.at[j, a], up.at[pl.ds(RANK * j, RANK)]) for j in range(3)]
        + [(dn_any.at[j, a], dn.at[pl.ds(RANK * j, RANK)]) for j in range(3)]
        + [(w_any.at[j], w.at[j]) for j in range(3)],
        sems,
    )
    for j in range(3):
        for s in range(seq):
            gy[j, :, s * cols : (s + 1) * cols] = grads_ref[s, 0:tokens, j * cols : (j + 1) * cols]
    for copy in copies[:6]:
        copy.wait()
    place = iota((tokens, 3 * RANK), 1) // RANK
    granks = jnp.zeros((tokens, 3 * RANK), F32)
    for j in range(3):
        granks = jnp.where(place == j, against(gy[j], up[...]), granks)
    total[...] = product(granks.astype(BF16), dn[...])

    def one(j, carry):
        pltpu.make_async_copy(w_any.at[j], w.at[j], sems.at[6 + j]).wait()
        total[...] += against(gy[j], w[j])
        return carry

    lax.fori_loop(0, 3, one, 0)
    ready()
    x = x_ref[...].astype(F32)
    back = norm_back(x, inverse_norm(x), gain_row(gain_ref), total[...])
    out_ref[...] = (gmid_ref[...] + back).astype(BF16)


def sum_kernel(ready, parts_ref, out_ref):
    ready()
    total = parts_ref[0].astype(F32)
    for s in range(1, parts_ref.shape[0]):
        total = total + parts_ref[s].astype(F32)
    out_ref[...] = total.astype(BF16)


def stack_kernel(ready, *refs):
    for k in range(refs[-1].shape[0]):
        refs[-1][k] = refs[k][...]


def relative_marks(ids_ref, batches):
    plane = lax.axis_index("batch")
    absolute = adapter_marks(ids_ref, batches)
    marks = []
    for k in range(batches):
        source = lax.rem(plane + (batches - k), batches)
        mark = absolute[0]
        for b in range(1, batches):
            mark = jnp.where(source == b, absolute[b], mark)
        marks.append(mark)
    return marks


def adapter_marks(ids_ref, batches):
    step = ids_ref.shape[0] // batches
    return [ids_ref[b * step : b * step + 1, 0:1] // ADAPTER_STEP for b in range(batches)]


def spread_rows(parts, marks, runs, stage, sems):
    seq, batches = parts.shape[:2]
    for target, origin, base, count in runs:

        def put(i, target=target, origin=origin, base=base):
            return pltpu.make_async_copy(stage.at[base + i], target.at[origin + i], sems.at[base + i])

        def one(i, carry, put=put, base=base):
            start = pl.multiple_of((base + i) * RANK, RANK)
            rows = [
                jnp.concatenate([parts[s, k, pl.ds(start, RANK), :] for s in range(seq)], axis=1).astype(F32)
                for k in range(batches)
            ]
            for k in range(ADAPTERS):
                total = jnp.zeros(rows[0].shape, F32)
                for row, mark in zip(rows, marks, strict=True):
                    total = total + jnp.where(mark == k, row, 0.0)
                stage[base + i, k] = total
            put(i).start()
            return carry

        lax.fori_loop(0, count, one, 0)
    for target, origin, base, count in runs:
        for i in range(count):
            pltpu.make_async_copy(stage.at[base + i], target.at[origin + i], sems.at[base + i]).wait()


def spread_kernel(batches, ready, ids_ref, *refs):
    down_any, up_any, parts, stage, load_sems, sems = refs[-6:]
    seq = parts.shape[0]
    me = lax.axis_index("seq")
    copies = fetch([(refs[m % 2].at[m // 2], parts.at[me ^ m]) for m in range(seq)], load_sems)
    ready()
    marks = relative_marks(ids_ref, batches)
    for copy in copies:
        copy.wait()
    spread_rows(parts, marks, ((down_any, 3, 0, 4), (up_any, 3, 4, 4)), stage, sems)


def last_spread_kernel(batches, ready, ids_ref, down_in, up_in, *refs):
    down_any, up_any, parts, stage, load_sems, sems = refs[-6:]
    seq = parts.shape[0]
    me = lax.axis_index("seq")
    copies = fetch([(refs[m % 2].at[m // 2], parts.at[me ^ m]) for m in range(seq)], load_sems)
    ready()
    marks = relative_marks(ids_ref, batches)
    for copy in copies:
        copy.wait()
    spread_rows(parts, marks, ((down_any, 0, 0, 3), (up_any, 0, 3, 3)), stage, sems)


def along(values, axis, step, size):
    return lax.ppermute(values, axis, [(i, (i + step) % size) for i in range(size)])


def across(values, axis, mask, size):
    return lax.ppermute(values, axis, [(i, i ^ mask) for i in range(size)])


def to_pairs(values, axis, size):
    return [values] + [across(values, axis, m, size) for m in range(2, size, 2)]


def stacked(values, name, kind="V"):
    shape = shaped((len(values), *values[0].shape), values[0].dtype)
    return call(stack_kernel, name, "V" * len(values), [(kind, shape)], values)[0]


def exchange(values, axes):
    return lax.all_to_all(values, axes, split_axis=0, concat_axis=0, tiled=True)


def body(
    inputs, lengths, adapter_index, memory_picks, input_weights, output_weights, adapter_down, adapter_up,
    attention_gain, memory_gain, half_keys, memory_values, cotangent,
):
    both = ("batch", "seq")
    batches, seq = lax.axis_size("batch"), lax.axis_size("seq")
    owners = batches * seq
    tokens, width = inputs.shape[1], inputs.shape[2]
    rows, cols, half = tokens * seq, width // seq, width // 2
    rows_dev = memory_values.shape[0]
    capacity = 2 * tokens * MHEADS // owners
    groups = capacity // 8
    items = owners * capacity
    block = min(owners * 8, 256)
    small_block = RECALL_ROWS
    carried = 2 * groups * PICKS // cols * batches * 8
    x, cot = inputs[0], cotangent[0]
    down = jnp.swapaxes(adapter_down, 2, 3)
    gain_one, gain_two = attention_gain, memory_gain
    picks = jnp.transpose(memory_picks[0], (1, 2, 0))
    matrix = pltpu.VMEM((width, width), BF16)
    pair = pltpu.VMEM((2, width, width), BF16)
    triple = pltpu.VMEM((3, width, width), BF16)
    small = pltpu.VMEM((RANK, width), BF16)
    two_small = pltpu.VMEM((2, RANK, width), BF16)
    three_small = pltpu.VMEM((3 * RANK, width), BF16)
    token_low, token_wide = shaped((tokens, width), BF16), shaped((tokens, width), F32)
    token_rank, token_lanes = shaped((tokens, RANK), BF16), shaped((tokens, LANES), F32)
    fixed = functools.partial

    qkv, normed = call(
        qkv_kernel, "qkv", "MLLHHH",
        [("V", shaped((seq, tokens, 3 * cols), BF16)), ("S", shaped((tokens, width + LANES), BF16))],
        (adapter_index, x, gain_one, input_weights, down, adapter_up), [triple, three_small, three_small, sema(9)],
    )
    qkv_all = exchange(qkv, "seq").reshape(rows, 3 * cols)

    slot, slot_col, pick, *ids_out = call(
        fixed(route_kernel, rows_dev, owners), "route", "ML",
        [("S", shaped((8, tokens), I32)), ("S", shaped((tokens, tokens), I32)), ("S", shaped((tokens, LANES), I32)),
         *[("V", shaped((seq * 8 + 8, LANES), I32)) for _ in range(batches)]],
        (adapter_index, picks), [pltpu.VMEM((owners * 8, LANES), I32)],
    )
    ids_out = [ids_out[0]] + [along(ids_out[k], "batch", k, batches) for k in range(1, batches)]
    mix_grad, grank_six = call(
        mix_back_kernel, "mixback", "MLHHH", [("S", token_low), ("S", token_rank)],
        (adapter_index, cot, output_weights, down, adapter_up), [matrix, small, small, sema(3)],
    )

    qkv_all, ids_out, mix_grad = lax.optimization_barrier((qkv_all, ids_out, mix_grad))
    attended, lse, slots, qkv_saved = call(
        fixed(attend_kernel, groups, batches), "attend", "MV" + "V" * batches,
        [("V", shaped((seq, tokens + carried, cols), BF16)), ("S", shaped((8, rows), F32)),
         ("S", shaped((batches, 8, LANES), I32)), ("H", shaped((rows, 3 * cols), BF16))],
        (lengths, qkv_all, *ids_out),
        [pltpu.VMEM((rows, LANES), BF16), pltpu.VMEM((LANES, rows), BF16), pltpu.VMEM((LANES, rows), F32), sema(1)],
    )
    o_all = exchange(attended, "seq")
    normed, attended = lax.optimization_barrier((normed, attended))
    normed_all = to_pairs(normed, "seq", seq)

    left, right, same_two, ahead, sent, att, rank_pair, middle, normed_two, gate = call(
        middle_kernel, "middle", "MVLLLHHHH",
        [("V", shaped((tokens, half), BF16)), ("V", shaped((tokens, half), BF16)), ("V", token_low),
         ("V", shaped((width, width), BF16)), ("S", shaped((seq, carried, cols), BF16)), ("S", token_low),
         ("S", shaped((2, tokens, RANK), BF16)), ("S", token_wide), ("S", token_low), ("S", token_wide)],
        (adapter_index, o_all, x, gain_two, mix_grad, input_weights, output_weights, down, adapter_up),
        [pair, two_small, two_small, sema(7)],
    )
    lefts = [left] + [along(left, "batch", k, batches) for k in range(1, batches)]
    weight_out, rank_four, weights = call(
        fixed(scores_kernel, owners), "scores", "MVVLLLHH",
        [("V", shaped((owners * 8, LANES), BF16)), ("S", token_rank), ("S", token_lanes)],
        (adapter_index, same_two, ahead, pick, slot, half_keys, down, adapter_up), [small, small, sema(2)],
    )
    weight_out, normed_all = lax.optimization_barrier((weight_out, normed_all))
    weight_in = exchange(weight_out.reshape(owners, 8, LANES), both).reshape(owners * 8, LANES)
    right, lefts = lax.optimization_barrier((right, lefts))
    rights = [right] + [along(right, "batch", k, batches) for k in range(1, batches)]

    def scatter(parts, name):
        out = [("V", shaped((seq, batches, capacity, half), BF16))]
        return call(scatter_kernel, name, "L" + "V" * batches, out, (slots, *parts))[0]

    left_out = scatter(lefts, "scatterleft")
    normed_all, left_out = lax.optimization_barrier((normed_all, left_out))
    normed_all = stacked(normed_all, "pairsnorm", "S")
    sent, left_out = lax.optimization_barrier((sent, left_out))
    ids, index = call(
        fixed(prepare_kernel, groups, rows_dev, batches), "prepare", "L",
        [("S", shaped((owners * 8, LANES), I32)), ("H", shaped((items, rows_dev), jnp.int16))], (sent,),
        [pltpu.VMEM((2, LANES, rows_dev), jnp.int16), pltpu.VMEM((owners * 8 // LANES, LANES, LANES), I32), sema(2)],
    )
    left_out, weight_in, normed_all = lax.optimization_barrier((left_out, weight_in, normed_all))
    normed_all = (normed_all, across(normed_all, "seq", 1, seq))
    left_in = exchange(left_out, "seq").reshape(items, half)

    (sums,) = call(
        fixed(recall_kernel, groups), "recall", "VHH", [("H", shaped((seq, batches, capacity, width), BF16))],
        (weight_in, index, memory_values),
        [pltpu.VMEM((rows_dev, width), BF16), pltpu.VMEM((2, small_block, rows_dev), jnp.int16), pltpu.VMEM((2, small_block, rows_dev), BF16),
         pltpu.VMEM((2, small_block // 8, 8, width), BF16), sema(3 + 2 * (small_block // (8 * seq)))],
        flops=1 << 12,
    )
    sums, left_in = lax.optimization_barrier((sums, left_in))
    back = exchange(sums, "seq")

    def recall_back(part, name, grads, kind, dtype, *before):
        return call(
            fixed(recall_back_kernel, part, batches, groups), name, "L" + "L" * part + "VH",
            [(kind, shaped((owners * 8, LANES), dtype))], (ids, *before, grads, memory_values),
            [pltpu.VMEM((rows_dev, half), BF16), pltpu.VMEM((block, rows_dev), F32), sema(1)],
        )[0]

    rights, normed_all = lax.optimization_barrier((rights, normed_all))
    right_out = scatter(rights, "scatterright")
    found_left = recall_back(0, "recallleft", left_in, "S", F32)
    right_out, back, found_left = lax.optimization_barrier((right_out, back, found_left))
    right_in = exchange(right_out, "seq").reshape(items, half)
    pieces = call(
        gather_kernel, "gather", "LV", [("V", token_low) for _ in range(batches)], (slots, back),
    )
    pieces = [pieces[0]] + [along(pieces[k], "batch", batches - k, batches) for k in range(1, batches)]
    found = recall_back(1, "recallright", right_in, "V", BF16, found_left)
    found_back = exchange(found.reshape(owners, 8, LANES), both).reshape(owners * 8, LANES)

    mixed, grank_five, ggate, part = call(
        fixed(memory_kernel, batches), "memory", "MLL" + "V" * batches + "HHH",
        [("S", token_low), ("S", token_rank), ("S", token_low), ("S", token_wide)],
        (adapter_index, gate, mix_grad, *pieces, input_weights, down, adapter_up), [matrix, small, small, sema(3)],
    )

    go, gquery, grank_pair, gmid = call(
        fixed(query_kernel, owners, rows_dev), "query", "MMVLLLLLLLLHHHH",
        [("V", shaped((seq, tokens, cols), BF16)), ("S", token_low), ("S", shaped((2, tokens, RANK), BF16)), ("S", token_wide)],
        (lengths, adapter_index, found_back, slot_col, picks, weights, part, middle, cot, gain_two, half_keys,
         input_weights, output_weights, down, adapter_up),
        [pair, two_small, two_small, pltpu.VMEM((LANES, tokens), F32), sema(6)],
    )
    go_all = exchange(go, "seq").reshape(rows, cols)
    mixed, go = lax.optimization_barrier((mixed, go))
    output, rank_six = call(
        output_kernel, "output", "MLLHHH", [("S", token_low), ("S", token_rank)],
        (adapter_index, mixed, middle, output_weights, down, adapter_up), [matrix, small, small, sema(3)],
    )
    (factors,) = call(
        factor_kernel, "factors", "L" * 13, [("V", shaped((seq, 8 * RANK, cols), BF16))],
        (att, normed_two, mixed, gmid, gquery, ggate, cot, rank_pair, rank_four, rank_six, grank_pair, grank_five, grank_six),
    )
    factors, go_all = lax.optimization_barrier((factors, go_all))
    early_parts = exchange(factors, "seq")

    grads, up_grads = call(
        attend_back_kernel, "attendback", "MMLVLHHH",
        [("V", shaped((seq, tokens + RANK, 3 * cols), BF16)), ("S", shaped((3 * RANK, cols), BF16))],
        (lengths, adapter_index, qkv_saved, go_all, lse, *normed_all, adapter_up),
        [pltpu.VMEM((rows, LANES), F32), pltpu.VMEM((rows, LANES), F32), pltpu.VMEM((LANES, rows), F32),
         pltpu.VMEM((rows, LANES), BF16), pltpu.VMEM((LANES, rows), BF16), pltpu.VMEM((rows, LANES), BF16),
         pltpu.VMEM((rows, 3 * cols), BF16), pltpu.VMEM((rows, width + LANES), BF16), three_small, sema(3 + seq)],
    )
    grads, early_parts = lax.optimization_barrier((grads, early_parts))
    grads_all = exchange(grads, "seq")
    (some,) = call(sum_kernel, "sumearly", "V", [("V", shaped((8 * RANK, cols), BF16))], (early_parts,))
    some = [some] + [along(some, "batch", k, batches) for k in range(1, batches)]
    some = stacked(some, "stackearly")
    some = to_pairs(some, "seq", seq)
    (late_sum,) = call(late_kernel, "late", "VL", [("V", shaped((6 * RANK, cols), BF16))], (grads_all, up_grads))
    (grad_input,) = call(
        entry_kernel, "entry", "MVLLLHHH", [("S", token_low)],
        (adapter_index, grads_all, x, gain_one, gmid, input_weights, down, adapter_up),
        [triple, pltpu.VMEM((3, tokens, width), BF16), pltpu.VMEM((tokens, width), F32), three_small, three_small, sema(9)],
    )
    late_sums = [late_sum] + [along(late_sum, "batch", k, batches) for k in range(1, batches)]
    some = stacked(some, "pairsearly")
    late_sums, some, grad_input = lax.optimization_barrier((late_sums, some, grad_input))
    late_all = to_pairs(stacked(late_sums, "stacklate"), "seq", seq)
    some = (some, across(some, "seq", 1, seq))
    full = shaped((7, ADAPTERS, RANK, width), F32)
    grad_down, grad_up = call(
        fixed(spread_kernel, batches), "spread", "LVV", [("H", full), ("H", full)], (ids, *some),
        [pltpu.VMEM((seq, batches, 8 * RANK, cols), BF16), pltpu.VMEM((8, ADAPTERS, RANK, width), F32), sema(seq), sema(8)],
    )
    late_all, grad_down, grad_up = lax.optimization_barrier((late_all, grad_down, grad_up))
    late_all = stacked(late_all, "pairslate")
    late_all = (late_all, across(late_all, "seq", 1, seq))
    grad_down, grad_up = call(
        fixed(last_spread_kernel, batches), "lastspread", "LHHVV", [("H", full), ("H", full)],
        (ids, grad_down, grad_up, *late_all),
        [pltpu.VMEM((seq, batches, 6 * RANK, cols), BF16), pltpu.VMEM((6, ADAPTERS, RANK, width), F32), sema(seq), sema(6)],
        aliases={1: 0, 2: 1},
    )
    return (output[None], grad_input[None], jnp.swapaxes(grad_down, 2, 3), grad_up)


def solution(mesh):
    split = P("batch", "seq", None)
    return jax.shard_map(
        body,
        mesh=mesh,
        in_specs=(
            split, P("batch"), P("batch"), P("batch", "seq", None, None), P(), P(), P(), P(), P(), P(), P(),
            P(("batch", "seq"), None), split,
        ),
        out_specs=(split, split, P(), P()),
        check_vma=False,
    )
```

```python
import functools

import jax
import jax.numpy as jnp
from jax import lax
from jax.experimental import pallas as pl
from jax.experimental.pallas import tpu as pltpu
from jax.sharding import PartitionSpec as P

HEAD_DIM = 64
MHEADS = 4
KHALF = 128
NSUB = 256
PICKS = 32
ADAPTERS = 8
RANK = 16
LANES = 128
ADAPTER_STEP = 4096
QUERY_UNROLL = 8
RECALL_ROWS = 256
EPS = 1e-06
NEG = -1e30
F32 = jnp.float32
BF16 = jnp.bfloat16
I32 = jnp.int32
HBM = pl.BlockSpec(memory_space=pltpu.HBM)
SMEM = pl.BlockSpec(memory_space=pltpu.SMEM)
VMEM = pl.BlockSpec(memory_space=pltpu.VMEM)
MIB = 1 << 20


def product(left, right):
    return lax.dot_general(left, right, (((1,), (0,)), ((), ())), preferred_element_type=F32)


def against(left, right):
    return lax.dot_general(left, right, (((1,), (1,)), ((), ())), preferred_element_type=F32)


def contract(left, right):
    return lax.dot_general(left, right, (((0,), (0,)), ((), ())), preferred_element_type=F32)


def iota(shape, axis):
    return lax.broadcasted_iota(I32, shape, axis)


def short_pick(table, index):
    numbers = lax.GatherDimensionNumbers(
        offset_dims=(), collapsed_slice_dims=(1,), start_index_map=(1,), operand_batching_dims=(0,), start_indices_batching_dims=(0,)
    )
    return lax.gather(table, index[:, :, None], numbers, (1, 1), mode=lax.GatherScatterMode.PROMISE_IN_BOUNDS)


def lane_pick(table, index):
    return jnp.take_along_axis(table, index, axis=1, mode="promise_in_bounds")


def shaped(shape, dtype):
    return jax.ShapeDtypeStruct(shape, dtype)


class Stage:
    def __init__(self, loads, stores):
        self.loads, self.stores = loads, stores
        self.waited, self.begun = set(), set()
        for _, copy, later in loads:
            if not later:
                copy.start()

    def begin(self):
        for _, copy, later in self.loads:
            if later:
                copy.start()

    def __call__(self, *refs):
        for at, (ref, copy, _) in enumerate(self.loads):
            if at not in self.waited and (not refs or any(ref is one for one in refs)):
                self.waited.add(at)
                copy.wait()

    def send(self, *refs):
        for at, (ref, copy) in enumerate(self.stores):
            if at not in self.begun and (not refs or any(ref is one for one in refs)):
                self.begun.add(at)
                copy.start()

    def finish(self):
        self()
        self.send()
        for _, copy in self.stores:
            copy.wait()


def call(kernel, name, ins, outs, args, scratch=(), vmem=40, flops=1 << 12, moved=1 << 12, aliases=None):
    shapes = [(args[i].shape, args[i].dtype) for i, kind in enumerate(ins) if kind in "LD"]
    stored = [(out.shape, out.dtype) for kind, out in outs if kind == "S"]
    count_in, count_out, count_user = len(ins), len(outs), len(scratch)

    def wrapped(*refs):
        given, results = list(refs[:count_in]), list(refs[count_in : count_in + count_out])
        rest = list(refs[count_in + count_out :])
        user, buffers = rest[:count_user], rest[count_user:]
        loads, stores = [], []
        for i, kind in enumerate(ins):
            if kind in "LD":
                at = len(loads)
                copy = pltpu.make_async_copy(given[i], buffers[at], buffers[-1].at[at])
                loads.append((buffers[at], copy, kind == "D"))
                given[i] = buffers[at]
        for i, (kind, _) in enumerate(outs):
            if kind == "S":
                at = len(loads) + len(stores)
                stores.append((buffers[at], pltpu.make_async_copy(buffers[at], results[i], buffers[-1].at[at])))
                results[i] = buffers[at]
        stage = Stage(loads, stores)
        kernel(stage, *given, *results, *user)
        stage.finish()

    spaces = {"V": VMEM, "L": HBM, "D": HBM, "S": HBM, "H": HBM, "M": SMEM}
    autos = [pltpu.VMEM(*one) for one in shapes + stored]
    args = [
        pltpu.with_memory_space_constraint(one, pltpu.HBM) if kind in "LDH" else one
        for kind, one in zip(ins, args, strict=True)
    ]
    return pl.pallas_call(
        wrapped,
        name=name,
        out_shape=[pltpu.HBM(out.shape, out.dtype) if kind in "SH" else out for kind, out in outs],
        in_specs=[spaces[kind] for kind in ins],
        out_specs=[spaces[kind] for kind, _ in outs],
        input_output_aliases=aliases or {},
        scratch_shapes=list(scratch) + autos + ([sema(len(autos))] if autos else []),
        compiler_params=pltpu.CompilerParams(vmem_limit_bytes=vmem * MIB),
        cost_estimate=pl.CostEstimate(flops=flops, bytes_accessed=moved, transcendentals=0),
    )(*args)


def fetch(pairs, sems):
    copies = [
        pltpu.make_async_copy(source, target, sems.at[place])
        for place, (source, target) in enumerate(pairs)
    ]
    for copy in copies:
        copy.start()
    return copies


def sema(count):
    return pltpu.SemaphoreType.DMA((count,))


def gain_row(ref):
    return ref[...].astype(F32).reshape(1, ref.shape[0])


def inverse_norm(values):
    return lax.rsqrt(jnp.mean(values * values, axis=1, keepdims=True) + EPS)


def norm_back(values, inverse, scales, incoming):
    weighted = incoming * scales
    inner = jnp.mean(weighted * values, axis=1, keepdims=True)
    return weighted * inverse - values * inverse * inverse * inverse * inner


def qkv_kernel(ready, adapter, x_ref, gain_ref, w_any, dn_any, up_any, out_ref, norm_ref, w, dn, up, sems):
    groups, tokens, wide = out_ref.shape
    cols = wide // 3
    a = adapter[0]
    copies = fetch(
        [(dn_any.at[j, a], dn.at[pl.ds(RANK * j, RANK)]) for j in range(3)]
        + [(up_any.at[j, a], up.at[pl.ds(RANK * j, RANK)]) for j in range(3)]
        + [(w_any.at[j], w.at[j]) for j in range(3)],
        sems,
    )
    ready()
    x = x_ref[...].astype(F32)
    normed = (x * inverse_norm(x) * gain_row(gain_ref)).astype(BF16)
    width = normed.shape[1]
    norm_ref[:, :width] = normed
    for copy in copies[:6]:
        copy.wait()
    ranks = against(normed, dn[...])
    norm_ref[:, width:] = widen(ranks).astype(BF16)
    ready.send(norm_ref)
    place = iota((tokens, 3 * RANK), 1) // RANK
    for j in range(3):
        own = jnp.where(place == j, ranks, 0.0).astype(BF16)
        extra = product(own, up[...])
        copies[6 + j].wait()
        result = (product(normed, w[j]) + extra).astype(BF16)
        for s in range(groups):
            out_ref[s, :, j * cols : (j + 1) * cols] = result[:, s * cols : (s + 1) * cols]


def mix_back_kernel(ready, adapter, cot_ref, w_any, dn_any, up_any, grad_ref, rank_ref, w, dn, up, sems):
    a = adapter[0]
    copies = fetch([(up_any.at[6, a], up), (dn_any.at[6, a], dn), (w_any.at[1], w)], sems)
    ready()
    gy = cot_ref[...]
    copies[0].wait()
    ranks = against(gy, up[...]).astype(BF16)
    rank_ref[...] = ranks
    copies[1].wait()
    extra = product(ranks, dn[...])
    copies[2].wait()
    grad_ref[...] = (against(gy, w[...]) + extra).astype(BF16)


def route_kernel(rows_dev, owners, ready, adapter, picks_ref, slot_ref, slot_col_ref, pick_ref, *ids_refs):
    ready()
    heads, picks, tokens = picks_ref.shape
    capacity = 2 * heads * tokens // owners
    groups = capacity // 8
    visits = heads * tokens
    owner = jnp.concatenate([picks_ref[h, 0:1, :] for h in range(heads)], axis=1) // rows_dev
    hot = jnp.where(iota((owners, visits), 0) == owner, 1.0, 0.0)
    before = jnp.where(iota((visits, visits), 0) < iota((visits, visits), 1), 1.0, 0.0).astype(BF16)
    counts = product(hot.astype(BF16), before)
    within = jnp.sum(hot * counts, axis=0, keepdims=True).astype(I32)
    slot = owner * capacity + within
    rows = [slot[:, h * tokens : (h + 1) * tokens] for h in range(heads)]
    stacked = jnp.concatenate(rows + [jnp.full((8 - heads, tokens), -1, I32)], axis=0)
    slot_ref[...] = stacked
    tall = jnp.concatenate([stacked, jnp.full((tokens - 8, tokens), -1, I32)], axis=0)
    slot_col_ref[...] = jnp.transpose(tall)
    packed = jnp.concatenate([picks_ref[h] for h in range(heads)], axis=0)
    by_token = jnp.transpose(packed)
    pick_ref[...] = by_token
    local = by_token % rows_dev
    lanes = iota((tokens, LANES), 1)
    total = jnp.zeros((owners * 8, LANES), F32)
    out_lane = iota((owners * 8, LANES), 1) // PICKS
    place = iota((owners * 8, tokens), 0)
    base = (place // 8) * capacity + place % 8
    for g in range(groups):
        high = jnp.zeros((owners * 8, LANES), F32)
        low = jnp.zeros((owners * 8, LANES), F32)
        for h in range(heads):
            chosen = jnp.where(base + g * 8 == rows[h], 1.0, 0.0).astype(BF16)
            own = jnp.where(lanes // PICKS == h, local, 0)
            own = tile_groups(own.astype(F32), heads).astype(I32)
            high = high + product(chosen, (own // 256).astype(F32).astype(BF16))
            low = low + product(chosen, (own % 256).astype(F32).astype(BF16))
        total = jnp.where(out_lane == g, high * 256.0 + low, total)
    batches = len(ids_refs) - 1
    part = owners * 8 // batches
    ids_refs[-1][...] = total.astype(I32) + adapter[0] * ADAPTER_STEP
    for k in range(batches):
        target = lax.rem(lax.axis_index("batch") + k, batches)
        ids_refs[k][0:part, :] = ids_refs[-1][pl.ds(pl.multiple_of(target * part, part), part), :]
        ids_refs[k][part:, :] = stacked


def tile_groups(values, count):
    total = values
    for turn in range(1, count):
        total = total + pltpu.roll(values, turn * PICKS, 1)
    return total


def prepare_kernel(groups, rows_dev, batches, ready, sent_ref, ids_ref, index_any, stage, turned, sems):
    ready()
    seq, _, cols = sent_ref.shape
    lanes = groups * PICKS
    chunks = 2 * lanes // cols
    for k in range(batches):
        source = lax.rem(lax.axis_index("batch") + (batches - k), batches)
        for s in range(seq):
            both = [
                sent_ref[s, (chunk * batches + k) * 8 : (chunk * batches + k + 1) * 8, :].astype(F32)
                for chunk in range(chunks)
            ]
            both = jnp.concatenate(both, axis=1).astype(I32)
            ids = widen(both[:, :lanes] * 256 + both[:, lanes:])
            ids_ref[pl.ds(pl.multiple_of((source * seq + s) * 8, 8), 8), :] = ids
    ready.send(ids_ref)
    places = ids_ref.shape[0]
    chunks = rows_dev // LANES
    high_rows = max(8, chunks)
    steps = groups * (places // LANES)
    for k in range(places // LANES):
        turned[k] = jnp.transpose(ids_ref[k * LANES : (k + 1) * LANES, :] & (ADAPTER_STEP - 1))

    def put(step, slot):
        target = index_any.at[pl.ds(pl.multiple_of(step * LANES, LANES), LANES)]
        return pltpu.make_async_copy(stage.at[slot], target, sems.at[slot])

    def one(step, carry):
        k, g = lax.rem(step, places // LANES), step // (places // LANES)
        slot = lax.rem(step, 2)
        mask = jnp.zeros((LANES, LANES), I32)
        highs = jnp.zeros((high_rows, LANES), I32)
        for r in range(PICKS):
            bit = (1 << r) if r < 31 else -(1 << 31)
            row = turned[k, pl.ds(g * PICKS + r, 1), :]
            mask = mask | jnp.where(row & 127 == iota((LANES, LANES), 0), bit, 0)
            highs = highs | jnp.where(row >> 7 == iota((high_rows, LANES), 0), bit, 0)

        @pl.when(step >= 2)
        def _():
            put(step - 2, slot).wait()

        for c in range(chunks):
            index = 31 - lax.clz(mask & highs[c : c + 1, :])
            stage[slot, :, c * LANES : (c + 1) * LANES] = jnp.transpose(index.astype(jnp.int16))
        put(step, slot).start()
        return carry

    lax.fori_loop(0, steps, one, 0)
    for step in range(max(0, steps - 2), steps):
        put(step, step % 2).wait()


def recall_kernel(groups, ready, weight_ref, index_any, mem_any, out_any, mem, index, dense, staged, sems):
    places = weight_ref.shape[0]
    rows_dev = mem.shape[0]
    chunks = rows_dev // LANES
    block = dense.shape[1]
    per_group = places // block
    blocks = groups * per_group
    seq = out_any.shape[0]
    planes = block // (8 * seq)

    def load(b, slot):
        source = index_any.at[pl.ds(pl.multiple_of(b * block, block), block)]
        return pltpu.make_async_copy(source, index.at[slot], sems.at[1 + slot])

    load(0, 0).start()
    copy = pltpu.make_async_copy(mem_any, mem, sems.at[0])
    copy.start()

    def gather(b, side):
        load(b, side).wait()

        @pl.when(b + 1 < blocks)
        def _():
            load(b + 1, 1 - side).start()

        pick(b, side)

    def pick(b, side):
        g, k = b // per_group, lax.rem(b, per_group)
        for start in range(0, block, 16):
            weights = weight_ref[pl.ds(pl.multiple_of(k * block + start, 16), 16), :]
            shift = jnp.full((16, LANES), g * PICKS, I32).astype(jnp.int16)
            for c in range(chunks):
                at = index[side, start : start + 16, c * LANES : (c + 1) * LANES]
                value = short_pick(weights, (at + shift) & jnp.int16(127))
                dense[side, start : start + 16, c * LANES : (c + 1) * LANES] = jnp.where(at >= 0, value, jnp.zeros((), BF16))

    def save(b, side):
        g, k = b // per_group, lax.rem(b, per_group)
        return [
            pltpu.make_async_copy(
                staged.at[side, pl.ds(i * seq, seq)],
                out_any.at[:, k * planes + i, pl.ds(pl.multiple_of(g * 8, 8), 8), :],
                sems.at[3 + side * planes + i],
            )
            for i in range(planes)
        ]

    def multiply(b, side):
        result = product(dense[side], mem[...]).astype(BF16)

        @pl.when(b >= 2)
        def _():
            for one in save(b - 2, side):
                one.wait()

        staged[side] = result.reshape(block // 8, 8, result.shape[1])
        for one in save(b, side):
            one.start()

    gather(0, 0)
    copy.wait()

    def whole(i, carry):
        gather(2 * i + 1, 1)
        multiply(2 * i, 0)

        @pl.when(2 * i + 2 < blocks)
        def _():
            load(2 * i + 2, 0).wait()
            load(2 * i + 3, 1).start()

        pick(jnp.minimum(2 * i + 2, blocks - 1), 0)
        multiply(2 * i + 1, 1)
        return carry

    lax.fori_loop(0, blocks // 2, whole, 0)
    for b in range(blocks - 2, blocks):
        for one in save(b, b % 2):
            one.wait()


def recall_back_kernel(part, batches, groups, ready, ids_ref, *refs):
    before_ref = refs[0] if part else None
    grad_ref, mem_any, out_ref, mem, scores, sems = refs[part:]
    items, half = grad_ref.shape
    seq = items // (batches * groups * 8)
    rows_dev = mem.shape[0]
    capacity = groups * 8
    chunks = rows_dev // LANES
    block = scores.shape[0]
    per_block = block // capacity
    blocks = items // block
    copies = fetch([(mem_any.at[:, pl.ds(part * half, half)], mem)], sems)
    ready()
    copies[0].wait()

    def whole(b, outer):
        scores[...] = against(grad_ref[pl.ds(pl.multiple_of(b * block, block), block), :], mem[...])

        lane_group = iota((8, LANES), 1) // PICKS
        for local in range(per_block):
            sender = b * per_block + local
            spot = lax.rem(sender, batches) * seq + sender // batches
            start = pl.multiple_of(spot * 8, 8)
            ids = ids_ref[pl.ds(start, 8), :] & (ADAPTER_STEP - 1)
            low = ids & 127
            high = ids >> 7
            total = before_ref[pl.ds(start, 8), :] if part else jnp.zeros((8, LANES), F32)
            for g in range(groups):
                key = jnp.where(lane_group == g, high, -1)
                here = jnp.zeros((8, LANES), F32)
                row = local * capacity + g * 8
                for c in range(chunks):
                    found = scores[row : row + 8, c * LANES : (c + 1) * LANES]
                    here = jnp.where(key == c, lane_pick(found, low), here)
                total = total + here
            out_ref[pl.ds(start, 8), :] = total.astype(out_ref.dtype)
        return outer

    lax.fori_loop(0, blocks, whole, 0)


def head_parts(values, h, spare):
    lane = iota(values.shape, 1)
    return jnp.where(lane // HEAD_DIM == h, values, jnp.where(lane == (1 - h) * HEAD_DIM, spare, 0.0)).astype(BF16)


def widen(values):
    if values.shape[1] == LANES:
        return values
    return jnp.concatenate([values, jnp.zeros((values.shape[0], LANES - values.shape[1]), values.dtype)], axis=1)


def attend_kernel(groups, batches, ready, length, qkv_ref, *refs):
    o_ref, lse_ref, slots_ref, saved_any, parts, values_t, mixed, sems = refs[batches:]
    ready()
    saving = pltpu.make_async_copy(qkv_ref, saved_any, sems.at[0])
    saving.start()
    rows, wide = qkv_ref.shape
    cols = wide // 3
    seq = o_ref.shape[0]
    lanes = groups * PICKS
    for k in range(batches):
        slots_ref[k] = refs[k][seq * 8 :, :]
    ready.send(slots_ref)
    for s in range(seq):
        ids = jnp.concatenate([refs[k][s * 8 : (s + 1) * 8, :lanes] for k in range(batches)], axis=0)
        both = jnp.concatenate([ids // 256, ids % 256], axis=1).astype(F32).astype(BF16)
        for chunk in range(2 * lanes // cols):
            start = rows // seq + chunk * batches * 8
            o_ref[s, start : start + batches * 8, :] = both[:, chunk * cols : (chunk + 1) * cols]
    heads = cols // HEAD_DIM
    size = min(256, rows)
    valid = length[0]
    bias = jnp.where(iota((rows, LANES), 0) < valid, 0.0, NEG)
    keys = widen(qkv_ref[:, cols : 2 * cols].astype(F32))
    values_t[...] = jnp.transpose(widen(qkv_ref[:, 2 * cols :].astype(F32))).astype(BF16)
    lse_ref[...] = jnp.zeros_like(lse_ref)

    def one(h, carry):
        parts[...] = head_parts(keys, h, bias)
        for i in range(rows // size):
            first, last = i * size, (i + 1) * size
            queries = widen(qkv_ref[first:last, 0:cols].astype(F32)) * (HEAD_DIM**-0.5)
            query = head_parts(queries, h, 1.0)
            near = against(parts[first:last], query)
            near = jnp.where(iota((size, size), 0) <= iota((size, size), 1), near, NEG)
            high = jnp.max(near, axis=0, keepdims=True)
            if i:
                far = against(parts[:first], query)
                high = jnp.maximum(high, jnp.max(far, axis=0, keepdims=True))
            near = jnp.exp(near - high)
            summed = jnp.sum(near, axis=0, keepdims=True)
            result = product(values_t[:, first:last], near.astype(BF16))
            if i:
                far = jnp.exp(far - high)
                summed = summed + jnp.sum(far, axis=0, keepdims=True)
                result = result + product(values_t[:, :first], far.astype(BF16))
            lse_ref[pl.ds(h, 1), first:last] = high + jnp.log(summed)
            own = iota((LANES, size), 0) // HEAD_DIM == h
            mixed[:, first:last] = jnp.where(own, result / summed, mixed[:, first:last])
        return carry

    mixed[...] = jnp.zeros_like(mixed)
    lax.fori_loop(0, heads, one, 0)
    ready.send(lse_ref)
    tokens = rows // seq
    for s in range(seq):
        first = s * tokens
        kept = jnp.where(first + iota((LANES, tokens), 1) < valid, mixed[:, first : first + tokens], 0.0)
        o_ref[s, 0:tokens, :] = jnp.transpose(kept)[:, :cols].astype(BF16)
    saving.wait()


def attend_back_kernel(
    ready, length, adapter, qkv_ref, go_ref, lse_ref, even_ref, odd_ref, up_any,
    out_ref, upgrad_ref, dk, dv, dq, parts, keys_t, values, grads_all, norms, up, sems,
):
    a = adapter[0]
    seq = out_ref.shape[0]
    me = lax.axis_index("seq")
    tokens = even_ref.shape[1]
    copies = fetch(
        [(up_any.at[j, a], up.at[pl.ds(RANK * j, RANK)]) for j in range(3)]
        + [
            ((even_ref, odd_ref)[m % 2].at[m // 2], norms.at[pl.ds(pl.multiple_of((me ^ m) * tokens, tokens), tokens)])
            for m in range(seq)
        ],
        sems,
    )
    ready()
    rows, wide = qkv_ref.shape
    cols = wide // 3
    heads = cols // HEAD_DIM
    size = min(256, rows)
    valid = length[0]
    scaling = HEAD_DIM**-0.5
    bias = jnp.where(iota((rows, LANES), 0) < valid, 0.0, NEG)
    keys = widen(qkv_ref[:, cols : 2 * cols].astype(F32))
    keys_t[...] = jnp.transpose(keys).astype(BF16)
    values[...] = widen(qkv_ref[:, 2 * cols :])
    dk[...] = jnp.zeros_like(dk)
    dv[...] = jnp.zeros_like(dv)
    dq[...] = jnp.zeros_like(dq)

    def one(h, carry):
        parts[...] = head_parts(keys, h, bias)
        for i in range(rows // size):
            first, last = i * size, (i + 1) * size
            queries = widen(qkv_ref[first:last, 0:cols].astype(F32)) * scaling
            grads = widen(go_ref[first:last, :].astype(F32))
            query = head_parts(queries, h, 1.0)
            plain = head_parts(queries, h, 0.0)
            grad = head_parts(grads, h, 0.0)
            lse = lse_ref[pl.ds(h, 1), first:last]
            near = against(parts[first:last], query)
            near = jnp.where(iota((size, size), 0) <= iota((size, size), 1), near, NEG)
            near = jnp.exp(near - lse)
            near_gp = against(values[first:last], grad)
            delta = jnp.sum(near * near_gp, axis=0, keepdims=True)
            if i:
                far = jnp.exp(against(parts[:first], query) - lse)
                far_gp = against(values[:first], grad)
                delta = delta + jnp.sum(far * far_gp, axis=0, keepdims=True)
            near_gs = (near * (near_gp - delta)).astype(BF16)
            result = product(keys_t[:, first:last], near_gs)
            dk[first:last] += product(near_gs, plain)
            dv[first:last] += product(near.astype(BF16), grad)
            if i:
                far_gs = (far * (far_gp - delta)).astype(BF16)
                result = result + product(keys_t[:, :first], far_gs)
                dk[:first] += product(far_gs, plain)
                dv[:first] += product(far.astype(BF16), grad)
            own = iota((LANES, size), 0) // HEAD_DIM == h
            dq[:, first:last] = jnp.where(own, result, dq[:, first:last])
        return carry

    lax.fori_loop(0, heads, one, 0)
    grads_all[:, 0:cols] = (jnp.transpose(dq[...]) * scaling)[:, :cols].astype(BF16)
    grads_all[:, cols : 2 * cols] = dk[:, :cols].astype(BF16)
    grads_all[:, 2 * cols :] = dv[:, :cols].astype(BF16)
    for s in range(seq):
        out_ref[s, 0:tokens, :] = grads_all[s * tokens : (s + 1) * tokens, :]
    for copy in copies:
        copy.wait()
    own = jnp.zeros((3 * RANK, cols), F32)
    for s in range(seq):
        own = jnp.where(me == s, up[:, s * cols : (s + 1) * cols].astype(F32), own)
    own = own.astype(BF16)
    place = iota((rows, 3 * RANK), 1) // RANK
    granks = jnp.zeros((rows, 3 * RANK), F32)
    for j in range(3):
        granks = jnp.where(place == j, against(grads_all[:, j * cols : (j + 1) * cols], own), granks)
    width = norms.shape[1] - LANES
    down = contract(granks.astype(BF16), norms[:, :width]).astype(BF16)
    both = contract(norms[:, width:], grads_all[...]).astype(BF16)
    for j in range(3):
        row = j * RANK
        upgrad_ref[row : row + RANK, :] = both[row : row + RANK, j * cols : (j + 1) * cols]
        for s in range(seq):
            out_ref[s, tokens:, j * cols : (j + 1) * cols] = down[row : row + RANK, s * cols : (s + 1) * cols]


def pick_chosen(tables, index):
    tokens = index.shape[0]
    low = index & 127
    key = (index >> 7) + (iota((tokens, LANES), 1) // PICKS) * (NSUB // LANES)
    total = jnp.zeros((tokens, LANES), F32)
    for h in range(MHEADS):
        for c in range(NSUB // LANES):
            found = lane_pick(tables[h][:, c * LANES : (c + 1) * LANES], low)
            total = jnp.where(key == h * (NSUB // LANES) + c, found, total)
    return total


def group_reduce(values, reducer, fill):
    group = iota(values.shape, 1) // PICKS
    total = jnp.zeros(values.shape, F32)
    for h in range(MHEADS):
        one = reducer(jnp.where(group == h, values, fill), axis=1, keepdims=True)
        total = jnp.where(group == h, one, total)
    return total


def middle_kernel(
    ready, adapter, o_ref, x_ref, gain_ref, mix_ref, w_in_any, w_out_any, dn_any, up_any,
    left_ref, right_ref, same_ref, ahead_ref, sent_ref, att_ref, rank_ref, mid_ref, norm_ref, gate_ref, w, dn, up, sems,
):
    groups = o_ref.shape[0]
    a = adapter[0]
    copies = fetch(
        [(dn_any.at[3, a], dn.at[0]), (dn_any.at[5, a], dn.at[1]), (up_any.at[3, a], up.at[0]), (up_any.at[5, a], up.at[1]),
         (w_out_any.at[0], w.at[0]), (w_in_any.at[4], w.at[1]), (w_in_any.at[3], ahead_ref)],
        sems,
    )
    tokens = att_ref.shape[0]
    attended = jnp.concatenate([o_ref[s, 0:tokens, :] for s in range(groups)], axis=1)
    sent_ref[...] = o_ref[:, tokens:, :]
    ready.send(sent_ref)
    att_ref[...] = attended
    ready.send(att_ref)
    for copy in copies[:4]:
        copy.wait()
    rank_three = against(attended, dn[0]).astype(BF16)
    extra = product(rank_three, up[0])
    copies[4].wait()
    ready(x_ref, gain_ref)
    middle = x_ref[...].astype(F32) + (product(attended, w[0]) + extra)
    mid_ref[...] = middle
    normed = (middle * inverse_norm(middle) * gain_row(gain_ref)).astype(BF16)
    norm_ref[...] = normed
    same_ref[...] = normed
    ready.send(mid_ref, norm_ref)
    rank_five = against(normed, dn[1]).astype(BF16)
    rank_ref[0] = rank_three
    rank_ref[1] = rank_five
    extra = product(rank_five, up[1])
    copies[5].wait()
    gate = product(normed, w[1]) + extra
    gate_ref[...] = gate
    ready.send(rank_ref, gate_ref)
    ready(mix_ref)
    memory_grad = (mix_ref[...].astype(F32) * (gate * jax.nn.sigmoid(gate))).astype(BF16)
    half = left_ref.shape[1]
    left_ref[...] = memory_grad[:, :half]
    right_ref[...] = memory_grad[:, half:]
    copies[6].wait()


def scores_kernel(
    owners, ready, adapter, normed_ref, w_ref, picks_ref, slot_ref, keys_ref, dn_any, up_any,
    send_ref, rank_ref, weight_ref, dn, up, sems,
):
    a = adapter[0]
    copies = fetch([(dn_any.at[4, a], dn), (up_any.at[4, a], up)], sems)
    normed = normed_ref[...]
    copies[0].wait()
    ranks = against(normed, dn[...]).astype(BF16)
    rank_ref[...] = ranks
    copies[1].wait()
    extra = product(ranks, up[...])
    query = (product(normed, w_ref[...]) + extra).astype(BF16)
    ready()
    ready.send(rank_ref)
    first, second = [], []
    for h in range(MHEADS):
        base = 2 * h * KHALF
        first.append(against(query[:, base : base + KHALF], keys_ref[0, h]))
        second.append(against(query[:, base + KHALF : base + 2 * KHALF], keys_ref[1, h]))
    picks = picks_ref[...]
    scores = pick_chosen(first, picks // NSUB) + pick_chosen(second, picks % NSUB)
    exponent = jnp.exp(scores - group_reduce(scores, jnp.max, NEG))
    weights = exponent / group_reduce(exponent, jnp.sum, 0.0)
    weight_ref[...] = weights
    ready.send(weight_ref)
    send_ref[...] = to_slots(weights, slot_ref, owners).astype(BF16)


def to_slots(weights, slot_ref, owners):
    tokens = weights.shape[0]
    capacity = 2 * MHEADS * tokens // owners
    lane_group = iota((tokens, LANES), 1) // PICKS
    tiled = [
        tile_groups(jnp.where(lane_group == h, weights, 0.0), MHEADS).astype(BF16) for h in range(MHEADS)
    ]
    place = iota((owners * 8, tokens), 0)
    base = (place // 8) * capacity + place % 8
    out_group = iota((owners * 8, LANES), 1) // PICKS
    total = jnp.zeros((owners * 8, LANES), F32)
    for g in range(capacity // 8):
        part = jnp.zeros((owners * 8, LANES), F32)
        for h in range(MHEADS):
            chosen = jnp.where(base + g * 8 == slot_ref[h : h + 1, :], 1.0, 0.0).astype(BF16)
            part = part + product(chosen, tiled[h])
        total = jnp.where(out_group == g, part, total)
    return total


def plane_hits(slots_ref, k, plane, seq, capacity):
    tokens = slots_ref.shape[2]
    place = plane * (seq * capacity) + iota((seq * capacity, tokens), 0)
    chosen = jnp.zeros((seq * capacity, tokens), F32)
    for h in range(MHEADS):
        chosen = jnp.where(place == slots_ref[k, h : h + 1, :], 1.0, chosen)
    return chosen.astype(BF16)


def scatter_kernel(ready, slots_ref, *refs):
    ready()
    out_ref = refs[-1]
    seq, batches, capacity, wide = out_ref.shape
    plane = lax.axis_index("batch")
    for k in range(batches):
        chosen = plane_hits(slots_ref, k, plane, seq, capacity)
        rows = product(chosen, refs[k][...]).astype(BF16)
        source = lax.rem(plane + (batches - k), batches)
        out_ref[:, pl.ds(source, 1)] = rows.reshape(seq, 1, capacity, wide)


def gather_kernel(ready, slots_ref, back_ref, *refs):
    ready()
    seq, batches, capacity, wide = back_ref.shape
    plane = lax.axis_index("batch")
    for k in range(batches):
        chosen = plane_hits(slots_ref, k, plane, seq, capacity)
        source = lax.rem(plane + (batches - k), batches)
        rows = back_ref[:, pl.ds(source, 1)].reshape(seq * capacity, wide)
        refs[k][...] = contract(chosen, rows).astype(BF16)


def memory_kernel(batches, ready, adapter, gate_ref, mix_ref, *refs):
    w_in_any, dn_any, up_any, mixed_ref, grank_ref, ggate_ref, part_ref, w, dn, up, sems = refs[batches:]
    a = adapter[0]
    copies = fetch([(dn_any.at[5, a], dn), (up_any.at[5, a], up), (w_in_any.at[4], w)], sems)
    ready()
    memory = refs[0][...].astype(F32)
    for k in range(1, batches):
        memory = memory + refs[k][...].astype(F32)
    gate = gate_ref[...]
    sigmoid = jax.nn.sigmoid(gate)
    mixed_ref[...] = (memory * (gate * sigmoid)).astype(BF16)
    ggate = (mix_ref[...].astype(F32) * memory * sigmoid * (1.0 + gate * (1.0 - sigmoid))).astype(BF16)
    ggate_ref[...] = ggate
    for copy in copies[:2]:
        copy.wait()
    granks = against(ggate, up[...]).astype(BF16)
    grank_ref[...] = granks
    extra = product(granks, dn[...])
    copies[2].wait()
    ready.send(mixed_ref, ggate_ref, grank_ref)
    part_ref[...] = against(ggate, w[...]) + extra


def output_kernel(ready, adapter, mixed_ref, mid_ref, w_out_any, dn_any, up_any, out_ref, rank_ref, w, dn, up, sems):
    a = adapter[0]
    copies = fetch([(dn_any.at[6, a], dn), (up_any.at[6, a], up), (w_out_any.at[1], w)], sems)
    ready()
    mixed = mixed_ref[...]
    for copy in copies[:2]:
        copy.wait()
    ranks = against(mixed, dn[...]).astype(BF16)
    rank_ref[...] = ranks
    extra = product(ranks, up[...])
    copies[2].wait()
    out_ref[...] = (mid_ref[...] + (product(mixed, w[...]) + extra)).astype(BF16)


def query_kernel(
    owners, rows_dev, ready, length, adapter, back_ref, slot_ref, picks_ref, weight_ref, part_ref, mid_ref, cot_ref, gain_ref,
    keys_ref, w_in_any, w_out_any, dn_any, up_any,
    go_ref, gquery_ref, grank_ref, gmid_ref, w, dn, up, turned, spots, sems,
):
    groups, tokens, cols = go_ref.shape
    a = adapter[0]
    ready(slot_ref, weight_ref)
    capacity = 2 * MHEADS * tokens // owners
    slots = iota((tokens, owners * 8), 1)
    base = (slots // 8) * capacity + slots % 8
    lane_group = iota((tokens, LANES), 1) // PICKS
    back = back_ref[...]
    gw = jnp.zeros((tokens, LANES), F32)
    for h in range(MHEADS):
        part = jnp.zeros((tokens, LANES), F32)
        for g in range(capacity // 8):
            chosen = jnp.where(base + g * 8 == slot_ref[:, h : h + 1], 1.0, 0.0).astype(BF16)
            part = jnp.where(lane_group == g, product(chosen, back), part)
        gw = jnp.where(lane_group == h, tile_groups(part, MHEADS), gw)
    weights = weight_ref[...]
    gscore = jnp.transpose(weights * (gw - group_reduce(weights * gw, jnp.sum, 0.0)))
    turned[...] = gscore
    ready(picks_ref, keys_ref)
    ready.begin()
    copies = fetch(
        [(dn_any.at[3, a], dn.at[0]), (dn_any.at[4, a], dn.at[1]), (up_any.at[3, a], up.at[0]),
         (up_any.at[4, a], up.at[1]), (w_in_any.at[3], w.at[0]), (w_out_any.at[0], w.at[1])],
        sems,
    )
    span = rows_dev // NSUB

    def head(h, carry):
        def one(r, sums):
            pick = picks_ref[h, pl.ds(r, 1), :]
            value = turned[pl.ds(h * PICKS + r, 1), :]
            low = jnp.where((pick // NSUB) % span == iota((8, tokens), 0), value, 0.0)
            hit = (pick % NSUB).astype(jnp.int16) == lax.broadcasted_iota(jnp.int16, (NSUB, tokens), 0)
            return sums[0] + low, sums[1] + jnp.where(hit, value.astype(BF16), jnp.zeros((), BF16))

        start = (jnp.zeros((8, tokens), F32), jnp.zeros((NSUB, tokens), BF16))
        first, second = lax.fori_loop(0, PICKS, one, start, unroll=QUERY_UNROLL)
        origin = picks_ref[h, 0:1, :] // rows_dev
        place = iota((NSUB, tokens), 0)
        wide = jnp.concatenate([first[:span]] * (NSUB // span), axis=0)
        wide = jnp.where(place // span == origin, wide, 0.0)
        spots[h, 0] = wide.astype(BF16)
        spots[h, 1] = second
        return carry

    lax.fori_loop(0, MHEADS, head, 0)
    halves = [contract(spots[h, half], keys_ref[half, h]) for h in range(MHEADS) for half in range(2)]
    gquery = jnp.concatenate(halves, axis=1).astype(BF16)
    gquery_ref[...] = gquery
    ready.send(gquery_ref)
    ready()
    for copy in copies[:4]:
        copy.wait()
    granks = against(gquery, up[1]).astype(BF16)
    grank_ref[1] = granks
    extra = product(granks, dn[1])
    copies[4].wait()
    gnormed = against(gquery, w[0]) + extra + part_ref[...]
    middle = mid_ref[...]
    gmid = cot_ref[...].astype(F32) + norm_back(middle, inverse_norm(middle), gain_row(gain_ref), gnormed)
    gmid_ref[...] = gmid
    ready.send(gmid_ref)
    low = gmid.astype(BF16)
    granks = against(low, up[0]).astype(BF16)
    grank_ref[0] = granks
    ready.send(grank_ref)
    extra = product(granks, dn[0])
    copies[5].wait()
    go = against(low, w[1]) + extra
    row = lax.axis_index("seq") * tokens + iota((tokens, 1), 0)
    go = jnp.where(row < length[0], go, 0.0).astype(BF16)
    for s in range(groups):
        go_ref[s] = go[:, s * cols : (s + 1) * cols]


def place_columns(out_ref, row, values):
    groups, _, cols = out_ref.shape
    low = values.astype(BF16)
    for s in range(groups):
        out_ref[s, row : row + values.shape[0], :] = low[:, s * cols : (s + 1) * cols]


def factor_kernel(ready, att_ref, norm_ref, mixed_ref, gmid_ref, gquery_ref, ggate_ref, cot_ref, r35, r4, r6, g34, g5, g6, out_ref):
    ready()
    half = 4 * RANK
    sides = (
        (att_ref[...], gmid_ref[...].astype(BF16), r35[0], g34[0]),
        (norm_ref[...], gquery_ref[...], r4[...], g34[1]),
        (norm_ref[...], ggate_ref[...], r35[1], g5[...]),
        (mixed_ref[...], cot_ref[...], r6[...], g6[...]),
    )
    for j, (value, gy, rank, grank) in enumerate(sides):
        place_columns(out_ref, j * RANK, contract(grank, value))
        place_columns(out_ref, half + j * RANK, contract(rank, gy))


def late_kernel(ready, grads_ref, upgrad_ref, out_ref):
    seq, _, wide = grads_ref.shape
    cols = wide // 3
    tokens = grads_ref.shape[1] - RANK
    total = grads_ref[0, tokens:, :].astype(F32)
    for s in range(1, seq):
        total = total + grads_ref[s, tokens:, :].astype(F32)
    total = total.astype(BF16)
    for j in range(3):
        out_ref[j * RANK : (j + 1) * RANK, :] = total[:, j * cols : (j + 1) * cols]
    ready()
    out_ref[3 * RANK :, :] = upgrad_ref[...]


def entry_kernel(ready, adapter, grads_ref, x_ref, gain_ref, gmid_ref, w_any, dn_any, up_any, out_ref, w, gy, total, dn, up, sems):
    a = adapter[0]
    seq, _, wide = grads_ref.shape
    cols = wide // 3
    tokens = out_ref.shape[0]
    copies = fetch(
        [(up_any.at[j, a], up.at[pl.ds(RANK * j, RANK)]) for j in range(3)]
        + [(dn_any.at[j, a], dn.at[pl.ds(RANK * j, RANK)]) for j in range(3)]
        + [(w_any.at[j], w.at[j]) for j in range(3)],
        sems,
    )
    for j in range(3):
        for s in range(seq):
            gy[j, :, s * cols : (s + 1) * cols] = grads_ref[s, 0:tokens, j * cols : (j + 1) * cols]
    for copy in copies[:6]:
        copy.wait()
    place = iota((tokens, 3 * RANK), 1) // RANK
    granks = jnp.zeros((tokens, 3 * RANK), F32)
    for j in range(3):
        granks = jnp.where(place == j, against(gy[j], up[...]), granks)
    total[...] = product(granks.astype(BF16), dn[...])

    def one(j, carry):
        pltpu.make_async_copy(w_any.at[j], w.at[j], sems.at[6 + j]).wait()
        total[...] += against(gy[j], w[j])
        return carry

    lax.fori_loop(0, 3, one, 0)
    ready()
    x = x_ref[...].astype(F32)
    back = norm_back(x, inverse_norm(x), gain_row(gain_ref), total[...])
    out_ref[...] = (gmid_ref[...] + back).astype(BF16)


def sum_kernel(ready, parts_ref, out_ref):
    ready()
    total = parts_ref[0].astype(F32)
    for s in range(1, parts_ref.shape[0]):
        total = total + parts_ref[s].astype(F32)
    out_ref[...] = total.astype(BF16)


def stack_kernel(ready, *refs):
    for k in range(refs[-1].shape[0]):
        refs[-1][k] = refs[k][...]


def relative_marks(ids_ref, batches):
    plane = lax.axis_index("batch")
    absolute = adapter_marks(ids_ref, batches)
    marks = []
    for k in range(batches):
        source = lax.rem(plane + (batches - k), batches)
        mark = absolute[0]
        for b in range(1, batches):
            mark = jnp.where(source == b, absolute[b], mark)
        marks.append(mark)
    return marks


def adapter_marks(ids_ref, batches):
    step = ids_ref.shape[0] // batches
    return [ids_ref[b * step : b * step + 1, 0:1] // ADAPTER_STEP for b in range(batches)]


def spread_rows(parts, marks, runs, stage, sems):
    seq, batches = parts.shape[:2]
    for target, origin, base, count in runs:

        def put(i, target=target, origin=origin, base=base):
            return pltpu.make_async_copy(stage.at[base + i], target.at[origin + i], sems.at[base + i])

        def one(i, carry, put=put, base=base):
            start = pl.multiple_of((base + i) * RANK, RANK)
            rows = [
                jnp.concatenate([parts[s, k, pl.ds(start, RANK), :] for s in range(seq)], axis=1).astype(F32)
                for k in range(batches)
            ]
            for k in range(ADAPTERS):
                total = jnp.zeros(rows[0].shape, F32)
                for row, mark in zip(rows, marks, strict=True):
                    total = total + jnp.where(mark == k, row, 0.0)
                stage[base + i, k] = total
            put(i).start()
            return carry

        lax.fori_loop(0, count, one, 0)
    for target, origin, base, count in runs:
        for i in range(count):
            pltpu.make_async_copy(stage.at[base + i], target.at[origin + i], sems.at[base + i]).wait()


def spread_kernel(batches, ready, ids_ref, *refs):
    down_any, up_any, parts, stage, load_sems, sems = refs[-6:]
    seq = parts.shape[0]
    me = lax.axis_index("seq")
    copies = fetch([(refs[m % 2].at[m // 2], parts.at[me ^ m]) for m in range(seq)], load_sems)
    ready()
    marks = relative_marks(ids_ref, batches)
    for copy in copies:
        copy.wait()
    spread_rows(parts, marks, ((down_any, 3, 0, 4), (up_any, 3, 4, 4)), stage, sems)


def last_spread_kernel(batches, ready, ids_ref, down_in, up_in, *refs):
    down_any, up_any, parts, stage, load_sems, sems = refs[-6:]
    seq = parts.shape[0]
    me = lax.axis_index("seq")
    copies = fetch([(refs[m % 2].at[m // 2], parts.at[me ^ m]) for m in range(seq)], load_sems)
    ready()
    marks = relative_marks(ids_ref, batches)
    for copy in copies:
        copy.wait()
    spread_rows(parts, marks, ((down_any, 0, 0, 3), (up_any, 0, 3, 3)), stage, sems)


def along(values, axis, step, size):
    return lax.ppermute(values, axis, [(i, (i + step) % size) for i in range(size)])


def across(values, axis, mask, size):
    return lax.ppermute(values, axis, [(i, i ^ mask) for i in range(size)])


def to_pairs(values, axis, size):
    return [values] + [across(values, axis, m, size) for m in range(2, size, 2)]


def stacked(values, name, kind="V"):
    shape = shaped((len(values), *values[0].shape), values[0].dtype)
    return call(stack_kernel, name, "V" * len(values), [(kind, shape)], values)[0]


def exchange(values, axes):
    return lax.all_to_all(values, axes, split_axis=0, concat_axis=0, tiled=True)


def body(
    inputs, lengths, adapter_index, memory_picks, input_weights, output_weights, adapter_down, adapter_up,
    attention_gain, memory_gain, half_keys, memory_values, cotangent,
):
    both = ("batch", "seq")
    batches, seq = lax.axis_size("batch"), lax.axis_size("seq")
    owners = batches * seq
    tokens, width = inputs.shape[1], inputs.shape[2]
    rows, cols, half = tokens * seq, width // seq, width // 2
    rows_dev = memory_values.shape[0]
    capacity = 2 * tokens * MHEADS // owners
    groups = capacity // 8
    items = owners * capacity
    block = min(owners * 8, 256)
    small_block = RECALL_ROWS
    carried = 2 * groups * PICKS // cols * batches * 8
    x, cot = inputs[0], cotangent[0]
    down = jnp.swapaxes(adapter_down, 2, 3)
    gain_one, gain_two = attention_gain, memory_gain
    picks = jnp.transpose(memory_picks[0], (1, 2, 0))
    matrix = pltpu.VMEM((width, width), BF16)
    pair = pltpu.VMEM((2, width, width), BF16)
    triple = pltpu.VMEM((3, width, width), BF16)
    small = pltpu.VMEM((RANK, width), BF16)
    two_small = pltpu.VMEM((2, RANK, width), BF16)
    three_small = pltpu.VMEM((3 * RANK, width), BF16)
    token_low, token_wide = shaped((tokens, width), BF16), shaped((tokens, width), F32)
    token_rank, token_lanes = shaped((tokens, RANK), BF16), shaped((tokens, LANES), F32)
    fixed = functools.partial

    qkv, normed = call(
        qkv_kernel, "qkv", "MLLHHH",
        [("V", shaped((seq, tokens, 3 * cols), BF16)), ("S", shaped((tokens, width + LANES), BF16))],
        (adapter_index, x, gain_one, input_weights, down, adapter_up), [triple, three_small, three_small, sema(9)],
    )
    qkv_all = exchange(qkv, "seq").reshape(rows, 3 * cols)

    slot, slot_col, pick, *ids_out = call(
        fixed(route_kernel, rows_dev, owners), "route", "ML",
        [("S", shaped((8, tokens), I32)), ("S", shaped((tokens, tokens), I32)), ("S", shaped((tokens, LANES), I32)),
         *[("V", shaped((seq * 8 + 8, LANES), I32)) for _ in range(batches)]],
        (adapter_index, picks), [pltpu.VMEM((owners * 8, LANES), I32)],
    )
    ids_out = [ids_out[0]] + [along(ids_out[k], "batch", k, batches) for k in range(1, batches)]
    mix_grad, grank_six = call(
        mix_back_kernel, "mixback", "MLHHH", [("S", token_low), ("S", token_rank)],
        (adapter_index, cot, output_weights, down, adapter_up), [matrix, small, small, sema(3)],
    )

    qkv_all, ids_out, mix_grad = lax.optimization_barrier((qkv_all, ids_out, mix_grad))
    attended, lse, slots, qkv_saved = call(
        fixed(attend_kernel, groups, batches), "attend", "MV" + "V" * batches,
        [("V", shaped((seq, tokens + carried, cols), BF16)), ("S", shaped((8, rows), F32)),
         ("S", shaped((batches, 8, LANES), I32)), ("H", shaped((rows, 3 * cols), BF16))],
        (lengths, qkv_all, *ids_out),
        [pltpu.VMEM((rows, LANES), BF16), pltpu.VMEM((LANES, rows), BF16), pltpu.VMEM((LANES, rows), F32), sema(1)],
    )
    o_all = exchange(attended, "seq")
    normed, attended = lax.optimization_barrier((normed, attended))
    normed_all = to_pairs(normed, "seq", seq)

    left, right, same_two, ahead, sent, att, rank_pair, middle, normed_two, gate = call(
        middle_kernel, "middle", "MVLLLHHHH",
        [("V", shaped((tokens, half), BF16)), ("V", shaped((tokens, half), BF16)), ("V", token_low),
         ("V", shaped((width, width), BF16)), ("S", shaped((seq, carried, cols), BF16)), ("S", token_low),
         ("S", shaped((2, tokens, RANK), BF16)), ("S", token_wide), ("S", token_low), ("S", token_wide)],
        (adapter_index, o_all, x, gain_two, mix_grad, input_weights, output_weights, down, adapter_up),
        [pair, two_small, two_small, sema(7)],
    )
    lefts = [left] + [along(left, "batch", k, batches) for k in range(1, batches)]
    weight_out, rank_four, weights = call(
        fixed(scores_kernel, owners), "scores", "MVVLLLHH",
        [("V", shaped((owners * 8, LANES), BF16)), ("S", token_rank), ("S", token_lanes)],
        (adapter_index, same_two, ahead, pick, slot, half_keys, down, adapter_up), [small, small, sema(2)],
    )
    weight_out, normed_all = lax.optimization_barrier((weight_out, normed_all))
    weight_in = exchange(weight_out.reshape(owners, 8, LANES), both).reshape(owners * 8, LANES)
    right, lefts = lax.optimization_barrier((right, lefts))
    rights = [right] + [along(right, "batch", k, batches) for k in range(1, batches)]

    def scatter(parts, name):
        out = [("V", shaped((seq, batches, capacity, half), BF16))]
        return call(scatter_kernel, name, "L" + "V" * batches, out, (slots, *parts))[0]

    left_out = scatter(lefts, "scatterleft")
    normed_all, left_out = lax.optimization_barrier((normed_all, left_out))
    normed_all = stacked(normed_all, "pairsnorm", "S")
    sent, left_out = lax.optimization_barrier((sent, left_out))
    ids, index = call(
        fixed(prepare_kernel, groups, rows_dev, batches), "prepare", "L",
        [("S", shaped((owners * 8, LANES), I32)), ("H", shaped((items, rows_dev), jnp.int16))], (sent,),
        [pltpu.VMEM((2, LANES, rows_dev), jnp.int16), pltpu.VMEM((owners * 8 // LANES, LANES, LANES), I32), sema(2)],
    )
    left_out, weight_in, normed_all = lax.optimization_barrier((left_out, weight_in, normed_all))
    normed_all = (normed_all, across(normed_all, "seq", 1, seq))
    left_in = exchange(left_out, "seq").reshape(items, half)

    (sums,) = call(
        fixed(recall_kernel, groups), "recall", "VHH", [("H", shaped((seq, batches, capacity, width), BF16))],
        (weight_in, index, memory_values),
        [pltpu.VMEM((rows_dev, width), BF16), pltpu.VMEM((2, small_block, rows_dev), jnp.int16), pltpu.VMEM((2, small_block, rows_dev), BF16),
         pltpu.VMEM((2, small_block // 8, 8, width), BF16), sema(3 + 2 * (small_block // (8 * seq)))],
        flops=1 << 12,
    )
    sums, left_in = lax.optimization_barrier((sums, left_in))
    back = exchange(sums, "seq")

    def recall_back(part, name, grads, kind, dtype, *before):
        return call(
            fixed(recall_back_kernel, part, batches, groups), name, "L" + "L" * part + "VH",
            [(kind, shaped((owners * 8, LANES), dtype))], (ids, *before, grads, memory_values),
            [pltpu.VMEM((rows_dev, half), BF16), pltpu.VMEM((block, rows_dev), F32), sema(1)],
        )[0]

    rights, normed_all = lax.optimization_barrier((rights, normed_all))
    right_out = scatter(rights, "scatterright")
    found_left = recall_back(0, "recallleft", left_in, "S", F32)
    right_out, back, found_left = lax.optimization_barrier((right_out, back, found_left))
    right_in = exchange(right_out, "seq").reshape(items, half)
    pieces = call(
        gather_kernel, "gather", "LV", [("V", token_low) for _ in range(batches)], (slots, back),
    )
    pieces = [pieces[0]] + [along(pieces[k], "batch", batches - k, batches) for k in range(1, batches)]
    found = recall_back(1, "recallright", right_in, "V", BF16, found_left)
    found_back = exchange(found.reshape(owners, 8, LANES), both).reshape(owners * 8, LANES)

    mixed, grank_five, ggate, part = call(
        fixed(memory_kernel, batches), "memory", "MLL" + "V" * batches + "HHH",
        [("S", token_low), ("S", token_rank), ("S", token_low), ("V", token_wide)],
        (adapter_index, gate, mix_grad, *pieces, input_weights, down, adapter_up), [matrix, small, small, sema(3)],
    )

    go, gquery, grank_pair, gmid = call(
        fixed(query_kernel, owners, rows_dev), "query", "MMVLLLVDDDLHHHH",
        [("V", shaped((seq, tokens, cols), BF16)), ("S", token_low), ("S", shaped((2, tokens, RANK), BF16)), ("S", token_wide)],
        (lengths, adapter_index, found_back, slot_col, picks, weights, part, middle, cot, gain_two, half_keys,
         input_weights, output_weights, down, adapter_up),
        [pair, two_small, two_small, pltpu.VMEM((LANES, tokens), F32), pltpu.VMEM((MHEADS, 2, NSUB, tokens), BF16), sema(6)],
    )
    go_all = exchange(go, "seq").reshape(rows, cols)
    mixed, go = lax.optimization_barrier((mixed, go))
    output, rank_six = call(
        output_kernel, "output", "MLLHHH", [("S", token_low), ("S", token_rank)],
        (adapter_index, mixed, middle, output_weights, down, adapter_up), [matrix, small, small, sema(3)],
    )
    (factors,) = call(
        factor_kernel, "factors", "L" * 13, [("V", shaped((seq, 8 * RANK, cols), BF16))],
        (att, normed_two, mixed, gmid, gquery, ggate, cot, rank_pair, rank_four, rank_six, grank_pair, grank_five, grank_six),
    )
    factors, go_all = lax.optimization_barrier((factors, go_all))
    early_parts = exchange(factors, "seq")

    grads, up_grads = call(
        attend_back_kernel, "attendback", "MMLVLHHH",
        [("V", shaped((seq, tokens + RANK, 3 * cols), BF16)), ("S", shaped((3 * RANK, cols), BF16))],
        (lengths, adapter_index, qkv_saved, go_all, lse, *normed_all, adapter_up),
        [pltpu.VMEM((rows, LANES), F32), pltpu.VMEM((rows, LANES), F32), pltpu.VMEM((LANES, rows), F32),
         pltpu.VMEM((rows, LANES), BF16), pltpu.VMEM((LANES, rows), BF16), pltpu.VMEM((rows, LANES), BF16),
         pltpu.VMEM((rows, 3 * cols), BF16), pltpu.VMEM((rows, width + LANES), BF16), three_small, sema(3 + seq)],
    )
    grads, early_parts = lax.optimization_barrier((grads, early_parts))
    grads_all = exchange(grads, "seq")
    (some,) = call(sum_kernel, "sumearly", "V", [("V", shaped((8 * RANK, cols), BF16))], (early_parts,))
    some = [some] + [along(some, "batch", k, batches) for k in range(1, batches)]
    some = stacked(some, "stackearly")
    some = to_pairs(some, "seq", seq)
    (late_sum,) = call(late_kernel, "late", "VL", [("V", shaped((6 * RANK, cols), BF16))], (grads_all, up_grads))
    (grad_input,) = call(
        entry_kernel, "entry", "MVLLLHHH", [("S", token_low)],
        (adapter_index, grads_all, x, gain_one, gmid, input_weights, down, adapter_up),
        [triple, pltpu.VMEM((3, tokens, width), BF16), pltpu.VMEM((tokens, width), F32), three_small, three_small, sema(9)],
    )
    late_sums = [late_sum] + [along(late_sum, "batch", k, batches) for k in range(1, batches)]
    some = stacked(some, "pairsearly")
    late_sums, some, grad_input = lax.optimization_barrier((late_sums, some, grad_input))
    late_all = to_pairs(stacked(late_sums, "stacklate"), "seq", seq)
    some = (some, across(some, "seq", 1, seq))
    full = shaped((7, ADAPTERS, RANK, width), F32)
    grad_down, grad_up = call(
        fixed(spread_kernel, batches), "spread", "LVV", [("H", full), ("H", full)], (ids, *some),
        [pltpu.VMEM((seq, batches, 8 * RANK, cols), BF16), pltpu.VMEM((8, ADAPTERS, RANK, width), F32), sema(seq), sema(8)],
    )
    late_all, grad_down, grad_up = lax.optimization_barrier((late_all, grad_down, grad_up))
    late_all = stacked(late_all, "pairslate")
    late_all = (late_all, across(late_all, "seq", 1, seq))
    grad_down, grad_up = call(
        fixed(last_spread_kernel, batches), "lastspread", "LHHVV", [("H", full), ("H", full)],
        (ids, grad_down, grad_up, *late_all),
        [pltpu.VMEM((seq, batches, 6 * RANK, cols), BF16), pltpu.VMEM((6, ADAPTERS, RANK, width), F32), sema(seq), sema(6)],
        aliases={1: 0, 2: 1},
    )
    return (output[None], grad_input[None], jnp.swapaxes(grad_down, 2, 3), grad_up)


def solution(mesh):
    split = P("batch", "seq", None)
    return jax.shard_map(
        body,
        mesh=mesh,
        in_specs=(
            split, P("batch"), P("batch"), P("batch", "seq", None, None), P(), P(), P(), P(), P(), P(), P(),
            P(("batch", "seq"), None), split,
        ),
        out_specs=(split, split, P(), P()),
        check_vma=False,
    )
```

```python
import functools

import jax
import jax.numpy as jnp
from jax import lax
from jax.experimental import pallas as pl
from jax.experimental.pallas import tpu as pltpu
from jax.sharding import PartitionSpec as P

HEAD_DIM = 64
MHEADS = 4
KHALF = 128
NSUB = 256
PICKS = 32
ADAPTERS = 8
RANK = 16
LANES = 128
ADAPTER_STEP = 4096
QUERY_UNROLL = 8
RECALL_ROWS = 256
EPS = 1e-06
NEG = -1e30
F32 = jnp.float32
BF16 = jnp.bfloat16
I32 = jnp.int32
HBM = pl.BlockSpec(memory_space=pltpu.HBM)
SMEM = pl.BlockSpec(memory_space=pltpu.SMEM)
VMEM = pl.BlockSpec(memory_space=pltpu.VMEM)
MIB = 1 << 20


def product(left, right):
    return lax.dot_general(left, right, (((1,), (0,)), ((), ())), preferred_element_type=F32)


def against(left, right):
    return lax.dot_general(left, right, (((1,), (1,)), ((), ())), preferred_element_type=F32)


def contract(left, right):
    return lax.dot_general(left, right, (((0,), (0,)), ((), ())), preferred_element_type=F32)


def iota(shape, axis):
    return lax.broadcasted_iota(I32, shape, axis)


def short_pick(table, index):
    numbers = lax.GatherDimensionNumbers(
        offset_dims=(), collapsed_slice_dims=(1,), start_index_map=(1,), operand_batching_dims=(0,), start_indices_batching_dims=(0,)
    )
    return lax.gather(table, index[:, :, None], numbers, (1, 1), mode=lax.GatherScatterMode.PROMISE_IN_BOUNDS)


def lane_pick(table, index):
    return jnp.take_along_axis(table, index, axis=1, mode="promise_in_bounds")


def shaped(shape, dtype):
    return jax.ShapeDtypeStruct(shape, dtype)


class Stage:
    def __init__(self, loads, stores):
        self.loads, self.stores = loads, stores
        self.waited, self.begun = set(), set()
        for _, copy, later in loads:
            if not later:
                copy.start()

    def begin(self):
        for _, copy, later in self.loads:
            if later:
                copy.start()

    def __call__(self, *refs):
        for at, (ref, copy, _) in enumerate(self.loads):
            if at not in self.waited and (not refs or any(ref is one for one in refs)):
                self.waited.add(at)
                copy.wait()

    def send(self, *refs):
        for at, (ref, copy) in enumerate(self.stores):
            if at not in self.begun and (not refs or any(ref is one for one in refs)):
                self.begun.add(at)
                copy.start()

    def finish(self):
        self()
        self.send()
        for _, copy in self.stores:
            copy.wait()


def call(kernel, name, ins, outs, args, scratch=(), vmem=40, flops=1 << 12, moved=1 << 12, aliases=None):
    shapes = [(args[i].shape, args[i].dtype) for i, kind in enumerate(ins) if kind in "LD"]
    stored = [(out.shape, out.dtype) for kind, out in outs if kind == "S"]
    count_in, count_out, count_user = len(ins), len(outs), len(scratch)

    def wrapped(*refs):
        given, results = list(refs[:count_in]), list(refs[count_in : count_in + count_out])
        rest = list(refs[count_in + count_out :])
        user, buffers = rest[:count_user], rest[count_user:]
        loads, stores = [], []
        for i, kind in enumerate(ins):
            if kind in "LD":
                at = len(loads)
                copy = pltpu.make_async_copy(given[i], buffers[at], buffers[-1].at[at])
                loads.append((buffers[at], copy, kind == "D"))
                given[i] = buffers[at]
        for i, (kind, _) in enumerate(outs):
            if kind == "S":
                at = len(loads) + len(stores)
                stores.append((buffers[at], pltpu.make_async_copy(buffers[at], results[i], buffers[-1].at[at])))
                results[i] = buffers[at]
        stage = Stage(loads, stores)
        kernel(stage, *given, *results, *user)
        stage.finish()

    spaces = {"V": VMEM, "L": HBM, "D": HBM, "S": HBM, "H": HBM, "M": SMEM}
    autos = [pltpu.VMEM(*one) for one in shapes + stored]
    args = [
        pltpu.with_memory_space_constraint(one, pltpu.HBM) if kind in "LDH" else one
        for kind, one in zip(ins, args, strict=True)
    ]
    return pl.pallas_call(
        wrapped,
        name=name,
        out_shape=[pltpu.HBM(out.shape, out.dtype) if kind in "SH" else out for kind, out in outs],
        in_specs=[spaces[kind] for kind in ins],
        out_specs=[spaces[kind] for kind, _ in outs],
        input_output_aliases=aliases or {},
        scratch_shapes=list(scratch) + autos + ([sema(len(autos))] if autos else []),
        compiler_params=pltpu.CompilerParams(vmem_limit_bytes=vmem * MIB),
        cost_estimate=pl.CostEstimate(flops=flops, bytes_accessed=moved, transcendentals=0),
    )(*args)


def fetch(pairs, sems):
    copies = [
        pltpu.make_async_copy(source, target, sems.at[place])
        for place, (source, target) in enumerate(pairs)
    ]
    for copy in copies:
        copy.start()
    return copies


def sema(count):
    return pltpu.SemaphoreType.DMA((count,))


def gain_row(ref):
    return ref[...].astype(F32).reshape(1, ref.shape[0])


def inverse_norm(values):
    return lax.rsqrt(jnp.mean(values * values, axis=1, keepdims=True) + EPS)


def norm_back(values, inverse, scales, incoming):
    weighted = incoming * scales
    inner = jnp.mean(weighted * values, axis=1, keepdims=True)
    return weighted * inverse - values * inverse * inverse * inverse * inner


def qkv_kernel(ready, adapter, x_ref, gain_ref, w_any, dn_any, up_any, out_ref, norm_ref, w, dn, up, sems):
    groups, tokens, wide = out_ref.shape
    cols = wide // 3
    a = adapter[0]
    copies = fetch(
        [(dn_any.at[j, a], dn.at[pl.ds(RANK * j, RANK)]) for j in range(3)]
        + [(up_any.at[j, a], up.at[pl.ds(RANK * j, RANK)]) for j in range(3)]
        + [(w_any.at[0], w.at[0])],
        sems,
    )
    copies += [pltpu.make_async_copy(w_any.at[j], w.at[j], sems.at[6 + j]) for j in (1, 2)]
    ready()
    copies[7].start()
    copies[8].start()
    x = x_ref[...].astype(F32)
    normed = (x * inverse_norm(x) * gain_row(gain_ref)).astype(BF16)
    width = normed.shape[1]
    norm_ref[:, :width] = normed
    for copy in copies[:6]:
        copy.wait()
    ranks = against(normed, dn[...])
    norm_ref[:, width:] = widen(ranks).astype(BF16)
    ready.send(norm_ref)
    place = iota((tokens, 3 * RANK), 1) // RANK
    for j in range(3):
        own = jnp.where(place == j, ranks, 0.0).astype(BF16)
        extra = product(own, up[...])
        copies[6 + j].wait()
        result = (product(normed, w[j]) + extra).astype(BF16)
        for s in range(groups):
            out_ref[s, :, j * cols : (j + 1) * cols] = result[:, s * cols : (s + 1) * cols]


def mix_back_kernel(ready, adapter, cot_ref, w_any, dn_any, up_any, grad_ref, rank_ref, w, dn, up, sems):
    a = adapter[0]
    copies = fetch([(up_any.at[6, a], up), (dn_any.at[6, a], dn), (w_any.at[1], w)], sems)
    ready()
    gy = cot_ref[...]
    copies[0].wait()
    ranks = against(gy, up[...]).astype(BF16)
    rank_ref[...] = ranks
    copies[1].wait()
    extra = product(ranks, dn[...])
    copies[2].wait()
    grad_ref[...] = (against(gy, w[...]) + extra).astype(BF16)


def route_kernel(rows_dev, owners, ready, adapter, picks_ref, slot_ref, slot_col_ref, pick_ref, *ids_refs):
    ready()
    heads, picks, tokens = picks_ref.shape
    capacity = 2 * heads * tokens // owners
    groups = capacity // 8
    visits = heads * tokens
    owner = jnp.concatenate([picks_ref[h, 0:1, :] for h in range(heads)], axis=1) // rows_dev
    hot = jnp.where(iota((owners, visits), 0) == owner, 1.0, 0.0)
    before = jnp.where(iota((visits, visits), 0) < iota((visits, visits), 1), 1.0, 0.0).astype(BF16)
    counts = product(hot.astype(BF16), before)
    within = jnp.sum(hot * counts, axis=0, keepdims=True).astype(I32)
    slot = owner * capacity + within
    rows = [slot[:, h * tokens : (h + 1) * tokens] for h in range(heads)]
    stacked = jnp.concatenate(rows + [jnp.full((8 - heads, tokens), -1, I32)], axis=0)
    slot_ref[...] = stacked
    tall = jnp.concatenate([stacked, jnp.full((tokens - 8, tokens), -1, I32)], axis=0)
    slot_col_ref[...] = jnp.transpose(tall)
    packed = jnp.concatenate([picks_ref[h] for h in range(heads)], axis=0)
    by_token = jnp.transpose(packed)
    pick_ref[...] = by_token
    local = by_token % rows_dev
    lanes = iota((tokens, LANES), 1)
    total = jnp.zeros((owners * 8, LANES), F32)
    out_lane = iota((owners * 8, LANES), 1) // PICKS
    place = iota((owners * 8, tokens), 0)
    base = (place // 8) * capacity + place % 8
    for g in range(groups):
        high = jnp.zeros((owners * 8, LANES), F32)
        low = jnp.zeros((owners * 8, LANES), F32)
        for h in range(heads):
            chosen = jnp.where(base + g * 8 == rows[h], 1.0, 0.0).astype(BF16)
            own = jnp.where(lanes // PICKS == h, local, 0)
            own = tile_groups(own.astype(F32), heads).astype(I32)
            high = high + product(chosen, (own // 256).astype(F32).astype(BF16))
            low = low + product(chosen, (own % 256).astype(F32).astype(BF16))
        total = jnp.where(out_lane == g, high * 256.0 + low, total)
    batches = len(ids_refs) - 1
    part = owners * 8 // batches
    ids_refs[-1][...] = total.astype(I32) + adapter[0] * ADAPTER_STEP
    for k in range(batches):
        target = lax.rem(lax.axis_index("batch") + k, batches)
        ids_refs[k][0:part, :] = ids_refs[-1][pl.ds(pl.multiple_of(target * part, part), part), :]
        ids_refs[k][part:, :] = stacked


def tile_groups(values, count):
    total = values
    for turn in range(1, count):
        total = total + pltpu.roll(values, turn * PICKS, 1)
    return total


def prepare_kernel(groups, rows_dev, batches, ready, sent_ref, ids_ref, index_any, stage, turned, sems):
    ready()
    seq, _, cols = sent_ref.shape
    lanes = groups * PICKS
    chunks = 2 * lanes // cols
    for k in range(batches):
        source = lax.rem(lax.axis_index("batch") + (batches - k), batches)
        for s in range(seq):
            both = [
                sent_ref[s, (chunk * batches + k) * 8 : (chunk * batches + k + 1) * 8, :].astype(F32)
                for chunk in range(chunks)
            ]
            both = jnp.concatenate(both, axis=1).astype(I32)
            ids = widen(both[:, :lanes] * 256 + both[:, lanes:])
            ids_ref[pl.ds(pl.multiple_of((source * seq + s) * 8, 8), 8), :] = ids
    ready.send(ids_ref)
    places = ids_ref.shape[0]
    chunks = rows_dev // LANES
    high_rows = max(8, chunks)
    steps = groups * (places // LANES)
    for k in range(places // LANES):
        turned[k] = jnp.transpose(ids_ref[k * LANES : (k + 1) * LANES, :] & (ADAPTER_STEP - 1))

    def put(step, slot):
        target = index_any.at[pl.ds(pl.multiple_of(step * LANES, LANES), LANES)]
        return pltpu.make_async_copy(stage.at[slot], target, sems.at[slot])

    def one(step, carry):
        k, g = lax.rem(step, places // LANES), step // (places // LANES)
        slot = lax.rem(step, 2)
        mask = jnp.zeros((LANES, LANES), I32)
        highs = jnp.zeros((high_rows, LANES), I32)
        for r in range(PICKS):
            bit = (1 << r) if r < 31 else -(1 << 31)
            row = turned[k, pl.ds(g * PICKS + r, 1), :]
            mask = mask | jnp.where(row & 127 == iota((LANES, LANES), 0), bit, 0)
            highs = highs | jnp.where(row >> 7 == iota((high_rows, LANES), 0), bit, 0)

        @pl.when(step >= 2)
        def _():
            put(step - 2, slot).wait()

        for c in range(chunks):
            index = 31 - lax.clz(mask & highs[c : c + 1, :])
            stage[slot, :, c * LANES : (c + 1) * LANES] = jnp.transpose(index.astype(jnp.int16))
        put(step, slot).start()
        return carry

    lax.fori_loop(0, steps, one, 0)
    for step in range(max(0, steps - 2), steps):
        put(step, step % 2).wait()


def recall_kernel(groups, ready, weight_ref, index_any, mem_any, out_any, mem, index, dense, staged, sems):
    places = weight_ref.shape[0]
    rows_dev = mem.shape[0]
    chunks = rows_dev // LANES
    block = dense.shape[1]
    per_group = places // block
    blocks = groups * per_group
    seq = out_any.shape[0]
    planes = block // (8 * seq)

    def load(b, slot):
        source = index_any.at[pl.ds(pl.multiple_of(b * block, block), block)]
        return pltpu.make_async_copy(source, index.at[slot], sems.at[1 + slot])

    load(0, 0).start()
    copy = pltpu.make_async_copy(mem_any, mem, sems.at[0])
    copy.start()

    def gather(b, side):
        load(b, side).wait()

        @pl.when(b + 1 < blocks)
        def _():
            load(b + 1, 1 - side).start()

        pick(b, side)

    def pick(b, side):
        g, k = b // per_group, lax.rem(b, per_group)
        for start in range(0, block, 16):
            weights = weight_ref[pl.ds(pl.multiple_of(k * block + start, 16), 16), :]
            shift = jnp.full((16, LANES), g * PICKS, I32).astype(jnp.int16)
            for c in range(chunks):
                at = index[side, start : start + 16, c * LANES : (c + 1) * LANES]
                value = short_pick(weights, (at + shift) & jnp.int16(127))
                dense[side, start : start + 16, c * LANES : (c + 1) * LANES] = jnp.where(at >= 0, value, jnp.zeros((), BF16))

    def save(b, side):
        g, k = b // per_group, lax.rem(b, per_group)
        return [
            pltpu.make_async_copy(
                staged.at[side, pl.ds(i * seq, seq)],
                out_any.at[:, k * planes + i, pl.ds(pl.multiple_of(g * 8, 8), 8), :],
                sems.at[3 + side * planes + i],
            )
            for i in range(planes)
        ]

    def multiply(b, side):
        result = product(dense[side], mem[...]).astype(BF16)

        @pl.when(b >= 2)
        def _():
            for one in save(b - 2, side):
                one.wait()

        staged[side] = result.reshape(block // 8, 8, result.shape[1])
        for one in save(b, side):
            one.start()

    gather(0, 0)
    copy.wait()

    def whole(i, carry):
        gather(2 * i + 1, 1)
        multiply(2 * i, 0)

        @pl.when(2 * i + 2 < blocks)
        def _():
            load(2 * i + 2, 0).wait()
            load(2 * i + 3, 1).start()

        pick(jnp.minimum(2 * i + 2, blocks - 1), 0)
        multiply(2 * i + 1, 1)
        return carry

    lax.fori_loop(0, blocks // 2, whole, 0)
    for b in range(blocks - 2, blocks):
        for one in save(b, b % 2):
            one.wait()


def recall_back_kernel(part, batches, groups, ready, ids_ref, *refs):
    before_ref = refs[0] if part else None
    grad_ref, mem_any, out_ref, mem, scores, sems = refs[part:]
    items, half = grad_ref.shape
    seq = items // (batches * groups * 8)
    rows_dev = mem.shape[0]
    capacity = groups * 8
    chunks = rows_dev // LANES
    block = scores.shape[0]
    per_block = block // capacity
    blocks = items // block
    copies = fetch([(mem_any.at[:, pl.ds(part * half, half)], mem)], sems)
    ready()
    copies[0].wait()

    def whole(b, outer):
        scores[...] = against(grad_ref[pl.ds(pl.multiple_of(b * block, block), block), :], mem[...]).astype(BF16)
        step = min(2, groups) * 8

        lane_group = iota((8, LANES), 1) // PICKS
        for local in range(per_block):
            sender = b * per_block + local
            spot = lax.rem(sender, batches) * seq + sender // batches
            start = pl.multiple_of(spot * 8, 8)
            ids = ids_ref[pl.ds(start, 8), :] & (ADAPTER_STEP - 1)
            low = ids & 127
            high = ids >> 7
            total = before_ref[pl.ds(start, 8), :] if part else jnp.zeros((8, LANES), F32)
            for g in range(0, groups, 2):
                key = jnp.concatenate([jnp.where(lane_group == g + i, high, -1) for i in range(step // 8)], axis=0)
                index = jnp.concatenate([low] * (step // 8), axis=0)
                key, index = key.astype(jnp.int16), index.astype(jnp.int16)
                here = jnp.zeros((step, LANES), BF16)
                row = local * capacity + g * 8
                for c in range(chunks):
                    found = scores[row : row + step, c * LANES : (c + 1) * LANES]
                    here = jnp.where(key == jnp.int16(c), short_pick(found, index), here)
                here = here.astype(F32)
                for i in range(step // 8):
                    total = total + here[i * 8 : (i + 1) * 8]
            out_ref[pl.ds(start, 8), :] = total.astype(out_ref.dtype)
        return outer

    lax.fori_loop(0, blocks, whole, 0)


def head_parts(values, h, spare):
    lane = iota(values.shape, 1)
    return jnp.where(lane // HEAD_DIM == h, values, jnp.where(lane == (1 - h) * HEAD_DIM, spare, 0.0)).astype(BF16)


def widen(values):
    if values.shape[1] == LANES:
        return values
    return jnp.concatenate([values, jnp.zeros((values.shape[0], LANES - values.shape[1]), values.dtype)], axis=1)


def attend_kernel(groups, batches, ready, length, qkv_ref, *refs):
    o_ref, lse_ref, slots_ref, saved_any, parts, values_t, mixed, sems = refs[batches:]
    ready()
    saving = pltpu.make_async_copy(qkv_ref, saved_any, sems.at[0])
    saving.start()
    rows, wide = qkv_ref.shape
    cols = wide // 3
    seq = o_ref.shape[0]
    lanes = groups * PICKS
    for k in range(batches):
        slots_ref[k] = refs[k][seq * 8 :, :]
    ready.send(slots_ref)
    for s in range(seq):
        ids = jnp.concatenate([refs[k][s * 8 : (s + 1) * 8, :lanes] for k in range(batches)], axis=0)
        both = jnp.concatenate([ids // 256, ids % 256], axis=1).astype(F32).astype(BF16)
        for chunk in range(2 * lanes // cols):
            start = rows // seq + chunk * batches * 8
            o_ref[s, start : start + batches * 8, :] = both[:, chunk * cols : (chunk + 1) * cols]
    heads = cols // HEAD_DIM
    size = min(256, rows)
    valid = length[0]
    bias = jnp.where(iota((rows, LANES), 0) < valid, 0.0, NEG)
    keys = widen(qkv_ref[:, cols : 2 * cols].astype(F32))
    values_t[...] = jnp.transpose(widen(qkv_ref[:, 2 * cols :].astype(F32))).astype(BF16)
    lse_ref[...] = jnp.zeros_like(lse_ref)

    def one(h, carry):
        parts[...] = head_parts(keys, h, bias)
        for i in range(rows // size):
            first, last = i * size, (i + 1) * size
            queries = widen(qkv_ref[first:last, 0:cols].astype(F32)) * (HEAD_DIM**-0.5)
            query = head_parts(queries, h, 1.0)
            near = against(parts[first:last], query)
            near = jnp.where(iota((size, size), 0) <= iota((size, size), 1), near, NEG)
            high = jnp.max(near, axis=0, keepdims=True)
            if i:
                far = against(parts[:first], query)
                high = jnp.maximum(high, jnp.max(far, axis=0, keepdims=True))
            near = jnp.exp(near - high)
            summed = jnp.sum(near, axis=0, keepdims=True)
            result = product(values_t[:, first:last], near.astype(BF16))
            if i:
                far = jnp.exp(far - high)
                summed = summed + jnp.sum(far, axis=0, keepdims=True)
                result = result + product(values_t[:, :first], far.astype(BF16))
            lse_ref[pl.ds(h, 1), first:last] = high + jnp.log(summed)
            own = iota((LANES, size), 0) // HEAD_DIM == h
            mixed[:, first:last] = jnp.where(own, result / summed, mixed[:, first:last])
        return carry

    mixed[...] = jnp.zeros_like(mixed)
    lax.fori_loop(0, heads, one, 0)
    ready.send(lse_ref)
    tokens = rows // seq
    for s in range(seq):
        first = s * tokens
        kept = jnp.where(first + iota((LANES, tokens), 1) < valid, mixed[:, first : first + tokens], 0.0)
        o_ref[s, 0:tokens, :] = jnp.transpose(kept)[:, :cols].astype(BF16)
    saving.wait()


def attend_back_kernel(
    ready, length, adapter, qkv_ref, go_ref, lse_ref, even_ref, odd_ref, up_any,
    out_ref, upgrad_ref, dk, dv, dq, parts, keys_t, values, grads_all, norms, up, sems,
):
    a = adapter[0]
    seq = out_ref.shape[0]
    me = lax.axis_index("seq")
    tokens = even_ref.shape[1]
    copies = fetch(
        [(up_any.at[j, a], up.at[pl.ds(RANK * j, RANK)]) for j in range(3)]
        + [
            ((even_ref, odd_ref)[m % 2].at[m // 2], norms.at[pl.ds(pl.multiple_of((me ^ m) * tokens, tokens), tokens)])
            for m in range(seq)
        ],
        sems,
    )
    ready()
    rows, wide = qkv_ref.shape
    cols = wide // 3
    heads = cols // HEAD_DIM
    size = min(256, rows)
    valid = length[0]
    scaling = HEAD_DIM**-0.5
    bias = jnp.where(iota((rows, LANES), 0) < valid, 0.0, NEG)
    keys = widen(qkv_ref[:, cols : 2 * cols].astype(F32))
    keys_t[...] = jnp.transpose(keys).astype(BF16)
    values[...] = widen(qkv_ref[:, 2 * cols :])
    dk[...] = jnp.zeros_like(dk)
    dv[...] = jnp.zeros_like(dv)
    dq[...] = jnp.zeros_like(dq)

    def one(h, carry):
        parts[...] = head_parts(keys, h, bias)
        for i in range(rows // size):
            first, last = i * size, (i + 1) * size
            queries = widen(qkv_ref[first:last, 0:cols].astype(F32)) * scaling
            grads = widen(go_ref[first:last, :].astype(F32))
            query = head_parts(queries, h, 1.0)
            plain = head_parts(queries, h, 0.0)
            grad = head_parts(grads, h, 0.0)
            lse = lse_ref[pl.ds(h, 1), first:last]
            near = against(parts[first:last], query)
            near = jnp.where(iota((size, size), 0) <= iota((size, size), 1), near, NEG)
            near = jnp.exp(near - lse)
            near_gp = against(values[first:last], grad)
            delta = jnp.sum(near * near_gp, axis=0, keepdims=True)
            if i:
                far = jnp.exp(against(parts[:first], query) - lse)
                far_gp = against(values[:first], grad)
                delta = delta + jnp.sum(far * far_gp, axis=0, keepdims=True)
            near_gs = (near * (near_gp - delta)).astype(BF16)
            result = product(keys_t[:, first:last], near_gs)
            dk[first:last] += product(near_gs, plain)
            dv[first:last] += product(near.astype(BF16), grad)
            if i:
                far_gs = (far * (far_gp - delta)).astype(BF16)
                result = result + product(keys_t[:, :first], far_gs)
                dk[:first] += product(far_gs, plain)
                dv[:first] += product(far.astype(BF16), grad)
            own = iota((LANES, size), 0) // HEAD_DIM == h
            dq[:, first:last] = jnp.where(own, result, dq[:, first:last])
        return carry

    for h in range(heads):
        one(h, 0)
    grads_all[:, 0:cols] = (jnp.transpose(dq[...]) * scaling)[:, :cols].astype(BF16)
    grads_all[:, cols : 2 * cols] = dk[:, :cols].astype(BF16)
    grads_all[:, 2 * cols :] = dv[:, :cols].astype(BF16)
    for s in range(seq):
        out_ref[s, 0:tokens, :] = grads_all[s * tokens : (s + 1) * tokens, :]
    for copy in copies:
        copy.wait()
    own = jnp.zeros((3 * RANK, cols), F32)
    for s in range(seq):
        own = jnp.where(me == s, up[:, s * cols : (s + 1) * cols].astype(F32), own)
    own = own.astype(BF16)
    place = iota((rows, 3 * RANK), 1) // RANK
    granks = jnp.zeros((rows, 3 * RANK), F32)
    for j in range(3):
        granks = jnp.where(place == j, against(grads_all[:, j * cols : (j + 1) * cols], own), granks)
    width = norms.shape[1] - LANES
    down = contract(granks.astype(BF16), norms[:, :width]).astype(BF16)
    both = contract(norms[:, width:], grads_all[...]).astype(BF16)
    for j in range(3):
        row = j * RANK
        upgrad_ref[row : row + RANK, :] = both[row : row + RANK, j * cols : (j + 1) * cols]
        for s in range(seq):
            out_ref[s, tokens:, j * cols : (j + 1) * cols] = down[row : row + RANK, s * cols : (s + 1) * cols]


def pick_chosen(tables, index):
    tokens = index.shape[0]
    low = index & 127
    key = (index >> 7) + (iota((tokens, LANES), 1) // PICKS) * (NSUB // LANES)
    total = jnp.zeros((tokens, LANES), F32)
    for h in range(MHEADS):
        for c in range(NSUB // LANES):
            found = lane_pick(tables[h][:, c * LANES : (c + 1) * LANES], low)
            total = jnp.where(key == h * (NSUB // LANES) + c, found, total)
    return total


def group_reduce(values, reducer, fill):
    group = iota(values.shape, 1) // PICKS
    total = jnp.zeros(values.shape, F32)
    for h in range(MHEADS):
        one = reducer(jnp.where(group == h, values, fill), axis=1, keepdims=True)
        total = jnp.where(group == h, one, total)
    return total


def middle_kernel(
    ready, adapter, o_ref, x_ref, gain_ref, mix_ref, w_in_any, w_out_any, dn_any, up_any,
    left_ref, right_ref, same_ref, ahead_ref, sent_ref, att_ref, rank_ref, mid_ref, norm_ref, gate_ref, w, dn, up, sems,
):
    groups = o_ref.shape[0]
    a = adapter[0]
    copies = fetch(
        [(dn_any.at[3, a], dn.at[0]), (dn_any.at[5, a], dn.at[1]), (up_any.at[3, a], up.at[0]), (up_any.at[5, a], up.at[1]),
         (w_out_any.at[0], w.at[0]), (w_in_any.at[4], w.at[1]), (w_in_any.at[3], ahead_ref)],
        sems,
    )
    tokens = att_ref.shape[0]
    attended = jnp.concatenate([o_ref[s, 0:tokens, :] for s in range(groups)], axis=1)
    sent_ref[...] = o_ref[:, tokens:, :]
    ready.send(sent_ref)
    att_ref[...] = attended
    ready.send(att_ref)
    for copy in copies[:4]:
        copy.wait()
    rank_three = against(attended, dn[0]).astype(BF16)
    extra = product(rank_three, up[0])
    copies[4].wait()
    ready(x_ref, gain_ref)
    middle = x_ref[...].astype(F32) + (product(attended, w[0]) + extra)
    mid_ref[...] = middle
    normed = (middle * inverse_norm(middle) * gain_row(gain_ref)).astype(BF16)
    norm_ref[...] = normed
    same_ref[...] = normed
    ready.send(mid_ref, norm_ref)
    rank_five = against(normed, dn[1]).astype(BF16)
    rank_ref[0] = rank_three
    rank_ref[1] = rank_five
    extra = product(rank_five, up[1])
    copies[5].wait()
    gate = product(normed, w[1]) + extra
    gate_ref[...] = gate
    ready.send(rank_ref, gate_ref)
    ready(mix_ref)
    memory_grad = (mix_ref[...].astype(F32) * (gate * jax.nn.sigmoid(gate))).astype(BF16)
    half = left_ref.shape[1]
    left_ref[...] = memory_grad[:, :half]
    right_ref[...] = memory_grad[:, half:]
    copies[6].wait()


def scores_kernel(
    owners, ready, adapter, normed_ref, w_ref, picks_ref, slot_ref, keys_ref, dn_any, up_any,
    send_ref, rank_ref, weight_ref, dn, up, sems,
):
    a = adapter[0]
    copies = fetch([(dn_any.at[4, a], dn), (up_any.at[4, a], up)], sems)
    normed = normed_ref[...]
    copies[0].wait()
    ranks = against(normed, dn[...]).astype(BF16)
    rank_ref[...] = ranks
    copies[1].wait()
    extra = product(ranks, up[...])
    query = (product(normed, w_ref[...]) + extra).astype(BF16)
    ready()
    ready.send(rank_ref)
    first, second = [], []
    for h in range(MHEADS):
        base = 2 * h * KHALF
        first.append(against(query[:, base : base + KHALF], keys_ref[0, h]))
        second.append(against(query[:, base + KHALF : base + 2 * KHALF], keys_ref[1, h]))
    picks = picks_ref[...]
    scores = pick_chosen(first, picks // NSUB) + pick_chosen(second, picks % NSUB)
    exponent = jnp.exp(scores - group_reduce(scores, jnp.max, NEG))
    weights = exponent / group_reduce(exponent, jnp.sum, 0.0)
    weight_ref[...] = weights
    ready.send(weight_ref)
    send_ref[...] = to_slots(weights, slot_ref, owners).astype(BF16)


def to_slots(weights, slot_ref, owners):
    tokens = weights.shape[0]
    capacity = 2 * MHEADS * tokens // owners
    lane_group = iota((tokens, LANES), 1) // PICKS
    tiled = [
        tile_groups(jnp.where(lane_group == h, weights, 0.0), MHEADS).astype(BF16) for h in range(MHEADS)
    ]
    place = iota((owners * 8, tokens), 0)
    base = (place // 8) * capacity + place % 8
    out_group = iota((owners * 8, LANES), 1) // PICKS
    total = jnp.zeros((owners * 8, LANES), F32)
    for g in range(capacity // 8):
        part = jnp.zeros((owners * 8, LANES), F32)
        for h in range(MHEADS):
            chosen = jnp.where(base + g * 8 == slot_ref[h : h + 1, :], 1.0, 0.0).astype(BF16)
            part = part + product(chosen, tiled[h])
        total = jnp.where(out_group == g, part, total)
    return total


def plane_hits(slots_ref, k, plane, seq, capacity):
    tokens = slots_ref.shape[2]
    place = plane * (seq * capacity) + iota((seq * capacity, tokens), 0)
    chosen = jnp.zeros((seq * capacity, tokens), F32)
    for h in range(MHEADS):
        chosen = jnp.where(place == slots_ref[k, h : h + 1, :], 1.0, chosen)
    return chosen.astype(BF16)


def scatter_kernel(ready, slots_ref, *refs):
    ready()
    out_ref = refs[-1]
    seq, batches, capacity, wide = out_ref.shape
    plane = lax.axis_index("batch")
    for k in range(batches):
        chosen = plane_hits(slots_ref, k, plane, seq, capacity)
        rows = product(chosen, refs[k][...]).astype(BF16)
        source = lax.rem(plane + (batches - k), batches)
        out_ref[:, pl.ds(source, 1)] = rows.reshape(seq, 1, capacity, wide)


def gather_kernel(ready, slots_ref, back_ref, *refs):
    ready()
    seq, batches, capacity, wide = back_ref.shape
    plane = lax.axis_index("batch")
    for k in range(batches):
        chosen = plane_hits(slots_ref, k, plane, seq, capacity)
        source = lax.rem(plane + (batches - k), batches)
        rows = back_ref[:, pl.ds(source, 1)].reshape(seq * capacity, wide)
        refs[k][...] = contract(chosen, rows).astype(BF16)


def memory_kernel(batches, ready, adapter, gate_ref, mix_ref, *refs):
    w_in_any, dn_any, up_any, mixed_ref, grank_ref, ggate_ref, part_ref, w, dn, up, sems = refs[batches:]
    a = adapter[0]
    copies = fetch([(dn_any.at[5, a], dn), (up_any.at[5, a], up), (w_in_any.at[4], w)], sems)
    ready()
    memory = refs[0][...].astype(F32)
    for k in range(1, batches):
        memory = memory + refs[k][...].astype(F32)
    gate = gate_ref[...]
    sigmoid = jax.nn.sigmoid(gate)
    mixed_ref[...] = (memory * (gate * sigmoid)).astype(BF16)
    ggate = (mix_ref[...].astype(F32) * memory * sigmoid * (1.0 + gate * (1.0 - sigmoid))).astype(BF16)
    ggate_ref[...] = ggate
    for copy in copies[:2]:
        copy.wait()
    granks = against(ggate, up[...]).astype(BF16)
    grank_ref[...] = granks
    extra = product(granks, dn[...])
    copies[2].wait()
    ready.send(mixed_ref, ggate_ref, grank_ref)
    part_ref[...] = against(ggate, w[...]) + extra


def output_kernel(ready, adapter, mixed_ref, mid_ref, w_out_any, dn_any, up_any, out_ref, rank_ref, w, dn, up, sems):
    a = adapter[0]
    copies = fetch([(dn_any.at[6, a], dn), (up_any.at[6, a], up), (w_out_any.at[1], w)], sems)
    ready()
    mixed = mixed_ref[...]
    for copy in copies[:2]:
        copy.wait()
    ranks = against(mixed, dn[...]).astype(BF16)
    rank_ref[...] = ranks
    extra = product(ranks, up[...])
    copies[2].wait()
    out_ref[...] = (mid_ref[...] + (product(mixed, w[...]) + extra)).astype(BF16)


def query_kernel(
    owners, rows_dev, ready, length, adapter, back_ref, slot_ref, picks_ref, weight_ref, part_ref, mid_ref, cot_ref, gain_ref,
    keys_ref, w_in_any, w_out_any, dn_any, up_any,
    go_ref, gquery_ref, grank_ref, gmid_ref, w, dn, up, turned, spots, sems,
):
    groups, tokens, cols = go_ref.shape
    a = adapter[0]
    ready(slot_ref, weight_ref)
    capacity = 2 * MHEADS * tokens // owners
    slots = iota((tokens, owners * 8), 1)
    base = (slots // 8) * capacity + slots % 8
    lane_group = iota((tokens, LANES), 1) // PICKS
    back = back_ref[...]
    gw = jnp.zeros((tokens, LANES), F32)
    for h in range(MHEADS):
        part = jnp.zeros((tokens, LANES), F32)
        for g in range(capacity // 8):
            chosen = jnp.where(base + g * 8 == slot_ref[:, h : h + 1], 1.0, 0.0).astype(BF16)
            part = jnp.where(lane_group == g, product(chosen, back), part)
        gw = jnp.where(lane_group == h, tile_groups(part, MHEADS), gw)
    weights = weight_ref[...]
    gscore = jnp.transpose(weights * (gw - group_reduce(weights * gw, jnp.sum, 0.0)))
    turned[...] = gscore
    ready(picks_ref, keys_ref)
    ready.begin()
    copies = fetch(
        [(dn_any.at[3, a], dn.at[0]), (dn_any.at[4, a], dn.at[1]), (up_any.at[3, a], up.at[0]),
         (up_any.at[4, a], up.at[1]), (w_in_any.at[3], w.at[0]), (w_out_any.at[0], w.at[1])],
        sems,
    )
    span = rows_dev // NSUB

    def head(h, carry):
        def one(r, sums):
            pick = picks_ref[h, pl.ds(r, 1), :]
            value = turned[pl.ds(h * PICKS + r, 1), :]
            low = jnp.where((pick // NSUB) % span == iota((8, tokens), 0), value, 0.0)
            hit = (pick % NSUB).astype(jnp.int16) == lax.broadcasted_iota(jnp.int16, (NSUB, tokens), 0)
            return sums[0] + low, sums[1] + jnp.where(hit, value.astype(BF16), jnp.zeros((), BF16))

        start = (jnp.zeros((8, tokens), F32), jnp.zeros((NSUB, tokens), BF16))
        first, second = lax.fori_loop(0, PICKS, one, start, unroll=QUERY_UNROLL)
        origin = picks_ref[h, 0:1, :] // rows_dev
        place = iota((NSUB, tokens), 0)
        wide = jnp.concatenate([first[:span]] * (NSUB // span), axis=0)
        wide = jnp.where(place // span == origin, wide, 0.0)
        spots[h, 0] = wide.astype(BF16)
        spots[h, 1] = second
        return carry

    lax.fori_loop(0, MHEADS, head, 0)
    halves = [contract(spots[h, half], keys_ref[half, h]) for h in range(MHEADS) for half in range(2)]
    gquery = jnp.concatenate(halves, axis=1).astype(BF16)
    gquery_ref[...] = gquery
    ready.send(gquery_ref)
    ready()
    for copy in copies[:4]:
        copy.wait()
    granks = against(gquery, up[1]).astype(BF16)
    grank_ref[1] = granks
    extra = product(granks, dn[1])
    copies[4].wait()
    gnormed = against(gquery, w[0]) + extra + part_ref[...]
    middle = mid_ref[...]
    gmid = cot_ref[...].astype(F32) + norm_back(middle, inverse_norm(middle), gain_row(gain_ref), gnormed)
    gmid_ref[...] = gmid
    ready.send(gmid_ref)
    low = gmid.astype(BF16)
    granks = against(low, up[0]).astype(BF16)
    grank_ref[0] = granks
    ready.send(grank_ref)
    extra = product(granks, dn[0])
    copies[5].wait()
    go = against(low, w[1]) + extra
    row = lax.axis_index("seq") * tokens + iota((tokens, 1), 0)
    go = jnp.where(row < length[0], go, 0.0).astype(BF16)
    for s in range(groups):
        go_ref[s] = go[:, s * cols : (s + 1) * cols]


def place_columns(out_ref, row, values):
    groups, _, cols = out_ref.shape
    low = values.astype(BF16)
    for s in range(groups):
        out_ref[s, row : row + values.shape[0], :] = low[:, s * cols : (s + 1) * cols]


def factor_kernel(ready, att_ref, norm_ref, mixed_ref, gmid_ref, gquery_ref, ggate_ref, cot_ref, r35, r4, r6, g34, g5, g6, out_ref):
    ready()
    half = 4 * RANK
    sides = (
        (att_ref[...], gmid_ref[...].astype(BF16), r35[0], g34[0]),
        (norm_ref[...], gquery_ref[...], r4[...], g34[1]),
        (norm_ref[...], ggate_ref[...], r35[1], g5[...]),
        (mixed_ref[...], cot_ref[...], r6[...], g6[...]),
    )
    for j, (value, gy, rank, grank) in enumerate(sides):
        place_columns(out_ref, j * RANK, contract(grank, value))
        place_columns(out_ref, half + j * RANK, contract(rank, gy))


def late_kernel(ready, grads_ref, upgrad_ref, out_ref):
    seq, _, wide = grads_ref.shape
    cols = wide // 3
    tokens = grads_ref.shape[1] - RANK
    total = grads_ref[0, tokens:, :].astype(F32)
    for s in range(1, seq):
        total = total + grads_ref[s, tokens:, :].astype(F32)
    total = total.astype(BF16)
    for j in range(3):
        out_ref[j * RANK : (j + 1) * RANK, :] = total[:, j * cols : (j + 1) * cols]
    ready()
    out_ref[3 * RANK :, :] = upgrad_ref[...]


def entry_kernel(ready, adapter, grads_ref, x_ref, gain_ref, gmid_ref, w_any, dn_any, up_any, out_ref, w, gy, total, dn, up, sems):
    a = adapter[0]
    seq, _, wide = grads_ref.shape
    cols = wide // 3
    tokens = out_ref.shape[0]
    copies = fetch(
        [(up_any.at[j, a], up.at[pl.ds(RANK * j, RANK)]) for j in range(3)]
        + [(dn_any.at[j, a], dn.at[pl.ds(RANK * j, RANK)]) for j in range(3)]
        + [(w_any.at[j], w.at[j]) for j in range(3)],
        sems,
    )
    for j in range(3):
        for s in range(seq):
            gy[j, :, s * cols : (s + 1) * cols] = grads_ref[s, 0:tokens, j * cols : (j + 1) * cols]
    for copy in copies[:6]:
        copy.wait()
    place = iota((tokens, 3 * RANK), 1) // RANK
    granks = jnp.zeros((tokens, 3 * RANK), F32)
    for j in range(3):
        granks = jnp.where(place == j, against(gy[j], up[...]), granks)
    total[...] = product(granks.astype(BF16), dn[...])

    def one(j, carry):
        pltpu.make_async_copy(w_any.at[j], w.at[j], sems.at[6 + j]).wait()
        total[...] += against(gy[j], w[j])
        return carry

    lax.fori_loop(0, 3, one, 0)
    ready()
    x = x_ref[...].astype(F32)
    back = norm_back(x, inverse_norm(x), gain_row(gain_ref), total[...])
    out_ref[...] = (gmid_ref[...] + back).astype(BF16)


def sum_kernel(ready, parts_ref, out_ref):
    ready()
    total = parts_ref[0].astype(F32)
    for s in range(1, parts_ref.shape[0]):
        total = total + parts_ref[s].astype(F32)
    out_ref[...] = total.astype(BF16)


def stack_kernel(ready, *refs):
    for k in range(refs[-1].shape[0]):
        refs[-1][k] = refs[k][...]


def relative_marks(ids_ref, batches):
    plane = lax.axis_index("batch")
    absolute = adapter_marks(ids_ref, batches)
    marks = []
    for k in range(batches):
        source = lax.rem(plane + (batches - k), batches)
        mark = absolute[0]
        for b in range(1, batches):
            mark = jnp.where(source == b, absolute[b], mark)
        marks.append(mark)
    return marks


def adapter_marks(ids_ref, batches):
    step = ids_ref.shape[0] // batches
    return [ids_ref[b * step : b * step + 1, 0:1] // ADAPTER_STEP for b in range(batches)]


def spread_rows(parts, marks, runs, stage, sems):
    seq, batches = parts.shape[:2]
    for target, origin, base, count in runs:

        def put(i, target=target, origin=origin, base=base):
            return pltpu.make_async_copy(stage.at[base + i], target.at[origin + i], sems.at[base + i])

        def one(i, carry, put=put, base=base):
            start = pl.multiple_of((base + i) * RANK, RANK)
            rows = [
                jnp.concatenate([parts[s, k, pl.ds(start, RANK), :] for s in range(seq)], axis=1).astype(F32)
                for k in range(batches)
            ]
            for k in range(ADAPTERS):
                total = jnp.zeros(rows[0].shape, F32)
                for row, mark in zip(rows, marks, strict=True):
                    total = total + jnp.where(mark == k, row, 0.0)
                stage[base + i, k] = total
            put(i).start()
            return carry

        lax.fori_loop(0, count, one, 0)
    for target, origin, base, count in runs:
        for i in range(count):
            pltpu.make_async_copy(stage.at[base + i], target.at[origin + i], sems.at[base + i]).wait()


def spread_kernel(batches, ready, ids_ref, *refs):
    down_any, up_any, parts, stage, load_sems, sems = refs[-6:]
    seq = parts.shape[0]
    me = lax.axis_index("seq")
    copies = fetch([(refs[m % 2].at[m // 2], parts.at[me ^ m]) for m in range(seq)], load_sems)
    ready()
    marks = relative_marks(ids_ref, batches)
    for copy in copies:
        copy.wait()
    spread_rows(parts, marks, ((down_any, 3, 0, 4), (up_any, 3, 4, 4)), stage, sems)


def last_spread_kernel(batches, ready, ids_ref, down_in, up_in, *refs):
    down_any, up_any, parts, stage, load_sems, sems = refs[-6:]
    seq = parts.shape[0]
    me = lax.axis_index("seq")
    copies = fetch([(refs[m % 2].at[m // 2], parts.at[me ^ m]) for m in range(seq)], load_sems)
    ready()
    marks = relative_marks(ids_ref, batches)
    for copy in copies:
        copy.wait()
    spread_rows(parts, marks, ((down_any, 0, 0, 3), (up_any, 0, 3, 3)), stage, sems)


def along(values, axis, step, size):
    return lax.ppermute(values, axis, [(i, (i + step) % size) for i in range(size)])


def across(values, axis, mask, size):
    return lax.ppermute(values, axis, [(i, i ^ mask) for i in range(size)])


def to_pairs(values, axis, size):
    return [values] + [across(values, axis, m, size) for m in range(2, size, 2)]


def stacked(values, name, kind="V"):
    shape = shaped((len(values), *values[0].shape), values[0].dtype)
    return call(stack_kernel, name, "V" * len(values), [(kind, shape)], values)[0]


def exchange(values, axes):
    return lax.all_to_all(values, axes, split_axis=0, concat_axis=0, tiled=True)


def body(
    inputs, lengths, adapter_index, memory_picks, input_weights, output_weights, adapter_down, adapter_up,
    attention_gain, memory_gain, half_keys, memory_values, cotangent,
):
    both = ("batch", "seq")
    batches, seq = lax.axis_size("batch"), lax.axis_size("seq")
    owners = batches * seq
    tokens, width = inputs.shape[1], inputs.shape[2]
    rows, cols, half = tokens * seq, width // seq, width // 2
    rows_dev = memory_values.shape[0]
    capacity = 2 * tokens * MHEADS // owners
    groups = capacity // 8
    items = owners * capacity
    block = min(owners * 8, 256)
    small_block = RECALL_ROWS
    carried = 2 * groups * PICKS // cols * batches * 8
    x, cot = inputs[0], cotangent[0]
    down = jnp.swapaxes(adapter_down, 2, 3)
    gain_one, gain_two = attention_gain, memory_gain
    picks = jnp.transpose(memory_picks[0], (1, 2, 0))
    matrix = pltpu.VMEM((width, width), BF16)
    pair = pltpu.VMEM((2, width, width), BF16)
    triple = pltpu.VMEM((3, width, width), BF16)
    small = pltpu.VMEM((RANK, width), BF16)
    two_small = pltpu.VMEM((2, RANK, width), BF16)
    three_small = pltpu.VMEM((3 * RANK, width), BF16)
    token_low, token_wide = shaped((tokens, width), BF16), shaped((tokens, width), F32)
    token_rank, token_lanes = shaped((tokens, RANK), BF16), shaped((tokens, LANES), F32)
    fixed = functools.partial

    qkv, normed = call(
        qkv_kernel, "qkv", "MLLHHH",
        [("V", shaped((seq, tokens, 3 * cols), BF16)), ("S", shaped((tokens, width + LANES), BF16))],
        (adapter_index, x, gain_one, input_weights, down, adapter_up), [triple, three_small, three_small, sema(9)],
    )
    qkv_all = exchange(qkv, "seq").reshape(rows, 3 * cols)

    slot, slot_col, pick, *ids_out = call(
        fixed(route_kernel, rows_dev, owners), "route", "ML",
        [("S", shaped((8, tokens), I32)), ("S", shaped((tokens, tokens), I32)), ("S", shaped((tokens, LANES), I32)),
         *[("V", shaped((seq * 8 + 8, LANES), I32)) for _ in range(batches)]],
        (adapter_index, picks), [pltpu.VMEM((owners * 8, LANES), I32)],
    )
    ids_out = [ids_out[0]] + [along(ids_out[k], "batch", k, batches) for k in range(1, batches)]
    mix_grad, grank_six = call(
        mix_back_kernel, "mixback", "MLHHH", [("S", token_low), ("S", token_rank)],
        (adapter_index, cot, output_weights, down, adapter_up), [matrix, small, small, sema(3)],
    )

    qkv_all, ids_out, mix_grad = lax.optimization_barrier((qkv_all, ids_out, mix_grad))
    attended, lse, slots, qkv_saved = call(
        fixed(attend_kernel, groups, batches), "attend", "MV" + "V" * batches,
        [("V", shaped((seq, tokens + carried, cols), BF16)), ("S", shaped((8, rows), F32)),
         ("S", shaped((batches, 8, LANES), I32)), ("H", shaped((rows, 3 * cols), BF16))],
        (lengths, qkv_all, *ids_out),
        [pltpu.VMEM((rows, LANES), BF16), pltpu.VMEM((LANES, rows), BF16), pltpu.VMEM((LANES, rows), F32), sema(1)],
    )
    o_all = exchange(attended, "seq")
    normed, attended = lax.optimization_barrier((normed, attended))
    normed_all = to_pairs(normed, "seq", seq)

    left, right, same_two, ahead, sent, att, rank_pair, middle, normed_two, gate = call(
        middle_kernel, "middle", "MVLLLHHHH",
        [("V", shaped((tokens, half), BF16)), ("V", shaped((tokens, half), BF16)), ("V", token_low),
         ("V", shaped((width, width), BF16)), ("S", shaped((seq, carried, cols), BF16)), ("S", token_low),
         ("S", shaped((2, tokens, RANK), BF16)), ("S", token_wide), ("S", token_low), ("S", token_wide)],
        (adapter_index, o_all, x, gain_two, mix_grad, input_weights, output_weights, down, adapter_up),
        [pair, two_small, two_small, sema(7)],
    )
    lefts = [left] + [along(left, "batch", k, batches) for k in range(1, batches)]
    weight_out, rank_four, weights = call(
        fixed(scores_kernel, owners), "scores", "MVVLLLHH",
        [("V", shaped((owners * 8, LANES), BF16)), ("S", token_rank), ("S", token_lanes)],
        (adapter_index, same_two, ahead, pick, slot, half_keys, down, adapter_up), [small, small, sema(2)],
    )
    weight_out, normed_all = lax.optimization_barrier((weight_out, normed_all))
    weight_in = exchange(weight_out.reshape(owners, 8, LANES), both).reshape(owners * 8, LANES)
    right, lefts = lax.optimization_barrier((right, lefts))
    rights = [right] + [along(right, "batch", k, batches) for k in range(1, batches)]

    def scatter(parts, name):
        out = [("V", shaped((seq, batches, capacity, half), BF16))]
        return call(scatter_kernel, name, "L" + "V" * batches, out, (slots, *parts))[0]

    left_out = scatter(lefts, "scatterleft")
    normed_all, left_out = lax.optimization_barrier((normed_all, left_out))
    normed_all = stacked(normed_all, "pairsnorm", "S")
    sent, left_out = lax.optimization_barrier((sent, left_out))
    ids, index = call(
        fixed(prepare_kernel, groups, rows_dev, batches), "prepare", "L",
        [("S", shaped((owners * 8, LANES), I32)), ("H", shaped((items, rows_dev), jnp.int16))], (sent,),
        [pltpu.VMEM((2, LANES, rows_dev), jnp.int16), pltpu.VMEM((owners * 8 // LANES, LANES, LANES), I32), sema(2)],
    )
    left_out, weight_in, normed_all = lax.optimization_barrier((left_out, weight_in, normed_all))
    normed_all = (normed_all, across(normed_all, "seq", 1, seq))
    left_in = exchange(left_out, "seq").reshape(items, half)

    (sums,) = call(
        fixed(recall_kernel, groups), "recall", "VHH", [("H", shaped((seq, batches, capacity, width), BF16))],
        (weight_in, index, memory_values),
        [pltpu.VMEM((rows_dev, width), BF16), pltpu.VMEM((2, small_block, rows_dev), jnp.int16), pltpu.VMEM((2, small_block, rows_dev), BF16),
         pltpu.VMEM((2, small_block // 8, 8, width), BF16), sema(3 + 2 * (small_block // (8 * seq)))],
        flops=1 << 12,
    )
    sums, left_in = lax.optimization_barrier((sums, left_in))
    back = exchange(sums, "seq")

    def recall_back(part, name, grads, kind, dtype, *before):
        return call(
            fixed(recall_back_kernel, part, batches, groups), name, "L" + "L" * part + "VH",
            [(kind, shaped((owners * 8, LANES), dtype))], (ids, *before, grads, memory_values),
            [pltpu.VMEM((rows_dev, half), BF16), pltpu.VMEM((block, rows_dev), BF16), sema(1)],
        )[0]

    rights, normed_all = lax.optimization_barrier((rights, normed_all))
    right_out = scatter(rights, "scatterright")
    found_left = recall_back(0, "recallleft", left_in, "S", F32)
    right_out, back, found_left = lax.optimization_barrier((right_out, back, found_left))
    right_in = exchange(right_out, "seq").reshape(items, half)
    pieces = call(
        gather_kernel, "gather", "LV", [("V", token_low) for _ in range(batches)], (slots, back),
    )
    pieces = [pieces[0]] + [along(pieces[k], "batch", batches - k, batches) for k in range(1, batches)]
    found = recall_back(1, "recallright", right_in, "V", BF16, found_left)
    found_back = exchange(found.reshape(owners, 8, LANES), both).reshape(owners * 8, LANES)

    mixed, grank_five, ggate, part = call(
        fixed(memory_kernel, batches), "memory", "MLL" + "V" * batches + "HHH",
        [("S", token_low), ("S", token_rank), ("S", token_low), ("V", token_wide)],
        (adapter_index, gate, mix_grad, *pieces, input_weights, down, adapter_up), [matrix, small, small, sema(3)],
    )

    go, gquery, grank_pair, gmid = call(
        fixed(query_kernel, owners, rows_dev), "query", "MMVLLLVDDDLHHHH",
        [("V", shaped((seq, tokens, cols), BF16)), ("S", token_low), ("S", shaped((2, tokens, RANK), BF16)), ("S", token_wide)],
        (lengths, adapter_index, found_back, slot_col, picks, weights, part, middle, cot, gain_two, half_keys,
         input_weights, output_weights, down, adapter_up),
        [pair, two_small, two_small, pltpu.VMEM((LANES, tokens), F32), pltpu.VMEM((MHEADS, 2, NSUB, tokens), BF16), sema(6)],
    )
    go_all = exchange(go, "seq").reshape(rows, cols)
    mixed, go = lax.optimization_barrier((mixed, go))
    output, rank_six = call(
        output_kernel, "output", "MLLHHH", [("S", token_low), ("S", token_rank)],
        (adapter_index, mixed, middle, output_weights, down, adapter_up), [matrix, small, small, sema(3)],
    )
    (factors,) = call(
        factor_kernel, "factors", "L" * 13, [("V", shaped((seq, 8 * RANK, cols), BF16))],
        (att, normed_two, mixed, gmid, gquery, ggate, cot, rank_pair, rank_four, rank_six, grank_pair, grank_five, grank_six),
    )
    factors, go_all = lax.optimization_barrier((factors, go_all))
    early_parts = exchange(factors, "seq")

    grads, up_grads = call(
        attend_back_kernel, "attendback", "MMLVLHHH",
        [("V", shaped((seq, tokens + RANK, 3 * cols), BF16)), ("S", shaped((3 * RANK, cols), BF16))],
        (lengths, adapter_index, qkv_saved, go_all, lse, *normed_all, adapter_up),
        [pltpu.VMEM((rows, LANES), F32), pltpu.VMEM((rows, LANES), F32), pltpu.VMEM((LANES, rows), F32),
         pltpu.VMEM((rows, LANES), BF16), pltpu.VMEM((LANES, rows), BF16), pltpu.VMEM((rows, LANES), BF16),
         pltpu.VMEM((rows, 3 * cols), BF16), pltpu.VMEM((rows, width + LANES), BF16), three_small, sema(3 + seq)],
    )
    grads, early_parts = lax.optimization_barrier((grads, early_parts))
    grads_all = exchange(grads, "seq")
    (some,) = call(sum_kernel, "sumearly", "V", [("V", shaped((8 * RANK, cols), BF16))], (early_parts,))
    some = [some] + [along(some, "batch", k, batches) for k in range(1, batches)]
    some = stacked(some, "stackearly")
    some = to_pairs(some, "seq", seq)
    (late_sum,) = call(late_kernel, "late", "VL", [("V", shaped((6 * RANK, cols), BF16))], (grads_all, up_grads))
    (grad_input,) = call(
        entry_kernel, "entry", "MVLLLHHH", [("S", token_low)],
        (adapter_index, grads_all, x, gain_one, gmid, input_weights, down, adapter_up),
        [triple, pltpu.VMEM((3, tokens, width), BF16), pltpu.VMEM((tokens, width), F32), three_small, three_small, sema(9)],
    )
    late_sums = [late_sum] + [along(late_sum, "batch", k, batches) for k in range(1, batches)]
    some = stacked(some, "pairsearly")
    late_sums, some, grad_input = lax.optimization_barrier((late_sums, some, grad_input))
    late_all = to_pairs(stacked(late_sums, "stacklate"), "seq", seq)
    some = (some, across(some, "seq", 1, seq))
    full = shaped((7, ADAPTERS, RANK, width), F32)
    grad_down, grad_up = call(
        fixed(spread_kernel, batches), "spread", "LVV", [("H", full), ("H", full)], (ids, *some),
        [pltpu.VMEM((seq, batches, 8 * RANK, cols), BF16), pltpu.VMEM((8, ADAPTERS, RANK, width), F32), sema(seq), sema(8)],
    )
    late_all, grad_down, grad_up = lax.optimization_barrier((late_all, grad_down, grad_up))
    late_all = stacked(late_all, "pairslate")
    late_all = (late_all, across(late_all, "seq", 1, seq))
    grad_down, grad_up = call(
        fixed(last_spread_kernel, batches), "lastspread", "LHHVV", [("H", full), ("H", full)],
        (ids, grad_down, grad_up, *late_all),
        [pltpu.VMEM((seq, batches, 6 * RANK, cols), BF16), pltpu.VMEM((6, ADAPTERS, RANK, width), F32), sema(seq), sema(6)],
        aliases={1: 0, 2: 1},
    )
    return (output[None], grad_input[None], jnp.swapaxes(grad_down, 2, 3), grad_up)


def solution(mesh):
    split = P("batch", "seq", None)
    return jax.shard_map(
        body,
        mesh=mesh,
        in_specs=(
            split, P("batch"), P("batch"), P("batch", "seq", None, None), P(), P(), P(), P(), P(), P(), P(),
            P(("batch", "seq"), None), split,
        ),
        out_specs=(split, split, P(), P()),
        check_vma=False,
    )
```

```python
import functools

import jax
import jax.numpy as jnp
from jax import lax
from jax.experimental import pallas as pl
from jax.experimental.pallas import tpu as pltpu
from jax.sharding import PartitionSpec as P

HEAD_DIM = 64
MHEADS = 4
KHALF = 128
NSUB = 256
PICKS = 32
ADAPTERS = 8
RANK = 16
LANES = 128
ADAPTER_STEP = 4096
QUERY_UNROLL = 8
RECALL_ROWS = 256
EPS = 1e-06
NEG = -1e30
F32 = jnp.float32
BF16 = jnp.bfloat16
I32 = jnp.int32
HBM = pl.BlockSpec(memory_space=pltpu.HBM)
SMEM = pl.BlockSpec(memory_space=pltpu.SMEM)
VMEM = pl.BlockSpec(memory_space=pltpu.VMEM)
MIB = 1 << 20


def product(left, right):
    return lax.dot_general(left, right, (((1,), (0,)), ((), ())), preferred_element_type=F32)


def against(left, right):
    return lax.dot_general(left, right, (((1,), (1,)), ((), ())), preferred_element_type=F32)


def contract(left, right):
    return lax.dot_general(left, right, (((0,), (0,)), ((), ())), preferred_element_type=F32)


def iota(shape, axis):
    return lax.broadcasted_iota(I32, shape, axis)


def short_pick(table, index):
    numbers = lax.GatherDimensionNumbers(
        offset_dims=(), collapsed_slice_dims=(1,), start_index_map=(1,), operand_batching_dims=(0,), start_indices_batching_dims=(0,)
    )
    return lax.gather(table, index[:, :, None], numbers, (1, 1), mode=lax.GatherScatterMode.PROMISE_IN_BOUNDS)


def lane_pick(table, index):
    return jnp.take_along_axis(table, index, axis=1, mode="promise_in_bounds")


def shaped(shape, dtype):
    return jax.ShapeDtypeStruct(shape, dtype)


class Stage:
    def __init__(self, loads, stores):
        self.loads, self.stores = loads, stores
        self.waited, self.begun = set(), set()
        for _, copy, later in loads:
            if not later:
                copy.start()

    def begin(self):
        for _, copy, later in self.loads:
            if later:
                copy.start()

    def __call__(self, *refs):
        for at, (ref, copy, _) in enumerate(self.loads):
            if at not in self.waited and (not refs or any(ref is one for one in refs)):
                self.waited.add(at)
                copy.wait()

    def send(self, *refs):
        for at, (ref, copy) in enumerate(self.stores):
            if at not in self.begun and (not refs or any(ref is one for one in refs)):
                self.begun.add(at)
                copy.start()

    def finish(self):
        self()
        self.send()
        for _, copy in self.stores:
            copy.wait()


def call(kernel, name, ins, outs, args, scratch=(), vmem=40, flops=1 << 12, moved=1 << 12, aliases=None):
    shapes = [(args[i].shape, args[i].dtype) for i, kind in enumerate(ins) if kind in "LD"]
    stored = [(out.shape, out.dtype) for kind, out in outs if kind == "S"]
    count_in, count_out, count_user = len(ins), len(outs), len(scratch)

    def wrapped(*refs):
        given, results = list(refs[:count_in]), list(refs[count_in : count_in + count_out])
        rest = list(refs[count_in + count_out :])
        user, buffers = rest[:count_user], rest[count_user:]
        loads, stores = [], []
        for i, kind in enumerate(ins):
            if kind in "LD":
                at = len(loads)
                copy = pltpu.make_async_copy(given[i], buffers[at], buffers[-1].at[at])
                loads.append((buffers[at], copy, kind == "D"))
                given[i] = buffers[at]
        for i, (kind, _) in enumerate(outs):
            if kind == "S":
                at = len(loads) + len(stores)
                stores.append((buffers[at], pltpu.make_async_copy(buffers[at], results[i], buffers[-1].at[at])))
                results[i] = buffers[at]
        stage = Stage(loads, stores)
        kernel(stage, *given, *results, *user)
        stage.finish()

    spaces = {"V": VMEM, "L": HBM, "D": HBM, "S": HBM, "H": HBM, "M": SMEM}
    autos = [pltpu.VMEM(*one) for one in shapes + stored]
    args = [
        pltpu.with_memory_space_constraint(one, pltpu.HBM) if kind in "LDH" else one
        for kind, one in zip(ins, args, strict=True)
    ]
    return pl.pallas_call(
        wrapped,
        name=name,
        out_shape=[pltpu.HBM(out.shape, out.dtype) if kind in "SH" else out for kind, out in outs],
        in_specs=[spaces[kind] for kind in ins],
        out_specs=[spaces[kind] for kind, _ in outs],
        input_output_aliases=aliases or {},
        scratch_shapes=list(scratch) + autos + ([sema(len(autos))] if autos else []),
        compiler_params=pltpu.CompilerParams(vmem_limit_bytes=vmem * MIB),
        cost_estimate=pl.CostEstimate(flops=flops, bytes_accessed=moved, transcendentals=0),
    )(*args)


def fetch(pairs, sems):
    copies = [
        pltpu.make_async_copy(source, target, sems.at[place])
        for place, (source, target) in enumerate(pairs)
    ]
    for copy in copies:
        copy.start()
    return copies


def sema(count):
    return pltpu.SemaphoreType.DMA((count,))


def gain_row(ref):
    return ref[...].astype(F32).reshape(1, ref.shape[0])


def inverse_norm(values):
    return lax.rsqrt(jnp.mean(values * values, axis=1, keepdims=True) + EPS)


def norm_back(values, inverse, scales, incoming):
    weighted = incoming * scales
    inner = jnp.mean(weighted * values, axis=1, keepdims=True)
    return weighted * inverse - values * inverse * inverse * inverse * inner


def qkv_kernel(ready, adapter, x_ref, gain_ref, w_any, dn_any, up_any, out_ref, norm_ref, w, dn, up, sems):
    groups, tokens, wide = out_ref.shape
    cols = wide // 3
    a = adapter[0]
    copies = fetch(
        [(dn_any.at[j, a], dn.at[pl.ds(RANK * j, RANK)]) for j in range(3)]
        + [(up_any.at[j, a], up.at[pl.ds(RANK * j, RANK)]) for j in range(3)]
        + [(w_any.at[0], w.at[0])],
        sems,
    )
    copies += [pltpu.make_async_copy(w_any.at[j], w.at[j], sems.at[6 + j]) for j in (1, 2)]
    ready()
    copies[7].start()
    copies[8].start()
    x = x_ref[...].astype(F32)
    normed = (x * inverse_norm(x) * gain_row(gain_ref)).astype(BF16)
    width = normed.shape[1]
    norm_ref[:, :width] = normed
    for copy in copies[:6]:
        copy.wait()
    ranks = against(normed, dn[...])
    norm_ref[:, width:] = widen(ranks).astype(BF16)
    ready.send(norm_ref)
    place = iota((tokens, 3 * RANK), 1) // RANK
    for j in range(3):
        own = jnp.where(place == j, ranks, 0.0).astype(BF16)
        extra = product(own, up[...])
        copies[6 + j].wait()
        result = (product(normed, w[j]) + extra).astype(BF16)
        for s in range(groups):
            out_ref[s, :, j * cols : (j + 1) * cols] = result[:, s * cols : (s + 1) * cols]


def mix_back_kernel(ready, adapter, cot_ref, w_any, dn_any, up_any, grad_ref, rank_ref, w, dn, up, sems):
    a = adapter[0]
    copies = fetch([(up_any.at[6, a], up), (dn_any.at[6, a], dn), (w_any.at[1], w)], sems)
    ready()
    gy = cot_ref[...]
    copies[0].wait()
    ranks = against(gy, up[...]).astype(BF16)
    rank_ref[...] = ranks
    copies[1].wait()
    extra = product(ranks, dn[...])
    copies[2].wait()
    grad_ref[...] = (against(gy, w[...]) + extra).astype(BF16)


def route_kernel(rows_dev, owners, ready, adapter, picks_ref, slot_ref, slot_col_ref, pick_ref, *ids_refs):
    ready()
    heads, picks, tokens = picks_ref.shape
    capacity = 2 * heads * tokens // owners
    groups = capacity // 8
    visits = heads * tokens
    owner = jnp.concatenate([picks_ref[h, 0:1, :] for h in range(heads)], axis=1) // rows_dev
    hot = jnp.where(iota((owners, visits), 0) == owner, 1.0, 0.0)
    before = jnp.where(iota((visits, visits), 0) < iota((visits, visits), 1), 1.0, 0.0).astype(BF16)
    counts = product(hot.astype(BF16), before)
    within = jnp.sum(hot * counts, axis=0, keepdims=True).astype(I32)
    slot = owner * capacity + within
    rows = [slot[:, h * tokens : (h + 1) * tokens] for h in range(heads)]
    stacked = jnp.concatenate(rows + [jnp.full((8 - heads, tokens), -1, I32)], axis=0)
    slot_ref[...] = stacked
    tall = jnp.concatenate([stacked, jnp.full((tokens - 8, tokens), -1, I32)], axis=0)
    slot_col_ref[...] = jnp.transpose(tall)
    packed = jnp.concatenate([picks_ref[h] for h in range(heads)], axis=0)
    by_token = jnp.transpose(packed)
    pick_ref[...] = by_token
    local = by_token % rows_dev
    lanes = iota((tokens, LANES), 1)
    total = jnp.zeros((owners * 8, LANES), F32)
    out_lane = iota((owners * 8, LANES), 1) // PICKS
    place = iota((owners * 8, tokens), 0)
    base = (place // 8) * capacity + place % 8
    for g in range(groups):
        high = jnp.zeros((owners * 8, LANES), F32)
        low = jnp.zeros((owners * 8, LANES), F32)
        for h in range(heads):
            chosen = jnp.where(base + g * 8 == rows[h], 1.0, 0.0).astype(BF16)
            own = jnp.where(lanes // PICKS == h, local, 0)
            own = tile_groups(own.astype(F32), heads).astype(I32)
            high = high + product(chosen, (own // 256).astype(F32).astype(BF16))
            low = low + product(chosen, (own % 256).astype(F32).astype(BF16))
        total = jnp.where(out_lane == g, high * 256.0 + low, total)
    batches = len(ids_refs) - 1
    part = owners * 8 // batches
    ids_refs[-1][...] = total.astype(I32) + adapter[0] * ADAPTER_STEP
    for k in range(batches):
        target = lax.rem(lax.axis_index("batch") + k, batches)
        ids_refs[k][0:part, :] = ids_refs[-1][pl.ds(pl.multiple_of(target * part, part), part), :]
        ids_refs[k][part:, :] = stacked


def tile_groups(values, count):
    total = values
    for turn in range(1, count):
        total = total + pltpu.roll(values, turn * PICKS, 1)
    return total


def prepare_kernel(groups, rows_dev, batches, ready, sent_ref, ids_ref, index_any, stage, turned, sems):
    ready()
    seq, _, cols = sent_ref.shape
    lanes = groups * PICKS
    chunks = 2 * lanes // cols
    for k in range(batches):
        source = lax.rem(lax.axis_index("batch") + (batches - k), batches)
        for s in range(seq):
            both = [
                sent_ref[s, (chunk * batches + k) * 8 : (chunk * batches + k + 1) * 8, :].astype(F32)
                for chunk in range(chunks)
            ]
            both = jnp.concatenate(both, axis=1).astype(I32)
            ids = widen(both[:, :lanes] * 256 + both[:, lanes:])
            ids_ref[pl.ds(pl.multiple_of((source * seq + s) * 8, 8), 8), :] = ids
    ready.send(ids_ref)
    places = ids_ref.shape[0]
    chunks = rows_dev // LANES
    high_rows = max(8, chunks)
    steps = groups * (places // LANES)
    for k in range(places // LANES):
        turned[k] = jnp.transpose(ids_ref[k * LANES : (k + 1) * LANES, :] & (ADAPTER_STEP - 1))

    def put(step, slot):
        target = index_any.at[pl.ds(pl.multiple_of(step * LANES, LANES), LANES)]
        return pltpu.make_async_copy(stage.at[slot], target, sems.at[slot])

    def one(step, carry):
        k, g = lax.rem(step, places // LANES), step // (places // LANES)
        slot = lax.rem(step, 2)
        mask = jnp.zeros((LANES, LANES), I32)
        highs = jnp.zeros((high_rows, LANES), I32)
        for r in range(PICKS):
            bit = (1 << r) if r < 31 else -(1 << 31)
            row = turned[k, pl.ds(g * PICKS + r, 1), :]
            mask = mask | jnp.where(row & 127 == iota((LANES, LANES), 0), bit, 0)
            highs = highs | jnp.where(row >> 7 == iota((high_rows, LANES), 0), bit, 0)

        @pl.when(step >= 2)
        def _():
            put(step - 2, slot).wait()

        for c in range(chunks):
            index = 31 - lax.clz(mask & highs[c : c + 1, :])
            stage[slot, :, c * LANES : (c + 1) * LANES] = jnp.transpose(index.astype(jnp.int16))
        put(step, slot).start()
        return carry

    lax.fori_loop(0, steps, one, 0)
    for step in range(max(0, steps - 2), steps):
        put(step, step % 2).wait()


def recall_kernel(groups, ready, weight_ref, index_any, mem_any, out_any, mem, index, dense, staged, sems):
    places = weight_ref.shape[0]
    rows_dev = mem.shape[0]
    chunks = rows_dev // LANES
    block = dense.shape[1]
    per_group = places // block
    blocks = groups * per_group
    seq = out_any.shape[0]
    planes = block // (8 * seq)

    def load(b, slot):
        source = index_any.at[pl.ds(pl.multiple_of(b * block, block), block)]
        return pltpu.make_async_copy(source, index.at[slot], sems.at[1 + slot])

    load(0, 0).start()
    copy = pltpu.make_async_copy(mem_any, mem, sems.at[0])
    copy.start()

    def gather(b, side):
        load(b, side).wait()

        @pl.when(b + 1 < blocks)
        def _():
            load(b + 1, 1 - side).start()

        pick(b, side)

    def pick(b, side):
        g, k = b // per_group, lax.rem(b, per_group)
        for start in range(0, block, 16):
            weights = weight_ref[pl.ds(pl.multiple_of(k * block + start, 16), 16), :]
            shift = jnp.full((16, LANES), g * PICKS, I32).astype(jnp.int16)
            for c in range(chunks):
                at = index[side, start : start + 16, c * LANES : (c + 1) * LANES]
                value = short_pick(weights, (at + shift) & jnp.int16(127))
                dense[side, start : start + 16, c * LANES : (c + 1) * LANES] = jnp.where(at >= 0, value, jnp.zeros((), BF16))

    def save(b, side):
        g, k = b // per_group, lax.rem(b, per_group)
        return [
            pltpu.make_async_copy(
                staged.at[side, pl.ds(i * seq, seq)],
                out_any.at[:, k * planes + i, pl.ds(pl.multiple_of(g * 8, 8), 8), :],
                sems.at[3 + side * planes + i],
            )
            for i in range(planes)
        ]

    def multiply(b, side):
        result = product(dense[side], mem[...]).astype(BF16)

        @pl.when(b >= 2)
        def _():
            for one in save(b - 2, side):
                one.wait()

        staged[side] = result.reshape(block // 8, 8, result.shape[1])
        for one in save(b, side):
            one.start()

    gather(0, 0)
    copy.wait()

    def whole(i, carry):
        gather(2 * i + 1, 1)
        multiply(2 * i, 0)

        @pl.when(2 * i + 2 < blocks)
        def _():
            load(2 * i + 2, 0).wait()
            load(2 * i + 3, 1).start()

        pick(jnp.minimum(2 * i + 2, blocks - 1), 0)
        multiply(2 * i + 1, 1)
        return carry

    lax.fori_loop(0, blocks // 2, whole, 0)
    for b in range(blocks - 2, blocks):
        for one in save(b, b % 2):
            one.wait()


def recall_back_kernel(part, batches, groups, ready, ids_ref, *refs):
    before_ref = refs[0] if part else None
    grad_ref, mem_any, out_ref, mem, scores, sems = refs[part:]
    items, half = grad_ref.shape
    seq = items // (batches * groups * 8)
    rows_dev = mem.shape[0]
    capacity = groups * 8
    chunks = rows_dev // LANES
    block = scores.shape[0]
    per_block = block // capacity
    blocks = items // block
    copies = fetch([(mem_any.at[:, pl.ds(part * half, half)], mem)], sems)
    ready()
    copies[0].wait()

    def whole(b, outer):
        scores[...] = against(grad_ref[pl.ds(pl.multiple_of(b * block, block), block), :], mem[...]).astype(BF16)
        step = min(2, groups) * 8

        lane_group = iota((8, LANES), 1) // PICKS
        for local in range(per_block):
            sender = b * per_block + local
            spot = lax.rem(sender, batches) * seq + sender // batches
            start = pl.multiple_of(spot * 8, 8)
            ids = ids_ref[pl.ds(start, 8), :] & (ADAPTER_STEP - 1)
            low = ids & 127
            high = ids >> 7
            total = before_ref[pl.ds(start, 8), :] if part else jnp.zeros((8, LANES), F32)
            for g in range(0, groups, 2):
                key = jnp.concatenate([jnp.where(lane_group == g + i, high, -1) for i in range(step // 8)], axis=0)
                index = jnp.concatenate([low] * (step // 8), axis=0)
                key, index = key.astype(jnp.int16), index.astype(jnp.int16)
                here = jnp.zeros((step, LANES), BF16)
                row = local * capacity + g * 8
                for c in range(chunks):
                    found = scores[row : row + step, c * LANES : (c + 1) * LANES]
                    here = jnp.where(key == jnp.int16(c), short_pick(found, index), here)
                here = here.astype(F32)
                for i in range(step // 8):
                    total = total + here[i * 8 : (i + 1) * 8]
            out_ref[pl.ds(start, 8), :] = total.astype(out_ref.dtype)
        return outer

    lax.fori_loop(0, blocks, whole, 0)


def head_parts(values, h, spare):
    lane = iota(values.shape, 1)
    return jnp.where(lane // HEAD_DIM == h, values, jnp.where(lane == (1 - h) * HEAD_DIM, spare, 0.0)).astype(BF16)


def widen(values):
    if values.shape[1] == LANES:
        return values
    return jnp.concatenate([values, jnp.zeros((values.shape[0], LANES - values.shape[1]), values.dtype)], axis=1)


def attend_kernel(groups, batches, ready, length, qkv_ref, *refs):
    o_ref, lse_ref, slots_ref, saved_any, parts, values_t, mixed, sems = refs[batches:]
    ready()
    saving = pltpu.make_async_copy(qkv_ref, saved_any, sems.at[0])
    saving.start()
    rows, wide = qkv_ref.shape
    cols = wide // 3
    seq = o_ref.shape[0]
    lanes = groups * PICKS
    for k in range(batches):
        slots_ref[k] = refs[k][seq * 8 :, :]
    ready.send(slots_ref)
    for s in range(seq):
        ids = jnp.concatenate([refs[k][s * 8 : (s + 1) * 8, :lanes] for k in range(batches)], axis=0)
        both = jnp.concatenate([ids // 256, ids % 256], axis=1).astype(F32).astype(BF16)
        for chunk in range(2 * lanes // cols):
            start = rows // seq + chunk * batches * 8
            o_ref[s, start : start + batches * 8, :] = both[:, chunk * cols : (chunk + 1) * cols]
    heads = cols // HEAD_DIM
    size = min(256, rows)
    valid = length[0]
    bias = jnp.where(iota((rows, LANES), 0) < valid, 0.0, NEG)
    keys = widen(qkv_ref[:, cols : 2 * cols].astype(F32))
    values_t[...] = jnp.transpose(widen(qkv_ref[:, 2 * cols :].astype(F32))).astype(BF16)
    lse_ref[...] = jnp.zeros_like(lse_ref)

    def one(h, carry):
        parts[...] = head_parts(keys, h, bias)
        for i in range(rows // size):
            first, last = i * size, (i + 1) * size
            queries = widen(qkv_ref[first:last, 0:cols].astype(F32)) * (HEAD_DIM**-0.5)
            query = head_parts(queries, h, 1.0)
            near = against(parts[first:last], query)
            near = jnp.where(iota((size, size), 0) <= iota((size, size), 1), near, NEG)
            high = jnp.max(near, axis=0, keepdims=True)
            if i:
                far = against(parts[:first], query)
                high = jnp.maximum(high, jnp.max(far, axis=0, keepdims=True))
            near = jnp.exp(near - high)
            summed = jnp.sum(near, axis=0, keepdims=True)
            result = product(values_t[:, first:last], near.astype(BF16))
            if i:
                far = jnp.exp(far - high)
                summed = summed + jnp.sum(far, axis=0, keepdims=True)
                result = result + product(values_t[:, :first], far.astype(BF16))
            lse_ref[pl.ds(h, 1), first:last] = high + jnp.log(summed)
            own = iota((LANES, size), 0) // HEAD_DIM == h
            mixed[:, first:last] = jnp.where(own, result / summed, mixed[:, first:last])
        return carry

    mixed[...] = jnp.zeros_like(mixed)
    lax.fori_loop(0, heads, one, 0)
    ready.send(lse_ref)
    tokens = rows // seq
    for s in range(seq):
        first = s * tokens
        kept = jnp.where(first + iota((LANES, tokens), 1) < valid, mixed[:, first : first + tokens], 0.0)
        o_ref[s, 0:tokens, :] = jnp.transpose(kept)[:, :cols].astype(BF16)
    saving.wait()


def attend_back_kernel(
    ready, length, adapter, qkv_ref, go_ref, lse_ref, even_ref, odd_ref, up_any,
    out_ref, upgrad_ref, dk, dv, dq, parts, keys_t, values, grads_all, norms, up, sems,
):
    a = adapter[0]
    seq = out_ref.shape[0]
    me = lax.axis_index("seq")
    tokens = even_ref.shape[1]
    copies = fetch(
        [(up_any.at[j, a], up.at[pl.ds(RANK * j, RANK)]) for j in range(3)]
        + [
            ((even_ref, odd_ref)[m % 2].at[m // 2], norms.at[pl.ds(pl.multiple_of((me ^ m) * tokens, tokens), tokens)])
            for m in range(seq)
        ],
        sems,
    )
    ready()
    rows, wide = qkv_ref.shape
    cols = wide // 3
    heads = cols // HEAD_DIM
    size = min(256, rows)
    valid = length[0]
    scaling = HEAD_DIM**-0.5
    bias = jnp.where(iota((rows, LANES), 0) < valid, 0.0, NEG)
    keys = widen(qkv_ref[:, cols : 2 * cols].astype(F32))
    keys_t[...] = jnp.transpose(keys).astype(BF16)
    values[...] = widen(qkv_ref[:, 2 * cols :])
    dk[...] = jnp.zeros_like(dk)
    dv[...] = jnp.zeros_like(dv)
    dq[...] = jnp.zeros_like(dq)

    def one(h, carry):
        parts[...] = head_parts(keys, h, bias)
        for i in range(rows // size):
            first, last = i * size, (i + 1) * size
            queries = widen(qkv_ref[first:last, 0:cols].astype(F32)) * scaling
            grads = widen(go_ref[first:last, :].astype(F32))
            query = head_parts(queries, h, 1.0)
            plain = head_parts(queries, h, 0.0)
            grad = head_parts(grads, h, 0.0)
            lse = lse_ref[pl.ds(h, 1), first:last]
            near = against(parts[first:last], query)
            near = jnp.where(iota((size, size), 0) <= iota((size, size), 1), near, NEG)
            near = jnp.exp(near - lse)
            near_gp = against(values[first:last], grad)
            delta = jnp.sum(near * near_gp, axis=0, keepdims=True)
            if i:
                far = jnp.exp(against(parts[:first], query) - lse)
                far_gp = against(values[:first], grad)
                delta = delta + jnp.sum(far * far_gp, axis=0, keepdims=True)
            near_gs = (near * (near_gp - delta)).astype(BF16)
            result = product(keys_t[:, first:last], near_gs)
            dk[first:last] += product(near_gs, plain)
            dv[first:last] += product(near.astype(BF16), grad)
            if i:
                far_gs = (far * (far_gp - delta)).astype(BF16)
                result = result + product(keys_t[:, :first], far_gs)
                dk[:first] += product(far_gs, plain)
                dv[:first] += product(far.astype(BF16), grad)
            own = iota((LANES, size), 0) // HEAD_DIM == h
            dq[:, first:last] = jnp.where(own, result, dq[:, first:last])
        return carry

    for h in range(heads):
        one(h, 0)
    grads_all[:, 0:cols] = (jnp.transpose(dq[...]) * scaling)[:, :cols].astype(BF16)
    grads_all[:, cols : 2 * cols] = dk[:, :cols].astype(BF16)
    grads_all[:, 2 * cols :] = dv[:, :cols].astype(BF16)
    for s in range(seq):
        out_ref[s, 0:tokens, :] = grads_all[s * tokens : (s + 1) * tokens, :]
    for copy in copies:
        copy.wait()
    own = jnp.zeros((3 * RANK, cols), F32)
    for s in range(seq):
        own = jnp.where(me == s, up[:, s * cols : (s + 1) * cols].astype(F32), own)
    own = own.astype(BF16)
    place = iota((rows, 3 * RANK), 1) // RANK
    granks = jnp.zeros((rows, 3 * RANK), F32)
    for j in range(3):
        granks = jnp.where(place == j, against(grads_all[:, j * cols : (j + 1) * cols], own), granks)
    width = norms.shape[1] - LANES
    down = contract(granks.astype(BF16), norms[:, :width]).astype(BF16)
    both = contract(norms[:, width:], grads_all[...]).astype(BF16)
    for j in range(3):
        row = j * RANK
        upgrad_ref[row : row + RANK, :] = both[row : row + RANK, j * cols : (j + 1) * cols]
        for s in range(seq):
            out_ref[s, tokens:, j * cols : (j + 1) * cols] = down[row : row + RANK, s * cols : (s + 1) * cols]


def pick_chosen(tables, index):
    tokens = index.shape[0]
    low = index & 127
    key = (index >> 7) + (iota((tokens, LANES), 1) // PICKS) * (NSUB // LANES)
    total = jnp.zeros((tokens, LANES), F32)
    for h in range(MHEADS):
        for c in range(NSUB // LANES):
            found = lane_pick(tables[h][:, c * LANES : (c + 1) * LANES], low)
            total = jnp.where(key == h * (NSUB // LANES) + c, found, total)
    return total


def group_reduce(values, reducer, fill):
    group = iota(values.shape, 1) // PICKS
    total = jnp.zeros(values.shape, F32)
    for h in range(MHEADS):
        one = reducer(jnp.where(group == h, values, fill), axis=1, keepdims=True)
        total = jnp.where(group == h, one, total)
    return total


def middle_kernel(
    ready, adapter, o_ref, x_ref, gain_ref, mix_ref, w_in_any, w_out_any, dn_any, up_any,
    left_ref, right_ref, same_ref, ahead_ref, sent_ref, att_ref, rank_ref, mid_ref, norm_ref, gate_ref, w, dn, up, sems,
):
    groups = o_ref.shape[0]
    a = adapter[0]
    copies = fetch(
        [(dn_any.at[3, a], dn.at[0]), (dn_any.at[5, a], dn.at[1]), (up_any.at[3, a], up.at[0]), (up_any.at[5, a], up.at[1]),
         (w_out_any.at[0], w.at[0]), (w_in_any.at[4], w.at[1]), (w_in_any.at[3], ahead_ref)],
        sems,
    )
    tokens = att_ref.shape[0]
    attended = jnp.concatenate([o_ref[s, 0:tokens, :] for s in range(groups)], axis=1)
    sent_ref[...] = o_ref[:, tokens:, :]
    ready.send(sent_ref)
    att_ref[...] = attended
    ready.send(att_ref)
    for copy in copies[:4]:
        copy.wait()
    rank_three = against(attended, dn[0]).astype(BF16)
    extra = product(rank_three, up[0])
    copies[4].wait()
    ready(x_ref, gain_ref)
    middle = x_ref[...].astype(F32) + (product(attended, w[0]) + extra)
    mid_ref[...] = middle
    normed = (middle * inverse_norm(middle) * gain_row(gain_ref)).astype(BF16)
    norm_ref[...] = normed
    same_ref[...] = normed
    ready.send(mid_ref, norm_ref)
    rank_five = against(normed, dn[1]).astype(BF16)
    rank_ref[0] = rank_three
    rank_ref[1] = rank_five
    extra = product(rank_five, up[1])
    copies[5].wait()
    gate = product(normed, w[1]) + extra
    gate_ref[...] = gate
    ready.send(rank_ref, gate_ref)
    ready(mix_ref)
    memory_grad = (mix_ref[...].astype(F32) * (gate * jax.nn.sigmoid(gate))).astype(BF16)
    half = left_ref.shape[1]
    left_ref[...] = memory_grad[:, :half]
    right_ref[...] = memory_grad[:, half:]
    copies[6].wait()


def scores_kernel(
    owners, ready, adapter, normed_ref, w_ref, picks_ref, slot_ref, keys_ref, dn_any, up_any,
    send_ref, rank_ref, weight_ref, dn, up, sems,
):
    a = adapter[0]
    copies = fetch([(dn_any.at[4, a], dn), (up_any.at[4, a], up)], sems)
    normed = normed_ref[...]
    copies[0].wait()
    ranks = against(normed, dn[...]).astype(BF16)
    rank_ref[...] = ranks
    copies[1].wait()
    extra = product(ranks, up[...])
    query = (product(normed, w_ref[...]) + extra).astype(BF16)
    ready()
    ready.send(rank_ref)
    first, second = [], []
    for h in range(MHEADS):
        base = 2 * h * KHALF
        first.append(against(query[:, base : base + KHALF], keys_ref[0, h]))
        second.append(against(query[:, base + KHALF : base + 2 * KHALF], keys_ref[1, h]))
    picks = picks_ref[...]
    scores = pick_chosen(first, picks // NSUB) + pick_chosen(second, picks % NSUB)
    exponent = jnp.exp(scores - group_reduce(scores, jnp.max, NEG))
    weights = exponent / group_reduce(exponent, jnp.sum, 0.0)
    weight_ref[...] = weights
    ready.send(weight_ref)
    send_ref[...] = to_slots(weights, slot_ref, owners).astype(BF16)


def to_slots(weights, slot_ref, owners):
    tokens = weights.shape[0]
    capacity = 2 * MHEADS * tokens // owners
    lane_group = iota((tokens, LANES), 1) // PICKS
    tiled = [
        tile_groups(jnp.where(lane_group == h, weights, 0.0), MHEADS).astype(BF16) for h in range(MHEADS)
    ]
    place = iota((owners * 8, tokens), 0)
    base = (place // 8) * capacity + place % 8
    out_group = iota((owners * 8, LANES), 1) // PICKS
    total = jnp.zeros((owners * 8, LANES), F32)
    for g in range(capacity // 8):
        part = jnp.zeros((owners * 8, LANES), F32)
        for h in range(MHEADS):
            chosen = jnp.where(base + g * 8 == slot_ref[h : h + 1, :], 1.0, 0.0).astype(BF16)
            part = part + product(chosen, tiled[h])
        total = jnp.where(out_group == g, part, total)
    return total


def plane_hits(slots_ref, k, plane, seq, capacity):
    tokens = slots_ref.shape[2]
    place = plane * (seq * capacity) + iota((seq * capacity, tokens), 0)
    chosen = jnp.zeros((seq * capacity, tokens), F32)
    for h in range(MHEADS):
        chosen = jnp.where(place == slots_ref[k, h : h + 1, :], 1.0, chosen)
    return chosen.astype(BF16)


def scatter_kernel(ready, slots_ref, *refs):
    ready()
    out_ref = refs[-1]
    seq, batches, capacity, wide = out_ref.shape
    plane = lax.axis_index("batch")
    for k in range(batches):
        chosen = plane_hits(slots_ref, k, plane, seq, capacity)
        rows = product(chosen, refs[k][...]).astype(BF16)
        source = lax.rem(plane + (batches - k), batches)
        out_ref[:, pl.ds(source, 1)] = rows.reshape(seq, 1, capacity, wide)


def gather_kernel(ready, slots_ref, back_ref, *refs):
    ready()
    seq, batches, capacity, wide = back_ref.shape
    plane = lax.axis_index("batch")
    for k in range(batches):
        chosen = plane_hits(slots_ref, k, plane, seq, capacity)
        source = lax.rem(plane + (batches - k), batches)
        rows = back_ref[:, pl.ds(source, 1)].reshape(seq * capacity, wide)
        refs[k][...] = contract(chosen, rows).astype(BF16)


def memory_kernel(batches, ready, adapter, gate_ref, mix_ref, *refs):
    w_in_any, dn_any, up_any, mixed_ref, grank_ref, ggate_ref, part_ref, w, dn, up, sems = refs[batches:]
    a = adapter[0]
    copies = fetch([(dn_any.at[5, a], dn), (up_any.at[5, a], up), (w_in_any.at[4], w)], sems)
    ready()
    memory = refs[0][...].astype(F32)
    for k in range(1, batches):
        memory = memory + refs[k][...].astype(F32)
    gate = gate_ref[...]
    sigmoid = jax.nn.sigmoid(gate)
    mixed_ref[...] = (memory * (gate * sigmoid)).astype(BF16)
    ggate = (mix_ref[...].astype(F32) * memory * sigmoid * (1.0 + gate * (1.0 - sigmoid))).astype(BF16)
    ggate_ref[...] = ggate
    for copy in copies[:2]:
        copy.wait()
    granks = against(ggate, up[...]).astype(BF16)
    grank_ref[...] = granks
    extra = product(granks, dn[...])
    copies[2].wait()
    ready.send(mixed_ref, ggate_ref, grank_ref)
    part_ref[...] = against(ggate, w[...]) + extra


def output_kernel(ready, adapter, mixed_ref, mid_ref, w_out_any, dn_any, up_any, out_ref, rank_ref, w, dn, up, sems):
    a = adapter[0]
    copies = fetch([(dn_any.at[6, a], dn), (up_any.at[6, a], up), (w_out_any.at[1], w)], sems)
    ready()
    mixed = mixed_ref[...]
    for copy in copies[:2]:
        copy.wait()
    ranks = against(mixed, dn[...]).astype(BF16)
    rank_ref[...] = ranks
    extra = product(ranks, up[...])
    copies[2].wait()
    out_ref[...] = (mid_ref[...] + (product(mixed, w[...]) + extra)).astype(BF16)


def query_kernel(
    owners, rows_dev, ready, length, adapter, back_ref, slot_ref, picks_ref, weight_ref, part_ref, mid_ref, cot_ref, gain_ref,
    keys_ref, w_in_any, w_out_any, dn_any, up_any,
    go_ref, gquery_ref, grank_ref, gmid_ref, w, dn, up, turned, spots, sems,
):
    groups, tokens, cols = go_ref.shape
    a = adapter[0]
    ready(slot_ref, weight_ref)
    capacity = 2 * MHEADS * tokens // owners
    slots = iota((tokens, owners * 8), 1)
    base = (slots // 8) * capacity + slots % 8
    lane_group = iota((tokens, LANES), 1) // PICKS
    back = back_ref[...]
    gw = jnp.zeros((tokens, LANES), F32)
    for h in range(MHEADS):
        part = jnp.zeros((tokens, LANES), F32)
        for g in range(capacity // 8):
            chosen = jnp.where(base + g * 8 == slot_ref[:, h : h + 1], 1.0, 0.0).astype(BF16)
            part = jnp.where(lane_group == g, product(chosen, back), part)
        gw = jnp.where(lane_group == h, tile_groups(part, MHEADS), gw)
    weights = weight_ref[...]
    gscore = jnp.transpose(weights * (gw - group_reduce(weights * gw, jnp.sum, 0.0)))
    turned[...] = gscore
    ready(picks_ref, keys_ref)
    ready.begin()
    copies = fetch(
        [(dn_any.at[3, a], dn.at[0]), (dn_any.at[4, a], dn.at[1]), (up_any.at[3, a], up.at[0]),
         (up_any.at[4, a], up.at[1]), (w_in_any.at[3], w.at[0]), (w_out_any.at[0], w.at[1])],
        sems,
    )
    span = rows_dev // NSUB

    def head(h, carry):
        def one(r, sums):
            pick = picks_ref[h, pl.ds(r, 1), :]
            value = turned[pl.ds(h * PICKS + r, 1), :]
            low = jnp.where((pick // NSUB) % span == iota((8, tokens), 0), value, 0.0)
            hit = (pick % NSUB).astype(jnp.int16) == lax.broadcasted_iota(jnp.int16, (NSUB, tokens), 0)
            return sums[0] + low, sums[1] + jnp.where(hit, value.astype(BF16), jnp.zeros((), BF16))

        start = (jnp.zeros((8, tokens), F32), jnp.zeros((NSUB, tokens), BF16))
        first, second = lax.fori_loop(0, PICKS, one, start, unroll=QUERY_UNROLL)
        origin = picks_ref[h, 0:1, :] // rows_dev
        place = iota((NSUB, tokens), 0)
        wide = jnp.concatenate([first[:span]] * (NSUB // span), axis=0)
        wide = jnp.where(place // span == origin, wide, 0.0)
        spots[h, 0] = wide.astype(BF16)
        spots[h, 1] = second
        return carry

    lax.fori_loop(0, MHEADS, head, 0)
    halves = [contract(spots[h, half], keys_ref[half, h]) for h in range(MHEADS) for half in range(2)]
    gquery = jnp.concatenate(halves, axis=1).astype(BF16)
    gquery_ref[...] = gquery
    ready.send(gquery_ref)
    ready()
    for copy in copies[:4]:
        copy.wait()
    granks = against(gquery, up[1]).astype(BF16)
    grank_ref[1] = granks
    extra = product(granks, dn[1])
    copies[4].wait()
    gnormed = against(gquery, w[0]) + extra + part_ref[...]
    middle = mid_ref[...]
    gmid = cot_ref[...].astype(F32) + norm_back(middle, inverse_norm(middle), gain_row(gain_ref), gnormed)
    gmid_ref[...] = gmid
    ready.send(gmid_ref)
    low = gmid.astype(BF16)
    granks = against(low, up[0]).astype(BF16)
    grank_ref[0] = granks
    ready.send(grank_ref)
    extra = product(granks, dn[0])
    copies[5].wait()
    go = against(low, w[1]) + extra
    row = lax.axis_index("seq") * tokens + iota((tokens, 1), 0)
    go = jnp.where(row < length[0], go, 0.0).astype(BF16)
    for s in range(groups):
        go_ref[s] = go[:, s * cols : (s + 1) * cols]


def place_columns(out_ref, row, values):
    groups, _, cols = out_ref.shape
    low = values.astype(BF16)
    for s in range(groups):
        out_ref[s, row : row + values.shape[0], :] = low[:, s * cols : (s + 1) * cols]


def factor_kernel(ready, att_ref, norm_ref, mixed_ref, gmid_ref, gquery_ref, ggate_ref, cot_ref, r35, r4, r6, g34, g5, g6, out_ref):
    ready()
    half = 4 * RANK
    sides = (
        (att_ref[...], gmid_ref[...].astype(BF16), r35[0], g34[0]),
        (norm_ref[...], gquery_ref[...], r4[...], g34[1]),
        (norm_ref[...], ggate_ref[...], r35[1], g5[...]),
        (mixed_ref[...], cot_ref[...], r6[...], g6[...]),
    )
    for j, (value, gy, rank, grank) in enumerate(sides):
        place_columns(out_ref, j * RANK, contract(grank, value))
        place_columns(out_ref, half + j * RANK, contract(rank, gy))


def late_kernel(ready, grads_ref, upgrad_ref, out_ref):
    seq, _, wide = grads_ref.shape
    cols = wide // 3
    tokens = grads_ref.shape[1] - RANK
    total = grads_ref[0, tokens:, :].astype(F32)
    for s in range(1, seq):
        total = total + grads_ref[s, tokens:, :].astype(F32)
    total = total.astype(BF16)
    for j in range(3):
        out_ref[j * RANK : (j + 1) * RANK, :] = total[:, j * cols : (j + 1) * cols]
    ready()
    out_ref[3 * RANK :, :] = upgrad_ref[...]


def entry_kernel(ready, adapter, grads_ref, x_ref, gain_ref, gmid_ref, w_any, dn_any, up_any, out_ref, w, gy, total, dn, up, sems):
    a = adapter[0]
    seq, _, wide = grads_ref.shape
    cols = wide // 3
    tokens = out_ref.shape[0]
    copies = fetch(
        [(up_any.at[j, a], up.at[pl.ds(RANK * j, RANK)]) for j in range(3)]
        + [(dn_any.at[j, a], dn.at[pl.ds(RANK * j, RANK)]) for j in range(3)]
        + [(w_any.at[j], w.at[j]) for j in range(3)],
        sems,
    )
    for j in range(3):
        for s in range(seq):
            gy[j, :, s * cols : (s + 1) * cols] = grads_ref[s, 0:tokens, j * cols : (j + 1) * cols]
    for copy in copies[:6]:
        copy.wait()
    place = iota((tokens, 3 * RANK), 1) // RANK
    granks = jnp.zeros((tokens, 3 * RANK), F32)
    for j in range(3):
        granks = jnp.where(place == j, against(gy[j], up[...]), granks)
    total[...] = product(granks.astype(BF16), dn[...])

    def one(j, carry):
        pltpu.make_async_copy(w_any.at[j], w.at[j], sems.at[6 + j]).wait()
        total[...] += against(gy[j], w[j])
        return carry

    lax.fori_loop(0, 3, one, 0)
    ready()
    x = x_ref[...].astype(F32)
    back = norm_back(x, inverse_norm(x), gain_row(gain_ref), total[...])
    out_ref[...] = (gmid_ref[...] + back).astype(BF16)


def sum_kernel(ready, parts_ref, out_ref):
    ready()
    total = parts_ref[0].astype(F32)
    for s in range(1, parts_ref.shape[0]):
        total = total + parts_ref[s].astype(F32)
    out_ref[...] = total.astype(BF16)


def stack_kernel(ready, *refs):
    for k in range(refs[-1].shape[0]):
        refs[-1][k] = refs[k][...]


def relative_marks(ids_ref, batches):
    plane = lax.axis_index("batch")
    absolute = adapter_marks(ids_ref, batches)
    marks = []
    for k in range(batches):
        source = lax.rem(plane + (batches - k), batches)
        mark = absolute[0]
        for b in range(1, batches):
            mark = jnp.where(source == b, absolute[b], mark)
        marks.append(mark)
    return marks


def adapter_marks(ids_ref, batches):
    step = ids_ref.shape[0] // batches
    return [ids_ref[b * step : b * step + 1, 0:1] // ADAPTER_STEP for b in range(batches)]


def spread_rows(even, odd, marks, runs, stage, sems):
    pairs, batches = even.shape[:2]
    seq = 2 * pairs
    me = lax.axis_index("seq")

    def part(s, k, start):
        place = me ^ s
        at = place // 2
        rows = even[at, k, pl.ds(start, RANK), :].astype(F32), odd[at, k, pl.ds(start, RANK), :].astype(F32)
        return jnp.where(lax.rem(place, 2) == 0, rows[0], rows[1])

    for target, origin, base, count in runs:

        def put(i, target=target, origin=origin, base=base):
            return pltpu.make_async_copy(stage.at[base + i], target.at[origin + i], sems.at[base + i])

        def one(i, carry, put=put, base=base):
            start = pl.multiple_of((base + i) * RANK, RANK)
            rows = [
                jnp.concatenate([part(s, k, start) for s in range(seq)], axis=1)
                for k in range(batches)
            ]
            for k in range(ADAPTERS):
                total = jnp.zeros(rows[0].shape, F32)
                for row, mark in zip(rows, marks, strict=True):
                    total = total + jnp.where(mark == k, row, 0.0)
                stage[base + i, k] = total
            put(i).start()
            return carry

        lax.fori_loop(0, count, one, 0)
    for target, origin, base, count in runs:
        for i in range(count):
            pltpu.make_async_copy(stage.at[base + i], target.at[origin + i], sems.at[base + i]).wait()


def spread_kernel(batches, ready, ids_ref, even, odd, down_any, up_any, stage, sems):
    ready()
    marks = relative_marks(ids_ref, batches)
    spread_rows(even, odd, marks, ((down_any, 3, 0, 4), (up_any, 3, 4, 4)), stage, sems)


def last_spread_kernel(batches, ready, ids_ref, down_in, up_in, even, odd, down_any, up_any, stage, sems):
    ready()
    marks = relative_marks(ids_ref, batches)
    spread_rows(even, odd, marks, ((down_any, 0, 0, 3), (up_any, 0, 3, 3)), stage, sems)


def along(values, axis, step, size):
    return lax.ppermute(values, axis, [(i, (i + step) % size) for i in range(size)])


def across(values, axis, mask, size):
    return lax.ppermute(values, axis, [(i, i ^ mask) for i in range(size)])


def to_pairs(values, axis, size):
    return [values] + [across(values, axis, m, size) for m in range(2, size, 2)]


def stacked(values, name, kind="V"):
    shape = shaped((len(values), *values[0].shape), values[0].dtype)
    return call(stack_kernel, name, "V" * len(values), [(kind, shape)], values)[0]


def exchange(values, axes):
    return lax.all_to_all(values, axes, split_axis=0, concat_axis=0, tiled=True)


def body(
    inputs, lengths, adapter_index, memory_picks, input_weights, output_weights, adapter_down, adapter_up,
    attention_gain, memory_gain, half_keys, memory_values, cotangent,
):
    both = ("batch", "seq")
    batches, seq = lax.axis_size("batch"), lax.axis_size("seq")
    owners = batches * seq
    tokens, width = inputs.shape[1], inputs.shape[2]
    rows, cols, half = tokens * seq, width // seq, width // 2
    rows_dev = memory_values.shape[0]
    capacity = 2 * tokens * MHEADS // owners
    groups = capacity // 8
    items = owners * capacity
    block = min(owners * 8, 256)
    small_block = RECALL_ROWS
    carried = 2 * groups * PICKS // cols * batches * 8
    x, cot = inputs[0], cotangent[0]
    down = jnp.swapaxes(adapter_down, 2, 3)
    gain_one, gain_two = attention_gain, memory_gain
    picks = jnp.transpose(memory_picks[0], (1, 2, 0))
    matrix = pltpu.VMEM((width, width), BF16)
    pair = pltpu.VMEM((2, width, width), BF16)
    triple = pltpu.VMEM((3, width, width), BF16)
    small = pltpu.VMEM((RANK, width), BF16)
    two_small = pltpu.VMEM((2, RANK, width), BF16)
    three_small = pltpu.VMEM((3 * RANK, width), BF16)
    token_low, token_wide = shaped((tokens, width), BF16), shaped((tokens, width), F32)
    token_rank, token_lanes = shaped((tokens, RANK), BF16), shaped((tokens, LANES), F32)
    fixed = functools.partial

    qkv, normed = call(
        qkv_kernel, "qkv", "MLLHHH",
        [("V", shaped((seq, tokens, 3 * cols), BF16)), ("S", shaped((tokens, width + LANES), BF16))],
        (adapter_index, x, gain_one, input_weights, down, adapter_up), [triple, three_small, three_small, sema(9)],
    )
    qkv_all = exchange(qkv, "seq").reshape(rows, 3 * cols)

    slot, slot_col, pick, *ids_out = call(
        fixed(route_kernel, rows_dev, owners), "route", "ML",
        [("S", shaped((8, tokens), I32)), ("S", shaped((tokens, tokens), I32)), ("S", shaped((tokens, LANES), I32)),
         *[("V", shaped((seq * 8 + 8, LANES), I32)) for _ in range(batches)]],
        (adapter_index, picks), [pltpu.VMEM((owners * 8, LANES), I32)],
    )
    ids_out = [ids_out[0]] + [along(ids_out[k], "batch", k, batches) for k in range(1, batches)]
    mix_grad, grank_six = call(
        mix_back_kernel, "mixback", "MLHHH", [("S", token_low), ("S", token_rank)],
        (adapter_index, cot, output_weights, down, adapter_up), [matrix, small, small, sema(3)],
    )

    qkv_all, ids_out, mix_grad = lax.optimization_barrier((qkv_all, ids_out, mix_grad))
    attended, lse, slots, qkv_saved = call(
        fixed(attend_kernel, groups, batches), "attend", "MV" + "V" * batches,
        [("V", shaped((seq, tokens + carried, cols), BF16)), ("S", shaped((8, rows), F32)),
         ("S", shaped((batches, 8, LANES), I32)), ("H", shaped((rows, 3 * cols), BF16))],
        (lengths, qkv_all, *ids_out),
        [pltpu.VMEM((rows, LANES), BF16), pltpu.VMEM((LANES, rows), BF16), pltpu.VMEM((LANES, rows), F32), sema(1)],
    )
    o_all = exchange(attended, "seq")
    normed, attended = lax.optimization_barrier((normed, attended))
    normed_all = to_pairs(normed, "seq", seq)

    left, right, same_two, ahead, sent, att, rank_pair, middle, normed_two, gate = call(
        middle_kernel, "middle", "MVLLLHHHH",
        [("V", shaped((tokens, half), BF16)), ("V", shaped((tokens, half), BF16)), ("V", token_low),
         ("V", shaped((width, width), BF16)), ("S", shaped((seq, carried, cols), BF16)), ("S", token_low),
         ("S", shaped((2, tokens, RANK), BF16)), ("S", token_wide), ("S", token_low), ("S", token_wide)],
        (adapter_index, o_all, x, gain_two, mix_grad, input_weights, output_weights, down, adapter_up),
        [pair, two_small, two_small, sema(7)],
    )
    lefts = [left] + [along(left, "batch", k, batches) for k in range(1, batches)]
    weight_out, rank_four, weights = call(
        fixed(scores_kernel, owners), "scores", "MVVLLLHH",
        [("V", shaped((owners * 8, LANES), BF16)), ("S", token_rank), ("S", token_lanes)],
        (adapter_index, same_two, ahead, pick, slot, half_keys, down, adapter_up), [small, small, sema(2)],
    )
    weight_out, normed_all = lax.optimization_barrier((weight_out, normed_all))
    weight_in = exchange(weight_out.reshape(owners, 8, LANES), both).reshape(owners * 8, LANES)
    right, lefts = lax.optimization_barrier((right, lefts))
    rights = [right] + [along(right, "batch", k, batches) for k in range(1, batches)]

    def scatter(parts, name):
        out = [("V", shaped((seq, batches, capacity, half), BF16))]
        return call(scatter_kernel, name, "L" + "V" * batches, out, (slots, *parts))[0]

    left_out = scatter(lefts, "scatterleft")
    normed_all, left_out = lax.optimization_barrier((normed_all, left_out))
    normed_all = stacked(normed_all, "pairsnorm", "S")
    sent, left_out = lax.optimization_barrier((sent, left_out))
    ids, index = call(
        fixed(prepare_kernel, groups, rows_dev, batches), "prepare", "L",
        [("S", shaped((owners * 8, LANES), I32)), ("H", shaped((items, rows_dev), jnp.int16))], (sent,),
        [pltpu.VMEM((2, LANES, rows_dev), jnp.int16), pltpu.VMEM((owners * 8 // LANES, LANES, LANES), I32), sema(2)],
    )
    left_out, weight_in, normed_all = lax.optimization_barrier((left_out, weight_in, normed_all))
    normed_all = (normed_all, across(normed_all, "seq", 1, seq))
    left_in = exchange(left_out, "seq").reshape(items, half)

    (sums,) = call(
        fixed(recall_kernel, groups), "recall", "VHH", [("H", shaped((seq, batches, capacity, width), BF16))],
        (weight_in, index, memory_values),
        [pltpu.VMEM((rows_dev, width), BF16), pltpu.VMEM((2, small_block, rows_dev), jnp.int16), pltpu.VMEM((2, small_block, rows_dev), BF16),
         pltpu.VMEM((2, small_block // 8, 8, width), BF16), sema(3 + 2 * (small_block // (8 * seq)))],
        flops=1 << 12,
    )
    sums, left_in = lax.optimization_barrier((sums, left_in))
    back = exchange(sums, "seq")

    def recall_back(part, name, grads, kind, dtype, *before):
        return call(
            fixed(recall_back_kernel, part, batches, groups), name, "L" + "L" * part + "VH",
            [(kind, shaped((owners * 8, LANES), dtype))], (ids, *before, grads, memory_values),
            [pltpu.VMEM((rows_dev, half), BF16), pltpu.VMEM((block, rows_dev), BF16), sema(1)],
        )[0]

    rights, normed_all = lax.optimization_barrier((rights, normed_all))
    right_out = scatter(rights, "scatterright")
    found_left = recall_back(0, "recallleft", left_in, "S", F32)
    right_out, back, found_left = lax.optimization_barrier((right_out, back, found_left))
    right_in = exchange(right_out, "seq").reshape(items, half)
    pieces = call(
        gather_kernel, "gather", "LV", [("V", token_low) for _ in range(batches)], (slots, back),
    )
    pieces = [pieces[0]] + [along(pieces[k], "batch", batches - k, batches) for k in range(1, batches)]
    found = recall_back(1, "recallright", right_in, "V", BF16, found_left)
    found_back = exchange(found.reshape(owners, 8, LANES), both).reshape(owners * 8, LANES)

    mixed, grank_five, ggate, part = call(
        fixed(memory_kernel, batches), "memory", "MLL" + "V" * batches + "HHH",
        [("S", token_low), ("S", token_rank), ("S", token_low), ("V", token_wide)],
        (adapter_index, gate, mix_grad, *pieces, input_weights, down, adapter_up), [matrix, small, small, sema(3)],
    )

    go, gquery, grank_pair, gmid = call(
        fixed(query_kernel, owners, rows_dev), "query", "MMVLLLVDDDLHHHH",
        [("V", shaped((seq, tokens, cols), BF16)), ("S", token_low), ("S", shaped((2, tokens, RANK), BF16)), ("S", token_wide)],
        (lengths, adapter_index, found_back, slot_col, picks, weights, part, middle, cot, gain_two, half_keys,
         input_weights, output_weights, down, adapter_up),
        [pair, two_small, two_small, pltpu.VMEM((LANES, tokens), F32), pltpu.VMEM((MHEADS, 2, NSUB, tokens), BF16), sema(6)],
    )
    go_all = exchange(go, "seq").reshape(rows, cols)
    mixed, go = lax.optimization_barrier((mixed, go))
    output, rank_six = call(
        output_kernel, "output", "MLLHHH", [("S", token_low), ("S", token_rank)],
        (adapter_index, mixed, middle, output_weights, down, adapter_up), [matrix, small, small, sema(3)],
    )
    (factors,) = call(
        factor_kernel, "factors", "L" * 13, [("V", shaped((seq, 8 * RANK, cols), BF16))],
        (att, normed_two, mixed, gmid, gquery, ggate, cot, rank_pair, rank_four, rank_six, grank_pair, grank_five, grank_six),
    )
    factors, go_all = lax.optimization_barrier((factors, go_all))
    early_parts = exchange(factors, "seq")

    grads, up_grads = call(
        attend_back_kernel, "attendback", "MMLVLHHH",
        [("V", shaped((seq, tokens + RANK, 3 * cols), BF16)), ("S", shaped((3 * RANK, cols), BF16))],
        (lengths, adapter_index, qkv_saved, go_all, lse, *normed_all, adapter_up),
        [pltpu.VMEM((rows, LANES), F32), pltpu.VMEM((rows, LANES), F32), pltpu.VMEM((LANES, rows), F32),
         pltpu.VMEM((rows, LANES), BF16), pltpu.VMEM((LANES, rows), BF16), pltpu.VMEM((rows, LANES), BF16),
         pltpu.VMEM((rows, 3 * cols), BF16), pltpu.VMEM((rows, width + LANES), BF16), three_small, sema(3 + seq)],
    )
    grads, early_parts = lax.optimization_barrier((grads, early_parts))
    grads_all = exchange(grads, "seq")
    (some,) = call(sum_kernel, "sumearly", "V", [("V", shaped((8 * RANK, cols), BF16))], (early_parts,))
    some = [some] + [along(some, "batch", k, batches) for k in range(1, batches)]
    some = stacked(some, "stackearly")
    some = to_pairs(some, "seq", seq)
    (late_sum,) = call(late_kernel, "late", "VL", [("V", shaped((6 * RANK, cols), BF16))], (grads_all, up_grads))
    (grad_input,) = call(
        entry_kernel, "entry", "MVLLLHHH", [("S", token_low)],
        (adapter_index, grads_all, x, gain_one, gmid, input_weights, down, adapter_up),
        [triple, pltpu.VMEM((3, tokens, width), BF16), pltpu.VMEM((tokens, width), F32), three_small, three_small, sema(9)],
    )
    late_sums = [late_sum] + [along(late_sum, "batch", k, batches) for k in range(1, batches)]
    some = stacked(some, "pairsearly")
    late_sums, some, grad_input = lax.optimization_barrier((late_sums, some, grad_input))
    late_all = to_pairs(stacked(late_sums, "stacklate"), "seq", seq)
    some = (some, across(some, "seq", 1, seq))
    full = shaped((7, ADAPTERS, RANK, width), F32)
    grad_down, grad_up = call(
        fixed(spread_kernel, batches), "spread", "LVV", [("H", full), ("H", full)], (ids, *some),
        [pltpu.VMEM((8, ADAPTERS, RANK, width), F32), sema(8)],
    )
    late_all, grad_down, grad_up = lax.optimization_barrier((late_all, grad_down, grad_up))
    late_all = stacked(late_all, "pairslate")
    late_all = (late_all, across(late_all, "seq", 1, seq))
    grad_down, grad_up = call(
        fixed(last_spread_kernel, batches), "lastspread", "LHHVV", [("H", full), ("H", full)],
        (ids, grad_down, grad_up, *late_all),
        [pltpu.VMEM((6, ADAPTERS, RANK, width), F32), sema(6)],
        aliases={1: 0, 2: 1},
    )
    return (output[None], grad_input[None], jnp.swapaxes(grad_down, 2, 3), grad_up)


def solution(mesh):
    split = P("batch", "seq", None)
    return jax.shard_map(
        body,
        mesh=mesh,
        in_specs=(
            split, P("batch"), P("batch"), P("batch", "seq", None, None), P(), P(), P(), P(), P(), P(), P(),
            P(("batch", "seq"), None), split,
        ),
        out_specs=(split, split, P(), P()),
        check_vma=False,
    )
```
